32 devices in a mesh: gx: 4 (over z), gy: 8 (over y, x, core).
Axes of the slice: x: 2, y: 2, z: 4, core: 2. Of those that a mesh axis runs over, the one named last changes fastest.
Arguments:
- media: bfloat16 [16384, 1536], P(('gx', 'gy')), may hold values from -6 to 6
- latents: bfloat16 [2048, 1536], P(('gx', 'gy')), may hold values from -6 to 6
- frame_counts: int32 [8, 4], replicated, may hold values from 1 to 8, 16 in all within a row
- time_index: int32 [128], P(('gx', 'gy')), may hold values from 0 to 7
- valid: int32 [16384], P(('gx', 'gy')), may hold values from 0 to 1
- time_table: bfloat16 [8, 1536], P(None, ('gx', 'gy')), may hold values from -3 to 3
- media_gain: bfloat16 [1536], P(('gx', 'gy')), may hold values from 0.5 to 1.5
- latent_gain: bfloat16 [1536], P(('gx', 'gy')), may hold values from 0.5 to 1.5
- ffn_gain: bfloat16 [1536], P(('gx', 'gy')), may hold values from 0.5 to 1.5
- w_query: bfloat16 [1536, 1536], P(('gx', 'gy')), may hold values from -0.3125 to 0.3125
- w_key: bfloat16 [1536, 1536], P(('gx', 'gy')), may hold values from -0.15625 to 0.15625
- w_value: bfloat16 [1536, 1536], P(('gx', 'gy')), may hold values from -0.15625 to 0.15625
- w_out: bfloat16 [1536, 1536], P(('gx', 'gy')), may hold values from -0.625 to 0.625
- w_up: bfloat16 [1536, 6144], P(('gx', 'gy')), may hold values from -0.15625 to 0.15625
- w_down: bfloat16 [6144, 1536], P(('gx', 'gy')), may hold values from -0.078125 to 0.078125
- cotangent: bfloat16 [2048, 1536], P(('gx', 'gy')), may hold values from -6 to 6
Outputs:
- new_latents: bfloat16 [2048, 1536], P(('gx', 'gy'))
- media_grad: float32 [16384, 1536], P(('gx', 'gy'))
- latents_grad: float32 [2048, 1536], P(('gx', 'gy'))
- time_table_grad: float32 [8, 1536], P(None, ('gx', 'gy'))
- media_gain_grad: float32 [1536], P(('gx', 'gy'))
- latent_gain_grad: float32 [1536], P(('gx', 'gy'))
- feedforward_gain_gradient: float32 [1536], P(('gx', 'gy'))
- w_query_grad: float32 [1536, 1536], P(('gx', 'gy'))
- w_key_grad: float32 [1536, 1536], P(('gx', 'gy'))
- w_value_grad: float32 [1536, 1536], P(('gx', 'gy'))
- w_out_grad: float32 [1536, 1536], P(('gx', 'gy'))
- w_up_grad: float32 [1536, 6144], P(('gx', 'gy'))
- w_down_grad: float32 [6144, 1536], P(('gx', 'gy'))
The draws below stay inside these ranges and needn't reach their ends.
Inputs may be any that keep to these rules, and one draw needn't show every extreme that they name: `frame_counts`: entry (g, j) counts the frames of item j times the number of rows plus g, which lie in order of j; each row sums to 4 times its number of entries and holds one entry of exactly 8.
All inputs are finite; a program needn't handle non-finite values.
Results may differ from the reference program's by a relative error of at most 0.015.
Values may be sent and summed in bfloat16 or wider, within the bound.
A program may use at most 448 MiB of HBM per device.

```python
import math
import jax
import jax.numpy as jnp
import numpy as np
from jax import lax

D = 1536
H = 16
HD = 96
FF = 6144
L = 64
NT = 8
CLIP = 8
FR_DEV = 4
PATCH = 128
ITEMS = 32
FRAMES = 128
MEDIA = 16384
N_GX = 4
N_GY = 8


def draw_valid(key, part):
    position = jnp.arange(MEDIA, dtype=jnp.int32)
    threshold = 300 + 650 * position // MEDIA
    ticket = jax.random.randint(key, (MEDIA,), 0, 1000, dtype=jnp.int32)
    return (ticket < threshold).astype(jnp.int32)


def place_ends(result, stream_key, smallest, top_value):
    dims = result.shape
    place = [jax.random.randint(jax.random.fold_in(stream_key, axis), (), 0, dims[axis]) for axis in range(len(dims))]
    result = result.at[tuple(place)].set(smallest)
    longest = dims.index(max(dims))
    place[longest] = (place[longest] + 1) % dims[longest]
    return result.at[tuple(place)].set(top_value)


def levels(key, extent, cuts, low, high):
    def one(dim, parts):
        heights = jax.random.uniform(jax.random.fold_in(jax.random.fold_in(key, 6), dim), (parts,), jnp.float32, low / len(cuts), high / len(cuts))
        return jnp.repeat(jnp.exp(heights), extent[dim] // parts).reshape((-1,) + (1,) * (len(extent) - dim - 1))

    level = one(*cuts[0])
    for cut in cuts[1:]:
        level = level * one(*cut)
    return level


def length_profile(number_of, total, limit, skew):
    weights = [(1 << 20) // math.isqrt(grade ** skew) + 1 for grade in range(2, number_of + 1)]
    spare, counts = total - limit - (number_of - 1), [1] * (number_of - 1)
    while spare > 0:
        free = [i for i in range(number_of - 1) if counts[i] < limit]
        pool, left = sum([weights[i] for i in free]), spare
        for i in free:
            more = min(limit - counts[i], max(1, left * weights[i] // pool), spare)
            counts[i] = counts[i] + more
            spare = spare - more
    return np.array([limit] + counts)


def ragged(own_key, number_of, total, reach, lean):
    if number_of == 2:
        one = jax.random.randint(own_key, (), max(1, total - reach), min(reach, total - 1) + 1)
        return jnp.stack([one, total - one])
    sizes = jnp.asarray(length_profile(number_of, total, reach, lean), jnp.int32)
    pairs = (number_of - 1) // 2
    source_of, sink = sizes[1:1 + 2 * pairs:2], sizes[2:2 + 2 * pairs:2]
    slack = jnp.minimum(source_of - 1, reach - sink)
    passed = jax.random.randint(jax.random.fold_in(own_key, 1), (pairs,), 0, 1 << 20) % (slack + 1)
    sizes = sizes.at[1:1 + 2 * pairs:2].set(source_of - passed).at[2:2 + 2 * pairs:2].set(sink + passed)
    return sizes[jax.random.permutation(jax.random.fold_in(own_key, 2), number_of)]


def normal_values(stream_key, dims, width, limit, shards=(), held_as=jnp.bfloat16):
    result = jax.random.normal(stream_key, dims, jnp.float32) * width
    if len(shards) > 0:
        result = levels(stream_key, dims, shards, -0.22, 0.18) * result
    return jnp.clip(result, min=-limit, max=limit).astype(held_as)


def setup_inputs(seed: int = 0) -> dict:
    seeds = jax.random.split(jax.random.key(seed), 17)
    media = normal_values(seeds[0], (MEDIA, D), 1.0, 6.0, ((0, 32),))
    latents = normal_values(seeds[1], (ITEMS * L, D), 1.0, 6.0, ((0, 32),))
    frame_counts = jax.vmap(lambda own: ragged(own, N_GX, FR_DEV * N_GX, CLIP, 1))(jax.random.split(seeds[2], N_GY)).reshape((N_GY, N_GX)).astype(jnp.int32)
    time_index = place_ends(jax.random.randint(seeds[3], (FRAMES,), 0, NT), jax.random.fold_in(seeds[3], 1), 0, NT - 1).astype(jnp.int32)
    valid = draw_valid(jax.random.fold_in(seeds[16], 71), 0)
    time_table = normal_values(seeds[5], (NT, D), 0.5, 3.0, ((1, 32),))
    media_gain = jnp.clip(1.0 + 0.1 * jax.random.normal(seeds[6], (D,), jnp.float32), 0.5, 1.5).astype(jnp.bfloat16)
    latent_gain = jnp.clip(1.0 + 0.1 * jax.random.normal(seeds[7], (D,), jnp.float32), 0.5, 1.5).astype(jnp.bfloat16)
    ffn_gain = jnp.clip(1.0 + 0.1 * jax.random.normal(seeds[8], (D,), jnp.float32), 0.5, 1.5).astype(jnp.bfloat16)
    w_query = normal_values(seeds[9], (D, D), (D // 4) ** -0.5, 0.3125, ((0, 32),))
    w_key = normal_values(seeds[10], (D, D), D ** -0.5, 0.15625, ((0, 32),))
    w_value = normal_values(seeds[11], (D, D), D ** -0.5, 0.15625, ((0, 32),))
    w_out = normal_values(seeds[12], (D, D), (D // 16) ** -0.5, 0.625, ((0, 32),))
    w_up = normal_values(seeds[13], (D, FF), D ** -0.5, 0.15625, ((0, 32),))
    w_down = normal_values(seeds[14], (FF, D), FF ** -0.5, 0.078125, ((0, 32),))
    cotangent = normal_values(seeds[15], (ITEMS * L, D), 1.0, 6.0, ((0, 32),))
    return dict(media=media, latents=latents, frame_counts=frame_counts, time_index=time_index, valid=valid, time_table=time_table, media_gain=media_gain, latent_gain=latent_gain, ffn_gain=ffn_gain, w_query=w_query, w_key=w_key, w_value=w_value, w_out=w_out, w_up=w_up, w_down=w_down, cotangent=cotangent)


ENTROPY_WEIGHT = 4.0
NORM_STABILIZER = 1e-05
HIGHEST = lax.Precision.HIGHEST

@jax.custom_vjp
def low(v):
    return lax.optimization_barrier(v.astype(jnp.bfloat16)).astype(jnp.float32)

@jax.custom_vjp
def low_back(v):
    return v

def low_keep(v):
    return (low(v), None)

def low_pass(kept, grad):
    return (grad,)

def back_keep(v):
    return (v, None)

def back_low(kept, grad):
    return (low(grad),)
low.defvjp(low_keep, low_pass)
low_back.defvjp(back_keep, back_low)

def layer_norm(row_block, gain_row):
    row_mean = lax.optimization_barrier(jnp.mean(row_block, axis=-1, keepdims=True))
    centred = row_block - row_mean
    variance = lax.optimization_barrier(jnp.mean(centred * centred, axis=-1, keepdims=True))
    return centred * lax.rsqrt(variance + NORM_STABILIZER) * gain_row

def matmul(left_side, right_side):
    return jnp.dot(left_side, right_side, precision=HIGHEST, preferred_element_type=jnp.float32)

def frame_items(frame_counts):
    frame_ends = jnp.cumsum(frame_counts, axis=1).astype(jnp.int32)
    frame_number = jnp.arange(FRAMES, dtype=jnp.int32)
    block_id = (frame_number // FR_DEV).astype(jnp.int32)
    row_gy = (block_id % N_GY).astype(jnp.int32)
    position = (block_id // N_GY * FR_DEV + frame_number % FR_DEV).astype(jnp.int32)
    item_slot = lax.optimization_barrier(jnp.sum((frame_ends[row_gy] <= position[:, None]).astype(jnp.int32), axis=1)).astype(jnp.int32)
    return (item_slot * N_GY + row_gy).astype(jnp.int32)

def forward(media, latents, time_table, media_gain, latent_gain, ffn_gain, w_query, w_key, w_value, w_out, w_up, w_down, frame_item, time_index, valid, coefficient):
    score_scale = HD ** (-0.5)
    lat_norm = low(layer_norm(latents, latent_gain))
    queries = low(low_back(matmul(lat_norm, w_query)))
    latent_key = low(low_back(matmul(lat_norm, w_key)))
    latent_value = low(low_back(matmul(lat_norm, w_value)))
    query_head_count = queries.reshape(ITEMS, L, H, HD)
    key_heads = latent_key.reshape(ITEMS, L, H, HD)
    value_heads = latent_value.reshape(ITEMS, L, H, HD)
    latent_raw = low_back(jnp.einsum('ilhd,imhd->ilhm', query_head_count, key_heads, precision=HIGHEST))
    latent_score = latent_raw * score_scale
    latent_expo = jnp.exp(latent_score)
    totals = lax.optimization_barrier(jnp.sum(latent_expo, axis=-1))
    moment = lax.optimization_barrier(jnp.sum(latent_expo * latent_score, axis=-1))
    weighted = jnp.einsum('ilhm,imhd->ilhd', low(latent_expo), value_heads, precision=HIGHEST)

    def frame_block(pieces):
        media_part, time_part, valid_part, item_part = pieces
        onehot = (time_part[:, None] == jnp.arange(NT, dtype=jnp.int32)[None, :]).astype(jnp.float32)
        media_rows = media_part + matmul(onehot, time_table)[:, None, :]
        normed = low(layer_norm(media_rows, media_gain)).reshape(-1, D)
        key_rows = low(low_back(matmul(normed, w_key))).reshape(8, PATCH, H, HD)
        values = low(low_back(matmul(normed, w_value))).reshape(8, PATCH, H, HD)
        picked = query_head_count[item_part]
        raw_score = low_back(jnp.einsum('flhd,fphd->flhp', picked, key_rows, precision=HIGHEST))
        scaled = raw_score * score_scale
        exponent = jnp.where(valid_part[:, None, None, :] > 0, jnp.exp(scaled), jnp.zeros_like(scaled))
        block_sum = jnp.einsum('flhp,fphd->flhd', low(exponent), values, precision=HIGHEST)
        return (block_sum, lax.optimization_barrier(jnp.sum(exponent, axis=-1)), lax.optimization_barrier(jnp.sum(exponent * scaled, axis=-1)))
    shaped = (media.reshape(FRAMES // 8, 8, PATCH, D), time_index.reshape(-1, 8), valid.reshape(-1, 8, PATCH), frame_item.reshape(-1, 8))
    media_sums, media_totals, media_moments = lax.map(jax.checkpoint(frame_block), shaped)
    weighted = low_back(weighted + jax.ops.segment_sum(media_sums.reshape(FRAMES, L, H, HD), frame_item, num_segments=ITEMS))
    totals = totals + jax.ops.segment_sum(media_totals.reshape(FRAMES, L, H), frame_item, num_segments=ITEMS)
    moment = moment + jax.ops.segment_sum(media_moments.reshape(FRAMES, L, H), frame_item, num_segments=ITEMS)
    attention = weighted / totals[..., None]
    attn_low = low(attention).reshape(ITEMS * L, D)
    penalty = coefficient * jnp.sum(jnp.log(totals) - moment / totals)
    middle = latents + low_back(matmul(attn_low, w_out))
    ffn_normed = low(layer_norm(middle, ffn_gain))
    up_rows = low_back(matmul(ffn_normed, w_up))
    hidden = low(jax.nn.gelu(up_rows, approximate=False))
    return (middle + matmul(hidden, w_down), penalty)

def reference(media, latents, frame_counts, time_index, valid, time_table, media_gain, latent_gain, ffn_gain, w_query, w_key, w_value, w_out, w_up, w_down, cotangent):
    frame_item = frame_items(frame_counts)
    valid_total = jnp.sum(valid.astype(jnp.float32))
    coefficient = ENTROPY_WEIGHT * MEDIA / valid_total
    floats = tuple((array.astype(jnp.float32) for array in (media, latents, time_table, media_gain, latent_gain, ffn_gain, w_query, w_key, w_value, w_out, w_up, w_down)))

    def run_layer(*inputs):
        return forward(*inputs, frame_item, time_index, valid, coefficient)
    results, pull = jax.vjp(run_layer, *floats)
    grads = pull((cotangent.astype(jnp.float32), jnp.ones_like(results[1])))
    return (results[0].astype(jnp.bfloat16), grads[0], grads[1], grads[2], grads[3], grads[4], grads[5], grads[6], grads[7], grads[8], grads[9], grads[10], grads[11])
```

```python
from functools import partial

import jax
import jax.numpy as jnp
from jax import lax
from jax.experimental import pallas as pl
from jax.experimental.pallas import tpu as pltpu
from jax.sharding import PartitionSpec as P

H = 16


ENTROPY_WEIGHT = 4.0
NORM_STABILIZER = 1e-05
AXES = ("gx", "gy")
LINES = 4
PLANE = 4
HBM = pl.ANY
BF16 = jnp.bfloat16
F32 = jnp.float32


def here():
    z = lax.axis_index("gx")
    g = lax.axis_index("gy")
    return z, g, g // 2, g % 2


def sibling(g):
    return g + 1 - 2 * (g % 2)


def along_x(g):
    return g + 2 - 4 * ((g // 2) % 2)


def along_y(g):
    return (g + 4) % 8


def turn(z, k):
    return (z + k) % LINES


def greet(devices):
    barrier = pltpu.get_barrier_semaphore()
    for device in devices:
        pl.semaphore_signal(
            barrier, inc=1, device_id=device, device_id_type=pl.DeviceIdType.MESH
        )
    pl.semaphore_wait(barrier, len(devices))


def line_of(z, g):
    return [(turn(z, k), g) for k in (1, 2, 3)]


class Wires:
    def __init__(self, send_sems, recv_sems):
        self.send_sems, self.recv_sems, self.used, self.sent = send_sems, recv_sems, 0, []

    def send(self, source, target, device):
        n = self.used
        self.used += 1
        copy = pltpu.make_async_remote_copy(
            src_ref=source,
            dst_ref=target,
            send_sem=self.send_sems.at[n],
            recv_sem=self.recv_sems.at[n],
            device_id=device,
            device_id_type=pl.DeviceIdType.MESH,
        )
        copy.start()
        self.sent.append(copy)
        return copy

    def drain(self):
        for copy in self.sent:
            copy.wait_send()


class Spread:
    def __init__(self, wires, shard, slot, half, whole):
        self.wires, self.shard, self.slot, self.half, self.whole = wires, shard, slot, half, whole
        self.z, self.g, _, _ = here()
        self.zs = [turn(self.z, LINES - k) if k else self.z for k in range(LINES)]
        self.line, self.x, self.y, self.dx, self.dy, self.sib = {}, {}, {}, {}, {}, []

    def side(self, gy):
        return (self.z, gy)

    def to_sibling(self, source, where):
        if self.whole:
            self.sib.append(self.wires.send(source, where, self.side(sibling(self.g))))

    def first(self):
        own = self.slot(self.z, self.g)
        for k in (1, 3, 2):
            self.line[k] = self.wires.send(self.shard, own, (turn(self.z, k), self.g))
        self.x[0] = self.wires.send(self.shard, own, self.side(along_x(self.g)))
        self.y[0] = self.wires.send(self.shard, own, self.side(along_y(self.g)))
        self.to_sibling(self.shard, own)

    def column(self, k):
        self.line[k].wait_recv()
        held = self.slot(self.zs[k], self.g)
        self.x[k] = self.wires.send(held, held, self.side(along_x(self.g)))
        self.y[k] = self.wires.send(held, held, self.side(along_y(self.g)))
        self.to_sibling(held, held)

    def corner(self, k):
        self.x[k].wait_recv()
        held = self.slot(self.zs[k], along_x(self.g))
        part = self.half(held, 0)
        self.dy[k] = self.wires.send(part, part, self.side(along_y(self.g)))
        self.to_sibling(held, held)
        self.y[k].wait_recv()
        held = self.slot(self.zs[k], along_y(self.g))
        part = self.half(held, 1)
        self.dx[k] = self.wires.send(part, part, self.side(along_x(self.g)))
        self.to_sibling(held, held)

    def last(self, k):
        self.dy[k].wait_recv()
        self.dx[k].wait_recv()
        held = self.slot(self.zs[k], along_y(along_x(self.g)))
        self.to_sibling(held, held)

    def finish(self):
        for copy in self.sib:
            copy.wait_recv()


def spread_all(flows):
    for flow in flows:
        flow.first()
    for flow in flows:
        flow.corner(0)
    for k in (1, 3, 2):
        for flow in flows:
            flow.column(k)
    for k in (1, 3, 2):
        for flow in flows:
            flow.corner(k)
    for k in (0, 1, 3, 2):
        for flow in flows:
            flow.last(k)
    for flow in flows:
        flow.finish()


def spread_sems(flows, whole):
    return flows * (3 + 8 + 8 + (16 if whole else 0))


def columns_half(ref, which):
    width = ref.shape[-1] // 2
    return ref.at[..., pl.ds(which * width, width)]


def gather_kernel(count, small, whole, *refs):
    shards, outs = refs[:count], refs[count : 2 * count]
    send_sems, recv_sems, local_sems = refs[2 * count :]
    z, g, chip, core = here()
    others = line_of(z, g) + [(z, along_x(g)), (z, along_y(g))]
    if whole:
        others.append((z, sibling(g)))
    greet(others)
    wires = Wires(send_sems, recv_sems)

    def slot_of(out):
        if whole:
            return lambda zz, gg: out.at[zz * 8 + gg]
        return lambda zz, gg: out.at[zz * 4 + gg // 2]

    def rows_half(ref, which):
        rows = ref.shape[0] // 2
        return ref.at[pl.ds(which * rows, rows)]

    flows = [
        Spread(wires, shards[n], slot_of(outs[n]), rows_half if n in small else columns_half, whole)
        for n in range(count)
    ]
    kept = []
    for n in range(count):
        copy = pltpu.make_async_copy(shards[n], slot_of(outs[n])(z, g), local_sems.at[n])
        copy.start()
        kept.append(copy)
    spread_all(flows)
    for copy in kept:
        copy.wait()
    wires.drain()


def gather(shards, whole, ident, small=()):
    count = len(shards)
    slots = 32 if whole else 16
    sems = spread_sems(count, whole)
    return pl.pallas_call(
        partial(gather_kernel, count, small, whole),
        out_shape=[jax.ShapeDtypeStruct((slots,) + s.shape, s.dtype) for s in shards],
        in_specs=[pl.BlockSpec(memory_space=HBM)] * count,
        out_specs=[pl.BlockSpec(memory_space=HBM)] * count,
        scratch_shapes=[
            pltpu.SemaphoreType.DMA((sems,)),
            pltpu.SemaphoreType.DMA((sems,)),
            pltpu.SemaphoreType.DMA((count,)),
        ],
        compiler_params=pltpu.CompilerParams(collective_id=ident, has_side_effects=True),
        name="gather_%d" % ident,
    )(*shards)


def line_kernel(count, spread, *refs):
    sources, outs = refs[:count], refs[count : 2 * count]
    send_sems, recv_sems = refs[2 * count :]
    z, g, _, _ = here()
    greet(line_of(z, g))
    wires = Wires(send_sems, recv_sems)
    copies = []
    for k in (2, 1, 3):
        for source, out in zip(sources, outs):
            there = turn(z, k)
            piece = source if spread else source.at[there]
            copies.append(wires.send(piece, out.at[z], (there, g)))
    for source, out in zip(sources, outs):
        out[z] = source[...] if spread else source[z]
    for copy in copies:
        copy.wait_recv()
    wires.drain()


def along_line(arrays, spread, ident):
    count = len(arrays)
    shapes = [((LINES,) + a.shape) if spread else a.shape for a in arrays]
    return pl.pallas_call(
        partial(line_kernel, count, spread),
        out_shape=[jax.ShapeDtypeStruct(s, a.dtype) for s, a in zip(shapes, arrays)],
        in_specs=[pl.BlockSpec(memory_space=pltpu.VMEM)] * count,
        out_specs=[pl.BlockSpec(memory_space=pltpu.VMEM)] * count,
        scratch_shapes=[
            pltpu.SemaphoreType.DMA((3 * count,)),
            pltpu.SemaphoreType.DMA((3 * count,)),
        ],
        compiler_params=pltpu.CompilerParams(collective_id=ident, has_side_effects=True),
        name="line_%d" % ident,
    )(*arrays)


def add_slots(target, source, count):
    @pl.loop(0, count)
    def _(n):
        target[n] = (target[n].astype(F32) + source[n].astype(F32)).astype(target.dtype)


class Fold:
    def __init__(self, wires, parts, keep, whole, scratch, out, local_sem):
        self.wires, self.parts, self.whole, self.out = wires, parts, whole, out
        self.held, self.from_sib, self.cx, self.cy, self.fx, self.fy, self.fz = scratch
        self.z, self.g, self.chip, self.core = here()
        self.load = pltpu.make_async_copy(keep, self.held, local_sem)
        self.width = self.held.shape[-1] // 2

    def chip_of(self, gy):
        return gy // 2

    def half(self, ref, which):
        return ref.at[:, :, pl.ds(which * self.width, self.width)]

    def start(self, to_sibling):
        self.load.start()
        if self.whole:
            self.sib = self.wires.send(to_sibling, self.from_sib, (self.z, sibling(self.g)))

    def corner(self):
        self.load.wait()
        if self.whole:
            self.sib.wait_recv()

            @pl.loop(0, LINES)
            def _(n):
                for q in range(PLANE):
                    self.held[n, q] = (
                        self.held[n, q].astype(F32) + self.from_sib[n, q].astype(F32)
                    ).astype(BF16)

        far = self.held.at[:, self.chip_of(along_y(along_x(self.g)))]
        self.to_y = self.wires.send(self.half(far, 0), self.cy, (self.z, along_y(self.g)))
        self.to_x = self.wires.send(self.half(far, 1), self.cx, (self.z, along_x(self.g)))

    def sides(self):
        width = self.width
        self.to_y.wait_recv()
        near = self.chip_of(along_x(self.g))

        @pl.loop(0, LINES)
        def _(n):
            self.held[n, near, :, :width] = (
                self.held[n, near, :, :width].astype(F32) + self.cy[n].astype(F32)
            ).astype(BF16)

        self.along_x = self.wires.send(self.held.at[:, near], self.fx, (self.z, along_x(self.g)))
        self.to_x.wait_recv()
        beside = self.chip_of(along_y(self.g))

        @pl.loop(0, LINES)
        def _(n):
            self.held[n, beside, :, width:] = (
                self.held[n, beside, :, width:].astype(F32) + self.cx[n].astype(F32)
            ).astype(BF16)

        self.along_y = self.wires.send(self.held.at[:, beside], self.fy, (self.z, along_y(self.g)))

    def line(self):
        self.along_x.wait_recv()
        self.along_y.wait_recv()
        self.zs = []
        for k in (2, 1, 3):
            there = turn(self.z, k)
            self.fx[there] = (
                self.held[there, self.chip].astype(F32)
                + self.fx[there].astype(F32)
                + self.fy[there].astype(F32)
            ).astype(BF16)
            self.zs.append(
                self.wires.send(self.fx.at[there], self.fz.at[k - 1], (there, self.g))
            )
        z = self.z
        self.out[...] = (
            self.held[z, self.chip].astype(F32) + self.fx[z].astype(F32) + self.fy[z].astype(F32)
        )

    def finish(self):
        for copy in self.zs:
            copy.wait_recv()
        self.out[...] += (
            self.fz[0].astype(F32) + self.fz[1].astype(F32) + self.fz[2].astype(F32)
        )


def fold_scratch(rows, cols, whole):
    half = cols // 2
    return [
        pltpu.VMEM((LINES, PLANE, rows, cols), BF16),
        pltpu.VMEM((LINES, PLANE, rows, cols) if whole else (1, 1, 16, 128), BF16),
        pltpu.VMEM((LINES, rows, half), BF16),
        pltpu.VMEM((LINES, rows, half), BF16),
        pltpu.VMEM((LINES, rows, cols), BF16),
        pltpu.VMEM((LINES, rows, cols), BF16),
        pltpu.VMEM((LINES - 1, rows, cols), BF16),
    ]


def fold_sems(count, whole):
    return count * ((1 if whole else 0) + 4 + 3)


def fold_all(flows):
    stages = ("corner", "sides", "line", "finish")
    for tick in range(len(flows) + len(stages) - 1):
        for n in range(len(stages)):
            flow = tick - n
            if 0 <= flow < len(flows):
                getattr(flows[flow], stages[n])()


def scatter_kernel(count, whole, *refs):
    parts, outs = refs[:count], refs[count : 2 * count]
    rest = list(refs[2 * count :])
    send_sems, recv_sems, local_sems = rest[:3]
    scratch = rest[3:]
    z, g, chip, core = here()
    others = line_of(z, g) + [(z, along_x(g)), (z, along_y(g))]
    if whole:
        others.append((z, sibling(g)))
    greet(others)
    wires = Wires(send_sems, recv_sems)
    flows = []
    for n in range(count):
        ours = parts[n].at[:, :, core] if whole else parts[n]
        flows.append(
            Fold(
                wires, parts[n], ours, whole, scratch[7 * n : 7 * n + 7], outs[n], local_sems.at[n]
            )
        )
    for n, flow in enumerate(flows):
        flow.start(parts[n].at[:, :, 1 - core] if whole else None)
    fold_all(flows)
    wires.drain()


def scatter(parts, whole, ident):
    count = len(parts)
    rows, cols = parts[0].shape[-2:]
    scratch = []
    for _ in parts:
        scratch += fold_scratch(rows, cols, whole)
    sems = fold_sems(count, whole)
    return pl.pallas_call(
        partial(scatter_kernel, count, whole),
        out_shape=[jax.ShapeDtypeStruct((rows, cols), F32)] * count,
        in_specs=[pl.BlockSpec(memory_space=HBM)] * count,
        out_specs=[pl.BlockSpec(memory_space=pltpu.VMEM)] * count,
        scratch_shapes=[
            pltpu.SemaphoreType.DMA((sems,)),
            pltpu.SemaphoreType.DMA((sems,)),
            pltpu.SemaphoreType.DMA((count,)),
        ]
        + scratch,
        compiler_params=pltpu.CompilerParams(
            collective_id=ident, has_side_effects=True, vmem_limit_bytes=60 * 2**20
        ),
        name="scatter_%d" % ident,
    )(*parts)


def layer_norm(row_block, gain_row):
    row_mean = jnp.mean(row_block, axis=-1, keepdims=True)
    centred = row_block - row_mean
    variance = jnp.mean(centred * centred, axis=-1, keepdims=True)
    return centred * lax.rsqrt(variance + NORM_STABILIZER) * gain_row


def product(left_side, right_side):
    return jnp.dot(left_side, right_side, preferred_element_type=jnp.float32)


def inner_first(left_side, right_side):
    return lax.dot_general(
        left_side, right_side, (((0,), (0,)), ((), ())), preferred_element_type=jnp.float32
    )


def inner_last(left_side, right_side):
    return lax.dot_general(
        left_side, right_side, (((1,), (1,)), ((), ())), preferred_element_type=jnp.float32
    )


def collect(onehot_rows, value_rows):
    return lax.dot_general(
        onehot_rows,
        value_rows,
        (((0,), (0,)), ((), ())),
        precision=lax.Precision.HIGHEST,
        preferred_element_type=jnp.float32,
    )


def plain_device(
    media,
    latents,
    frame_counts,
    time_index,
    valid,
    time_table,
    media_gain,
    latent_gain,
    ffn_gain,
    w_query,
    w_key,
    w_value,
    w_out,
    w_up,
    w_down,
    cotangent,
):
    frames = time_index.shape[0]
    patches = valid.shape[0] // frames
    latent_rows = latents.shape[0]
    model_width = latents.shape[1]
    head_size = model_width // H
    score_scale = head_size ** (-0.5)
    across = lax.axis_size("gx")
    column = lax.axis_index("gx")
    row_index = lax.axis_index("gy")
    frame_ends = jnp.cumsum(frame_counts[row_index])
    position = column * frames + jnp.arange(frames, dtype=jnp.int32)
    item_index = jnp.sum((frame_ends[None, :] <= position[:, None]).astype(jnp.int32), axis=1)
    item_onehot = (item_index[:, None] == jnp.arange(across, dtype=jnp.int32)[None, :]).astype(
        jnp.float32
    )
    (
        full_query,
        full_key,
        full_value,
        full_out,
        full_up,
        full_down,
        full_media_gain,
        full_latent_gain,
        full_ffn_gain,
        full_time,
    ) = (
        lax.all_gather(w_query, ("gx", "gy"), axis=0, tiled=True),
        lax.all_gather(w_key, ("gx", "gy"), axis=0, tiled=True),
        lax.all_gather(w_value, ("gx", "gy"), axis=0, tiled=True),
        lax.all_gather(w_out, ("gx", "gy"), axis=0, tiled=True),
        lax.all_gather(w_up, ("gx", "gy"), axis=0, tiled=True),
        lax.all_gather(w_down, ("gx", "gy"), axis=0, tiled=True),
        lax.all_gather(media_gain, ("gx", "gy"), axis=0, tiled=True),
        lax.all_gather(latent_gain, ("gx", "gy"), axis=0, tiled=True),
        lax.all_gather(ffn_gain, ("gx", "gy"), axis=0, tiled=True),
        lax.all_gather(time_table, ("gx", "gy"), axis=1, tiled=True),
    )
    time_onehot = (
        time_index[:, None] == jnp.arange(full_time.shape[0], dtype=jnp.int32)[None, :]
    ).astype(jnp.float32)
    time_rows = product(time_onehot.astype(jnp.bfloat16), full_time)
    media_in = (
        media.astype(jnp.float32).reshape(frames, patches, model_width) + time_rows[:, None, :]
    ).reshape(-1, model_width)
    media_normed = layer_norm(media_in, full_media_gain.astype(jnp.float32)).astype(jnp.bfloat16)
    key_heads = (
        product(media_normed, full_key).astype(jnp.bfloat16).reshape(frames, patches, H, head_size)
    )
    value_heads = (
        product(media_normed, full_value)
        .astype(jnp.bfloat16)
        .reshape(frames, patches, H, head_size)
    )
    latent_in = latents.astype(jnp.float32)
    latent_normed = layer_norm(latent_in, full_latent_gain.astype(jnp.float32)).astype(jnp.bfloat16)
    own_query = product(latent_normed, full_query).astype(jnp.bfloat16)
    own_key = product(latent_normed, full_key).astype(jnp.bfloat16)
    own_value = product(latent_normed, full_value).astype(jnp.bfloat16)
    valid_total = lax.psum(jnp.sum(valid.astype(jnp.float32)), ("gx", "gy"))
    coefficient = ENTROPY_WEIGHT * (valid.shape[0] * lax.axis_size(("gx", "gy"))) / valid_total
    query_table = lax.all_gather(own_query, "gx", axis=0, tiled=True)
    picked = query_table.reshape(-1, latent_rows, H, head_size)[item_index]
    media_score = (
        jnp.einsum("flhd,fphd->flhp", picked, key_heads, preferred_element_type=jnp.float32)
        * score_scale
    )
    valid_mask = valid.reshape(frames, 1, 1, patches) > 0
    media_expo = jnp.where(valid_mask, jnp.exp(media_score), 0.0)
    expo_low = media_expo.astype(jnp.bfloat16)
    media_total = jnp.sum(media_expo, axis=-1)
    media_moment = jnp.sum(media_expo * media_score, axis=-1)
    media_weighted = jnp.einsum(
        "flhp,fphd->flhd", expo_low, value_heads, preferred_element_type=jnp.float32
    )
    dense_weighted = collect(item_onehot, media_weighted.reshape(frames, -1)).reshape(
        -1, model_width
    )
    dense_total = collect(item_onehot, media_total.reshape(frames, -1)).reshape(-1, H)
    dense_moment = collect(item_onehot, media_moment.reshape(frames, -1)).reshape(-1, H)
    got_weighted, got_total, got_moment = (
        lax.psum_scatter(dense_weighted, "gx", scatter_dimension=0, tiled=True),
        lax.psum_scatter(dense_total, "gx", scatter_dimension=0, tiled=True),
        lax.psum_scatter(dense_moment, "gx", scatter_dimension=0, tiled=True),
    )
    query_head_count = own_query.reshape(latent_rows, H, head_size)
    latent_key_rows = own_key.reshape(latent_rows, H, head_size)
    latent_value_rows = own_value.reshape(latent_rows, H, head_size)
    latent_score = (
        jnp.einsum(
            "uer,zer->uez", query_head_count, latent_key_rows, preferred_element_type=jnp.float32
        )
        * score_scale
    )
    latent_expo = jnp.exp(latent_score)
    latent_reduced_precision = latent_expo.astype(jnp.bfloat16)
    weighted = got_weighted.reshape(latent_rows, H, head_size) + jnp.einsum(
        "nwr,rwb->nwb",
        latent_reduced_precision,
        latent_value_rows,
        preferred_element_type=jnp.float32,
    )
    totals = got_total + jnp.sum(latent_expo, axis=-1)
    moment = got_moment + jnp.sum(latent_expo * latent_score, axis=-1)
    attention = weighted / totals[..., None]
    attn_low = attention.reshape(latent_rows, model_width).astype(jnp.bfloat16)
    middle = latent_in + product(attn_low, full_out)
    ffn_normed = layer_norm(middle, full_ffn_gain.astype(jnp.float32)).astype(jnp.bfloat16)
    up_rows = product(ffn_normed, full_up)
    hidden = jax.nn.gelu(up_rows, approximate=False).astype(jnp.bfloat16)
    new_latents = (middle + product(hidden, full_down)).astype(jnp.bfloat16)
    (
        back_query,
        back_key,
        back_value,
        back_out,
        back_up,
        back_down,
        back_media_gain,
        back_latent_gain,
        back_ffn_gain,
    ) = (
        lax.all_gather(w_query, ("gx", "gy"), axis=0, tiled=True),
        lax.all_gather(w_key, ("gx", "gy"), axis=0, tiled=True),
        lax.all_gather(w_value, ("gx", "gy"), axis=0, tiled=True),
        lax.all_gather(w_out, ("gx", "gy"), axis=0, tiled=True),
        lax.all_gather(w_up, ("gx", "gy"), axis=0, tiled=True),
        lax.all_gather(w_down, ("gx", "gy"), axis=0, tiled=True),
        lax.all_gather(media_gain, ("gx", "gy"), axis=0, tiled=True),
        lax.all_gather(latent_gain, ("gx", "gy"), axis=0, tiled=True),
        lax.all_gather(ffn_gain, ("gx", "gy"), axis=0, tiled=True),
    )
    owned_latent, owned_attn, owned_ffn, owned_hidden = (
        lax.all_to_all(latent_normed, ("gx", "gy"), split_axis=1, concat_axis=0, tiled=True),
        lax.all_to_all(attn_low, ("gx", "gy"), split_axis=1, concat_axis=0, tiled=True),
        lax.all_to_all(ffn_normed, ("gx", "gy"), split_axis=1, concat_axis=0, tiled=True),
        lax.all_to_all(hidden, ("gx", "gy"), split_axis=1, concat_axis=0, tiled=True),
    )
    hidden_grad = inner_last(cotangent, back_down)
    gelu_pull = jax.vjp(partial(jax.nn.gelu, approximate=False), up_rows)[1]
    up_grad = gelu_pull(hidden_grad)[0].astype(jnp.bfloat16)
    ffn_normed_grad = inner_last(up_grad, back_up)
    ffn_pull = jax.vjp(layer_norm, middle, back_ffn_gain.astype(jnp.float32))[1]
    middle_part, grad_ffn_gain = ffn_pull(ffn_normed_grad)
    middle_grad = cotangent.astype(jnp.float32) + middle_part
    middle_low = middle_grad.astype(jnp.bfloat16)
    attn_grad = inner_last(middle_low, back_out).reshape(latent_rows, H, head_size)
    weighted_sum_gradient = (attn_grad / totals[..., None]).astype(jnp.bfloat16)
    slope_term = -coefficient / totals
    shift_term = (
        -jnp.sum(attn_grad * attention, axis=-1) / totals
        + coefficient * (1.0 / totals + moment / (totals * totals))
        + slope_term
    )
    latent_mix = jnp.einsum(
        "uer,zer->uez", weighted_sum_gradient, latent_value_rows, preferred_element_type=jnp.float32
    )
    latent_sgrad = latent_expo * (
        latent_mix + shift_term[..., None] + slope_term[..., None] * latent_score
    )
    latent_residual_gradient = (latent_sgrad * score_scale).astype(jnp.bfloat16)
    query_part = jnp.einsum(
        "nwr,rwb->nwb",
        latent_residual_gradient,
        latent_key_rows,
        preferred_element_type=jnp.float32,
    )
    own_key_grad = (
        jnp.einsum(
            "zry,zrj->yrj",
            latent_residual_gradient,
            query_head_count,
            preferred_element_type=jnp.float32,
        )
        .astype(jnp.bfloat16)
        .reshape(latent_rows, model_width)
    )
    own_value_grad = (
        jnp.einsum(
            "zry,zrj->yrj",
            latent_reduced_precision,
            weighted_sum_gradient,
            preferred_element_type=jnp.float32,
        )
        .astype(jnp.bfloat16)
        .reshape(latent_rows, model_width)
    )
    grad_table = lax.all_gather(
        weighted_sum_gradient.reshape(latent_rows, model_width), "gx", axis=0, tiled=True
    )
    shift_table, slope_table = (
        lax.all_gather(shift_term, "gx", axis=0, tiled=True),
        lax.all_gather(slope_term, "gx", axis=0, tiled=True),
    )
    picked_grad = grad_table.reshape(-1, latent_rows, H, head_size)[item_index]
    picked_shift = shift_table.reshape(-1, latent_rows, H)[item_index]
    picked_slope = slope_table.reshape(-1, latent_rows, H)[item_index]
    media_mix = jnp.einsum(
        "flhd,fphd->flhp", picked_grad, value_heads, preferred_element_type=jnp.float32
    )
    media_sgrad = media_expo * (
        media_mix + picked_shift[..., None] + picked_slope[..., None] * media_score
    )
    media_rgrad = (media_sgrad * score_scale).astype(jnp.bfloat16)
    query_terms = jnp.einsum(
        "flhp,fphd->flhd", media_rgrad, key_heads, preferred_element_type=jnp.float32
    )
    dense_query = collect(item_onehot, query_terms.reshape(frames, -1)).reshape(-1, model_width)
    got_query = lax.psum_scatter(
        dense_query.astype(jnp.bfloat16), "gx", scatter_dimension=0, tiled=True
    ).astype(jnp.float32)
    media_key_grad = (
        jnp.einsum("flhp,flhd->fphd", media_rgrad, picked, preferred_element_type=jnp.float32)
        .astype(jnp.bfloat16)
        .reshape(-1, model_width)
    )
    media_value_grad = (
        jnp.einsum("flhp,flhd->fphd", expo_low, picked_grad, preferred_element_type=jnp.float32)
        .astype(jnp.bfloat16)
        .reshape(-1, model_width)
    )
    grad_key = inner_first(media_normed, media_key_grad) + inner_first(latent_normed, own_key_grad)
    grad_value = inner_first(media_normed, media_value_grad) + inner_first(
        latent_normed, own_value_grad
    )
    media_normed_grad = inner_last(media_key_grad, back_key) + inner_last(
        media_value_grad, back_value
    )
    media_pull = jax.vjp(layer_norm, media_in, back_media_gain.astype(jnp.float32))[1]
    media_grad, grad_media_gain = media_pull(media_normed_grad)
    frame_sums = jnp.sum(media_grad.reshape(frames, patches, model_width), axis=1)
    grad_time = collect(time_onehot, frame_sums)
    query_grad = (
        (got_query.reshape(latent_rows, H, head_size) + query_part)
        .astype(jnp.bfloat16)
        .reshape(latent_rows, model_width)
    )
    latent_normed_grad = (
        inner_last(query_grad, back_query)
        + inner_last(own_key_grad, back_key)
        + inner_last(own_value_grad, back_value)
    )
    latent_pull = jax.vjp(layer_norm, latent_in, back_latent_gain.astype(jnp.float32))[1]
    latent_part, grad_latent_gain = latent_pull(latent_normed_grad)
    latents_grad = middle_grad + latent_part
    piece_query = lax.all_gather(query_grad, ("gx", "gy"), axis=0, tiled=True)
    piece_middle = lax.all_gather(middle_low, ("gx", "gy"), axis=0, tiled=True)
    piece_up = lax.all_gather(up_grad, ("gx", "gy"), axis=0, tiled=True)
    piece_cot = lax.all_gather(cotangent, ("gx", "gy"), axis=0, tiled=True)
    shard_query = inner_first(owned_latent, piece_query)
    shard_out = inner_first(owned_attn, piece_middle)
    shard_up = inner_first(owned_ffn, piece_up)
    shard_down = inner_first(owned_hidden, piece_cot)
    shard_grads = (
        lax.psum_scatter(grad_key, ("gx", "gy"), scatter_dimension=0, tiled=True),
        lax.psum_scatter(grad_value, ("gx", "gy"), scatter_dimension=0, tiled=True),
        lax.psum_scatter(grad_media_gain, ("gx", "gy"), scatter_dimension=0, tiled=True),
        lax.psum_scatter(grad_latent_gain, ("gx", "gy"), scatter_dimension=0, tiled=True),
        lax.psum_scatter(grad_ffn_gain, ("gx", "gy"), scatter_dimension=0, tiled=True),
        lax.psum_scatter(grad_time, ("gx", "gy"), scatter_dimension=1, tiled=True),
    )
    return (
        new_latents,
        media_grad,
        latents_grad,
        shard_grads[5],
        shard_grads[2],
        shard_grads[3],
        shard_grads[4],
        shard_query,
        shard_grads[0],
        shard_grads[1],
        shard_out,
        shard_up,
        shard_down,
    )


GROUP = 4


def feed_kernel(
    up_ref, down_ref, cot_ref, up_out, down_out, cot_out, send_sems, recv_sems, local_sems
):
    z, g, chip, core = here()
    here_chip = 4 * z + chip
    me = 2 * here_chip + core
    width = up_out.shape[-1]
    mates = []
    for j in range(1, 16):
        there = (here_chip + j) % 16
        mates.append((there // 4, 2 * (there % 4) + core))
    near = (z, sibling(g))
    greet(mates + [near])
    wires = Wires(send_sems, recv_sems)

    def piece(there):
        return up_ref.at[:, pl.ds(pl.multiple_of(there * width, 128), width)]

    kept = [
        pltpu.make_async_copy(piece(here_chip), up_out.at[me], local_sems.at[0]),
        pltpu.make_async_copy(down_ref, down_out.at[core], local_sems.at[1]),
        pltpu.make_async_copy(cot_ref, cot_out.at[here_chip], local_sems.at[2]),
    ]
    for copy in kept:
        copy.start()
    flow = Spread(
        wires, cot_ref, lambda zz, gg: cot_out.at[zz * 4 + gg // 2], columns_half, False
    )
    flow.first()
    down = wires.send(down_ref, down_out.at[core], near)
    given = [wires.send(piece(here_chip), up_out.at[me], near)]
    moved = []
    for j in range(1, 16):
        moved.append(wires.send(piece((here_chip + j) % 16), up_out.at[me], mates[j - 1]))
    flow.corner(0)
    for k in (1, 3, 2):
        flow.column(k)
    for k in (1, 3, 2):
        flow.corner(k)
    for j in range(1, 16):
        moved[j - 1].wait_recv()
        origin = 2 * ((here_chip + 16 - j) % 16) + core
        given.append(wires.send(up_out.at[origin], up_out.at[origin], near))
    for k in (0, 1, 3, 2):
        flow.last(k)
    down.wait_recv()
    for copy in given:
        copy.wait_recv()
    for copy in kept:
        copy.wait()
    wires.drain()


def feed(w_up, w_down, cotangent):
    rows, width = w_up.shape
    sems = spread_sems(1, False) + 1 + 16 + 15
    return pl.pallas_call(
        feed_kernel,
        out_shape=[
            jax.ShapeDtypeStruct((32, rows, width // 16), BF16),
            jax.ShapeDtypeStruct((2,) + w_down.shape, BF16),
            jax.ShapeDtypeStruct((16,) + cotangent.shape, BF16),
        ],
        in_specs=[pl.BlockSpec(memory_space=HBM)] * 3,
        out_specs=[pl.BlockSpec(memory_space=HBM)] * 3,
        scratch_shapes=[
            pltpu.SemaphoreType.DMA((sems,)),
            pltpu.SemaphoreType.DMA((sems,)),
            pltpu.SemaphoreType.DMA((3,)),
        ],
        compiler_params=pltpu.CompilerParams(collective_id=1, has_side_effects=True),
        name="feed",
    )(w_up, w_down, cotangent)


def give_back_kernel(
    up_ref,
    down_ref,
    up_out,
    down_out,
    up_held,
    up_near,
    down_near,
    send_sems,
    recv_sems,
    local_sems,
):
    z, g, chip, core = here()
    here_chip = 4 * z + chip
    mates = []
    for j in range(1, 16):
        there = (here_chip + j) % 16
        mates.append((there // 4, 2 * (there % 4) + core))
    near = (z, sibling(g))
    greet(mates + [near])
    wires = Wires(send_sems, recv_sems)
    load_up = pltpu.make_async_copy(up_ref.at[:, core], up_held, local_sems.at[0])
    load_down = pltpu.make_async_copy(down_ref.at[core], down_out, local_sems.at[1])
    load_up.start()
    load_down.start()
    up = wires.send(up_ref.at[:, 1 - core], up_near, near)
    down = wires.send(down_ref.at[1 - core], down_near, near)
    load_up.wait()
    up.wait_recv()
    add_slots(up_held, up_near, 16)
    moved = []
    for j in range(1, 16):
        there = (here_chip + j) % 16
        moved.append(wires.send(up_held.at[there], up_out.at[here_chip], mates[j - 1]))
    up_out[here_chip] = up_held[here_chip]
    load_down.wait()
    down.wait_recv()
    rows = down_out.shape[0] // 8

    @pl.loop(0, 8)
    def _(n):
        block = pl.ds(pl.multiple_of(n * rows, 8), rows)
        down_out[block] = down_out[block] + down_near[block]

    for copy in moved:
        copy.wait_recv()
    wires.drain()


def give_back(up_part, down_part):
    rows, width = up_part.shape[-2:]
    down_shape = down_part.shape[1:]
    return pl.pallas_call(
        give_back_kernel,
        out_shape=[
            jax.ShapeDtypeStruct((16, rows, width), BF16),
            jax.ShapeDtypeStruct(down_shape, F32),
        ],
        in_specs=[pl.BlockSpec(memory_space=HBM)] * 2,
        out_specs=[pl.BlockSpec(memory_space=pltpu.VMEM)] * 2,
        scratch_shapes=[
            pltpu.VMEM((16, rows, width), BF16),
            pltpu.VMEM((16, rows, width), BF16),
            pltpu.VMEM(down_shape, F32),
            pltpu.SemaphoreType.DMA((17,)),
            pltpu.SemaphoreType.DMA((17,)),
            pltpu.SemaphoreType.DMA((2,)),
        ],
        compiler_params=pltpu.CompilerParams(collective_id=2, has_side_effects=True),
        name="give_back",
    )(up_part, down_part)


def total_kernel(mine, out, sums, got, send_sems, recv_sems):
    z, g, _, _ = here()
    sides = [(z, sibling(g)), (z, along_x(g)), (z, along_y(g))]
    line = line_of(z, g)
    greet(sides + line)
    wires = Wires(send_sems, recv_sems)
    source = mine
    for n, side in enumerate(sides):
        copy = wires.send(source, got.at[n], side)
        copy.wait_recv()
        sums[n] = source[...] + got[n]
        source = sums.at[n]
    copies = [wires.send(source, got.at[3 + k], line[k]) for k in range(3)]
    for copy in copies:
        copy.wait_recv()
    out[...] = source[...] + got[3] + got[4] + got[5]
    wires.drain()


def total(array):
    return pl.pallas_call(
        total_kernel,
        out_shape=jax.ShapeDtypeStruct(array.shape, F32),
        in_specs=[pl.BlockSpec(memory_space=pltpu.VMEM)],
        out_specs=pl.BlockSpec(memory_space=pltpu.VMEM),
        scratch_shapes=[
            pltpu.VMEM((3,) + array.shape, F32),
            pltpu.VMEM((6,) + array.shape, F32),
            pltpu.SemaphoreType.DMA((6,)),
            pltpu.SemaphoreType.DMA((6,)),
        ],
        compiler_params=pltpu.CompilerParams(collective_id=3, has_side_effects=True),
        name="total",
    )(array)


def head_masks(rows, width, head_size):
    lane = lax.broadcasted_iota(jnp.int32, (rows, width), 1)
    return [(lane >= h * head_size) & (lane < (h + 1) * head_size) for h in range(GROUP)]


def stacked(block, masks):
    zero = jnp.zeros_like(block)
    return jnp.concatenate([jnp.where(mask, block, zero) for mask in masks], axis=0)


def unstacked(block, masks):
    rows = block.shape[0] // GROUP
    total = jnp.where(masks[0], block[:rows], 0.0)
    for h in range(1, GROUP):
        total = jnp.where(masks[h], block[h * rows : (h + 1) * rows], total)
    return total


def dot_last(a, b):
    return lax.dot_general(a, b, (((1,), (1,)), ((), ())), preferred_element_type=F32)


def dot_first(a, b):
    return lax.dot_general(a, b, (((0,), (0,)), ((), ())), preferred_element_type=F32)


def spread_heads(columns, first, masks):
    out = jnp.where(masks[0], columns[:, first : first + 1], 0.0)
    for h in range(1, GROUP):
        out = jnp.where(masks[h], columns[:, first + h : first + h + 1], out)
    return out


def attend(queries, keys, values, valid, scale, masks):
    rows = queries.shape[0]
    score = dot_last(stacked(queries, masks), keys) * scale
    expo = jnp.exp(score)
    if valid is not None:
        expo = jnp.where(valid > 0, expo, 0.0)
    totals = jnp.sum(expo, axis=1, keepdims=True)
    moments = jnp.sum(expo * score, axis=1, keepdims=True)
    weighted = jnp.dot(expo.astype(BF16), values, preferred_element_type=F32)
    heads = [(totals[h * rows : (h + 1) * rows], moments[h * rows : (h + 1) * rows]) for h in range(GROUP)]
    return unstacked(weighted, masks), heads


def put_heads(heads, group, lane):
    out = jnp.zeros(lane.shape, F32)
    for h, (total, moment) in enumerate(heads):
        out = jnp.where(lane == group * GROUP + h, total, out)
        out = jnp.where(lane == H + group * GROUP + h, moment, out)
    return out


def forward_kernel(
    scale,
    item_ref,
    table_ref,
    key_ref,
    value_ref,
    valid_ref,
    own_query_ref,
    own_key_ref,
    own_value_ref,
    weighted_ref,
    stats_ref,
    own_weighted_ref,
    own_stats_ref,
    sums,
):
    items, rows, width = table_ref.shape
    frames = valid_ref.shape[0]
    patches = valid_ref.shape[2]
    groups = H // GROUP
    span = width // groups
    masks = head_masks(rows, span, span // GROUP)
    lane = lax.broadcasted_iota(jnp.int32, (rows, 128), 1)
    sums[...] = jnp.zeros_like(sums)
    stats_ref[...] = jnp.zeros_like(stats_ref)
    stats = jnp.zeros((rows, 128), F32)
    for group in range(groups):
        cols = pl.ds(group * span, span)
        weighted, heads = attend(
            own_query_ref[:, cols], own_key_ref[:, cols], own_value_ref[:, cols], None, scale, masks
        )
        own_weighted_ref[:, cols] = weighted
        stats = stats + put_heads(heads, group, lane)
    own_stats_ref[...] = stats

    @pl.loop(0, frames)
    def _(frame):
        item = item_ref[frame]
        block = pl.ds(pl.multiple_of(frame * patches, patches), patches)
        valid = valid_ref[frame]
        stats = jnp.zeros((rows, 128), F32)
        for group in range(groups):
            cols = pl.ds(group * span, span)
            weighted, heads = attend(
                table_ref[item, :, cols],
                key_ref[block, cols],
                value_ref[block, cols],
                valid,
                scale,
                masks,
            )
            sums[item, :, cols] += weighted
            stats = stats + put_heads(heads, group, lane)
        stats_ref[item] += stats

    weighted_ref[...] = sums[...].astype(BF16)


def forward(item_index, table, keys, values, valid, own, scale):
    items, rows, width = table.shape
    vmem = pl.BlockSpec(memory_space=pltpu.VMEM)
    return pl.pallas_call(
        partial(forward_kernel, scale),
        out_shape=[
            jax.ShapeDtypeStruct((items, rows, width), BF16),
            jax.ShapeDtypeStruct((items, rows, 128), F32),
            jax.ShapeDtypeStruct((rows, width), F32),
            jax.ShapeDtypeStruct((rows, 128), F32),
        ],
        in_specs=[pl.BlockSpec(memory_space=pltpu.SMEM)] + [vmem] * 7,
        out_specs=[vmem] * 4,
        scratch_shapes=[pltpu.VMEM((items, rows, width), F32)],
        name="attention_forward",
    )(item_index, table, keys, values, valid, *own)


def repel(queries, grads, keys, values, valid, shift, slope, scale, masks):
    query_stack = stacked(queries, masks)
    grad_stack = stacked(grads, masks)
    score = dot_last(query_stack, keys) * scale
    expo = jnp.exp(score)
    if valid is not None:
        expo = jnp.where(valid > 0, expo, 0.0)
    mix = dot_last(grad_stack, values)
    raw = (expo * (mix + shift + slope * score) * scale).astype(BF16)
    query_grad = unstacked(jnp.dot(raw, keys, preferred_element_type=F32), masks)
    key_grad = dot_first(raw, query_stack).astype(BF16)
    value_grad = dot_first(expo.astype(BF16), grad_stack).astype(BF16)
    return query_grad, key_grad, value_grad


def stacked_columns(terms, first):
    return jnp.concatenate([terms[:, first + h : first + h + 1] for h in range(GROUP)], axis=0)


def backward_kernel(
    scale,
    item_ref,
    table_ref,
    grad_ref,
    terms_ref,
    key_ref,
    value_ref,
    valid_ref,
    own_query_ref,
    own_grad_ref,
    own_terms_ref,
    own_key_ref,
    own_value_ref,
    query_grad_ref,
    key_grad_ref,
    value_grad_ref,
    own_query_grad_ref,
    own_key_grad_ref,
    own_value_grad_ref,
    sums,
):
    items, rows, width = table_ref.shape
    frames = valid_ref.shape[0]
    patches = valid_ref.shape[2]
    groups = H // GROUP
    span = width // groups
    masks = head_masks(rows, span, span // GROUP)
    sums[...] = jnp.zeros_like(sums)
    own_terms = own_terms_ref[...]
    for group in range(groups):
        cols = pl.ds(group * span, span)
        own_query_grad_ref[:, cols], own_key_grad_ref[:, cols], own_value_grad_ref[:, cols] = repel(
            own_query_ref[:, cols],
            own_grad_ref[:, cols],
            own_key_ref[:, cols],
            own_value_ref[:, cols],
            None,
            stacked_columns(own_terms, group * GROUP),
            stacked_columns(own_terms, H + group * GROUP),
            scale,
            masks,
        )

    @pl.loop(0, frames)
    def _(frame):
        item = item_ref[frame]
        block = pl.ds(pl.multiple_of(frame * patches, patches), patches)
        valid = valid_ref[frame]
        terms = terms_ref[item]
        for group in range(groups):
            cols = pl.ds(group * span, span)
            query_grad, key_grad_ref[block, cols], value_grad_ref[block, cols] = repel(
                table_ref[item, :, cols],
                grad_ref[item, :, cols],
                key_ref[block, cols],
                value_ref[block, cols],
                valid,
                stacked_columns(terms, group * GROUP),
                stacked_columns(terms, H + group * GROUP),
                scale,
                masks,
            )
            sums[item, :, cols] += query_grad

    query_grad_ref[...] = sums[...].astype(BF16)


def backward(item_index, table, grads, terms, keys, values, valid, own, scale):
    items, rows, width = table.shape
    vmem = pl.BlockSpec(memory_space=pltpu.VMEM)
    return pl.pallas_call(
        partial(backward_kernel, scale),
        out_shape=[
            jax.ShapeDtypeStruct((items, rows, width), BF16),
            jax.ShapeDtypeStruct(keys.shape, BF16),
            jax.ShapeDtypeStruct(keys.shape, BF16),
            jax.ShapeDtypeStruct((rows, width), F32),
            jax.ShapeDtypeStruct((rows, width), BF16),
            jax.ShapeDtypeStruct((rows, width), BF16),
        ],
        in_specs=[pl.BlockSpec(memory_space=pltpu.SMEM)] + [vmem] * 11,
        out_specs=[vmem] * 6,
        scratch_shapes=[pltpu.VMEM((items, rows, width), F32)],
        name="attention_backward",
    )(item_index, table, grads, terms, keys, values, valid, *own)


def settle_kernel(
    weighted_ref,
    stats_ref,
    own_weighted_ref,
    own_stats_ref,
    out_ref,
    latents_ref,
    gain_ref,
    attention_ref,
    attn_ref,
    sums_ref,
    middle_ref,
    normed_ref,
):
    rows, width = latents_ref.shape
    span = width // (H // GROUP)
    masks = head_masks(rows, span, span // GROUP)
    stats = own_stats_ref[...]
    for n in range(stats_ref.shape[0]):
        stats = stats + stats_ref[n]
    sums_ref[...] = stats
    for group in range(H // GROUP):
        cols = pl.ds(group * span, span)
        weighted = own_weighted_ref[:, cols]
        for n in range(weighted_ref.shape[0]):
            weighted = weighted + weighted_ref[n, :, cols].astype(F32)
        attention = weighted / spread_heads(stats, group * GROUP, masks)
        attention_ref[:, cols] = attention
        attn_ref[:, cols] = attention.astype(BF16)
    middle = latents_ref[...].astype(F32) + jnp.dot(
        attn_ref[...], out_ref[...], preferred_element_type=F32
    )
    middle_ref[...] = middle
    normed_ref[...] = layer_norm(middle, gain_ref[...]).astype(BF16)


def settle(weighted, stats, own_weighted, own_stats, w_out, latents, gain):
    vmem = pl.BlockSpec(memory_space=pltpu.VMEM)
    shape = latents.shape
    return pl.pallas_call(
        settle_kernel,
        out_shape=[
            jax.ShapeDtypeStruct(shape, F32),
            jax.ShapeDtypeStruct(shape, BF16),
            jax.ShapeDtypeStruct(own_stats.shape, F32),
            jax.ShapeDtypeStruct(shape, F32),
            jax.ShapeDtypeStruct(shape, BF16),
        ],
        in_specs=[vmem] * 7,
        out_specs=[vmem] * 5,
        name="settle",
    )(weighted, stats, own_weighted, own_stats, w_out, latents, gain)


def norm_pull(rows, gain, grad):
    mean = jnp.mean(rows, axis=-1, keepdims=True)
    centred = rows - mean
    inverse = lax.rsqrt(jnp.mean(centred * centred, axis=-1, keepdims=True) + NORM_STABILIZER)
    xhat = centred * inverse
    t = grad * gain
    pulled = (
        t
        - jnp.mean(t, axis=-1, keepdims=True)
        - xhat * jnp.mean(t * xhat, axis=-1, keepdims=True)
    ) * inverse
    return pulled, grad * xhat


def unsettle_kernel(
    normed_grad_ref,
    middle_ref,
    gain_ref,
    cot_ref,
    out_ref,
    attention_ref,
    stats_ref,
    coef_ref,
    middle_grad_ref,
    low_ref,
    gain_grad_ref,
    weighted_grad_ref,
    terms_ref,
    attn_grad,
):
    rows, width = middle_ref.shape
    span = width // (H // GROUP)
    masks = head_masks(rows, span, span // GROUP)
    pulled, summand = norm_pull(middle_ref[...], gain_ref[...], normed_grad_ref[...])
    gain_grad_ref[...] = jnp.sum(summand, axis=0, keepdims=True)
    middle_grad = cot_ref[...].astype(F32) + pulled
    middle_grad_ref[...] = middle_grad
    low_ref[...] = middle_grad.astype(BF16)
    attn_grad[...] = dot_last(low_ref[...], out_ref[...])
    stats = stats_ref[...]
    coef = coef_ref[0, 0]
    lane = lax.broadcasted_iota(jnp.int32, (rows, 128), 1)
    terms = jnp.zeros((rows, 128), F32)
    for group in range(H // GROUP):
        cols = pl.ds(group * span, span)
        grad = attn_grad[:, cols]
        first = group * GROUP
        weighted_grad_ref[:, cols] = (grad / spread_heads(stats, first, masks)).astype(BF16)
        along = grad * attention_ref[:, cols]
        for h in range(GROUP):
            inner = jnp.sum(jnp.where(masks[h], along, 0.0), axis=1, keepdims=True)
            total = stats[:, first + h : first + h + 1]
            moment = stats[:, H + first + h : H + first + h + 1]
            slope = -coef / total
            shift = -inner / total + coef * (1.0 / total + moment / (total * total)) + slope
            terms = jnp.where(lane == first + h, shift, terms)
            terms = jnp.where(lane == H + first + h, slope, terms)
    terms_ref[...] = terms


def unsettle(normed_grad, middle, gain, cotangent, w_out, attention, stats, coef):
    vmem = pl.BlockSpec(memory_space=pltpu.VMEM)
    shape = middle.shape
    return pl.pallas_call(
        unsettle_kernel,
        out_shape=[
            jax.ShapeDtypeStruct(shape, F32),
            jax.ShapeDtypeStruct(shape, BF16),
            jax.ShapeDtypeStruct((1, shape[1]), F32),
            jax.ShapeDtypeStruct(shape, BF16),
            jax.ShapeDtypeStruct(stats.shape, F32),
        ],
        in_specs=[vmem] * 7 + [pl.BlockSpec(memory_space=pltpu.SMEM)],
        out_specs=[vmem] * 5,
        scratch_shapes=[pltpu.VMEM(shape, F32)],
        name="unsettle",
    )(normed_grad, middle, gain, cotangent, w_out, attention, stats, coef)


def per_device(
    media,
    latents,
    frame_counts,
    time_index,
    valid,
    time_table,
    media_gain,
    latent_gain,
    ffn_gain,
    w_query,
    w_key,
    w_value,
    w_out,
    w_up,
    w_down,
    cotangent,
):
    frames = time_index.shape[0]
    patches = valid.shape[0] // frames
    latent_rows, width = latents.shape
    shard = media_gain.shape[0]
    scale = (width // H) ** (-0.5)
    column = lax.axis_index("gx")
    row_index = lax.axis_index("gy")
    frame_ends = jnp.cumsum(frame_counts[row_index])
    position = column * frames + jnp.arange(frames, dtype=jnp.int32)
    item_index = jnp.sum((frame_ends[None, :] <= position[:, None]).astype(jnp.int32), axis=1)
    item_index = jnp.clip(item_index, 0, LINES - 1).astype(jnp.int32)

    count = jnp.sum(valid.astype(F32))
    small = jnp.concatenate(
        [
            time_table.astype(F32),
            media_gain.astype(F32)[None],
            latent_gain.astype(F32)[None],
            ffn_gain.astype(F32)[None],
            jnp.full((1, shard), count, F32),
            jnp.zeros((4, shard), F32),
        ],
        axis=0,
    )
    small = jnp.pad(small, ((0, 0), (0, 128 - shard)))
    smalls, full_key, full_value, full_query, full_out = gather(
        [small, w_key, w_value, w_query, w_out], True, 0, small=(0,)
    )
    full_key, full_value, full_query, full_out = (
        w.reshape(width, width) for w in (full_key, full_value, full_query, full_out)
    )
    tables = jnp.swapaxes(smalls[:, :11, :shard], 0, 1).reshape(11, width)
    full_time = tables[:8].astype(BF16)
    full_media_gain, full_latent_gain, full_ffn_gain = tables[8:9], tables[9:10], tables[10:11]
    valid_total = jnp.sum(smalls[:, 11, 0])
    coefficient = ENTROPY_WEIGHT * (valid.shape[0] * lax.axis_size(AXES)) / valid_total
    up_cols, down_rows, cot_rows = feed(w_up, w_down, cotangent)
    up_cols = up_cols.reshape(width, -1)
    down_rows = down_rows.reshape(-1, width)
    cot_rows = cot_rows.reshape(-1, width)

    time_onehot = (
        time_index[:, None] == jnp.arange(full_time.shape[0], dtype=jnp.int32)[None, :]
    ).astype(F32)
    time_rows = product(time_onehot.astype(BF16), full_time)
    media_in = (
        media.astype(F32).reshape(frames, patches, width) + time_rows[:, None, :]
    ).reshape(-1, width)
    media_normed = layer_norm(media_in, full_media_gain).astype(BF16)
    media_key = product(media_normed, full_key).astype(BF16)
    media_value = product(media_normed, full_value).astype(BF16)
    latent_in = latents.astype(F32)
    latent_normed = layer_norm(latent_in, full_latent_gain).astype(BF16)
    own_query = product(latent_normed, full_query).astype(BF16)
    own_key = product(latent_normed, full_key).astype(BF16)
    own_value = product(latent_normed, full_value).astype(BF16)
    valid_rows = valid.reshape(frames, 1, patches)
    (table,) = along_line([own_query], True, 4)
    weighted, stats, own_weighted, own_stats = forward(
        item_index,
        table,
        media_key,
        media_value,
        valid_rows,
        (own_query, own_key, own_value),
        scale,
    )
    got_weighted, got_stats = along_line([weighted, stats], False, 5)
    attention, attn_low, sums, middle, ffn_normed = settle(
        got_weighted, got_stats, own_weighted, own_stats, full_out, latents, full_ffn_gain
    )
    (ffn_rows,) = gather([ffn_normed], False, 6)
    ffn_rows = ffn_rows.reshape(-1, width)
    up_rows = product(ffn_rows, up_cols)
    hidden = jax.nn.gelu(up_rows, approximate=False).astype(BF16)
    hidden_grad = inner_last(cot_rows, down_rows)
    gelu_pull = jax.vjp(partial(jax.nn.gelu, approximate=False), up_rows)[1]
    up_grad = gelu_pull(hidden_grad)[0].astype(BF16)
    normed_part = inner_last(up_grad, up_cols).astype(BF16)
    down_part = product(hidden, down_rows).astype(BF16)
    shape = (LINES, PLANE, latent_rows, width)
    ffn_normed_grad, down_sum = scatter(
        [normed_part.reshape(shape), down_part.reshape(shape)], False, 7
    )
    new_latents = (middle + down_sum).astype(BF16)
    up_grad_part = inner_first(ffn_rows, up_grad).astype(BF16)
    down_grad_part = inner_first(hidden, cot_rows)
    shard_up, shard_down = give_back(
        up_grad_part.reshape(16, 2, shard, -1), down_grad_part.reshape(2, -1, width)
    )
    shard_up = jnp.swapaxes(shard_up, 0, 1).reshape(shard, -1).astype(F32)
    middle_grad, middle_low, grad_ffn_gain, weighted_grad, terms = unsettle(
        ffn_normed_grad,
        middle,
        full_ffn_gain,
        cotangent,
        full_out,
        attention,
        sums,
        coefficient.reshape(1, 1),
    )
    grad_table, terms_table = along_line([weighted_grad, terms], True, 8)
    query_terms, media_key_grad, media_value_grad, query_part, own_key_grad, own_value_grad = backward(
        item_index,
        table,
        grad_table,
        terms_table,
        media_key,
        media_value,
        valid_rows,
        (own_query, weighted_grad, terms, own_key, own_value),
        scale,
    )
    (got_query,) = along_line([query_terms], False, 9)
    query_grad = (jnp.sum(got_query.astype(F32), axis=0) + query_part).astype(BF16)
    media_normed_grad = inner_last(media_key_grad, full_key) + inner_last(
        media_value_grad, full_value
    )
    media_grad, media_summand = norm_pull(media_in, full_media_gain, media_normed_grad)
    grad_media_gain = jnp.sum(media_summand, axis=0, keepdims=True)
    frame_sums = jnp.sum(media_grad.reshape(frames, patches, width), axis=1)
    grad_time = collect(time_onehot, frame_sums)
    latent_normed_grad = (
        inner_last(query_grad, full_query)
        + inner_last(own_key_grad, full_key)
        + inner_last(own_value_grad, full_value)
    )
    latent_part, latent_summand = norm_pull(latent_in, full_latent_gain, latent_normed_grad)
    grad_latent_gain = jnp.sum(latent_summand, axis=0, keepdims=True)
    latents_grad = middle_grad + latent_part
    key_part = inner_first(media_normed, media_key_grad) + inner_first(latent_normed, own_key_grad)
    value_part = inner_first(media_normed, media_value_grad) + inner_first(
        latent_normed, own_value_grad
    )
    out_part = inner_first(attn_low, middle_low)
    query_weight_part = inner_first(latent_normed, query_grad)
    slots = (LINES, PLANE, 2, shard, width)
    shard_out, shard_value, shard_key, shard_query = scatter(
        [
            part.astype(BF16).reshape(slots)
            for part in (out_part, value_part, key_part, query_weight_part)
        ],
        True,
        10,
    )
    smalls_grad = total(
        jnp.concatenate(
            [
                grad_time,
                grad_media_gain,
                grad_latent_gain,
                grad_ffn_gain,
                jnp.zeros((5, width), F32),
            ],
            axis=0,
        )
    )
    place = (column * 8 + row_index) * shard
    mine = lax.dynamic_slice(smalls_grad, (0, place), (16, shard))
    return (
        new_latents,
        media_grad,
        latents_grad,
        mine[:8],
        mine[8],
        mine[9],
        mine[10],
        shard_query,
        shard_key,
        shard_value,
        shard_out,
        shard_up,
        shard_down,
    )


def solution(mesh):
    in_specs = (
        P(("gx", "gy"), None),
        P(("gx", "gy"), None),
        P(),
        P(("gx", "gy")),
        P(("gx", "gy")),
        P(None, ("gx", "gy")),
        P(("gx", "gy")),
        P(("gx", "gy")),
        P(("gx", "gy")),
        P(("gx", "gy"), None),
        P(("gx", "gy"), None),
        P(("gx", "gy"), None),
        P(("gx", "gy"), None),
        P(("gx", "gy"), None),
        P(("gx", "gy"), None),
        P(("gx", "gy"), None),
    )
    out_specs = (
        P(("gx", "gy"), None),
        P(("gx", "gy"), None),
        P(("gx", "gy"), None),
        P(None, ("gx", "gy")),
        P(("gx", "gy")),
        P(("gx", "gy")),
        P(("gx", "gy")),
        P(("gx", "gy"), None),
        P(("gx", "gy"), None),
        P(("gx", "gy"), None),
        P(("gx", "gy"), None),
        P(("gx", "gy"), None),
        P(("gx", "gy"), None),
    )
    return jax.shard_map(
        per_device if dict(mesh.shape) == {"gx": 4, "gy": 8} else plain_device,
        mesh=mesh, in_specs=in_specs, out_specs=out_specs, check_vma=False
    )
```

```python
from functools import partial

import jax
import jax.numpy as jnp
from jax import lax
from jax.experimental import pallas as pl
from jax.experimental.pallas import tpu as pltpu
from jax.sharding import PartitionSpec as P

H = 16


ENTROPY_WEIGHT = 4.0
NORM_STABILIZER = 1e-05
AXES = ("gx", "gy")
LINES = 4
PLANE = 4
HBM = pl.ANY
BF16 = jnp.bfloat16
F32 = jnp.float32


def here():
    z = lax.axis_index("gx")
    g = lax.axis_index("gy")
    return z, g, g // 2, g % 2


def sibling(g):
    return g + 1 - 2 * (g % 2)


def along_x(g):
    return g + 2 - 4 * ((g // 2) % 2)


def along_y(g):
    return (g + 4) % 8


def turn(z, k):
    return (z + k) % LINES


def greet(devices):
    barrier = pltpu.get_barrier_semaphore()
    for device in devices:
        pl.semaphore_signal(
            barrier, inc=1, device_id=device, device_id_type=pl.DeviceIdType.MESH
        )
    pl.semaphore_wait(barrier, len(devices))


def line_of(z, g):
    return [(turn(z, k), g) for k in (1, 2, 3)]


class Wires:
    def __init__(self, send_sems, recv_sems):
        self.send_sems, self.recv_sems, self.used, self.sent = send_sems, recv_sems, 0, []

    def reserve(self, count):
        first = self.used
        self.used += count
        return first

    def copy(self, source, target, device, send, recv):
        return pltpu.make_async_remote_copy(
            src_ref=source,
            dst_ref=target,
            send_sem=self.send_sems.at[send],
            recv_sem=self.recv_sems.at[recv],
            device_id=device,
            device_id_type=pl.DeviceIdType.MESH,
        )

    def send(self, source, target, device):
        n = self.reserve(1)
        copy = self.copy(source, target, device, n, n)
        copy.start()
        self.sent.append((None, copy))
        return copy

    def send_if(self, condition, source, target, device, send, recv):
        copy = self.copy(source, target, device, send, recv)
        self.sent.append((condition, copy))

        @pl.when(condition)
        def _():
            copy.start()

        return copy

    def drain(self):
        for condition, copy in self.sent:
            if condition is None:
                copy.wait_send()
            else:
                pl.when(condition)(copy.wait_send)


class Line:
    def __init__(self, wires, shard, slot):
        self.wires, self.shard, self.slot = wires, shard, slot
        self.z, self.g, _, _ = here()
        self.base = wires.reserve(4)
        low, high = (3 - self.z) // 3, self.z // 3
        self.order = (1 + 2 * low, 3 - low - high, 2 - low + high)

    def first(self):
        z, g = self.z, self.g
        own = self.slot(z)
        base = self.base
        self.wires.send_if(z < 3, self.shard, own, (turn(z, 1), g), base + 1, base + 1)
        self.wires.send_if(z > 0, self.shard, own, (turn(z, 3), g), base + 3, base + 3)
        self.across = self.wires.copy(self.shard, own, (turn(z, 2), g), base + 2, base + 2)
        self.across.start()
        self.wires.sent.append((None, self.across))

    def take(self, step):
        z, g = self.z, self.g
        k = self.order[step]
        origin = turn(z, LINES - k)
        held = self.slot(origin)
        self.wires.copy(held, held, (z, g), 0, self.base + k).wait_recv()
        if step == 2:
            self.relay(z == 2, 3, 3)
        if step == 2:
            self.relay(z == 1, 0, 1)
        return origin

    def relay(self, condition, there, k):
        held = self.slot(turn(self.z, 2))
        self.wires.send_if(
            condition, held, held, (there, self.g), self.base, self.base + k
        )


class Spread:
    def __init__(self, wires, shard, slot, half, whole):
        self.wires, self.shard, self.slot, self.half, self.whole = wires, shard, slot, half, whole
        self.z, self.g, _, _ = here()
        self.line = Line(wires, shard, lambda z: slot(z, self.g))
        self.zs, self.x, self.y, self.dx, self.dy, self.sib = [self.z], [], [], {}, {}, []

    def side(self, gy):
        return (self.z, gy)

    def to_sibling(self, held):
        if self.whole:
            self.sib.append(self.wires.send(held, held, self.side(sibling(self.g))))

    def first(self):
        own = self.slot(self.z, self.g)
        self.line.first()
        self.x.append(self.wires.send(self.shard, own, self.side(along_x(self.g))))
        self.y.append(self.wires.send(self.shard, own, self.side(along_y(self.g))))
        if self.whole:
            self.sib.append(self.wires.send(self.shard, own, self.side(sibling(self.g))))

    def column(self, step):
        self.zs.append(self.line.take(step))
        held = self.slot(self.zs[-1], self.g)
        self.x.append(self.wires.send(held, held, self.side(along_x(self.g))))
        self.y.append(self.wires.send(held, held, self.side(along_y(self.g))))
        self.to_sibling(held)

    def corner(self, n):
        self.corner_x(n)
        self.corner_y(n)

    def corner_x(self, n):
        self.x[n].wait_recv()
        held = self.slot(self.zs[n], along_x(self.g))
        part = self.half(held, 0)
        self.dy[n] = self.wires.send(part, part, self.side(along_y(self.g)))
        self.to_sibling(held)

    def corner_y(self, n):
        self.y[n].wait_recv()
        held = self.slot(self.zs[n], along_y(self.g))
        part = self.half(held, 1)
        self.dx[n] = self.wires.send(part, part, self.side(along_x(self.g)))
        self.to_sibling(held)

    def last(self, n):
        self.dy[n].wait_recv()
        self.dx[n].wait_recv()
        self.to_sibling(self.slot(self.zs[n], along_y(along_x(self.g))))

    def finish(self):
        for copy in self.sib:
            copy.wait_recv()


def spread_all(flows):
    for flow in flows:
        flow.first()
    for flow in flows:
        flow.corner(0)
    for step in range(3):
        for flow in flows:
            flow.column(step)
        for flow in flows:
            flow.corner(step + 1)
    for n in range(4):
        for flow in flows:
            flow.last(n)
    for flow in flows:
        flow.finish()


LINE_SEMS = 4


def spread_sems(whole):
    return LINE_SEMS + 8 + 8 + (16 if whole else 0)


def columns_half(ref, which):
    width = ref.shape[-1] // 2
    return ref.at[..., pl.ds(which * width, width)]


def rows_half(ref, which):
    rows = ref.shape[0] // 2
    return ref.at[pl.ds(which * rows, rows)]


def sides_of(z, g, whole):
    near = [(z, along_x(g)), (z, along_y(g))]
    return near + [(z, sibling(g))] if whole else near


def params(ident):
    return pltpu.CompilerParams(
        collective_id=ident, has_side_effects=True, vmem_limit_bytes=60 * 2**20
    )


def sems(count):
    return pltpu.SemaphoreType.DMA((count,))


VMEM = pl.BlockSpec(memory_space=pltpu.VMEM)
LEFT = pl.BlockSpec(memory_space=HBM)


def gather_kernel(shard, out, send_sems, recv_sems, local_sem):
    z, g, chip, core = here()
    greet(line_of(z, g) + sides_of(z, g, False))
    wires = Wires(send_sems, recv_sems)
    copy = pltpu.make_async_copy(shard, out.at[4 * z + chip], local_sem)
    copy.start()
    spread_all([Spread(wires, shard, lambda zz, gg: out.at[zz * 4 + gg // 2], columns_half, False)])
    copy.wait()
    wires.drain()


def gather(shard, ident):
    return pl.pallas_call(
        gather_kernel,
        out_shape=jax.ShapeDtypeStruct((16,) + shard.shape, shard.dtype),
        in_specs=[LEFT],
        out_specs=LEFT,
        scratch_shapes=[sems(spread_sems(False)), sems(spread_sems(False)), pltpu.SemaphoreType.DMA],
        compiler_params=params(ident),
        name="gather",
    )(shard)


class Exchange:
    def __init__(self, wires, pairs):
        self.wires, self.pairs = wires, pairs
        self.z, self.g, _, _ = here()

    def first(self):
        z = self.z
        self.copies = []
        for k in (2, 1, 3):
            there = turn(z, k)
            for source, out in self.pairs:
                self.copies.append(
                    self.wires.send(source.at[there], out.at[z], (there, self.g))
                )
        for source, out in self.pairs:
            out[z] = source[z]

    def finish(self):
        for copy in self.copies:
            copy.wait_recv()


def add_slots(target, source, count):
    @pl.loop(0, count)
    def _(n):
        target[n] = (target[n].astype(F32) + source[n].astype(F32)).astype(target.dtype)


class Fold:
    def __init__(self, wires, parts, whole, scratch, out, local_sem):
        self.wires, self.parts, self.whole, self.out = wires, parts, whole, out
        self.held, self.from_sib, self.cx, self.cy, self.fx, self.fy, self.fz = scratch
        self.z, self.g, self.chip, self.core = here()
        ours = parts.at[:, :, self.core] if whole else parts
        self.load = pltpu.make_async_copy(ours, self.held, local_sem)
        self.width = self.held.shape[-1] // 2

    def chip_of(self, gy):
        return gy // 2

    def half(self, ref, which):
        return ref.at[:, :, pl.ds(which * self.width, self.width)]

    def start(self):
        self.load.start()
        if self.whole:
            theirs = self.parts.at[:, :, 1 - self.core]
            self.sib = self.wires.send(theirs, self.from_sib, (self.z, sibling(self.g)))

    def corner(self):
        self.load.wait()
        if self.whole:
            self.sib.wait_recv()

            @pl.loop(0, LINES)
            def _(n):
                for q in range(PLANE):
                    self.held[n, q] = (
                        self.held[n, q].astype(F32) + self.from_sib[n, q].astype(F32)
                    ).astype(BF16)

        far = self.held.at[:, self.chip_of(along_y(along_x(self.g)))]
        self.to_y = self.wires.send(self.half(far, 0), self.cy, (self.z, along_y(self.g)))
        self.to_x = self.wires.send(self.half(far, 1), self.cx, (self.z, along_x(self.g)))

    def sides(self):
        width = self.width
        self.to_y.wait_recv()
        near = self.chip_of(along_x(self.g))

        @pl.loop(0, LINES)
        def _(n):
            self.held[n, near, :, :width] = (
                self.held[n, near, :, :width].astype(F32) + self.cy[n].astype(F32)
            ).astype(BF16)

        self.along_x = self.wires.send(self.held.at[:, near], self.fx, (self.z, along_x(self.g)))
        self.to_x.wait_recv()
        beside = self.chip_of(along_y(self.g))

        @pl.loop(0, LINES)
        def _(n):
            self.held[n, beside, :, width:] = (
                self.held[n, beside, :, width:].astype(F32) + self.cx[n].astype(F32)
            ).astype(BF16)

        self.along_y = self.wires.send(self.held.at[:, beside], self.fy, (self.z, along_y(self.g)))

    def line(self):
        self.along_x.wait_recv()
        self.along_y.wait_recv()
        self.zs = []
        for k in (2, 1, 3):
            there = turn(self.z, k)
            self.fx[there] = (
                self.held[there, self.chip].astype(F32)
                + self.fx[there].astype(F32)
                + self.fy[there].astype(F32)
            ).astype(BF16)
            self.zs.append(
                self.wires.send(self.fx.at[there], self.fz.at[k - 1], (there, self.g))
            )
        z = self.z
        self.out[...] = (
            self.held[z, self.chip].astype(F32) + self.fx[z].astype(F32) + self.fy[z].astype(F32)
        )

    def finish(self):
        for copy in self.zs:
            copy.wait_recv()
        self.out[...] += (
            self.fz[0].astype(F32) + self.fz[1].astype(F32) + self.fz[2].astype(F32)
        )


def fold_scratch(rows, cols, whole):
    half = cols // 2
    return [
        pltpu.VMEM((LINES, PLANE, rows, cols), BF16),
        pltpu.VMEM((LINES, PLANE, rows, cols) if whole else (1, 1, 16, 128), BF16),
        pltpu.VMEM((LINES, rows, half), BF16),
        pltpu.VMEM((LINES, rows, half), BF16),
        pltpu.VMEM((LINES, rows, cols), BF16),
        pltpu.VMEM((LINES, rows, cols), BF16),
        pltpu.VMEM((LINES - 1, rows, cols), BF16),
    ]


def fold_sems(whole):
    return (1 if whole else 0) + 4 + 3


def fold_all(flows):
    stages = ("corner", "sides", "line", "finish")
    for tick in range(len(flows) + len(stages) - 1):
        for n in range(len(stages)):
            flow = tick - n
            if 0 <= flow < len(flows):
                getattr(flows[flow], stages[n])()


def scatter_kernel(count, whole, *refs):
    parts, outs = refs[:count], refs[count : 2 * count]
    send_sems, recv_sems, local_sems = refs[2 * count : 2 * count + 3]
    scratch = refs[2 * count + 3 :]
    z, g, chip, core = here()
    greet(line_of(z, g) + sides_of(z, g, whole))
    wires = Wires(send_sems, recv_sems)
    flows = [
        Fold(wires, parts[n], whole, scratch[7 * n : 7 * n + 7], outs[n], local_sems.at[n])
        for n in range(count)
    ]
    for flow in flows:
        flow.start()
    fold_all(flows)
    wires.drain()


def scatter(parts, whole, ident):
    count = len(parts)
    rows, cols = parts[0].shape[-2:]
    scratch = []
    for _ in parts:
        scratch += fold_scratch(rows, cols, whole)
    wires = count * fold_sems(whole)
    return pl.pallas_call(
        partial(scatter_kernel, count, whole),
        out_shape=[jax.ShapeDtypeStruct((rows, cols), F32)] * count,
        in_specs=[LEFT] * count,
        out_specs=[VMEM] * count,
        scratch_shapes=[sems(wires), sems(wires), sems(count)] + scratch,
        compiler_params=params(ident),
        name="scatter_%d" % ident,
    )(*parts)


def layer_norm(row_block, gain_row):
    row_mean = jnp.mean(row_block, axis=-1, keepdims=True)
    centred = row_block - row_mean
    variance = jnp.mean(centred * centred, axis=-1, keepdims=True)
    return centred * lax.rsqrt(variance + NORM_STABILIZER) * gain_row


def product(left_side, right_side):
    return jnp.dot(left_side, right_side, preferred_element_type=jnp.float32)


def inner_first(left_side, right_side):
    return lax.dot_general(
        left_side, right_side, (((0,), (0,)), ((), ())), preferred_element_type=jnp.float32
    )


def inner_last(left_side, right_side):
    return lax.dot_general(
        left_side, right_side, (((1,), (1,)), ((), ())), preferred_element_type=jnp.float32
    )


def collect(onehot_rows, value_rows):
    return lax.dot_general(
        onehot_rows,
        value_rows,
        (((0,), (0,)), ((), ())),
        precision=lax.Precision.HIGHEST,
        preferred_element_type=jnp.float32,
    )


def plain_device(
    media,
    latents,
    frame_counts,
    time_index,
    valid,
    time_table,
    media_gain,
    latent_gain,
    ffn_gain,
    w_query,
    w_key,
    w_value,
    w_out,
    w_up,
    w_down,
    cotangent,
):
    frames = time_index.shape[0]
    patches = valid.shape[0] // frames
    latent_rows = latents.shape[0]
    model_width = latents.shape[1]
    head_size = model_width // H
    score_scale = head_size ** (-0.5)
    across = lax.axis_size("gx")
    column = lax.axis_index("gx")
    row_index = lax.axis_index("gy")
    frame_ends = jnp.cumsum(frame_counts[row_index])
    position = column * frames + jnp.arange(frames, dtype=jnp.int32)
    item_index = jnp.sum((frame_ends[None, :] <= position[:, None]).astype(jnp.int32), axis=1)
    item_onehot = (item_index[:, None] == jnp.arange(across, dtype=jnp.int32)[None, :]).astype(
        jnp.float32
    )
    (
        full_query,
        full_key,
        full_value,
        full_out,
        full_up,
        full_down,
        full_media_gain,
        full_latent_gain,
        full_ffn_gain,
        full_time,
    ) = (
        lax.all_gather(w_query, ("gx", "gy"), axis=0, tiled=True),
        lax.all_gather(w_key, ("gx", "gy"), axis=0, tiled=True),
        lax.all_gather(w_value, ("gx", "gy"), axis=0, tiled=True),
        lax.all_gather(w_out, ("gx", "gy"), axis=0, tiled=True),
        lax.all_gather(w_up, ("gx", "gy"), axis=0, tiled=True),
        lax.all_gather(w_down, ("gx", "gy"), axis=0, tiled=True),
        lax.all_gather(media_gain, ("gx", "gy"), axis=0, tiled=True),
        lax.all_gather(latent_gain, ("gx", "gy"), axis=0, tiled=True),
        lax.all_gather(ffn_gain, ("gx", "gy"), axis=0, tiled=True),
        lax.all_gather(time_table, ("gx", "gy"), axis=1, tiled=True),
    )
    time_onehot = (
        time_index[:, None] == jnp.arange(full_time.shape[0], dtype=jnp.int32)[None, :]
    ).astype(jnp.float32)
    time_rows = product(time_onehot.astype(jnp.bfloat16), full_time)
    media_in = (
        media.astype(jnp.float32).reshape(frames, patches, model_width) + time_rows[:, None, :]
    ).reshape(-1, model_width)
    media_normed = layer_norm(media_in, full_media_gain.astype(jnp.float32)).astype(jnp.bfloat16)
    key_heads = (
        product(media_normed, full_key).astype(jnp.bfloat16).reshape(frames, patches, H, head_size)
    )
    value_heads = (
        product(media_normed, full_value)
        .astype(jnp.bfloat16)
        .reshape(frames, patches, H, head_size)
    )
    latent_in = latents.astype(jnp.float32)
    latent_normed = layer_norm(latent_in, full_latent_gain.astype(jnp.float32)).astype(jnp.bfloat16)
    own_query = product(latent_normed, full_query).astype(jnp.bfloat16)
    own_key = product(latent_normed, full_key).astype(jnp.bfloat16)
    own_value = product(latent_normed, full_value).astype(jnp.bfloat16)
    valid_total = lax.psum(jnp.sum(valid.astype(jnp.float32)), ("gx", "gy"))
    coefficient = ENTROPY_WEIGHT * (valid.shape[0] * lax.axis_size(("gx", "gy"))) / valid_total
    query_table = lax.all_gather(own_query, "gx", axis=0, tiled=True)
    picked = query_table.reshape(-1, latent_rows, H, head_size)[item_index]
    media_score = (
        jnp.einsum("flhd,fphd->flhp", picked, key_heads, preferred_element_type=jnp.float32)
        * score_scale
    )
    valid_mask = valid.reshape(frames, 1, 1, patches) > 0
    media_expo = jnp.where(valid_mask, jnp.exp(media_score), 0.0)
    expo_low = media_expo.astype(jnp.bfloat16)
    media_total = jnp.sum(media_expo, axis=-1)
    media_moment = jnp.sum(media_expo * media_score, axis=-1)
    media_weighted = jnp.einsum(
        "flhp,fphd->flhd", expo_low, value_heads, preferred_element_type=jnp.float32
    )
    dense_weighted = collect(item_onehot, media_weighted.reshape(frames, -1)).reshape(
        -1, model_width
    )
    dense_total = collect(item_onehot, media_total.reshape(frames, -1)).reshape(-1, H)
    dense_moment = collect(item_onehot, media_moment.reshape(frames, -1)).reshape(-1, H)
    got_weighted, got_total, got_moment = (
        lax.psum_scatter(dense_weighted, "gx", scatter_dimension=0, tiled=True),
        lax.psum_scatter(dense_total, "gx", scatter_dimension=0, tiled=True),
        lax.psum_scatter(dense_moment, "gx", scatter_dimension=0, tiled=True),
    )
    query_head_count = own_query.reshape(latent_rows, H, head_size)
    latent_key_rows = own_key.reshape(latent_rows, H, head_size)
    latent_value_rows = own_value.reshape(latent_rows, H, head_size)
    latent_score = (
        jnp.einsum(
            "uer,zer->uez", query_head_count, latent_key_rows, preferred_element_type=jnp.float32
        )
        * score_scale
    )
    latent_expo = jnp.exp(latent_score)
    latent_reduced_precision = latent_expo.astype(jnp.bfloat16)
    weighted = got_weighted.reshape(latent_rows, H, head_size) + jnp.einsum(
        "nwr,rwb->nwb",
        latent_reduced_precision,
        latent_value_rows,
        preferred_element_type=jnp.float32,
    )
    totals = got_total + jnp.sum(latent_expo, axis=-1)
    moment = got_moment + jnp.sum(latent_expo * latent_score, axis=-1)
    attention = weighted / totals[..., None]
    attn_low = attention.reshape(latent_rows, model_width).astype(jnp.bfloat16)
    middle = latent_in + product(attn_low, full_out)
    ffn_normed = layer_norm(middle, full_ffn_gain.astype(jnp.float32)).astype(jnp.bfloat16)
    up_rows = product(ffn_normed, full_up)
    hidden = jax.nn.gelu(up_rows, approximate=False).astype(jnp.bfloat16)
    new_latents = (middle + product(hidden, full_down)).astype(jnp.bfloat16)
    (
        back_query,
        back_key,
        back_value,
        back_out,
        back_up,
        back_down,
        back_media_gain,
        back_latent_gain,
        back_ffn_gain,
    ) = (
        lax.all_gather(w_query, ("gx", "gy"), axis=0, tiled=True),
        lax.all_gather(w_key, ("gx", "gy"), axis=0, tiled=True),
        lax.all_gather(w_value, ("gx", "gy"), axis=0, tiled=True),
        lax.all_gather(w_out, ("gx", "gy"), axis=0, tiled=True),
        lax.all_gather(w_up, ("gx", "gy"), axis=0, tiled=True),
        lax.all_gather(w_down, ("gx", "gy"), axis=0, tiled=True),
        lax.all_gather(media_gain, ("gx", "gy"), axis=0, tiled=True),
        lax.all_gather(latent_gain, ("gx", "gy"), axis=0, tiled=True),
        lax.all_gather(ffn_gain, ("gx", "gy"), axis=0, tiled=True),
    )
    owned_latent, owned_attn, owned_ffn, owned_hidden = (
        lax.all_to_all(latent_normed, ("gx", "gy"), split_axis=1, concat_axis=0, tiled=True),
        lax.all_to_all(attn_low, ("gx", "gy"), split_axis=1, concat_axis=0, tiled=True),
        lax.all_to_all(ffn_normed, ("gx", "gy"), split_axis=1, concat_axis=0, tiled=True),
        lax.all_to_all(hidden, ("gx", "gy"), split_axis=1, concat_axis=0, tiled=True),
    )
    hidden_grad = inner_last(cotangent, back_down)
    gelu_pull = jax.vjp(partial(jax.nn.gelu, approximate=False), up_rows)[1]
    up_grad = gelu_pull(hidden_grad)[0].astype(jnp.bfloat16)
    ffn_normed_grad = inner_last(up_grad, back_up)
    ffn_pull = jax.vjp(layer_norm, middle, back_ffn_gain.astype(jnp.float32))[1]
    middle_part, grad_ffn_gain = ffn_pull(ffn_normed_grad)
    middle_grad = cotangent.astype(jnp.float32) + middle_part
    middle_low = middle_grad.astype(jnp.bfloat16)
    attn_grad = inner_last(middle_low, back_out).reshape(latent_rows, H, head_size)
    weighted_sum_gradient = (attn_grad / totals[..., None]).astype(jnp.bfloat16)
    slope_term = -coefficient / totals
    shift_term = (
        -jnp.sum(attn_grad * attention, axis=-1) / totals
        + coefficient * (1.0 / totals + moment / (totals * totals))
        + slope_term
    )
    latent_mix = jnp.einsum(
        "uer,zer->uez", weighted_sum_gradient, latent_value_rows, preferred_element_type=jnp.float32
    )
    latent_sgrad = latent_expo * (
        latent_mix + shift_term[..., None] + slope_term[..., None] * latent_score
    )
    latent_residual_gradient = (latent_sgrad * score_scale).astype(jnp.bfloat16)
    query_part = jnp.einsum(
        "nwr,rwb->nwb",
        latent_residual_gradient,
        latent_key_rows,
        preferred_element_type=jnp.float32,
    )
    own_key_grad = (
        jnp.einsum(
            "zry,zrj->yrj",
            latent_residual_gradient,
            query_head_count,
            preferred_element_type=jnp.float32,
        )
        .astype(jnp.bfloat16)
        .reshape(latent_rows, model_width)
    )
    own_value_grad = (
        jnp.einsum(
            "zry,zrj->yrj",
            latent_reduced_precision,
            weighted_sum_gradient,
            preferred_element_type=jnp.float32,
        )
        .astype(jnp.bfloat16)
        .reshape(latent_rows, model_width)
    )
    grad_table = lax.all_gather(
        weighted_sum_gradient.reshape(latent_rows, model_width), "gx", axis=0, tiled=True
    )
    shift_table, slope_table = (
        lax.all_gather(shift_term, "gx", axis=0, tiled=True),
        lax.all_gather(slope_term, "gx", axis=0, tiled=True),
    )
    picked_grad = grad_table.reshape(-1, latent_rows, H, head_size)[item_index]
    picked_shift = shift_table.reshape(-1, latent_rows, H)[item_index]
    picked_slope = slope_table.reshape(-1, latent_rows, H)[item_index]
    media_mix = jnp.einsum(
        "flhd,fphd->flhp", picked_grad, value_heads, preferred_element_type=jnp.float32
    )
    media_sgrad = media_expo * (
        media_mix + picked_shift[..., None] + picked_slope[..., None] * media_score
    )
    media_rgrad = (media_sgrad * score_scale).astype(jnp.bfloat16)
    query_terms = jnp.einsum(
        "flhp,fphd->flhd", media_rgrad, key_heads, preferred_element_type=jnp.float32
    )
    dense_query = collect(item_onehot, query_terms.reshape(frames, -1)).reshape(-1, model_width)
    got_query = lax.psum_scatter(
        dense_query.astype(jnp.bfloat16), "gx", scatter_dimension=0, tiled=True
    ).astype(jnp.float32)
    media_key_grad = (
        jnp.einsum("flhp,flhd->fphd", media_rgrad, picked, preferred_element_type=jnp.float32)
        .astype(jnp.bfloat16)
        .reshape(-1, model_width)
    )
    media_value_grad = (
        jnp.einsum("flhp,flhd->fphd", expo_low, picked_grad, preferred_element_type=jnp.float32)
        .astype(jnp.bfloat16)
        .reshape(-1, model_width)
    )
    grad_key = inner_first(media_normed, media_key_grad) + inner_first(latent_normed, own_key_grad)
    grad_value = inner_first(media_normed, media_value_grad) + inner_first(
        latent_normed, own_value_grad
    )
    media_normed_grad = inner_last(media_key_grad, back_key) + inner_last(
        media_value_grad, back_value
    )
    media_pull = jax.vjp(layer_norm, media_in, back_media_gain.astype(jnp.float32))[1]
    media_grad, grad_media_gain = media_pull(media_normed_grad)
    frame_sums = jnp.sum(media_grad.reshape(frames, patches, model_width), axis=1)
    grad_time = collect(time_onehot, frame_sums)
    query_grad = (
        (got_query.reshape(latent_rows, H, head_size) + query_part)
        .astype(jnp.bfloat16)
        .reshape(latent_rows, model_width)
    )
    latent_normed_grad = (
        inner_last(query_grad, back_query)
        + inner_last(own_key_grad, back_key)
        + inner_last(own_value_grad, back_value)
    )
    latent_pull = jax.vjp(layer_norm, latent_in, back_latent_gain.astype(jnp.float32))[1]
    latent_part, grad_latent_gain = latent_pull(latent_normed_grad)
    latents_grad = middle_grad + latent_part
    piece_query = lax.all_gather(query_grad, ("gx", "gy"), axis=0, tiled=True)
    piece_middle = lax.all_gather(middle_low, ("gx", "gy"), axis=0, tiled=True)
    piece_up = lax.all_gather(up_grad, ("gx", "gy"), axis=0, tiled=True)
    piece_cot = lax.all_gather(cotangent, ("gx", "gy"), axis=0, tiled=True)
    shard_query = inner_first(owned_latent, piece_query)
    shard_out = inner_first(owned_attn, piece_middle)
    shard_up = inner_first(owned_ffn, piece_up)
    shard_down = inner_first(owned_hidden, piece_cot)
    shard_grads = (
        lax.psum_scatter(grad_key, ("gx", "gy"), scatter_dimension=0, tiled=True),
        lax.psum_scatter(grad_value, ("gx", "gy"), scatter_dimension=0, tiled=True),
        lax.psum_scatter(grad_media_gain, ("gx", "gy"), scatter_dimension=0, tiled=True),
        lax.psum_scatter(grad_latent_gain, ("gx", "gy"), scatter_dimension=0, tiled=True),
        lax.psum_scatter(grad_ffn_gain, ("gx", "gy"), scatter_dimension=0, tiled=True),
        lax.psum_scatter(grad_time, ("gx", "gy"), scatter_dimension=1, tiled=True),
    )
    return (
        new_latents,
        media_grad,
        latents_grad,
        shard_grads[5],
        shard_grads[2],
        shard_grads[3],
        shard_grads[4],
        shard_query,
        shard_grads[0],
        shard_grads[1],
        shard_out,
        shard_up,
        shard_down,
    )


GROUP = 4


def mates_of(z, chip, core):
    mates = []
    for j in range(1, 16):
        there = (4 * z + chip + j) % 16
        mates.append((there // 4, 2 * (there % 4) + core))
    return mates


class GiveBack:
    def __init__(self, wires, up_ref, down_ref, up_out, down_out, scratch, local_sems):
        self.wires, self.up_out, self.down_out = wires, up_out, down_out
        self.up_held, self.up_near, self.down_near = scratch
        self.z, self.g, self.chip, self.core = here()
        self.up_ref, self.down_ref = up_ref, down_ref
        self.load_up = pltpu.make_async_copy(
            up_ref.at[:, self.core], self.up_held, local_sems.at[0]
        )
        self.load_down = pltpu.make_async_copy(
            down_ref.at[self.core], down_out, local_sems.at[1]
        )

    def start(self):
        near = (self.z, sibling(self.g))
        self.load_up.start()
        self.load_down.start()
        self.up = self.wires.send(self.up_ref.at[:, 1 - self.core], self.up_near, near)
        self.down = self.wires.send(self.down_ref.at[1 - self.core], self.down_near, near)

    def columns(self):
        self.load_up.wait()
        self.up.wait_recv()
        add_slots(self.up_held, self.up_near, 16)
        here_chip = 4 * self.z + self.chip
        self.moved = []
        for j, mate in enumerate(mates_of(self.z, self.chip, self.core)):
            there = (here_chip + j + 1) % 16
            self.moved.append(
                self.wires.send(self.up_held.at[there], self.up_out.at[here_chip], mate)
            )
        self.up_out[here_chip] = self.up_held[here_chip]

    def rows(self):
        self.load_down.wait()
        self.down.wait_recv()
        rows = self.down_out.shape[0] // 8

        @pl.loop(0, 8)
        def _(n):
            block = pl.ds(pl.multiple_of(n * rows, 8), rows)
            self.down_out[block] = self.down_out[block] + self.down_near[block]

    def finish(self):
        for copy in self.moved:
            copy.wait_recv()


def turn_kernel(
    grad,
    terms,
    down_part,
    up_grad,
    down_grad,
    grad_out,
    terms_out,
    down_out,
    up_grad_out,
    down_grad_out,
    send_sems,
    recv_sems,
    local_sems,
    up_held,
    up_near,
    down_near,
    *fold,
):
    z, g, chip, core = here()
    greet(mates_of(z, chip, core) + [(z, sibling(g))])
    wires = Wires(send_sems, recv_sems)
    lines = [
        Line(wires, grad, lambda zz: grad_out.at[zz]),
        Line(wires, terms, lambda zz: terms_out.at[zz]),
    ]
    back = GiveBack(
        wires,
        up_grad,
        down_grad,
        up_grad_out,
        down_grad_out,
        (up_held, up_near, down_near),
        local_sems,
    )
    flow = Fold(wires, down_part, False, fold, down_out, local_sems.at[2])
    flow.start()
    for line in lines:
        line.first()
    back.start()
    flow.corner()
    grad_out[z] = grad[...]
    terms_out[z] = terms[...]
    back.columns()
    flow.sides()
    for step in range(3):
        for line in lines:
            line.take(step)
    back.rows()
    flow.line()
    flow.finish()
    back.finish()
    wires.drain()


def turn_back(grad, terms, down_part, up_grad, down_grad):
    rows, width = up_grad.shape[-2:]
    down_shape = down_grad.shape[1:]
    latent_rows, model_width = grad.shape
    wires = 2 * LINE_SEMS + fold_sems(False) + 17
    return pl.pallas_call(
        turn_kernel,
        out_shape=[
            jax.ShapeDtypeStruct((LINES,) + grad.shape, BF16),
            jax.ShapeDtypeStruct((LINES,) + terms.shape, F32),
            jax.ShapeDtypeStruct(grad.shape, F32),
            jax.ShapeDtypeStruct((16, rows, width), BF16),
            jax.ShapeDtypeStruct(down_shape, F32),
        ],
        in_specs=[VMEM, VMEM, LEFT, LEFT, LEFT],
        out_specs=[VMEM] * 5,
        scratch_shapes=[
            sems(wires),
            sems(wires),
            sems(3),
            pltpu.VMEM((16, rows, width), BF16),
            pltpu.VMEM((16, rows, width), BF16),
            pltpu.VMEM(down_shape, F32),
        ]
        + fold_scratch(latent_rows, model_width, False),
        compiler_params=params(2),
        name="turn_back",
    )(grad, terms, down_part, up_grad, down_grad)


def queries_kernel(parts, weight_part, out, weight_out, send_sems, recv_sems, local_sem, *fold):
    z, g, _, _ = here()
    greet(line_of(z, g) + sides_of(z, g, True))
    wires = Wires(send_sems, recv_sems)
    exchange = Exchange(wires, [(parts, out)])
    flow = Fold(wires, weight_part, True, fold, weight_out, local_sem)
    flow.start()
    exchange.first()
    fold_all([flow])
    exchange.finish()
    wires.drain()


def queries_home(parts, weight_part):
    rows, cols = weight_part.shape[-2:]
    wires = fold_sems(True) + 3
    return pl.pallas_call(
        queries_kernel,
        out_shape=[
            jax.ShapeDtypeStruct(parts.shape, BF16),
            jax.ShapeDtypeStruct((rows, cols), F32),
        ],
        in_specs=[VMEM, LEFT],
        out_specs=[VMEM, VMEM],
        scratch_shapes=[sems(wires), sems(wires), pltpu.SemaphoreType.DMA]
        + fold_scratch(rows, cols, True),
        compiler_params=params(3),
        name="queries_home",
    )(parts, weight_part)


class Total:
    def __init__(self, wires, mine, out, sums, got):
        self.wires, self.out, self.sums, self.got = wires, out, sums, got
        self.z, self.g, _, _ = here()
        self.source = mine
        self.step = 0

    def push(self):
        sides = [sibling(self.g), along_x(self.g), along_y(self.g)]
        if self.step < 3:
            self.copies = [
                self.wires.send(self.source, self.got.at[self.step], (self.z, sides[self.step]))
            ]
        else:
            self.copies = [
                self.wires.send(self.source, self.got.at[3 + k], device)
                for k, device in enumerate(line_of(self.z, self.g))
            ]

    def pull(self):
        for copy in self.copies:
            copy.wait_recv()
        if self.step < 3:
            self.sums[self.step] = self.source[...] + self.got[self.step]
            self.source = self.sums.at[self.step]
            self.step += 1
        else:
            self.out[...] = self.source[...] + self.got[3] + self.got[4] + self.got[5]


def ending_kernel(count, *refs):
    parts, small, outs = refs[:count], refs[count], refs[count + 1 : 2 * count + 1]
    small_out, send_sems, recv_sems, local_sems, small_sums, small_got = refs[
        2 * count + 1 : 2 * count + 7
    ]
    scratch = refs[2 * count + 7 :]
    z, g, _, _ = here()
    greet(line_of(z, g) + sides_of(z, g, True))
    wires = Wires(send_sems, recv_sems)
    flows = [
        Fold(wires, parts[n], True, scratch[7 * n : 7 * n + 7], outs[n], local_sems.at[n])
        for n in range(count)
    ]
    total = Total(wires, small, small_out, small_sums, small_got)
    total.push()
    for flow in flows:
        flow.start()
    stages = ("corner", "sides", "line", "finish")
    for tick in range(count + len(stages) - 1):
        for n in range(len(stages)):
            if 0 <= tick - n < count:
                getattr(flows[tick - n], stages[n])()
        if tick < 4:
            total.pull()
            if tick < 3:
                total.push()
    wires.drain()


def ending(parts, small):
    count = len(parts)
    rows, cols = parts[0].shape[-2:]
    scratch = []
    for _ in parts:
        scratch += fold_scratch(rows, cols, True)
    wires = count * fold_sems(True) + 6
    return pl.pallas_call(
        partial(ending_kernel, count),
        out_shape=[jax.ShapeDtypeStruct((rows, cols), F32)] * count
        + [jax.ShapeDtypeStruct(small.shape, F32)],
        in_specs=[LEFT] * count + [VMEM],
        out_specs=[VMEM] * (count + 1),
        scratch_shapes=[
            sems(wires),
            sems(wires),
            sems(count),
            pltpu.VMEM((3,) + small.shape, F32),
            pltpu.VMEM((6,) + small.shape, F32),
        ]
        + scratch,
        compiler_params=params(4),
        name="ending",
    )(*parts, small)


def head_masks(rows, width, head_size):
    lane = lax.broadcasted_iota(jnp.int32, (rows, width), 1)
    return [(lane >= h * head_size) & (lane < (h + 1) * head_size) for h in range(GROUP)]


def stacked(block, masks):
    zero = jnp.zeros_like(block)
    return jnp.concatenate([jnp.where(mask, block, zero) for mask in masks], axis=0)


def unstacked(block, masks):
    rows = block.shape[0] // GROUP
    total = jnp.where(masks[0], block[:rows], 0.0)
    for h in range(1, GROUP):
        total = jnp.where(masks[h], block[h * rows : (h + 1) * rows], total)
    return total


def dot_last(a, b):
    return lax.dot_general(a, b, (((1,), (1,)), ((), ())), preferred_element_type=F32)


def dot_first(a, b):
    return lax.dot_general(a, b, (((0,), (0,)), ((), ())), preferred_element_type=F32)


def spread_heads(columns, first, masks):
    out = jnp.where(masks[0], columns[:, first : first + 1], 0.0)
    for h in range(1, GROUP):
        out = jnp.where(masks[h], columns[:, first + h : first + h + 1], out)
    return out


def attend(queries, keys, values, valid, scale, masks):
    rows = queries.shape[0]
    score = dot_last(stacked(queries, masks), keys) * scale
    expo = jnp.exp(score)
    if valid is not None:
        expo = jnp.where(valid > 0, expo, 0.0)
    totals = jnp.sum(expo, axis=1, keepdims=True)
    moments = jnp.sum(expo * score, axis=1, keepdims=True)
    weighted = jnp.dot(expo.astype(BF16), values, preferred_element_type=F32)
    heads = [(totals[h * rows : (h + 1) * rows], moments[h * rows : (h + 1) * rows]) for h in range(GROUP)]
    return unstacked(weighted, masks), heads


def put_heads(heads, group, lane):
    out = jnp.zeros(lane.shape, F32)
    for h, (total, moment) in enumerate(heads):
        out = jnp.where(lane == group * GROUP + h, total, out)
        out = jnp.where(lane == H + group * GROUP + h, moment, out)
    return out


def multiply(left, right, out, tile):
    @pl.loop(0, right.shape[1] // tile)
    def _(n):
        cols = pl.ds(pl.multiple_of(n * tile, 128), tile)
        out[:, cols] = jnp.dot(left[...], right[:, cols], preferred_element_type=F32).astype(BF16)


def assemble(smalls, out):
    count, rows, lanes = smalls.shape
    shard = out.shape[1] // count
    block = 8
    row = lax.broadcasted_iota(jnp.int32, (block * lanes, block * shard), 0)
    col = lax.broadcasted_iota(jnp.int32, (block * lanes, block * shard), 1)
    lane = row % lanes
    chosen = ((row // lanes) * shard + lane == col) & (lane < shard)
    place = jnp.where(chosen, 1.0, 0.0).astype(BF16)
    for n in range(count // block):
        pieces = jnp.concatenate([smalls[n * block + d] for d in range(block)], axis=1)
        out[:, n * block * shard : (n + 1) * block * shard] = jnp.dot(
            pieces.astype(BF16), place, preferred_element_type=F32
        )


def up_places(z, chip):
    places = []
    for dz in range(LINES):
        for dx, dy in ((0, 0), (1, 0), (0, 1), (1, 1)):
            if dz or dx or dy:
                x, y = chip % 2, chip // 2
                there = (y + dy) % 2 * 2 + (x + dx) % 2
                places.append(((turn(z, dz), there), (turn(z, LINES - dz) if dz else z, there)))
    return places


def opening_kernel(scale, *refs):
    (
        small_ref,
        key_shard,
        value_shard,
        query_shard,
        out_shard,
        latents_ref,
        up_ref,
        down_ref,
        cot_ref,
        media_ref,
        valid_ref,
        times_ref,
        item_ref,
        tables_out,
        counts_out,
        key_weight_out,
        value_weight_out,
        query_weight_out,
        out_weight_out,
        up_out,
        down_out,
        cot_out,
        normed_out,
        keys_out,
        values_out,
        table_out,
        got_weighted,
        got_stats,
        own_weighted,
        own_stats,
        send_sems,
        recv_sems,
        local_sems,
        smalls,
        key_weight,
        value_weight,
        query_weight,
        line_latents,
        line_normed,
        normed,
        keys,
        values,
        table,
        time_rows,
        sums,
        weighted,
        stats,
    ) = refs
    z, g, chip, core = here()
    here_chip = 4 * z + chip
    me = 2 * here_chip + core
    items, rows, width = line_latents.shape
    frames, _, patches = valid_ref.shape
    shard = key_shard.shape[0]
    span = width // (H // GROUP)
    up_width = up_out.shape[-1]
    near = (z, sibling(g))
    places = up_places(z, chip)
    greet([(there[0], 2 * there[1] + core) for there, _ in places] + [near])
    wires = Wires(send_sems, recv_sems)
    masks = head_masks(rows, span, span // GROUP)
    lane = lax.broadcasted_iota(jnp.int32, (rows, 128), 1)
    local = []

    def keep(source, target):
        copy = pltpu.make_async_copy(source, target, local_sems.at[len(local)])
        copy.start()
        local.append(copy)
        return copy

    def rows_of(ref):
        return lambda zz, gg: ref.at[pl.ds(pl.multiple_of((zz * 8 + gg) * shard, 16), shard)]

    def piece(place):
        return up_ref.at[:, pl.ds(pl.multiple_of((4 * place[0] + place[1]) * up_width, 128), up_width)]

    def whole(source, slot):
        return Spread(wires, source, slot, columns_half, True), keep(source, slot(z, g))

    def small_slot(zz, gg):
        return smalls.at[zz * 8 + gg]

    small = Spread(wires, small_ref, small_slot, rows_half, True)
    small_kept = keep(small_ref, small_slot(z, g))
    key, key_kept = whole(key_shard, rows_of(key_weight))
    value, value_kept = whole(value_shard, rows_of(value_weight))
    query, query_kept = whole(query_shard, rows_of(query_weight))
    out, out_kept = whole(out_shard, rows_of(out_weight_out))
    cot = Spread(wires, cot_ref, lambda zz, gg: cot_out.at[zz * 4 + gg // 2], columns_half, False)
    line = Line(wires, latents_ref, lambda zz: line_latents.at[zz])
    exchange = Exchange(wires, [(weighted, got_weighted), (stats, got_stats)])
    line_kept = keep(latents_ref, line_latents.at[z])
    late = [
        out_kept,
        keep(cot_ref, cot_out.at[here_chip]),
        keep(piece((z, chip)), up_out.at[me]),
        keep(down_ref, down_out.at[core]),
    ]
    prompt = len(local)
    moved, given, down = [], [], []
    chunk = 32

    def normalise(first, last):
        @pl.loop(first, last)
        def _(n):
            block = pl.ds(pl.multiple_of(n * chunk, chunk), chunk)
            frame = n // (patches // chunk)
            row = media_ref[block].astype(F32) + time_rows[pl.ds(frame, 1)]
            normed[block] = layer_norm(row, tables_out[8:9]).astype(BF16)

    def normalise_latents():
        gain = tables_out[9:10]
        line_kept.wait()
        for item in range(items):

            @pl.loop(0, rows // chunk)
            def _(n):
                block = pl.ds(pl.multiple_of(n * chunk, chunk), chunk)
                row = line_latents[item, block].astype(F32)
                line_normed[item, block] = layer_norm(row, gain).astype(BF16)

        normed[frames * patches :] = line_normed[z]

    def tabulate():
        small_kept.wait()
        assemble(smalls, tables_out)
        counts = smalls[0, 8:]
        for n in range(1, smalls.shape[0]):
            counts = counts + smalls[n, 8:]
        counts_out[...] = counts
        time_rows[...] = jnp.dot(
            times_ref[...], tables_out[...].astype(BF16), preferred_element_type=F32
        )

    def project_keys():
        key_kept.wait()
        keep(key_weight, key_weight_out)
        keep(normed, normed_out)
        multiply(normed, key_weight, keys, span)
        keep(keys, keys_out)

    def project_values():
        value_kept.wait()
        keep(value_weight, value_weight_out)
        multiply(normed, value_weight, values, span)
        keep(values, values_out)

    def project_queries():
        query_kept.wait()
        keep(query_weight, query_weight_out)

        @pl.loop(0, width // span)
        def _(n):
            cols = pl.ds(pl.multiple_of(n * span, 128), span)
            for item in range(items):
                table[item, :, cols] = jnp.dot(
                    line_normed[item], query_weight[:, cols], preferred_element_type=F32
                ).astype(BF16)

        keep(table, table_out)

    def attend_own():
        sums[...] = jnp.zeros_like(sums)
        stats[...] = jnp.zeros_like(stats)
        last = slice(frames * patches, frames * patches + rows)
        own = jnp.zeros((rows, 128), F32)
        for group in range(H // GROUP):
            cols = slice(group * span, (group + 1) * span)
            part, heads = attend(
                table[z, :, cols], keys[last, cols], values[last, cols], None, scale, masks
            )
            own_weighted[:, cols] = part
            own = own + put_heads(heads, group, lane)
        own_stats[...] = own

    def attend_frames(first, last):
        @pl.loop(first, last)
        def _(frame):
            block = pl.ds(pl.multiple_of(frame * patches, patches), patches)
            valid = valid_ref[frame]
            found = jnp.zeros((rows, 128), F32)
            for group in range(H // GROUP):
                cols = slice(group * span, (group + 1) * span)
                chosen = item_ref[frame, 0] * table[0, :, cols].astype(F32)
                for item in range(1, items):
                    chosen = chosen + item_ref[frame, item] * table[item, :, cols].astype(F32)
                part, heads = attend(
                    chosen.astype(BF16), keys[block, cols], values[block, cols], valid, scale, masks
                )
                found = found + put_heads(heads, group, lane)
                for item in range(items):
                    sums[item, :, cols] += item_ref[frame, item] * part
            for item in range(items):
                stats[item] += item_ref[frame, item] * found

    def down_first():
        down.append(wires.send(down_ref, down_out.at[core], near))

    def up_first():
        given.append(wires.send(piece((z, chip)), up_out.at[me], near))
        for there, _ in places:
            moved.append(
                wires.send(piece(there), up_out.at[me], (there[0], 2 * there[1] + core))
            )

    def up_last():
        for n, (_, origin) in enumerate(places):
            moved[n].wait_recv()
            held = up_out.at[2 * (4 * origin[0] + origin[1]) + core]
            given.append(wires.send(held, held, near))
        for copy in given:
            copy.wait_recv()

    def sums_first():
        weighted[...] = sums[...].astype(BF16)
        exchange.first()

    key.first()
    small.first()
    query.first()
    key.column(0)
    small.corner_y(0)
    small.column(0)
    key.column(1)
    down_first()
    query.corner_x(0)
    value.first()
    query.column(0)
    query.column(1)
    key.corner_y(1)
    key.corner_x(1)
    value.column(0)
    key.column(2)
    small.corner_x(1)
    small.corner_y(1)
    value.corner_y(0)
    query.corner_y(2)
    line.first()
    small.corner_x(0)
    query.corner_y(0)
    value.corner_y(1)
    key.corner_y(0)
    query.corner_x(1)
    small.column(1)
    query.corner_y(1)
    small.column(2)
    key.corner_x(2)
    key.corner_x(0)
    cot.first()
    value.column(1)
    value.corner_x(0)
    key.corner_x(3)
    value.column(2)
    small.last(0)
    key.last(1)
    key.corner_y(3)
    small.corner_y(2)
    value.corner_x(1)
    query.last(0)
    query.corner_x(2)
    small.corner_x(2)
    key.last(0)
    small.corner_x(3)
    out.first()
    small.corner_y(3)
    query.last(1)
    value.corner_y(3)
    small.last(1)
    value.corner_x(2)
    small.last(2)
    key.corner_y(2)
    query.column(2)
    small.last(3)
    value.last(0)
    query.last(2)
    key.last(3)
    small.finish()
    line.take(0)
    down[0].wait_recv()
    value.last(1)
    tabulate()
    out.column(0)
    query.corner_x(3)
    query.corner_y(3)
    value.corner_x(3)
    value.corner_y(2)
    line.take(1)
    normalise(0, 8)
    cot.column(0)
    cot.corner_y(0)
    line.take(2)
    up_first()
    out.column(1)
    query.last(3)
    cot.column(1)
    out.corner_y(0)
    normalise_latents()
    query.finish()
    value.last(3)
    project_queries()
    value.last(2)
    key.last(2)
    cot.corner_x(0)
    normalise(8, 16)
    out.column(2)
    value.finish()
    cot.corner_y(1)
    project_values()
    key.finish()
    project_keys()
    cot.corner_x(1)
    attend_own()
    attend_frames(0, frames // 2)
    cot.corner_y(2)
    attend_frames(frames // 2, frames)
    sums_first()
    out.corner_y(2)
    out.corner_x(2)
    cot.corner_x(2)
    cot.column(2)
    exchange.finish()
    out.corner_y(3)
    out.corner_x(1)
    cot.corner_x(3)
    cot.last(2)
    cot.corner_y(3)
    cot.last(0)
    out.corner_y(1)
    cot.last(1)
    out.corner_x(3)
    out.last(1)
    cot.last(3)
    out.corner_x(0)
    out.last(2)
    out.last(0)
    up_last()
    out.last(3)
    out.finish()
    for copy in late + local[prompt:]:
        copy.wait()
    wires.drain()


def opening(scale, small, weights, latents, w_up, w_down, cotangent, media, valid, times, items):
    rows, width = latents.shape
    shard = weights[0].shape[0]
    up_rows, up_width = w_up.shape
    all_rows = media.shape[0] + rows
    wires = 5 * spread_sems(True) + spread_sems(False) + LINE_SEMS + 31 + 1 + 6
    square = jax.ShapeDtypeStruct((width, width), BF16)
    table = jax.ShapeDtypeStruct((LINES, rows, width), BF16)
    keys = jax.ShapeDtypeStruct((all_rows, width), BF16)
    return pl.pallas_call(
        partial(opening_kernel, scale),
        out_shape=[
            jax.ShapeDtypeStruct((16, width), F32),
            jax.ShapeDtypeStruct((8, 128), F32),
            square,
            square,
            square,
            square,
            jax.ShapeDtypeStruct((32, up_rows, up_width // 16), BF16),
            jax.ShapeDtypeStruct((2,) + w_down.shape, BF16),
            jax.ShapeDtypeStruct((16,) + cotangent.shape, BF16),
            keys,
            keys,
            keys,
            table,
            table,
            jax.ShapeDtypeStruct((LINES, rows, 128), F32),
            jax.ShapeDtypeStruct((rows, width), F32),
            jax.ShapeDtypeStruct((rows, 128), F32),
        ],
        in_specs=[LEFT] * 9 + [VMEM] * 3 + [pl.BlockSpec(memory_space=pltpu.SMEM)],
        out_specs=[VMEM] * 2 + [LEFT] * 11 + [VMEM] * 4,
        scratch_shapes=[
            sems(wires),
            sems(wires),
            sems(16),
            pltpu.VMEM((32,) + small.shape, F32),
            pltpu.VMEM((width, width), BF16),
            pltpu.VMEM((width, width), BF16),
            pltpu.VMEM((width, width), BF16),
            pltpu.VMEM((LINES, rows, width), BF16),
            pltpu.VMEM((LINES, rows, width), BF16),
            pltpu.VMEM((all_rows, width), BF16),
            pltpu.VMEM((all_rows, width), BF16),
            pltpu.VMEM((all_rows, width), BF16),
            pltpu.VMEM((LINES, rows, width), BF16),
            pltpu.VMEM((8, width), F32),
            pltpu.VMEM((LINES, rows, width), F32),
            pltpu.VMEM((LINES, rows, width), BF16),
            pltpu.VMEM((LINES, rows, 128), F32),
        ],
        compiler_params=params(0),
        name="opening",
    )(small, *weights, latents, w_up, w_down, cotangent, media, valid, times, items)


def repel(queries, grads, keys, values, valid, shift, slope, scale, masks):
    query_stack = stacked(queries, masks)
    grad_stack = stacked(grads, masks)
    score = dot_last(query_stack, keys) * scale
    expo = jnp.exp(score)
    if valid is not None:
        expo = jnp.where(valid > 0, expo, 0.0)
    mix = dot_last(grad_stack, values)
    raw = (expo * (mix + shift + slope * score) * scale).astype(BF16)
    query_grad = unstacked(jnp.dot(raw, keys, preferred_element_type=F32), masks)
    key_grad = dot_first(raw, query_stack).astype(BF16)
    value_grad = dot_first(expo.astype(BF16), grad_stack).astype(BF16)
    return query_grad, key_grad, value_grad


def stacked_columns(terms, first):
    return jnp.concatenate([terms[:, first + h : first + h + 1] for h in range(GROUP)], axis=0)


def backward_kernel(
    scale,
    item_ref,
    table_ref,
    grad_ref,
    terms_ref,
    key_ref,
    value_ref,
    valid_ref,
    own_query_ref,
    own_grad_ref,
    own_terms_ref,
    own_key_ref,
    own_value_ref,
    query_grad_ref,
    key_grad_ref,
    value_grad_ref,
    own_query_grad_ref,
    own_key_grad_ref,
    own_value_grad_ref,
    sums,
):
    items, rows, width = table_ref.shape
    frames = valid_ref.shape[0]
    patches = valid_ref.shape[2]
    groups = H // GROUP
    span = width // groups
    masks = head_masks(rows, span, span // GROUP)
    sums[...] = jnp.zeros_like(sums)
    own_terms = own_terms_ref[...]
    for group in range(groups):
        cols = pl.ds(group * span, span)
        own_query_grad_ref[:, cols], own_key_grad_ref[:, cols], own_value_grad_ref[:, cols] = repel(
            own_query_ref[:, cols],
            own_grad_ref[:, cols],
            own_key_ref[:, cols],
            own_value_ref[:, cols],
            None,
            stacked_columns(own_terms, group * GROUP),
            stacked_columns(own_terms, H + group * GROUP),
            scale,
            masks,
        )

    @pl.loop(0, frames)
    def _(frame):
        item = item_ref[frame]
        block = pl.ds(pl.multiple_of(frame * patches, patches), patches)
        valid = valid_ref[frame]
        terms = terms_ref[item]
        for group in range(groups):
            cols = pl.ds(group * span, span)
            query_grad, key_grad_ref[block, cols], value_grad_ref[block, cols] = repel(
                table_ref[item, :, cols],
                grad_ref[item, :, cols],
                key_ref[block, cols],
                value_ref[block, cols],
                valid,
                stacked_columns(terms, group * GROUP),
                stacked_columns(terms, H + group * GROUP),
                scale,
                masks,
            )
            sums[item, :, cols] += query_grad

    query_grad_ref[...] = sums[...].astype(BF16)


def backward(item_index, table, grads, terms, keys, values, valid, own, scale):
    items, rows, width = table.shape
    vmem = pl.BlockSpec(memory_space=pltpu.VMEM)
    return pl.pallas_call(
        partial(backward_kernel, scale),
        out_shape=[
            jax.ShapeDtypeStruct((items, rows, width), BF16),
            jax.ShapeDtypeStruct(keys.shape, BF16),
            jax.ShapeDtypeStruct(keys.shape, BF16),
            jax.ShapeDtypeStruct((rows, width), F32),
            jax.ShapeDtypeStruct((rows, width), BF16),
            jax.ShapeDtypeStruct((rows, width), BF16),
        ],
        in_specs=[pl.BlockSpec(memory_space=pltpu.SMEM)] + [vmem] * 11,
        out_specs=[vmem] * 6,
        scratch_shapes=[pltpu.VMEM((items, rows, width), F32)],
        name="attention_backward",
    )(item_index, table, grads, terms, keys, values, valid, *own)


def settle_kernel(
    weighted_ref,
    stats_ref,
    own_weighted_ref,
    own_stats_ref,
    out_ref,
    latents_ref,
    gain_ref,
    attention_ref,
    attn_ref,
    sums_ref,
    middle_ref,
    normed_ref,
):
    rows, width = latents_ref.shape
    span = width // (H // GROUP)
    masks = head_masks(rows, span, span // GROUP)
    stats = own_stats_ref[...]
    for n in range(stats_ref.shape[0]):
        stats = stats + stats_ref[n]
    sums_ref[...] = stats
    for group in range(H // GROUP):
        cols = pl.ds(group * span, span)
        weighted = own_weighted_ref[:, cols]
        for n in range(weighted_ref.shape[0]):
            weighted = weighted + weighted_ref[n, :, cols].astype(F32)
        attention = weighted / spread_heads(stats, group * GROUP, masks)
        attention_ref[:, cols] = attention
        attn_ref[:, cols] = attention.astype(BF16)
    middle = latents_ref[...].astype(F32) + jnp.dot(
        attn_ref[...], out_ref[...], preferred_element_type=F32
    )
    middle_ref[...] = middle
    normed_ref[...] = layer_norm(middle, gain_ref[...]).astype(BF16)


def settle(weighted, stats, own_weighted, own_stats, w_out, latents, gain):
    vmem = pl.BlockSpec(memory_space=pltpu.VMEM)
    shape = latents.shape
    return pl.pallas_call(
        settle_kernel,
        out_shape=[
            jax.ShapeDtypeStruct(shape, F32),
            jax.ShapeDtypeStruct(shape, BF16),
            jax.ShapeDtypeStruct(own_stats.shape, F32),
            jax.ShapeDtypeStruct(shape, F32),
            jax.ShapeDtypeStruct(shape, BF16),
        ],
        in_specs=[vmem] * 7,
        out_specs=[vmem] * 5,
        name="settle",
    )(weighted, stats, own_weighted, own_stats, w_out, latents, gain)


def norm_pull(rows, gain, grad):
    mean = jnp.mean(rows, axis=-1, keepdims=True)
    centred = rows - mean
    inverse = lax.rsqrt(jnp.mean(centred * centred, axis=-1, keepdims=True) + NORM_STABILIZER)
    xhat = centred * inverse
    t = grad * gain
    pulled = (
        t
        - jnp.mean(t, axis=-1, keepdims=True)
        - xhat * jnp.mean(t * xhat, axis=-1, keepdims=True)
    ) * inverse
    return pulled, grad * xhat


def unsettle_kernel(
    normed_grad_ref,
    middle_ref,
    gain_ref,
    cot_ref,
    out_ref,
    attention_ref,
    stats_ref,
    coef_ref,
    middle_grad_ref,
    low_ref,
    gain_grad_ref,
    weighted_grad_ref,
    terms_ref,
    attn_grad,
):
    rows, width = middle_ref.shape
    span = width // (H // GROUP)
    masks = head_masks(rows, span, span // GROUP)
    pulled, summand = norm_pull(middle_ref[...], gain_ref[...], normed_grad_ref[...])
    gain_grad_ref[...] = jnp.sum(summand, axis=0, keepdims=True)
    middle_grad = cot_ref[...].astype(F32) + pulled
    middle_grad_ref[...] = middle_grad
    low_ref[...] = middle_grad.astype(BF16)
    attn_grad[...] = dot_last(low_ref[...], out_ref[...])
    stats = stats_ref[...]
    coef = coef_ref[0, 0]
    lane = lax.broadcasted_iota(jnp.int32, (rows, 128), 1)
    terms = jnp.zeros((rows, 128), F32)
    for group in range(H // GROUP):
        cols = pl.ds(group * span, span)
        grad = attn_grad[:, cols]
        first = group * GROUP
        weighted_grad_ref[:, cols] = (grad / spread_heads(stats, first, masks)).astype(BF16)
        along = grad * attention_ref[:, cols]
        for h in range(GROUP):
            inner = jnp.sum(jnp.where(masks[h], along, 0.0), axis=1, keepdims=True)
            total = stats[:, first + h : first + h + 1]
            moment = stats[:, H + first + h : H + first + h + 1]
            slope = -coef / total
            shift = -inner / total + coef * (1.0 / total + moment / (total * total)) + slope
            terms = jnp.where(lane == first + h, shift, terms)
            terms = jnp.where(lane == H + first + h, slope, terms)
    terms_ref[...] = terms


def unsettle(normed_grad, middle, gain, cotangent, w_out, attention, stats, coef):
    vmem = pl.BlockSpec(memory_space=pltpu.VMEM)
    shape = middle.shape
    return pl.pallas_call(
        unsettle_kernel,
        out_shape=[
            jax.ShapeDtypeStruct(shape, F32),
            jax.ShapeDtypeStruct(shape, BF16),
            jax.ShapeDtypeStruct((1, shape[1]), F32),
            jax.ShapeDtypeStruct(shape, BF16),
            jax.ShapeDtypeStruct(stats.shape, F32),
        ],
        in_specs=[vmem] * 7 + [pl.BlockSpec(memory_space=pltpu.SMEM)],
        out_specs=[vmem] * 5,
        scratch_shapes=[pltpu.VMEM(shape, F32)],
        name="unsettle",
    )(normed_grad, middle, gain, cotangent, w_out, attention, stats, coef)


def per_device(
    media,
    latents,
    frame_counts,
    time_index,
    valid,
    time_table,
    media_gain,
    latent_gain,
    ffn_gain,
    w_query,
    w_key,
    w_value,
    w_out,
    w_up,
    w_down,
    cotangent,
):
    frames = time_index.shape[0]
    patches = valid.shape[0] // frames
    latent_rows, width = latents.shape
    shard = media_gain.shape[0]
    scale = (width // H) ** (-0.5)
    column = lax.axis_index("gx")
    row_index = lax.axis_index("gy")
    frame_ends = jnp.cumsum(frame_counts[row_index])
    position = column * frames + jnp.arange(frames, dtype=jnp.int32)
    item_index = jnp.sum((frame_ends[None, :] <= position[:, None]).astype(jnp.int32), axis=1)
    item_index = jnp.clip(item_index, 0, LINES - 1).astype(jnp.int32)

    count = jnp.sum(valid.astype(F32))
    small = jnp.concatenate(
        [
            time_table.astype(F32),
            media_gain.astype(F32)[None],
            latent_gain.astype(F32)[None],
            ffn_gain.astype(F32)[None],
            jnp.full((1, shard), count, F32),
            jnp.zeros((4, shard), F32),
        ],
        axis=0,
    )
    small = jnp.pad(small, ((0, 0), (0, 128 - shard)))
    times = (time_index[:, None] == jnp.arange(16, dtype=jnp.int32)[None, :]).astype(BF16)
    times = jnp.pad(times, ((0, 8 - frames), (0, 0)))
    items = (item_index[:, None] == jnp.arange(LINES, dtype=jnp.int32)[None, :]).astype(F32)
    valid_rows = valid.reshape(frames, 1, patches)
    (
        tables,
        counts,
        full_key,
        full_value,
        full_query,
        full_out,
        up_cols,
        down_rows,
        cot_rows,
        normed,
        keys,
        values,
        table,
        got_weighted,
        got_stats,
        own_weighted,
        own_stats,
    ) = opening(
        scale,
        small,
        (w_key, w_value, w_query, w_out),
        latents,
        w_up,
        w_down,
        cotangent,
        media,
        valid_rows,
        times,
        items,
    )
    full_time = tables[:8].astype(BF16)
    full_media_gain, full_latent_gain, full_ffn_gain = tables[8:9], tables[9:10], tables[10:11]
    valid_total = counts[3, 0]
    coefficient = ENTROPY_WEIGHT * (valid.shape[0] * lax.axis_size(AXES)) / valid_total
    up_cols = up_cols.reshape(width, -1)
    down_rows = down_rows.reshape(-1, width)
    cot_rows = cot_rows.reshape(-1, width)
    time_onehot = times[:frames, :8].astype(F32)
    time_rows = product(times[:frames, :8], full_time)
    media_in = (
        media.astype(F32).reshape(frames, patches, width) + time_rows[:, None, :]
    ).reshape(-1, width)
    latent_in = latents.astype(F32)
    media_rows = media.shape[0]
    media_normed, latent_normed = normed[:media_rows], normed[media_rows:]
    media_key, own_key = keys[:media_rows], keys[media_rows:]
    media_value, own_value = values[:media_rows], values[media_rows:]
    own_query = lax.dynamic_index_in_dim(table, column, 0, keepdims=False)
    attention, attn_low, sums, middle, ffn_normed = settle(
        got_weighted, got_stats, own_weighted, own_stats, full_out, latents, full_ffn_gain
    )
    ffn_rows = gather(ffn_normed, 5).reshape(-1, width)
    up_rows = product(ffn_rows, up_cols)
    hidden = jax.nn.gelu(up_rows, approximate=False).astype(BF16)
    hidden_grad = inner_last(cot_rows, down_rows)
    gelu_pull = jax.vjp(partial(jax.nn.gelu, approximate=False), up_rows)[1]
    up_grad = gelu_pull(hidden_grad)[0].astype(BF16)
    normed_part = inner_last(up_grad, up_cols).astype(BF16)
    down_part = product(hidden, down_rows).astype(BF16)
    shape = (LINES, PLANE, latent_rows, width)
    (ffn_normed_grad,) = scatter([normed_part.reshape(shape)], False, 6)
    up_grad_part = inner_first(ffn_rows, up_grad).astype(BF16)
    down_grad_part = inner_first(hidden, cot_rows)
    middle_grad, middle_low, grad_ffn_gain, weighted_grad, terms = unsettle(
        ffn_normed_grad,
        middle,
        full_ffn_gain,
        cotangent,
        full_out,
        attention,
        sums,
        coefficient.reshape(1, 1),
    )
    grad_table, terms_table, down_sum, shard_up, shard_down = turn_back(
        weighted_grad,
        terms,
        down_part.reshape(shape),
        up_grad_part.reshape(16, 2, shard, -1),
        down_grad_part.reshape(2, -1, width),
    )
    new_latents = (middle + down_sum).astype(BF16)
    shard_up = jnp.swapaxes(shard_up, 0, 1).reshape(shard, -1).astype(F32)
    query_terms, media_key_grad, media_value_grad, query_part, own_key_grad, own_value_grad = backward(
        item_index,
        table,
        grad_table,
        terms_table,
        media_key,
        media_value,
        valid_rows,
        (own_query, weighted_grad, terms, own_key, own_value),
        scale,
    )
    slots = (LINES, PLANE, 2, shard, width)
    out_part = inner_first(attn_low, middle_low).astype(BF16).reshape(slots)
    got_query, shard_out = queries_home(query_terms, out_part)
    query_grad = (jnp.sum(got_query.astype(F32), axis=0) + query_part).astype(BF16)
    media_normed_grad = inner_last(media_key_grad, full_key) + inner_last(
        media_value_grad, full_value
    )
    media_grad, media_summand = norm_pull(media_in, full_media_gain, media_normed_grad)
    grad_media_gain = jnp.sum(media_summand, axis=0, keepdims=True)
    frame_sums = jnp.sum(media_grad.reshape(frames, patches, width), axis=1)
    grad_time = collect(time_onehot, frame_sums)
    latent_normed_grad = (
        inner_last(query_grad, full_query)
        + inner_last(own_key_grad, full_key)
        + inner_last(own_value_grad, full_value)
    )
    latent_part, latent_summand = norm_pull(latent_in, full_latent_gain, latent_normed_grad)
    grad_latent_gain = jnp.sum(latent_summand, axis=0, keepdims=True)
    latents_grad = middle_grad + latent_part
    key_part = inner_first(media_normed, media_key_grad) + inner_first(latent_normed, own_key_grad)
    value_part = inner_first(media_normed, media_value_grad) + inner_first(
        latent_normed, own_value_grad
    )
    query_weight_part = inner_first(latent_normed, query_grad)
    small_part = jnp.concatenate(
        [grad_time, grad_media_gain, grad_latent_gain, grad_ffn_gain, jnp.zeros((5, width), F32)],
        axis=0,
    )
    shard_value, shard_key, shard_query, smalls_grad = ending(
        [
            part.astype(BF16).reshape(slots)
            for part in (value_part, key_part, query_weight_part)
        ],
        small_part,
    )
    place = (column * 8 + row_index) * shard
    mine = lax.dynamic_slice(smalls_grad, (0, place), (16, shard))
    return (
        new_latents,
        media_grad,
        latents_grad,
        mine[:8],
        mine[8],
        mine[9],
        mine[10],
        shard_query,
        shard_key,
        shard_value,
        shard_out,
        shard_up,
        shard_down,
    )


def solution(mesh):
    in_specs = (
        P(("gx", "gy"), None),
        P(("gx", "gy"), None),
        P(),
        P(("gx", "gy")),
        P(("gx", "gy")),
        P(None, ("gx", "gy")),
        P(("gx", "gy")),
        P(("gx", "gy")),
        P(("gx", "gy")),
        P(("gx", "gy"), None),
        P(("gx", "gy"), None),
        P(("gx", "gy"), None),
        P(("gx", "gy"), None),
        P(("gx", "gy"), None),
        P(("gx", "gy"), None),
        P(("gx", "gy"), None),
    )
    out_specs = (
        P(("gx", "gy"), None),
        P(("gx", "gy"), None),
        P(("gx", "gy"), None),
        P(None, ("gx", "gy")),
        P(("gx", "gy")),
        P(("gx", "gy")),
        P(("gx", "gy")),
        P(("gx", "gy"), None),
        P(("gx", "gy"), None),
        P(("gx", "gy"), None),
        P(("gx", "gy"), None),
        P(("gx", "gy"), None),
        P(("gx", "gy"), None),
    )
    return jax.shard_map(
        per_device if dict(mesh.shape) == {"gx": 4, "gy": 8} else plain_device,
        mesh=mesh, in_specs=in_specs, out_specs=out_specs, check_vma=False
    )
```

```python
from functools import partial

import jax
import jax.numpy as jnp
from jax import lax
from jax.experimental import pallas as pl
from jax.experimental.pallas import tpu as pltpu
from jax.sharding import PartitionSpec as P

H = 16


ENTROPY_WEIGHT = 4.0
NORM_STABILIZER = 1e-05
AXES = ("gx", "gy")
LINES = 4
PLANE = 4
HBM = pl.ANY
BF16 = jnp.bfloat16
F32 = jnp.float32


def here():
    z = lax.axis_index("gx")
    g = lax.axis_index("gy")
    return z, g, g // 2, g % 2


def sibling(g):
    return g + 1 - 2 * (g % 2)


def along_x(g):
    return g + 2 - 4 * ((g // 2) % 2)


def along_y(g):
    return (g + 4) % 8


def turn(z, k):
    return (z + k) % LINES


def greet(devices):
    barrier = pltpu.get_barrier_semaphore()
    for device in devices:
        pl.semaphore_signal(
            barrier, inc=1, device_id=device, device_id_type=pl.DeviceIdType.MESH
        )
    pl.semaphore_wait(barrier, len(devices))


def line_of(z, g):
    return [(turn(z, k), g) for k in (1, 2, 3)]


class Wires:
    def __init__(self, send_sems, recv_sems):
        self.send_sems, self.recv_sems, self.used, self.sent = send_sems, recv_sems, 0, []

    def reserve(self, count):
        first = self.used
        self.used += count
        return first

    def copy(self, source, target, device, send, recv):
        return pltpu.make_async_remote_copy(
            src_ref=source,
            dst_ref=target,
            send_sem=self.send_sems.at[send],
            recv_sem=self.recv_sems.at[recv],
            device_id=device,
            device_id_type=pl.DeviceIdType.MESH,
        )

    def send(self, source, target, device):
        n = self.reserve(1)
        copy = self.copy(source, target, device, n, n)
        copy.start()
        self.sent.append((None, copy))
        return copy

    def send_if(self, condition, source, target, device, send, recv):
        copy = self.copy(source, target, device, send, recv)
        self.sent.append((condition, copy))

        @pl.when(condition)
        def _():
            copy.start()

        return copy

    def drain(self):
        for condition, copy in self.sent:
            if condition is None:
                copy.wait_send()
            else:
                pl.when(condition)(copy.wait_send)


class Line:
    def __init__(self, wires, shard, slot):
        self.wires, self.shard, self.slot = wires, shard, slot
        self.z, self.g, _, _ = here()
        self.base = wires.reserve(4)
        low, high = (3 - self.z) // 3, self.z // 3
        self.order = (1 + 2 * low, 3 - low - high, 2 - low + high)

    def first(self):
        z, g = self.z, self.g
        own = self.slot(z)
        base = self.base
        self.wires.send_if(z < 3, self.shard, own, (turn(z, 1), g), base + 1, base + 1)
        self.wires.send_if(z > 0, self.shard, own, (turn(z, 3), g), base + 3, base + 3)
        self.across = self.wires.copy(self.shard, own, (turn(z, 2), g), base + 2, base + 2)
        self.across.start()
        self.wires.sent.append((None, self.across))

    def take(self, step):
        z, g = self.z, self.g
        k = self.order[step]
        origin = turn(z, LINES - k)
        held = self.slot(origin)
        self.wires.copy(held, held, (z, g), 0, self.base + k).wait_recv()
        if step == 2:
            self.relay(z == 2, 3, 3)
        if step == 2:
            self.relay(z == 1, 0, 1)
        return origin

    def relay(self, condition, there, k):
        held = self.slot(turn(self.z, 2))
        self.wires.send_if(
            condition, held, held, (there, self.g), self.base, self.base + k
        )


class Spread:
    def __init__(self, wires, shard, slot, half, whole):
        self.wires, self.shard, self.slot, self.half, self.whole = wires, shard, slot, half, whole
        self.z, self.g, _, _ = here()
        self.line = Line(wires, shard, lambda z: slot(z, self.g))
        self.zs, self.x, self.y, self.dx, self.dy, self.sib = [self.z], [], [], {}, {}, []

    def side(self, gy):
        return (self.z, gy)

    def to_sibling(self, held):
        if self.whole:
            self.sib.append(self.wires.send(held, held, self.side(sibling(self.g))))

    def first(self):
        own = self.slot(self.z, self.g)
        self.line.first()
        self.x.append(self.wires.send(self.shard, own, self.side(along_x(self.g))))
        self.y.append(self.wires.send(self.shard, own, self.side(along_y(self.g))))
        if self.whole:
            self.sib.append(self.wires.send(self.shard, own, self.side(sibling(self.g))))

    def column(self, step):
        self.zs.append(self.line.take(step))
        held = self.slot(self.zs[-1], self.g)
        self.x.append(self.wires.send(held, held, self.side(along_x(self.g))))
        self.y.append(self.wires.send(held, held, self.side(along_y(self.g))))
        self.to_sibling(held)

    def corner(self, n):
        self.corner_x(n)
        self.corner_y(n)

    def corner_x(self, n):
        self.x[n].wait_recv()
        held = self.slot(self.zs[n], along_x(self.g))
        part = self.half(held, 0)
        self.dy[n] = self.wires.send(part, part, self.side(along_y(self.g)))
        self.to_sibling(held)

    def corner_y(self, n):
        self.y[n].wait_recv()
        held = self.slot(self.zs[n], along_y(self.g))
        part = self.half(held, 1)
        self.dx[n] = self.wires.send(part, part, self.side(along_x(self.g)))
        self.to_sibling(held)

    def last(self, n):
        self.dy[n].wait_recv()
        self.dx[n].wait_recv()
        self.to_sibling(self.slot(self.zs[n], along_y(along_x(self.g))))

    def finish(self):
        for copy in self.sib:
            copy.wait_recv()


def spread_all(flows):
    for flow in flows:
        flow.first()
    for flow in flows:
        flow.corner(0)
    for step in range(3):
        for flow in flows:
            flow.column(step)
        for flow in flows:
            flow.corner(step + 1)
    for n in range(4):
        for flow in flows:
            flow.last(n)
    for flow in flows:
        flow.finish()


LINE_SEMS = 4


def spread_sems(whole):
    return LINE_SEMS + 8 + 8 + (16 if whole else 0)


def columns_half(ref, which):
    width = ref.shape[-1] // 2
    return ref.at[..., pl.ds(which * width, width)]


def rows_half(ref, which):
    rows = ref.shape[0] // 2
    return ref.at[pl.ds(which * rows, rows)]


def sides_of(z, g, whole):
    near = [(z, along_x(g)), (z, along_y(g))]
    return near + [(z, sibling(g))] if whole else near


def params(ident):
    return pltpu.CompilerParams(
        collective_id=ident, has_side_effects=True, vmem_limit_bytes=60 * 2**20
    )


def sems(count):
    return pltpu.SemaphoreType.DMA((count,))


VMEM = pl.BlockSpec(memory_space=pltpu.VMEM)
LEFT = pl.BlockSpec(memory_space=HBM)


def gather_kernel(shard, out, send_sems, recv_sems, local_sem):
    z, g, chip, core = here()
    greet(line_of(z, g) + sides_of(z, g, False))
    wires = Wires(send_sems, recv_sems)
    copy = pltpu.make_async_copy(shard, out.at[4 * z + chip], local_sem)
    copy.start()
    spread_all([Spread(wires, shard, lambda zz, gg: out.at[zz * 4 + gg // 2], columns_half, False)])
    copy.wait()
    wires.drain()


def gather(shard, ident):
    return pl.pallas_call(
        gather_kernel,
        out_shape=jax.ShapeDtypeStruct((16,) + shard.shape, shard.dtype),
        in_specs=[LEFT],
        out_specs=LEFT,
        scratch_shapes=[sems(spread_sems(False)), sems(spread_sems(False)), pltpu.SemaphoreType.DMA],
        compiler_params=params(ident),
        name="gather",
    )(shard)


class Exchange:
    def __init__(self, wires, pairs):
        self.wires, self.pairs = wires, pairs
        self.z, self.g, _, _ = here()

    def first(self):
        z = self.z
        self.copies = []
        for k in (2, 1, 3):
            there = turn(z, k)
            for source, out in self.pairs:
                self.copies.append(
                    self.wires.send(source.at[there], out.at[z], (there, self.g))
                )
        for source, out in self.pairs:
            out[z] = source[z]

    def finish(self):
        for copy in self.copies:
            copy.wait_recv()


def add_slots(target, source, count):
    @pl.loop(0, count)
    def _(n):
        target[n] = (target[n].astype(F32) + source[n].astype(F32)).astype(target.dtype)


class Fold:
    def __init__(self, wires, parts, whole, scratch, out):
        self.wires, self.parts, self.whole, self.out = wires, parts, whole, out
        self.from_sib, self.cx, self.cy, self.fx, self.fy, self.fz = scratch
        self.z, self.g, self.chip, self.core = here()
        self.width = parts.shape[-1] // 2
        self.sends = []

    def send(self, source, target, gy):
        copy = self.wires.send(source, target, (self.z, gy))
        self.sends.append(copy)
        return copy

    def column(self, q):
        return self.parts.at[:, q, self.core] if self.whole else self.parts.at[:, q]

    def half(self, ref, which):
        return ref.at[:, :, pl.ds(which * self.width, self.width)]

    def merge(self, q):
        if self.whole:
            core = self.core

            @pl.loop(0, LINES)
            def _(n):
                self.parts[n, q, core] = self.parts[n, q, core] + self.from_sib[n, q]

    def start(self):
        if self.whole:
            theirs = self.parts.at[:, :, 1 - self.core]
            self.sib = self.send(theirs, self.from_sib, sibling(self.g))

    def corner(self):
        if self.whole:
            self.sib.wait_recv()
        q = along_y(along_x(self.g)) // 2
        self.merge(q)
        far = self.column(q)
        self.to_y = self.send(self.half(far, 0), self.cy, along_y(self.g))
        self.to_x = self.send(self.half(far, 1), self.cx, along_x(self.g))

    def side(self, gy, came, corner, which, target):
        q = gy // 2
        self.merge(q)
        came.wait_recv()
        column = self.column(q)
        cols = slice(which * self.width, (which + 1) * self.width)

        @pl.loop(0, LINES)
        def _(n):
            column[n, :, cols] = column[n, :, cols] + corner[n]

        return self.send(column, target, gy)

    def side_x(self):
        self.by_x = self.side(along_x(self.g), self.to_y, self.cy, 0, self.fx)

    def side_y(self):
        self.by_y = self.side(along_y(self.g), self.to_x, self.cx, 1, self.fy)

    def line(self):
        self.merge(self.chip)
        self.by_x.wait_recv()
        self.by_y.wait_recv()
        column = self.column(self.chip)
        self.zs = []
        for k in (2, 1, 3):
            there = turn(self.z, k)
            self.fx[there] = (
                column[there].astype(F32)
                + self.fx[there].astype(F32)
                + self.fy[there].astype(F32)
            ).astype(BF16)
            self.zs.append(
                self.wires.send(self.fx.at[there], self.fz.at[k - 1], (there, self.g))
            )
        z = self.z
        self.out[...] = column[z].astype(F32) + self.fx[z].astype(F32) + self.fy[z].astype(F32)

    def finish(self):
        for copy in self.zs:
            copy.wait_recv()
        self.out[...] += (
            self.fz[0].astype(F32) + self.fz[1].astype(F32) + self.fz[2].astype(F32)
        )

    def release(self):
        for copy in self.sends:
            copy.wait_send()
        waited = [id(copy) for copy in self.sends]
        self.wires.sent = [entry for entry in self.wires.sent if id(entry[1]) not in waited]


def fold_scratch(rows, cols, whole):
    half = cols // 2
    return [
        pltpu.VMEM((LINES, PLANE, rows, cols) if whole else (1, 1, 16, 128), BF16),
        pltpu.VMEM((LINES, rows, half), BF16),
        pltpu.VMEM((LINES, rows, half), BF16),
        pltpu.VMEM((LINES, rows, cols), BF16),
        pltpu.VMEM((LINES, rows, cols), BF16),
        pltpu.VMEM((LINES - 1, rows, cols), BF16),
    ]


FOLD = 6


def fold_sems(whole):
    return (1 if whole else 0) + 4 + 3


def scatter_kernel(parts, out, send_sems, recv_sems, *scratch):
    z, g, _, _ = here()
    greet(line_of(z, g) + sides_of(z, g, False))
    wires = Wires(send_sems, recv_sems)
    flow = Fold(wires, parts, False, scratch, out)
    flow.start()
    flow.corner()
    flow.side_x()
    flow.side_y()
    flow.line()
    flow.finish()
    wires.drain()


def scatter(parts, ident):
    rows, cols = parts.shape[-2:]
    wires = fold_sems(False)
    return pl.pallas_call(
        scatter_kernel,
        out_shape=jax.ShapeDtypeStruct((rows, cols), F32),
        in_specs=[VMEM],
        out_specs=VMEM,
        scratch_shapes=[sems(wires), sems(wires)] + fold_scratch(rows, cols, False),
        compiler_params=params(6),
        name="scatter",
        input_output_aliases={},
    )(parts)


def layer_norm(row_block, gain_row):
    row_mean = jnp.mean(row_block, axis=-1, keepdims=True)
    centred = row_block - row_mean
    variance = jnp.mean(centred * centred, axis=-1, keepdims=True)
    return centred * lax.rsqrt(variance + NORM_STABILIZER) * gain_row


def product(left_side, right_side):
    return jnp.dot(left_side, right_side, preferred_element_type=jnp.float32)


def inner_first(left_side, right_side):
    return lax.dot_general(
        left_side, right_side, (((0,), (0,)), ((), ())), preferred_element_type=jnp.float32
    )


def inner_last(left_side, right_side):
    return lax.dot_general(
        left_side, right_side, (((1,), (1,)), ((), ())), preferred_element_type=jnp.float32
    )


def collect(onehot_rows, value_rows):
    return lax.dot_general(
        onehot_rows,
        value_rows,
        (((0,), (0,)), ((), ())),
        precision=lax.Precision.HIGHEST,
        preferred_element_type=jnp.float32,
    )


def plain_device(
    media,
    latents,
    frame_counts,
    time_index,
    valid,
    time_table,
    media_gain,
    latent_gain,
    ffn_gain,
    w_query,
    w_key,
    w_value,
    w_out,
    w_up,
    w_down,
    cotangent,
):
    frames = time_index.shape[0]
    patches = valid.shape[0] // frames
    latent_rows = latents.shape[0]
    model_width = latents.shape[1]
    head_size = model_width // H
    score_scale = head_size ** (-0.5)
    across = lax.axis_size("gx")
    column = lax.axis_index("gx")
    row_index = lax.axis_index("gy")
    frame_ends = jnp.cumsum(frame_counts[row_index])
    position = column * frames + jnp.arange(frames, dtype=jnp.int32)
    item_index = jnp.sum((frame_ends[None, :] <= position[:, None]).astype(jnp.int32), axis=1)
    item_onehot = (item_index[:, None] == jnp.arange(across, dtype=jnp.int32)[None, :]).astype(
        jnp.float32
    )
    (
        full_query,
        full_key,
        full_value,
        full_out,
        full_up,
        full_down,
        full_media_gain,
        full_latent_gain,
        full_ffn_gain,
        full_time,
    ) = (
        lax.all_gather(w_query, ("gx", "gy"), axis=0, tiled=True),
        lax.all_gather(w_key, ("gx", "gy"), axis=0, tiled=True),
        lax.all_gather(w_value, ("gx", "gy"), axis=0, tiled=True),
        lax.all_gather(w_out, ("gx", "gy"), axis=0, tiled=True),
        lax.all_gather(w_up, ("gx", "gy"), axis=0, tiled=True),
        lax.all_gather(w_down, ("gx", "gy"), axis=0, tiled=True),
        lax.all_gather(media_gain, ("gx", "gy"), axis=0, tiled=True),
        lax.all_gather(latent_gain, ("gx", "gy"), axis=0, tiled=True),
        lax.all_gather(ffn_gain, ("gx", "gy"), axis=0, tiled=True),
        lax.all_gather(time_table, ("gx", "gy"), axis=1, tiled=True),
    )
    time_onehot = (
        time_index[:, None] == jnp.arange(full_time.shape[0], dtype=jnp.int32)[None, :]
    ).astype(jnp.float32)
    time_rows = product(time_onehot.astype(jnp.bfloat16), full_time)
    media_in = (
        media.astype(jnp.float32).reshape(frames, patches, model_width) + time_rows[:, None, :]
    ).reshape(-1, model_width)
    media_normed = layer_norm(media_in, full_media_gain.astype(jnp.float32)).astype(jnp.bfloat16)
    key_heads = (
        product(media_normed, full_key).astype(jnp.bfloat16).reshape(frames, patches, H, head_size)
    )
    value_heads = (
        product(media_normed, full_value)
        .astype(jnp.bfloat16)
        .reshape(frames, patches, H, head_size)
    )
    latent_in = latents.astype(jnp.float32)
    latent_normed = layer_norm(latent_in, full_latent_gain.astype(jnp.float32)).astype(jnp.bfloat16)
    own_query = product(latent_normed, full_query).astype(jnp.bfloat16)
    own_key = product(latent_normed, full_key).astype(jnp.bfloat16)
    own_value = product(latent_normed, full_value).astype(jnp.bfloat16)
    valid_total = lax.psum(jnp.sum(valid.astype(jnp.float32)), ("gx", "gy"))
    coefficient = ENTROPY_WEIGHT * (valid.shape[0] * lax.axis_size(("gx", "gy"))) / valid_total
    query_table = lax.all_gather(own_query, "gx", axis=0, tiled=True)
    picked = query_table.reshape(-1, latent_rows, H, head_size)[item_index]
    media_score = (
        jnp.einsum("flhd,fphd->flhp", picked, key_heads, preferred_element_type=jnp.float32)
        * score_scale
    )
    valid_mask = valid.reshape(frames, 1, 1, patches) > 0
    media_expo = jnp.where(valid_mask, jnp.exp(media_score), 0.0)
    expo_low = media_expo.astype(jnp.bfloat16)
    media_total = jnp.sum(media_expo, axis=-1)
    media_moment = jnp.sum(media_expo * media_score, axis=-1)
    media_weighted = jnp.einsum(
        "flhp,fphd->flhd", expo_low, value_heads, preferred_element_type=jnp.float32
    )
    dense_weighted = collect(item_onehot, media_weighted.reshape(frames, -1)).reshape(
        -1, model_width
    )
    dense_total = collect(item_onehot, media_total.reshape(frames, -1)).reshape(-1, H)
    dense_moment = collect(item_onehot, media_moment.reshape(frames, -1)).reshape(-1, H)
    got_weighted, got_total, got_moment = (
        lax.psum_scatter(dense_weighted, "gx", scatter_dimension=0, tiled=True),
        lax.psum_scatter(dense_total, "gx", scatter_dimension=0, tiled=True),
        lax.psum_scatter(dense_moment, "gx", scatter_dimension=0, tiled=True),
    )
    query_head_count = own_query.reshape(latent_rows, H, head_size)
    latent_key_rows = own_key.reshape(latent_rows, H, head_size)
    latent_value_rows = own_value.reshape(latent_rows, H, head_size)
    latent_score = (
        jnp.einsum(
            "uer,zer->uez", query_head_count, latent_key_rows, preferred_element_type=jnp.float32
        )
        * score_scale
    )
    latent_expo = jnp.exp(latent_score)
    latent_reduced_precision = latent_expo.astype(jnp.bfloat16)
    weighted = got_weighted.reshape(latent_rows, H, head_size) + jnp.einsum(
        "nwr,rwb->nwb",
        latent_reduced_precision,
        latent_value_rows,
        preferred_element_type=jnp.float32,
    )
    totals = got_total + jnp.sum(latent_expo, axis=-1)
    moment = got_moment + jnp.sum(latent_expo * latent_score, axis=-1)
    attention = weighted / totals[..., None]
    attn_low = attention.reshape(latent_rows, model_width).astype(jnp.bfloat16)
    middle = latent_in + product(attn_low, full_out)
    ffn_normed = layer_norm(middle, full_ffn_gain.astype(jnp.float32)).astype(jnp.bfloat16)
    up_rows = product(ffn_normed, full_up)
    hidden = jax.nn.gelu(up_rows, approximate=False).astype(jnp.bfloat16)
    new_latents = (middle + product(hidden, full_down)).astype(jnp.bfloat16)
    (
        back_query,
        back_key,
        back_value,
        back_out,
        back_up,
        back_down,
        back_media_gain,
        back_latent_gain,
        back_ffn_gain,
    ) = (
        lax.all_gather(w_query, ("gx", "gy"), axis=0, tiled=True),
        lax.all_gather(w_key, ("gx", "gy"), axis=0, tiled=True),
        lax.all_gather(w_value, ("gx", "gy"), axis=0, tiled=True),
        lax.all_gather(w_out, ("gx", "gy"), axis=0, tiled=True),
        lax.all_gather(w_up, ("gx", "gy"), axis=0, tiled=True),
        lax.all_gather(w_down, ("gx", "gy"), axis=0, tiled=True),
        lax.all_gather(media_gain, ("gx", "gy"), axis=0, tiled=True),
        lax.all_gather(latent_gain, ("gx", "gy"), axis=0, tiled=True),
        lax.all_gather(ffn_gain, ("gx", "gy"), axis=0, tiled=True),
    )
    owned_latent, owned_attn, owned_ffn, owned_hidden = (
        lax.all_to_all(latent_normed, ("gx", "gy"), split_axis=1, concat_axis=0, tiled=True),
        lax.all_to_all(attn_low, ("gx", "gy"), split_axis=1, concat_axis=0, tiled=True),
        lax.all_to_all(ffn_normed, ("gx", "gy"), split_axis=1, concat_axis=0, tiled=True),
        lax.all_to_all(hidden, ("gx", "gy"), split_axis=1, concat_axis=0, tiled=True),
    )
    hidden_grad = inner_last(cotangent, back_down)
    gelu_pull = jax.vjp(partial(jax.nn.gelu, approximate=False), up_rows)[1]
    up_grad = gelu_pull(hidden_grad)[0].astype(jnp.bfloat16)
    ffn_normed_grad = inner_last(up_grad, back_up)
    ffn_pull = jax.vjp(layer_norm, middle, back_ffn_gain.astype(jnp.float32))[1]
    middle_part, grad_ffn_gain = ffn_pull(ffn_normed_grad)
    middle_grad = cotangent.astype(jnp.float32) + middle_part
    middle_low = middle_grad.astype(jnp.bfloat16)
    attn_grad = inner_last(middle_low, back_out).reshape(latent_rows, H, head_size)
    weighted_sum_gradient = (attn_grad / totals[..., None]).astype(jnp.bfloat16)
    slope_term = -coefficient / totals
    shift_term = (
        -jnp.sum(attn_grad * attention, axis=-1) / totals
        + coefficient * (1.0 / totals + moment / (totals * totals))
        + slope_term
    )
    latent_mix = jnp.einsum(
        "uer,zer->uez", weighted_sum_gradient, latent_value_rows, preferred_element_type=jnp.float32
    )
    latent_sgrad = latent_expo * (
        latent_mix + shift_term[..., None] + slope_term[..., None] * latent_score
    )
    latent_residual_gradient = (latent_sgrad * score_scale).astype(jnp.bfloat16)
    query_part = jnp.einsum(
        "nwr,rwb->nwb",
        latent_residual_gradient,
        latent_key_rows,
        preferred_element_type=jnp.float32,
    )
    own_key_grad = (
        jnp.einsum(
            "zry,zrj->yrj",
            latent_residual_gradient,
            query_head_count,
            preferred_element_type=jnp.float32,
        )
        .astype(jnp.bfloat16)
        .reshape(latent_rows, model_width)
    )
    own_value_grad = (
        jnp.einsum(
            "zry,zrj->yrj",
            latent_reduced_precision,
            weighted_sum_gradient,
            preferred_element_type=jnp.float32,
        )
        .astype(jnp.bfloat16)
        .reshape(latent_rows, model_width)
    )
    grad_table = lax.all_gather(
        weighted_sum_gradient.reshape(latent_rows, model_width), "gx", axis=0, tiled=True
    )
    shift_table, slope_table = (
        lax.all_gather(shift_term, "gx", axis=0, tiled=True),
        lax.all_gather(slope_term, "gx", axis=0, tiled=True),
    )
    picked_grad = grad_table.reshape(-1, latent_rows, H, head_size)[item_index]
    picked_shift = shift_table.reshape(-1, latent_rows, H)[item_index]
    picked_slope = slope_table.reshape(-1, latent_rows, H)[item_index]
    media_mix = jnp.einsum(
        "flhd,fphd->flhp", picked_grad, value_heads, preferred_element_type=jnp.float32
    )
    media_sgrad = media_expo * (
        media_mix + picked_shift[..., None] + picked_slope[..., None] * media_score
    )
    media_rgrad = (media_sgrad * score_scale).astype(jnp.bfloat16)
    query_terms = jnp.einsum(
        "flhp,fphd->flhd", media_rgrad, key_heads, preferred_element_type=jnp.float32
    )
    dense_query = collect(item_onehot, query_terms.reshape(frames, -1)).reshape(-1, model_width)
    got_query = lax.psum_scatter(
        dense_query.astype(jnp.bfloat16), "gx", scatter_dimension=0, tiled=True
    ).astype(jnp.float32)
    media_key_grad = (
        jnp.einsum("flhp,flhd->fphd", media_rgrad, picked, preferred_element_type=jnp.float32)
        .astype(jnp.bfloat16)
        .reshape(-1, model_width)
    )
    media_value_grad = (
        jnp.einsum("flhp,flhd->fphd", expo_low, picked_grad, preferred_element_type=jnp.float32)
        .astype(jnp.bfloat16)
        .reshape(-1, model_width)
    )
    grad_key = inner_first(media_normed, media_key_grad) + inner_first(latent_normed, own_key_grad)
    grad_value = inner_first(media_normed, media_value_grad) + inner_first(
        latent_normed, own_value_grad
    )
    media_normed_grad = inner_last(media_key_grad, back_key) + inner_last(
        media_value_grad, back_value
    )
    media_pull = jax.vjp(layer_norm, media_in, back_media_gain.astype(jnp.float32))[1]
    media_grad, grad_media_gain = media_pull(media_normed_grad)
    frame_sums = jnp.sum(media_grad.reshape(frames, patches, model_width), axis=1)
    grad_time = collect(time_onehot, frame_sums)
    query_grad = (
        (got_query.reshape(latent_rows, H, head_size) + query_part)
        .astype(jnp.bfloat16)
        .reshape(latent_rows, model_width)
    )
    latent_normed_grad = (
        inner_last(query_grad, back_query)
        + inner_last(own_key_grad, back_key)
        + inner_last(own_value_grad, back_value)
    )
    latent_pull = jax.vjp(layer_norm, latent_in, back_latent_gain.astype(jnp.float32))[1]
    latent_part, grad_latent_gain = latent_pull(latent_normed_grad)
    latents_grad = middle_grad + latent_part
    piece_query = lax.all_gather(query_grad, ("gx", "gy"), axis=0, tiled=True)
    piece_middle = lax.all_gather(middle_low, ("gx", "gy"), axis=0, tiled=True)
    piece_up = lax.all_gather(up_grad, ("gx", "gy"), axis=0, tiled=True)
    piece_cot = lax.all_gather(cotangent, ("gx", "gy"), axis=0, tiled=True)
    shard_query = inner_first(owned_latent, piece_query)
    shard_out = inner_first(owned_attn, piece_middle)
    shard_up = inner_first(owned_ffn, piece_up)
    shard_down = inner_first(owned_hidden, piece_cot)
    shard_grads = (
        lax.psum_scatter(grad_key, ("gx", "gy"), scatter_dimension=0, tiled=True),
        lax.psum_scatter(grad_value, ("gx", "gy"), scatter_dimension=0, tiled=True),
        lax.psum_scatter(grad_media_gain, ("gx", "gy"), scatter_dimension=0, tiled=True),
        lax.psum_scatter(grad_latent_gain, ("gx", "gy"), scatter_dimension=0, tiled=True),
        lax.psum_scatter(grad_ffn_gain, ("gx", "gy"), scatter_dimension=0, tiled=True),
        lax.psum_scatter(grad_time, ("gx", "gy"), scatter_dimension=1, tiled=True),
    )
    return (
        new_latents,
        media_grad,
        latents_grad,
        shard_grads[5],
        shard_grads[2],
        shard_grads[3],
        shard_grads[4],
        shard_query,
        shard_grads[0],
        shard_grads[1],
        shard_out,
        shard_up,
        shard_down,
    )


GROUP = 4


def mates_of(z, chip, core):
    mates = []
    for j in range(1, 16):
        there = (4 * z + chip + j) % 16
        mates.append((there // 4, 2 * (there % 4) + core))
    return mates


class GiveBack:
    def __init__(self, wires, up_ref, down_ref, up_out, down_out, scratch, local_sems):
        self.wires, self.up_out, self.down_out = wires, up_out, down_out
        self.up_held, self.up_near, self.down_near = scratch
        self.z, self.g, self.chip, self.core = here()
        self.up_ref, self.down_ref = up_ref, down_ref
        self.load_up = pltpu.make_async_copy(
            up_ref.at[:, self.core], self.up_held, local_sems.at[0]
        )
        self.load_down = pltpu.make_async_copy(
            down_ref.at[self.core], down_out, local_sems.at[1]
        )

    def start(self):
        near = (self.z, sibling(self.g))
        self.load_up.start()
        self.load_down.start()
        self.up = self.wires.send(self.up_ref.at[:, 1 - self.core], self.up_near, near)
        self.down = self.wires.send(self.down_ref.at[1 - self.core], self.down_near, near)

    def columns(self):
        self.load_up.wait()
        self.up.wait_recv()
        add_slots(self.up_held, self.up_near, 16)
        here_chip = 4 * self.z + self.chip
        self.moved = []
        for j, mate in enumerate(mates_of(self.z, self.chip, self.core)):
            there = (here_chip + j + 1) % 16
            self.moved.append(
                self.wires.send(self.up_held.at[there], self.up_out.at[here_chip], mate)
            )
        self.up_out[here_chip] = self.up_held[here_chip]

    def rows(self):
        self.load_down.wait()
        self.down.wait_recv()
        rows = self.down_out.shape[0] // 8

        @pl.loop(0, 8)
        def _(n):
            block = pl.ds(pl.multiple_of(n * rows, 8), rows)
            self.down_out[block] = self.down_out[block] + self.down_near[block]

    def finish(self):
        for copy in self.moved:
            copy.wait_recv()


def turn_kernel(
    grad,
    terms,
    down_part,
    up_grad,
    down_grad,
    grad_out,
    terms_out,
    down_out,
    up_grad_out,
    down_grad_out,
    send_sems,
    recv_sems,
    local_sems,
    up_held,
    up_near,
    down_near,
    down_held,
    *fold,
):
    z, g, chip, core = here()
    greet(mates_of(z, chip, core) + [(z, sibling(g))])
    wires = Wires(send_sems, recv_sems)
    lines = [
        Line(wires, grad, lambda zz: grad_out.at[zz]),
        Line(wires, terms, lambda zz: terms_out.at[zz]),
    ]
    back = GiveBack(
        wires,
        up_grad,
        down_grad,
        up_grad_out,
        down_grad_out,
        (up_held, up_near, down_near),
        local_sems,
    )
    flow = Fold(wires, down_held, False, fold, down_out)
    load = pltpu.make_async_copy(down_part, down_held, local_sems.at[2])
    load.start()
    for line in lines:
        line.first()
    back.start()
    load.wait()
    flow.corner()
    grad_out[z] = grad[...]
    terms_out[z] = terms[...]
    back.columns()
    flow.side_x()
    flow.side_y()
    for step in range(3):
        for line in lines:
            line.take(step)
    back.rows()
    flow.line()
    flow.finish()
    back.finish()
    wires.drain()


def turn_back(grad, terms, down_part, up_grad, down_grad):
    rows, width = up_grad.shape[-2:]
    down_shape = down_grad.shape[1:]
    latent_rows, model_width = grad.shape
    wires = 2 * LINE_SEMS + fold_sems(False) + 17
    return pl.pallas_call(
        turn_kernel,
        out_shape=[
            jax.ShapeDtypeStruct((LINES,) + grad.shape, BF16),
            jax.ShapeDtypeStruct((LINES,) + terms.shape, F32),
            jax.ShapeDtypeStruct(grad.shape, F32),
            jax.ShapeDtypeStruct((16, rows, width), BF16),
            jax.ShapeDtypeStruct(down_shape, F32),
        ],
        in_specs=[VMEM, VMEM, LEFT, LEFT, LEFT],
        out_specs=[VMEM] * 5,
        scratch_shapes=[
            sems(wires),
            sems(wires),
            sems(3),
            pltpu.VMEM((16, rows, width), BF16),
            pltpu.VMEM((16, rows, width), BF16),
            pltpu.VMEM(down_shape, F32),
            pltpu.VMEM((LINES, PLANE, latent_rows, model_width), BF16),
        ]
        + fold_scratch(latent_rows, model_width, False),
        compiler_params=params(2),
        name="turn_back",
    )(grad, terms, down_part, up_grad, down_grad)


class Total:
    def __init__(self, wires, mine, out, sums, got):
        self.wires, self.out, self.sums, self.got = wires, out, sums, got
        self.z, self.g, _, _ = here()
        self.source = mine
        self.step = 0

    def push(self):
        sides = [sibling(self.g), along_x(self.g), along_y(self.g)]
        if self.step < 3:
            self.copies = [
                self.wires.send(self.source, self.got.at[self.step], (self.z, sides[self.step]))
            ]
        else:
            self.copies = [
                self.wires.send(self.source, self.got.at[3 + k], device)
                for k, device in enumerate(line_of(self.z, self.g))
            ]

    def pull(self):
        for copy in self.copies:
            copy.wait_recv()
        if self.step < 3:
            self.sums[self.step] = self.source[...] + self.got[self.step]
            self.source = self.sums.at[self.step]
            self.step += 1
        else:
            self.out[...] = self.source[...] + self.got[3] + self.got[4] + self.got[5]


def head_masks(rows, width, head_size):
    lane = lax.broadcasted_iota(jnp.int32, (rows, width), 1)
    return [(lane >= h * head_size) & (lane < (h + 1) * head_size) for h in range(GROUP)]


def stacked(block, masks):
    zero = jnp.zeros_like(block)
    return jnp.concatenate([jnp.where(mask, block, zero) for mask in masks], axis=0)


def unstacked(block, masks):
    rows = block.shape[0] // GROUP
    total = jnp.where(masks[0], block[:rows], 0.0)
    for h in range(1, GROUP):
        total = jnp.where(masks[h], block[h * rows : (h + 1) * rows], total)
    return total


def dot_last(a, b):
    return lax.dot_general(a, b, (((1,), (1,)), ((), ())), preferred_element_type=F32)


def dot_first(a, b):
    return lax.dot_general(a, b, (((0,), (0,)), ((), ())), preferred_element_type=F32)


def spread_heads(columns, first, masks):
    out = jnp.where(masks[0], columns[:, first : first + 1], 0.0)
    for h in range(1, GROUP):
        out = jnp.where(masks[h], columns[:, first + h : first + h + 1], out)
    return out


def attend(queries, keys, values, valid, scale, masks):
    rows = queries.shape[0]
    score = dot_last(stacked(queries, masks), keys) * scale
    expo = jnp.exp(score)
    if valid is not None:
        expo = jnp.where(valid > 0, expo, 0.0)
    totals = jnp.sum(expo, axis=1, keepdims=True)
    moments = jnp.sum(expo * score, axis=1, keepdims=True)
    weighted = jnp.dot(expo.astype(BF16), values, preferred_element_type=F32)
    heads = [(totals[h * rows : (h + 1) * rows], moments[h * rows : (h + 1) * rows]) for h in range(GROUP)]
    return unstacked(weighted, masks), heads


def put_heads(heads, group, lane):
    out = jnp.zeros(lane.shape, F32)
    for h, (total, moment) in enumerate(heads):
        out = jnp.where(lane == group * GROUP + h, total, out)
        out = jnp.where(lane == H + group * GROUP + h, moment, out)
    return out


def multiply(left, right, out, tile):
    @pl.loop(0, right.shape[1] // tile)
    def _(n):
        cols = pl.ds(pl.multiple_of(n * tile, 128), tile)
        out[:, cols] = jnp.dot(left[...], right[:, cols], preferred_element_type=F32).astype(BF16)


def assemble(smalls, out):
    count, rows, lanes = smalls.shape
    shard = out.shape[1] // count
    block = 8
    row = lax.broadcasted_iota(jnp.int32, (block * lanes, block * shard), 0)
    col = lax.broadcasted_iota(jnp.int32, (block * lanes, block * shard), 1)
    lane = row % lanes
    chosen = ((row // lanes) * shard + lane == col) & (lane < shard)
    place = jnp.where(chosen, 1.0, 0.0).astype(BF16)
    for n in range(count // block):
        pieces = jnp.concatenate([smalls[n * block + d] for d in range(block)], axis=1)
        out[:, n * block * shard : (n + 1) * block * shard] = jnp.dot(
            pieces.astype(BF16), place, preferred_element_type=F32
        )


def up_places(z, chip):
    places = []
    for dz in range(LINES):
        for dx, dy in ((0, 0), (1, 0), (0, 1), (1, 1)):
            if dz or dx or dy:
                x, y = chip % 2, chip // 2
                there = (y + dy) % 2 * 2 + (x + dx) % 2
                places.append(((turn(z, dz), there), (turn(z, LINES - dz) if dz else z, there)))
    return places


def opening_kernel(scale, *refs):
    (
        small_ref,
        key_shard,
        value_shard,
        query_shard,
        out_shard,
        latents_ref,
        up_ref,
        down_ref,
        cot_ref,
        media_ref,
        valid_ref,
        times_ref,
        item_ref,
        tables_out,
        counts_out,
        key_weight_out,
        value_weight_out,
        query_weight_out,
        out_weight_out,
        up_out,
        down_out,
        cot_out,
        normed_out,
        keys_out,
        values_out,
        table_out,
        got_weighted,
        got_stats,
        own_weighted,
        own_stats,
        send_sems,
        recv_sems,
        local_sems,
        smalls,
        key_weight,
        value_weight,
        query_weight,
        line_latents,
        line_normed,
        normed,
        keys,
        values,
        table,
        time_rows,
        sums,
        weighted,
        stats,
    ) = refs
    z, g, chip, core = here()
    here_chip = 4 * z + chip
    me = 2 * here_chip + core
    items, rows, width = line_latents.shape
    frames, _, patches = valid_ref.shape
    shard = key_shard.shape[0]
    span = width // (H // GROUP)
    up_width = up_out.shape[-1]
    near = (z, sibling(g))
    places = up_places(z, chip)
    greet([(there[0], 2 * there[1] + core) for there, _ in places] + [near])
    wires = Wires(send_sems, recv_sems)
    masks = head_masks(rows, span, span // GROUP)
    lane = lax.broadcasted_iota(jnp.int32, (rows, 128), 1)
    local = []

    def keep(source, target):
        copy = pltpu.make_async_copy(source, target, local_sems.at[len(local)])
        copy.start()
        local.append(copy)
        return copy

    def rows_of(ref):
        return lambda zz, gg: ref.at[pl.ds(pl.multiple_of((zz * 8 + gg) * shard, 16), shard)]

    def piece(place):
        return up_ref.at[:, pl.ds(pl.multiple_of((4 * place[0] + place[1]) * up_width, 128), up_width)]

    def whole(source, slot):
        return Spread(wires, source, slot, columns_half, True), keep(source, slot(z, g))

    def small_slot(zz, gg):
        return smalls.at[zz * 8 + gg]

    small = Spread(wires, small_ref, small_slot, rows_half, True)
    small_kept = keep(small_ref, small_slot(z, g))
    key, key_kept = whole(key_shard, rows_of(key_weight))
    value, value_kept = whole(value_shard, rows_of(value_weight))
    query, query_kept = whole(query_shard, rows_of(query_weight))
    out, out_kept = whole(out_shard, rows_of(out_weight_out))
    cot = Spread(wires, cot_ref, lambda zz, gg: cot_out.at[zz * 4 + gg // 2], columns_half, False)
    line = Line(wires, latents_ref, lambda zz: line_latents.at[zz])
    exchange = Exchange(wires, [(weighted, got_weighted), (stats, got_stats)])
    line_kept = keep(latents_ref, line_latents.at[z])
    late = [
        out_kept,
        keep(cot_ref, cot_out.at[here_chip]),
        keep(piece((z, chip)), up_out.at[me]),
        keep(down_ref, down_out.at[core]),
    ]
    prompt = len(local)
    moved, given, down = [], [], []
    chunk = 32

    def normalise(first, last):
        @pl.loop(first, last)
        def _(n):
            block = pl.ds(pl.multiple_of(n * chunk, chunk), chunk)
            frame = n // (patches // chunk)
            row = media_ref[block].astype(F32) + time_rows[pl.ds(frame, 1)]
            normed[block] = layer_norm(row, tables_out[8:9]).astype(BF16)

    def normalise_latents():
        gain = tables_out[9:10]
        line_kept.wait()
        for item in range(items):

            @pl.loop(0, rows // chunk)
            def _(n):
                block = pl.ds(pl.multiple_of(n * chunk, chunk), chunk)
                row = line_latents[item, block].astype(F32)
                line_normed[item, block] = layer_norm(row, gain).astype(BF16)

        normed[frames * patches :] = line_normed[z]

    def tabulate():
        small_kept.wait()
        assemble(smalls, tables_out)
        counts = smalls[0, 8:]
        for n in range(1, smalls.shape[0]):
            counts = counts + smalls[n, 8:]
        counts_out[...] = counts
        time_rows[...] = jnp.dot(
            times_ref[...], tables_out[...].astype(BF16), preferred_element_type=F32
        )

    def project_keys():
        key_kept.wait()
        keep(key_weight, key_weight_out)
        keep(normed, normed_out)
        multiply(normed, key_weight, keys, span)
        keep(keys, keys_out)

    def project_values():
        value_kept.wait()
        keep(value_weight, value_weight_out)
        multiply(normed, value_weight, values, span)
        keep(values, values_out)

    def project_queries():
        query_kept.wait()
        keep(query_weight, query_weight_out)

        @pl.loop(0, width // span)
        def _(n):
            cols = pl.ds(pl.multiple_of(n * span, 128), span)
            for item in range(items):
                table[item, :, cols] = jnp.dot(
                    line_normed[item], query_weight[:, cols], preferred_element_type=F32
                ).astype(BF16)

        keep(table, table_out)

    def attend_own():
        sums[...] = jnp.zeros_like(sums)
        stats[...] = jnp.zeros_like(stats)
        last = slice(frames * patches, frames * patches + rows)
        own = jnp.zeros((rows, 128), F32)
        for group in range(H // GROUP):
            cols = slice(group * span, (group + 1) * span)
            part, heads = attend(
                table[z, :, cols], keys[last, cols], values[last, cols], None, scale, masks
            )
            own_weighted[:, cols] = part
            own = own + put_heads(heads, group, lane)
        own_stats[...] = own

    def attend_frames(first, last):
        @pl.loop(first, last)
        def _(frame):
            block = pl.ds(pl.multiple_of(frame * patches, patches), patches)
            valid = valid_ref[frame]
            found = jnp.zeros((rows, 128), F32)
            for group in range(H // GROUP):
                cols = slice(group * span, (group + 1) * span)
                chosen = item_ref[frame, 0] * table[0, :, cols].astype(F32)
                for item in range(1, items):
                    chosen = chosen + item_ref[frame, item] * table[item, :, cols].astype(F32)
                part, heads = attend(
                    chosen.astype(BF16), keys[block, cols], values[block, cols], valid, scale, masks
                )
                found = found + put_heads(heads, group, lane)
                for item in range(items):
                    sums[item, :, cols] += item_ref[frame, item] * part
            for item in range(items):
                stats[item] += item_ref[frame, item] * found

    def down_first():
        down.append(wires.send(down_ref, down_out.at[core], near))

    def up_first():
        given.append(wires.send(piece((z, chip)), up_out.at[me], near))
        for there, _ in places:
            moved.append(
                wires.send(piece(there), up_out.at[me], (there[0], 2 * there[1] + core))
            )

    def up_last():
        for n, (_, origin) in enumerate(places):
            moved[n].wait_recv()
            held = up_out.at[2 * (4 * origin[0] + origin[1]) + core]
            given.append(wires.send(held, held, near))
        for copy in given:
            copy.wait_recv()

    def sums_first():
        weighted[...] = sums[...].astype(BF16)
        exchange.first()

    key.first()
    small.first()
    query.first()
    key.column(0)
    small.corner_y(0)
    small.column(0)
    key.column(1)
    down_first()
    query.corner_x(0)
    value.first()
    query.column(0)
    query.column(1)
    key.corner_y(1)
    key.corner_x(1)
    value.column(0)
    key.column(2)
    small.corner_x(1)
    small.corner_y(1)
    value.corner_y(0)
    query.corner_y(2)
    line.first()
    small.corner_x(0)
    query.corner_y(0)
    value.corner_y(1)
    key.corner_y(0)
    query.corner_x(1)
    small.column(1)
    query.corner_y(1)
    small.column(2)
    key.corner_x(2)
    key.corner_x(0)
    cot.first()
    value.column(1)
    value.corner_x(0)
    key.corner_x(3)
    value.column(2)
    small.last(0)
    key.last(1)
    key.corner_y(3)
    small.corner_y(2)
    value.corner_x(1)
    query.last(0)
    query.corner_x(2)
    small.corner_x(2)
    key.last(0)
    small.corner_x(3)
    out.first()
    small.corner_y(3)
    query.last(1)
    value.corner_y(3)
    small.last(1)
    value.corner_x(2)
    small.last(2)
    key.corner_y(2)
    query.column(2)
    small.last(3)
    value.last(0)
    query.last(2)
    key.last(3)
    small.finish()
    line.take(0)
    down[0].wait_recv()
    value.last(1)
    tabulate()
    out.column(0)
    query.corner_x(3)
    query.corner_y(3)
    value.corner_x(3)
    value.corner_y(2)
    line.take(1)
    normalise(0, 8)
    cot.column(0)
    cot.corner_y(0)
    line.take(2)
    up_first()
    out.column(1)
    query.last(3)
    cot.column(1)
    out.corner_y(0)
    normalise_latents()
    query.finish()
    value.last(3)
    project_queries()
    value.last(2)
    key.last(2)
    cot.corner_x(0)
    normalise(8, 16)
    out.column(2)
    value.finish()
    cot.corner_y(1)
    project_values()
    key.finish()
    project_keys()
    cot.corner_x(1)
    attend_own()
    attend_frames(0, frames // 2)
    cot.corner_y(2)
    attend_frames(frames // 2, frames)
    sums_first()
    out.corner_y(2)
    out.corner_x(2)
    cot.corner_x(2)
    cot.column(2)
    exchange.finish()
    out.corner_y(3)
    out.corner_x(1)
    cot.corner_x(3)
    cot.last(2)
    cot.corner_y(3)
    cot.last(0)
    out.corner_y(1)
    cot.last(1)
    out.corner_x(3)
    out.last(1)
    cot.last(3)
    out.corner_x(0)
    out.last(2)
    out.last(0)
    up_last()
    out.last(3)
    out.finish()
    for copy in late + local[prompt:]:
        copy.wait()
    wires.drain()


def opening(scale, small, weights, latents, w_up, w_down, cotangent, media, valid, times, items):
    rows, width = latents.shape
    shard = weights[0].shape[0]
    up_rows, up_width = w_up.shape
    all_rows = media.shape[0] + rows
    wires = 5 * spread_sems(True) + spread_sems(False) + LINE_SEMS + 31 + 1 + 6
    square = jax.ShapeDtypeStruct((width, width), BF16)
    table = jax.ShapeDtypeStruct((LINES, rows, width), BF16)
    keys = jax.ShapeDtypeStruct((all_rows, width), BF16)
    return pl.pallas_call(
        partial(opening_kernel, scale),
        out_shape=[
            jax.ShapeDtypeStruct((16, width), F32),
            jax.ShapeDtypeStruct((8, 128), F32),
            square,
            square,
            square,
            square,
            jax.ShapeDtypeStruct((32, up_rows, up_width // 16), BF16),
            jax.ShapeDtypeStruct((2,) + w_down.shape, BF16),
            jax.ShapeDtypeStruct((16,) + cotangent.shape, BF16),
            keys,
            keys,
            keys,
            table,
            table,
            jax.ShapeDtypeStruct((LINES, rows, 128), F32),
            jax.ShapeDtypeStruct((rows, width), F32),
            jax.ShapeDtypeStruct((rows, 128), F32),
        ],
        in_specs=[LEFT] * 9 + [VMEM] * 3 + [pl.BlockSpec(memory_space=pltpu.SMEM)],
        out_specs=[VMEM] * 2 + [LEFT] * 11 + [VMEM] * 4,
        scratch_shapes=[
            sems(wires),
            sems(wires),
            sems(16),
            pltpu.VMEM((32,) + small.shape, F32),
            pltpu.VMEM((width, width), BF16),
            pltpu.VMEM((width, width), BF16),
            pltpu.VMEM((width, width), BF16),
            pltpu.VMEM((LINES, rows, width), BF16),
            pltpu.VMEM((LINES, rows, width), BF16),
            pltpu.VMEM((all_rows, width), BF16),
            pltpu.VMEM((all_rows, width), BF16),
            pltpu.VMEM((all_rows, width), BF16),
            pltpu.VMEM((LINES, rows, width), BF16),
            pltpu.VMEM((8, width), F32),
            pltpu.VMEM((LINES, rows, width), F32),
            pltpu.VMEM((LINES, rows, width), BF16),
            pltpu.VMEM((LINES, rows, 128), F32),
        ],
        compiler_params=params(0),
        name="opening",
    )(small, *weights, latents, w_up, w_down, cotangent, media, valid, times, items)


def repel(queries, grads, keys, values, valid, shift, slope, scale, masks):
    query_stack = stacked(queries, masks)
    grad_stack = stacked(grads, masks)
    score = dot_last(query_stack, keys) * scale
    expo = jnp.exp(score)
    if valid is not None:
        expo = jnp.where(valid > 0, expo, 0.0)
    mix = dot_last(grad_stack, values)
    raw = (expo * (mix + shift + slope * score) * scale).astype(BF16)
    query_grad = unstacked(jnp.dot(raw, keys, preferred_element_type=F32), masks)
    key_grad = dot_first(raw, query_stack).astype(BF16)
    value_grad = dot_first(expo.astype(BF16), grad_stack).astype(BF16)
    return query_grad, key_grad, value_grad


def stacked_columns(terms, first):
    return jnp.concatenate([terms[:, first + h : first + h + 1] for h in range(GROUP)], axis=0)


def closing_kernel(scale, *refs):
    (
        table_ref,
        grad_ref,
        terms_ref,
        keys_ref,
        values_ref,
        normed_ref,
        valid_ref,
        attn_ref,
        low_ref,
        own_grad_ref,
        own_terms_ref,
        key_weight_ref,
        value_weight_ref,
        query_weight_ref,
        media_ref,
        time_rows_ref,
        tables_ref,
        latents_ref,
        middle_grad_ref,
        ffn_gain_ref,
        item_ref,
        time_ref,
        media_grad_out,
        latents_grad_out,
        small_out,
        out_out,
        value_out,
        key_out,
        query_out,
        send_sems,
        recv_sems,
        local_sems,
        table,
        grads,
        keys,
        values,
        normed,
        key_grad,
        value_grad,
        weight_a,
        weight_b,
        sums,
        terms_query,
        got_query,
        query_grad,
        own_query_grad,
        media_grad,
        latent_grad,
        small,
        small_sums,
        small_got,
        part_a,
        part_b,
        part_c,
        *fold,
    ) = refs
    z, g, _, core = here()
    items, rows, width = table.shape
    frames, _, patches = valid_ref.shape
    media_rows = frames * patches
    shard = width // 32
    groups = H // GROUP
    span = width // groups
    masks = head_masks(rows, span, span // GROUP)
    greet(line_of(z, g) + sides_of(z, g, True))
    wires = Wires(send_sems, recv_sems)
    out = Fold(wires, part_a, True, fold[:FOLD], out_out)
    value = Fold(wires, part_b, True, fold[FOLD : 2 * FOLD], value_out)
    key = Fold(wires, part_c, True, fold[2 * FOLD : 3 * FOLD], key_out)
    query = Fold(wires, part_a, True, fold[3 * FOLD :], query_out)
    total = Total(wires, small, small_out, small_sums, small_got)
    exchange = Exchange(wires, [(terms_query, got_query)])
    local = []

    def load(source, target):
        copy = pltpu.make_async_copy(source, target, local_sems.at[len(local)])
        copy.start()
        local.append(copy)
        return copy

    loads = [
        load(table_ref, table),
        load(grad_ref, grads),
        load(keys_ref, keys),
        load(values_ref, values),
    ]
    normed_load = load(normed_ref, normed)
    key_load = load(key_weight_ref, weight_a)
    value_load = load(value_weight_ref, weight_b)
    stored = []

    def weight_part(part, left, right):
        @pl.loop(0, LINES)
        def _(n):
            cols = pl.ds(pl.multiple_of(n * span, 128), span)
            block = dot_first(left[:, cols], right[...]).astype(BF16)
            part[n] = block.reshape(PLANE, 2, shard, width)

    def out_part():
        weight_part(part_a, attn_ref, low_ref)
        out.start()

    def value_part():
        normed_load.wait()
        weight_part(part_b, normed, value_grad)
        value.start()

    def key_part():
        weight_part(part_c, normed, key_grad)
        key.start()

    def repel_own():
        for copy in loads:
            copy.wait()
        sums[...] = jnp.zeros_like(sums)
        own_terms = own_terms_ref[...]
        for group in range(groups):
            cols = slice(group * span, (group + 1) * span)
            (
                own_query_grad[:, cols],
                key_grad[media_rows:, cols],
                value_grad[media_rows:, cols],
            ) = repel(
                table[z, :, cols],
                own_grad_ref[:, cols],
                keys[media_rows:, cols],
                values[media_rows:, cols],
                None,
                stacked_columns(own_terms, group * GROUP),
                stacked_columns(own_terms, H + group * GROUP),
                scale,
                masks,
            )

    def repel_frames(first, last):
        @pl.loop(first, last)
        def _(frame):
            block = pl.ds(pl.multiple_of(frame * patches, patches), patches)
            valid = valid_ref[frame]
            share = [item_ref[frame, item] for item in range(items)]

            def pick(ref, cols):
                chosen = share[0] * ref[0, :, cols].astype(F32)
                for item in range(1, items):
                    chosen = chosen + share[item] * ref[item, :, cols].astype(F32)
                return chosen

            everything = slice(0, 128)
            terms = pick(terms_ref, everything)
            for group in range(groups):
                cols = slice(group * span, (group + 1) * span)
                query_part, key_grad[block, cols], value_grad[block, cols] = repel(
                    pick(table, cols).astype(BF16),
                    pick(grads, cols).astype(BF16),
                    keys[block, cols],
                    values[block, cols],
                    valid,
                    stacked_columns(terms, group * GROUP),
                    stacked_columns(terms, H + group * GROUP),
                    scale,
                    masks,
                )
                for item in range(items):
                    sums[item, :, cols] += share[item] * query_part

    def queries_first():
        terms_query[...] = sums[...].astype(BF16)
        exchange.first()

    def media_half(n):
        if n == 0:
            key_load.wait()
            value_load.wait()
            small[...] = jnp.zeros_like(small)
            small[10:11] = ffn_gain_ref[...]
        else:
            stored[-1].wait()
        count = media_rows // 2
        first = n * count
        block = slice(first, first + count)

        @pl.loop(0, groups)
        def _(t):
            cols = pl.ds(pl.multiple_of(t * span, 128), span)
            media_grad[:, cols] = dot_last(key_grad[block], weight_a[cols]) + dot_last(
                value_grad[block], weight_b[cols]
            )

        gain = tables_ref[8:9]
        chunk = 32
        per_frame = patches // chunk
        for f in range(count // patches):
            frame = n * (count // patches) + f
            moving = time_rows_ref[frame : frame + 1]

            def step(t, carry):
                gain_sum, row_sum = carry
                here_rows = pl.ds(pl.multiple_of(f * patches + t * chunk, chunk), chunk)
                there_rows = pl.ds(pl.multiple_of(first + f * patches + t * chunk, chunk), chunk)
                row = media_ref[there_rows].astype(F32) + moving
                pulled, summand = norm_pull(row, gain, media_grad[here_rows])
                media_grad[here_rows] = pulled
                return (
                    gain_sum + jnp.sum(summand, axis=0, keepdims=True),
                    row_sum + jnp.sum(pulled, axis=0, keepdims=True),
                )

            zero = jnp.zeros((1, width), F32)
            gain_sum, row_sum = lax.fori_loop(0, per_frame, step, (zero, zero))
            small[8:9] += gain_sum
            for t in range(8):
                small[t : t + 1] += time_ref[frame, t] * row_sum
        stored.append(load(media_grad, media_grad_out.at[pl.ds(first, count)]))

    def latents_side():
        @pl.loop(0, groups)
        def _(t):
            cols = pl.ds(pl.multiple_of(t * span, 128), span)
            latent_grad[:, cols] = dot_last(key_grad[media_rows:], weight_a[cols]) + dot_last(
                value_grad[media_rows:], weight_b[cols]
            )

        stored.append(load(query_weight_ref, weight_a))

    def query_part():
        found = own_query_grad[...]
        for item in range(items):
            found = found + got_query[item].astype(F32)
        query_grad[...] = found.astype(BF16)
        out.release()
        weight_part(part_a, normed.at[media_rows:], query_grad)
        query.start()

    def latents_end():
        stored[-1].wait()

        @pl.loop(0, groups)
        def _(t):
            cols = pl.ds(pl.multiple_of(t * span, 128), span)
            latent_grad[:, cols] += dot_last(query_grad[...], weight_a[cols])

        pulled, summand = norm_pull(
            latents_ref[...].astype(F32), tables_ref[9:10], latent_grad[...]
        )
        latents_grad_out[...] = middle_grad_ref[...] + pulled
        small[9:10] = jnp.sum(summand, axis=0, keepdims=True)
        total.push()

    def total_next():
        total.pull()
        total.push()

    out_part()
    repel_own()
    repel_frames(0, frames // 2)
    out.corner()
    repel_frames(frames // 2, frames)
    queries_first()
    out.side_x()
    out.side_y()
    value_part()
    key_part()
    value.corner()
    media_half(0)
    key.corner()
    value.side_x()
    value.side_y()
    out.line()
    media_half(1)
    key.side_x()
    exchange.finish()
    key.side_y()
    latents_side()
    query_part()
    value.line()
    latents_end()
    total_next()
    query.corner()
    key.line()
    total_next()
    query.side_x()
    value.finish()
    query.side_y()
    total_next()
    out.finish()
    query.line()
    key.finish()
    total.pull()
    query.finish()
    stored[1].wait()
    wires.drain()


def closing(scale, *args):
    (table, grads, terms, keys, values, normed) = args[:6]
    media, latents = args[14], args[17]
    rows, width = latents.shape
    shard = width // 32
    wires = 4 * fold_sems(True) + 6 + 3
    bf = [
        table.shape,
        table.shape,
        keys.shape,
        keys.shape,
        keys.shape,
        keys.shape,
        keys.shape,
        (width, width),
        (width, width),
    ]
    part = pltpu.VMEM((LINES, PLANE, 2, shard, width), BF16)
    small = (16, width)
    scratch = [pltpu.VMEM(shape, BF16) for shape in bf] + [
        pltpu.VMEM(table.shape, F32),
        pltpu.VMEM(table.shape, BF16),
        pltpu.VMEM(table.shape, BF16),
        pltpu.VMEM((rows, width), BF16),
        pltpu.VMEM((rows, width), F32),
        pltpu.VMEM((media.shape[0] // 2, width), F32),
        pltpu.VMEM((rows, width), F32),
        pltpu.VMEM(small, F32),
        pltpu.VMEM((3,) + small, F32),
        pltpu.VMEM((6,) + small, F32),
        part,
        part,
        part,
    ]
    for _ in range(4):
        scratch += fold_scratch(shard, width, True)
    smem = pl.BlockSpec(memory_space=pltpu.SMEM)
    return pl.pallas_call(
        partial(closing_kernel, scale),
        out_shape=[
            jax.ShapeDtypeStruct(media.shape, F32),
            jax.ShapeDtypeStruct(latents.shape, F32),
            jax.ShapeDtypeStruct(small, F32),
        ]
        + [jax.ShapeDtypeStruct((shard, width), F32)] * 4,
        in_specs=[LEFT, LEFT, VMEM, LEFT, LEFT, LEFT]
        + [VMEM] * 5
        + [LEFT] * 3
        + [VMEM] * 6
        + [smem] * 2,
        out_specs=[LEFT] + [VMEM] * 6,
        scratch_shapes=[sems(wires), sems(wires), sems(12)] + scratch,
        compiler_params=pltpu.CompilerParams(
            collective_id=3, has_side_effects=True, vmem_limit_bytes=67043328
        ),
        name="closing",
    )(*args)


def settle_kernel(
    weighted_ref,
    stats_ref,
    own_weighted_ref,
    own_stats_ref,
    out_ref,
    latents_ref,
    gain_ref,
    attention_ref,
    attn_ref,
    sums_ref,
    middle_ref,
    normed_ref,
):
    rows, width = latents_ref.shape
    span = width // (H // GROUP)
    masks = head_masks(rows, span, span // GROUP)
    stats = own_stats_ref[...]
    for n in range(stats_ref.shape[0]):
        stats = stats + stats_ref[n]
    sums_ref[...] = stats
    for group in range(H // GROUP):
        cols = pl.ds(group * span, span)
        weighted = own_weighted_ref[:, cols]
        for n in range(weighted_ref.shape[0]):
            weighted = weighted + weighted_ref[n, :, cols].astype(F32)
        attention = weighted / spread_heads(stats, group * GROUP, masks)
        attention_ref[:, cols] = attention
        attn_ref[:, cols] = attention.astype(BF16)
    middle = latents_ref[...].astype(F32) + jnp.dot(
        attn_ref[...], out_ref[...], preferred_element_type=F32
    )
    middle_ref[...] = middle
    normed_ref[...] = layer_norm(middle, gain_ref[...]).astype(BF16)


def settle(weighted, stats, own_weighted, own_stats, w_out, latents, gain):
    vmem = pl.BlockSpec(memory_space=pltpu.VMEM)
    shape = latents.shape
    return pl.pallas_call(
        settle_kernel,
        out_shape=[
            jax.ShapeDtypeStruct(shape, F32),
            jax.ShapeDtypeStruct(shape, BF16),
            jax.ShapeDtypeStruct(own_stats.shape, F32),
            jax.ShapeDtypeStruct(shape, F32),
            jax.ShapeDtypeStruct(shape, BF16),
        ],
        in_specs=[vmem] * 7,
        out_specs=[vmem] * 5,
        name="settle",
    )(weighted, stats, own_weighted, own_stats, w_out, latents, gain)


def norm_pull(rows, gain, grad):
    mean = jnp.mean(rows, axis=-1, keepdims=True)
    centred = rows - mean
    inverse = lax.rsqrt(jnp.mean(centred * centred, axis=-1, keepdims=True) + NORM_STABILIZER)
    xhat = centred * inverse
    t = grad * gain
    pulled = (
        t
        - jnp.mean(t, axis=-1, keepdims=True)
        - xhat * jnp.mean(t * xhat, axis=-1, keepdims=True)
    ) * inverse
    return pulled, grad * xhat


def unsettle_kernel(
    normed_grad_ref,
    middle_ref,
    gain_ref,
    cot_ref,
    out_ref,
    attention_ref,
    stats_ref,
    coef_ref,
    middle_grad_ref,
    low_ref,
    gain_grad_ref,
    weighted_grad_ref,
    terms_ref,
    attn_grad,
):
    rows, width = middle_ref.shape
    span = width // (H // GROUP)
    masks = head_masks(rows, span, span // GROUP)
    pulled, summand = norm_pull(middle_ref[...], gain_ref[...], normed_grad_ref[...])
    gain_grad_ref[...] = jnp.sum(summand, axis=0, keepdims=True)
    middle_grad = cot_ref[...].astype(F32) + pulled
    middle_grad_ref[...] = middle_grad
    low_ref[...] = middle_grad.astype(BF16)
    attn_grad[...] = dot_last(low_ref[...], out_ref[...])
    stats = stats_ref[...]
    coef = coef_ref[0, 0]
    lane = lax.broadcasted_iota(jnp.int32, (rows, 128), 1)
    terms = jnp.zeros((rows, 128), F32)
    for group in range(H // GROUP):
        cols = pl.ds(group * span, span)
        grad = attn_grad[:, cols]
        first = group * GROUP
        weighted_grad_ref[:, cols] = (grad / spread_heads(stats, first, masks)).astype(BF16)
        along = grad * attention_ref[:, cols]
        for h in range(GROUP):
            inner = jnp.sum(jnp.where(masks[h], along, 0.0), axis=1, keepdims=True)
            total = stats[:, first + h : first + h + 1]
            moment = stats[:, H + first + h : H + first + h + 1]
            slope = -coef / total
            shift = -inner / total + coef * (1.0 / total + moment / (total * total)) + slope
            terms = jnp.where(lane == first + h, shift, terms)
            terms = jnp.where(lane == H + first + h, slope, terms)
    terms_ref[...] = terms


def unsettle(normed_grad, middle, gain, cotangent, w_out, attention, stats, coef):
    vmem = pl.BlockSpec(memory_space=pltpu.VMEM)
    shape = middle.shape
    return pl.pallas_call(
        unsettle_kernel,
        out_shape=[
            jax.ShapeDtypeStruct(shape, F32),
            jax.ShapeDtypeStruct(shape, BF16),
            jax.ShapeDtypeStruct((1, shape[1]), F32),
            jax.ShapeDtypeStruct(shape, BF16),
            jax.ShapeDtypeStruct(stats.shape, F32),
        ],
        in_specs=[vmem] * 7 + [pl.BlockSpec(memory_space=pltpu.SMEM)],
        out_specs=[vmem] * 5,
        scratch_shapes=[pltpu.VMEM(shape, F32)],
        name="unsettle",
    )(normed_grad, middle, gain, cotangent, w_out, attention, stats, coef)


def per_device(
    media,
    latents,
    frame_counts,
    time_index,
    valid,
    time_table,
    media_gain,
    latent_gain,
    ffn_gain,
    w_query,
    w_key,
    w_value,
    w_out,
    w_up,
    w_down,
    cotangent,
):
    frames = time_index.shape[0]
    patches = valid.shape[0] // frames
    latent_rows, width = latents.shape
    shard = media_gain.shape[0]
    scale = (width // H) ** (-0.5)
    column = lax.axis_index("gx")
    row_index = lax.axis_index("gy")
    frame_ends = jnp.cumsum(frame_counts[row_index])
    position = column * frames + jnp.arange(frames, dtype=jnp.int32)
    item_index = jnp.sum((frame_ends[None, :] <= position[:, None]).astype(jnp.int32), axis=1)
    item_index = jnp.clip(item_index, 0, LINES - 1).astype(jnp.int32)

    count = jnp.sum(valid.astype(F32))
    small = jnp.concatenate(
        [
            time_table.astype(F32),
            media_gain.astype(F32)[None],
            latent_gain.astype(F32)[None],
            ffn_gain.astype(F32)[None],
            jnp.full((1, shard), count, F32),
            jnp.zeros((4, shard), F32),
        ],
        axis=0,
    )
    small = jnp.pad(small, ((0, 0), (0, 128 - shard)))
    times = (time_index[:, None] == jnp.arange(16, dtype=jnp.int32)[None, :]).astype(BF16)
    times = jnp.pad(times, ((0, 8 - frames), (0, 0)))
    items = (item_index[:, None] == jnp.arange(LINES, dtype=jnp.int32)[None, :]).astype(F32)
    valid_rows = valid.reshape(frames, 1, patches)
    (
        tables,
        counts,
        full_key,
        full_value,
        full_query,
        full_out,
        up_cols,
        down_rows,
        cot_rows,
        normed,
        keys,
        values,
        table,
        got_weighted,
        got_stats,
        own_weighted,
        own_stats,
    ) = opening(
        scale,
        small,
        (w_key, w_value, w_query, w_out),
        latents,
        w_up,
        w_down,
        cotangent,
        media,
        valid_rows,
        times,
        items,
    )
    full_time = tables[:8].astype(BF16)
    full_media_gain, full_latent_gain, full_ffn_gain = tables[8:9], tables[9:10], tables[10:11]
    valid_total = counts[3, 0]
    coefficient = ENTROPY_WEIGHT * (valid.shape[0] * lax.axis_size(AXES)) / valid_total
    up_cols = up_cols.reshape(width, -1)
    down_rows = down_rows.reshape(-1, width)
    cot_rows = cot_rows.reshape(-1, width)
    time_rows = product(times[:frames, :8], full_time)
    attention, attn_low, sums, middle, ffn_normed = settle(
        got_weighted, got_stats, own_weighted, own_stats, full_out, latents, full_ffn_gain
    )
    ffn_rows = gather(ffn_normed, 5).reshape(-1, width)
    up_rows = product(ffn_rows, up_cols)
    hidden = jax.nn.gelu(up_rows, approximate=False).astype(BF16)
    hidden_grad = inner_last(cot_rows, down_rows)
    gelu_pull = jax.vjp(partial(jax.nn.gelu, approximate=False), up_rows)[1]
    up_grad = gelu_pull(hidden_grad)[0].astype(BF16)
    normed_part = inner_last(up_grad, up_cols).astype(BF16)
    down_part = product(hidden, down_rows).astype(BF16)
    shape = (LINES, PLANE, latent_rows, width)
    ffn_normed_grad = scatter(normed_part.reshape(shape), 6)
    up_grad_part = inner_first(ffn_rows, up_grad).astype(BF16)
    down_grad_part = inner_first(hidden, cot_rows)
    middle_grad, middle_low, grad_ffn_gain, weighted_grad, terms = unsettle(
        ffn_normed_grad,
        middle,
        full_ffn_gain,
        cotangent,
        full_out,
        attention,
        sums,
        coefficient.reshape(1, 1),
    )
    grad_table, terms_table, down_sum, shard_up, shard_down = turn_back(
        weighted_grad,
        terms,
        down_part.reshape(shape),
        up_grad_part.reshape(16, 2, shard, -1),
        down_grad_part.reshape(2, -1, width),
    )
    new_latents = (middle + down_sum).astype(BF16)
    shard_up = jnp.swapaxes(shard_up, 0, 1).reshape(shard, -1).astype(F32)
    (
        media_grad,
        latents_grad,
        smalls_grad,
        shard_out,
        shard_value,
        shard_key,
        shard_query,
    ) = closing(
        scale,
        table,
        grad_table,
        terms_table,
        keys,
        values,
        normed,
        valid_rows,
        attn_low,
        middle_low,
        weighted_grad,
        terms,
        full_key,
        full_value,
        full_query,
        media,
        jnp.pad(time_rows, ((0, 8 - frames), (0, 0))),
        tables,
        latents,
        middle_grad,
        grad_ffn_gain,
        items,
        times[:frames, :8].astype(F32),
    )
    place = (column * 8 + row_index) * shard
    mine = lax.dynamic_slice(smalls_grad, (0, place), (16, shard))
    return (
        new_latents,
        media_grad,
        latents_grad,
        mine[:8],
        mine[8],
        mine[9],
        mine[10],
        shard_query,
        shard_key,
        shard_value,
        shard_out,
        shard_up,
        shard_down,
    )


def solution(mesh):
    in_specs = (
        P(("gx", "gy"), None),
        P(("gx", "gy"), None),
        P(),
        P(("gx", "gy")),
        P(("gx", "gy")),
        P(None, ("gx", "gy")),
        P(("gx", "gy")),
        P(("gx", "gy")),
        P(("gx", "gy")),
        P(("gx", "gy"), None),
        P(("gx", "gy"), None),
        P(("gx", "gy"), None),
        P(("gx", "gy"), None),
        P(("gx", "gy"), None),
        P(("gx", "gy"), None),
        P(("gx", "gy"), None),
    )
    out_specs = (
        P(("gx", "gy"), None),
        P(("gx", "gy"), None),
        P(("gx", "gy"), None),
        P(None, ("gx", "gy")),
        P(("gx", "gy")),
        P(("gx", "gy")),
        P(("gx", "gy")),
        P(("gx", "gy"), None),
        P(("gx", "gy"), None),
        P(("gx", "gy"), None),
        P(("gx", "gy"), None),
        P(("gx", "gy"), None),
        P(("gx", "gy"), None),
    )
    return jax.shard_map(
        per_device if dict(mesh.shape) == {"gx": 4, "gy": 8} else plain_device,
        mesh=mesh, in_specs=in_specs, out_specs=out_specs, check_vma=False
    )
```

```python
from functools import partial

import jax
import jax.numpy as jnp
from jax import lax
from jax.experimental import pallas as pl
from jax.experimental.pallas import tpu as pltpu
from jax.sharding import PartitionSpec as P

H = 16


ENTROPY_WEIGHT = 4.0
NORM_STABILIZER = 1e-05
AXES = ("gx", "gy")
LINES = 4
PLANE = 4
HBM = pl.ANY
BF16 = jnp.bfloat16
F32 = jnp.float32


def here():
    z = lax.axis_index("gx")
    g = lax.axis_index("gy")
    return z, g, g // 2, g % 2


def sibling(g):
    return g + 1 - 2 * (g % 2)


def along_x(g):
    return g + 2 - 4 * ((g // 2) % 2)


def along_y(g):
    return (g + 4) % 8


def turn(z, k):
    return (z + k) % LINES


def greet(devices):
    barrier = pltpu.get_barrier_semaphore()
    for device in devices:
        pl.semaphore_signal(
            barrier, inc=1, device_id=device, device_id_type=pl.DeviceIdType.MESH
        )
    pl.semaphore_wait(barrier, len(devices))


def line_of(z, g):
    return [(turn(z, k), g) for k in (1, 2, 3)]


class Wires:
    def __init__(self, send_sems, recv_sems):
        self.send_sems, self.recv_sems, self.used, self.sent = send_sems, recv_sems, 0, []

    def reserve(self, count):
        first = self.used
        self.used += count
        return first

    def copy(self, source, target, device, send, recv):
        return pltpu.make_async_remote_copy(
            src_ref=source,
            dst_ref=target,
            send_sem=self.send_sems.at[send],
            recv_sem=self.recv_sems.at[recv],
            device_id=device,
            device_id_type=pl.DeviceIdType.MESH,
        )

    def send(self, source, target, device):
        n = self.reserve(1)
        copy = self.copy(source, target, device, n, n)
        copy.start()
        self.sent.append((None, copy))
        return copy

    def send_if(self, condition, source, target, device, send, recv):
        copy = self.copy(source, target, device, send, recv)
        self.sent.append((condition, copy))

        @pl.when(condition)
        def _():
            copy.start()

        return copy

    def drain(self):
        for condition, copy in self.sent:
            if condition is None:
                copy.wait_send()
            else:
                pl.when(condition)(copy.wait_send)


class Line:
    def __init__(self, wires, shard, slot):
        self.wires, self.shard, self.slot = wires, shard, slot
        self.z, self.g, _, _ = here()
        self.base = wires.reserve(4)
        low, high = (3 - self.z) // 3, self.z // 3
        self.order = (1 + 2 * low, 3 - low - high, 2 - low + high)

    def first(self):
        z, g = self.z, self.g
        own = self.slot(z)
        base = self.base
        self.wires.send_if(z < 3, self.shard, own, (turn(z, 1), g), base + 1, base + 1)
        self.wires.send_if(z > 0, self.shard, own, (turn(z, 3), g), base + 3, base + 3)
        self.across = self.wires.copy(self.shard, own, (turn(z, 2), g), base + 2, base + 2)
        self.across.start()
        self.wires.sent.append((None, self.across))

    def take(self, step):
        z, g = self.z, self.g
        k = self.order[step]
        origin = turn(z, LINES - k)
        held = self.slot(origin)
        self.wires.copy(held, held, (z, g), 0, self.base + k).wait_recv()
        if step == 2:
            self.relay(z == 2, 3, 3)
        if step == 2:
            self.relay(z == 1, 0, 1)
        return origin

    def relay(self, condition, there, k):
        held = self.slot(turn(self.z, 2))
        self.wires.send_if(
            condition, held, held, (there, self.g), self.base, self.base + k
        )


class Spread:
    def __init__(self, wires, shard, slot, half, whole):
        self.wires, self.shard, self.slot, self.half, self.whole = wires, shard, slot, half, whole
        self.z, self.g, _, _ = here()
        self.line = Line(wires, shard, lambda z: slot(z, self.g))
        self.zs, self.x, self.y, self.dx, self.dy, self.sib = [self.z], [], [], {}, {}, []

    def side(self, gy):
        return (self.z, gy)

    def to_sibling(self, held):
        if self.whole:
            self.sib.append(self.wires.send(held, held, self.side(sibling(self.g))))

    def first(self):
        own = self.slot(self.z, self.g)
        self.line.first()
        self.x.append(self.wires.send(self.shard, own, self.side(along_x(self.g))))
        self.y.append(self.wires.send(self.shard, own, self.side(along_y(self.g))))
        if self.whole:
            self.sib.append(self.wires.send(self.shard, own, self.side(sibling(self.g))))

    def column(self, step):
        self.zs.append(self.line.take(step))
        held = self.slot(self.zs[-1], self.g)
        self.x.append(self.wires.send(held, held, self.side(along_x(self.g))))
        self.y.append(self.wires.send(held, held, self.side(along_y(self.g))))
        self.to_sibling(held)

    def corner(self, n):
        self.corner_x(n)
        self.corner_y(n)

    def corner_x(self, n):
        self.x[n].wait_recv()
        held = self.slot(self.zs[n], along_x(self.g))
        part = self.half(held, 0)
        self.dy[n] = self.wires.send(part, part, self.side(along_y(self.g)))
        self.to_sibling(held)

    def corner_y(self, n):
        self.y[n].wait_recv()
        held = self.slot(self.zs[n], along_y(self.g))
        part = self.half(held, 1)
        self.dx[n] = self.wires.send(part, part, self.side(along_x(self.g)))
        self.to_sibling(held)

    def last(self, n):
        self.dy[n].wait_recv()
        self.dx[n].wait_recv()
        self.to_sibling(self.slot(self.zs[n], along_y(along_x(self.g))))

    def finish(self):
        for copy in self.sib:
            copy.wait_recv()


def spread_all(flows):
    for flow in flows:
        flow.first()
    for flow in flows:
        flow.corner(0)
    for step in range(3):
        for flow in flows:
            flow.column(step)
        for flow in flows:
            flow.corner(step + 1)
    for n in range(4):
        for flow in flows:
            flow.last(n)
    for flow in flows:
        flow.finish()


LINE_SEMS = 4


def spread_sems(whole):
    return LINE_SEMS + 8 + 8 + (16 if whole else 0)


def columns_half(ref, which):
    width = ref.shape[-1] // 2
    return ref.at[..., pl.ds(which * width, width)]


def rows_half(ref, which):
    rows = ref.shape[0] // 2
    return ref.at[pl.ds(which * rows, rows)]


def sides_of(z, g, whole):
    near = [(z, along_x(g)), (z, along_y(g))]
    return near + [(z, sibling(g))] if whole else near


def params(ident):
    return pltpu.CompilerParams(
        collective_id=ident, has_side_effects=True, vmem_limit_bytes=60 * 2**20
    )


def sems(count):
    return pltpu.SemaphoreType.DMA((count,))


VMEM = pl.BlockSpec(memory_space=pltpu.VMEM)
LEFT = pl.BlockSpec(memory_space=HBM)


class Exchange:
    def __init__(self, wires, pairs):
        self.wires, self.pairs = wires, pairs
        self.z, self.g, _, _ = here()

    def first(self):
        z = self.z
        self.copies = []
        for k in (2, 1, 3):
            there = turn(z, k)
            for source, out in self.pairs:
                self.copies.append(
                    self.wires.send(source.at[there], out.at[z], (there, self.g))
                )
        for source, out in self.pairs:
            out[z] = source[z]

    def finish(self):
        for copy in self.copies:
            copy.wait_recv()


def add_slots(target, source, count):
    @pl.loop(0, count)
    def _(n):
        target[n] = (target[n].astype(F32) + source[n].astype(F32)).astype(target.dtype)


class Fold:
    def __init__(self, wires, parts, whole, scratch, out):
        self.wires, self.parts, self.whole, self.out = wires, parts, whole, out
        self.from_sib, self.cx, self.cy, self.fx, self.fy, self.fz = scratch
        self.z, self.g, self.chip, self.core = here()
        self.width = parts.shape[-1] // 2
        self.sends = []

    def send(self, source, target, gy):
        copy = self.wires.send(source, target, (self.z, gy))
        self.sends.append(copy)
        return copy

    def column(self, q):
        return self.parts.at[:, q, self.core] if self.whole else self.parts.at[:, q]

    def half(self, ref, which):
        return ref.at[:, :, pl.ds(which * self.width, self.width)]

    def merge(self, q):
        if self.whole:
            core = self.core

            @pl.loop(0, LINES)
            def _(n):
                self.parts[n, q, core] = self.parts[n, q, core] + self.from_sib[n, q]

    def start(self):
        if self.whole:
            theirs = self.parts.at[:, :, 1 - self.core]
            self.sib = self.send(theirs, self.from_sib, sibling(self.g))

    def corner(self):
        if self.whole:
            self.sib.wait_recv()
        q = along_y(along_x(self.g)) // 2
        self.merge(q)
        far = self.column(q)
        self.to_y = self.send(self.half(far, 0), self.cy, along_y(self.g))
        self.to_x = self.send(self.half(far, 1), self.cx, along_x(self.g))

    def side(self, gy, came, corner, which, target):
        q = gy // 2
        self.merge(q)
        came.wait_recv()
        column = self.column(q)
        cols = slice(which * self.width, (which + 1) * self.width)

        @pl.loop(0, LINES)
        def _(n):
            column[n, :, cols] = column[n, :, cols] + corner[n]

        return self.send(column, target, gy)

    def side_x(self):
        self.by_x = self.side(along_x(self.g), self.to_y, self.cy, 0, self.fx)

    def side_y(self):
        self.by_y = self.side(along_y(self.g), self.to_x, self.cx, 1, self.fy)

    def line(self):
        self.merge(self.chip)
        self.by_x.wait_recv()
        self.by_y.wait_recv()
        column = self.column(self.chip)
        self.zs = []
        for k in (2, 1, 3):
            there = turn(self.z, k)
            self.fx[there] = (
                column[there].astype(F32)
                + self.fx[there].astype(F32)
                + self.fy[there].astype(F32)
            ).astype(BF16)
            self.zs.append(
                self.wires.send(self.fx.at[there], self.fz.at[k - 1], (there, self.g))
            )
        z = self.z
        self.out[...] = column[z].astype(F32) + self.fx[z].astype(F32) + self.fy[z].astype(F32)

    def finish(self):
        for copy in self.zs:
            copy.wait_recv()
        self.out[...] += (
            self.fz[0].astype(F32) + self.fz[1].astype(F32) + self.fz[2].astype(F32)
        )

    def release(self):
        for copy in self.sends:
            copy.wait_send()
        waited = [id(copy) for copy in self.sends]
        self.wires.sent = [entry for entry in self.wires.sent if id(entry[1]) not in waited]


def fold_scratch(rows, cols, whole):
    half = cols // 2
    return [
        pltpu.VMEM((LINES, PLANE, rows, cols) if whole else (1, 1, 16, 128), BF16),
        pltpu.VMEM((LINES, rows, half), BF16),
        pltpu.VMEM((LINES, rows, half), BF16),
        pltpu.VMEM((LINES, rows, cols), BF16),
        pltpu.VMEM((LINES, rows, cols), BF16),
        pltpu.VMEM((LINES - 1, rows, cols), BF16),
    ]


FOLD = 6


def fold_sems(whole):
    return (1 if whole else 0) + 4 + 3


class FoldSteps:
    def __init__(self, wires, parts, scratch, out):
        self.wires, self.parts, self.out = wires, parts, out
        _, self.cx, self.cy, self.fx, self.fy, self.fz = scratch
        self.z, self.g, self.chip, _ = here()
        self.width = parts.shape[-1] // 2
        self.base = wires.reserve(LINES)
        low, high = (3 - self.z) // 3, self.z // 3
        back = (0, 1 + 2 * low, 3 - low - high, 2 - low + high)
        self.back = back
        self.zs = [turn(self.z, LINES - k) if n else self.z for n, k in enumerate(back)]
        self.to_x, self.to_y, self.by_x, self.by_y = {}, {}, {}, {}

    def half(self, n, q, which):
        return self.parts.at[self.zs[n], q, :, pl.ds(which * self.width, self.width)]

    def corner(self, n):
        far = along_y(along_x(self.g)) // 2
        place = self.zs[n]
        self.to_y[n] = self.wires.send(
            self.half(n, far, 0), self.cy.at[place], (self.z, along_y(self.g))
        )
        self.to_x[n] = self.wires.send(
            self.half(n, far, 1), self.cx.at[place], (self.z, along_x(self.g))
        )

    def side(self, n, gy, came, corner, which, target):
        came.wait_recv()
        q, place = gy // 2, self.zs[n]
        cols = slice(which * self.width, (which + 1) * self.width)
        self.parts[place, q, :, cols] = self.parts[place, q, :, cols] + corner[place]
        return self.wires.send(self.parts.at[place, q], target.at[place], (self.z, gy))

    def side_x(self, n):
        self.by_x[n] = self.side(n, along_x(self.g), self.to_y[n], self.cy, 0, self.fx)

    def side_y(self, n):
        self.by_y[n] = self.side(n, along_y(self.g), self.to_x[n], self.cx, 1, self.fy)

    def line(self, n):
        self.by_x[n].wait_recv()
        self.by_y[n].wait_recv()
        place = self.zs[n]
        found = (
            self.parts[place, self.chip].astype(F32)
            + self.fx[place].astype(F32)
            + self.fy[place].astype(F32)
        )
        if n == 0:
            self.out[...] = found
            return
        self.fx[place] = found.astype(BF16)
        k = LINES - self.back[n]
        copy = self.wires.copy(
            self.fx.at[place],
            self.fz.at[k - 1],
            (place, self.g),
            self.base + k,
            self.base + k,
        )
        copy.start()
        self.wires.sent.append((None, copy))

    def finish(self):
        for k in (1, 2, 3):
            held = self.fz.at[k - 1]
            self.wires.copy(held, held, (self.z, self.g), 0, self.base + k).wait_recv()
        self.out[...] += (
            self.fz[0].astype(F32) + self.fz[1].astype(F32) + self.fz[2].astype(F32)
        )


STEP_SEMS = 16 + LINES


def layer_norm(row_block, gain_row):
    row_mean = jnp.mean(row_block, axis=-1, keepdims=True)
    centred = row_block - row_mean
    variance = jnp.mean(centred * centred, axis=-1, keepdims=True)
    return centred * lax.rsqrt(variance + NORM_STABILIZER) * gain_row


def product(left_side, right_side):
    return jnp.dot(left_side, right_side, preferred_element_type=jnp.float32)


def inner_first(left_side, right_side):
    return lax.dot_general(
        left_side, right_side, (((0,), (0,)), ((), ())), preferred_element_type=jnp.float32
    )


def inner_last(left_side, right_side):
    return lax.dot_general(
        left_side, right_side, (((1,), (1,)), ((), ())), preferred_element_type=jnp.float32
    )


def collect(onehot_rows, value_rows):
    return lax.dot_general(
        onehot_rows,
        value_rows,
        (((0,), (0,)), ((), ())),
        precision=lax.Precision.HIGHEST,
        preferred_element_type=jnp.float32,
    )


def plain_device(
    media,
    latents,
    frame_counts,
    time_index,
    valid,
    time_table,
    media_gain,
    latent_gain,
    ffn_gain,
    w_query,
    w_key,
    w_value,
    w_out,
    w_up,
    w_down,
    cotangent,
):
    frames = time_index.shape[0]
    patches = valid.shape[0] // frames
    latent_rows = latents.shape[0]
    model_width = latents.shape[1]
    head_size = model_width // H
    score_scale = head_size ** (-0.5)
    across = lax.axis_size("gx")
    column = lax.axis_index("gx")
    row_index = lax.axis_index("gy")
    frame_ends = jnp.cumsum(frame_counts[row_index])
    position = column * frames + jnp.arange(frames, dtype=jnp.int32)
    item_index = jnp.sum((frame_ends[None, :] <= position[:, None]).astype(jnp.int32), axis=1)
    item_onehot = (item_index[:, None] == jnp.arange(across, dtype=jnp.int32)[None, :]).astype(
        jnp.float32
    )
    (
        full_query,
        full_key,
        full_value,
        full_out,
        full_up,
        full_down,
        full_media_gain,
        full_latent_gain,
        full_ffn_gain,
        full_time,
    ) = (
        lax.all_gather(w_query, ("gx", "gy"), axis=0, tiled=True),
        lax.all_gather(w_key, ("gx", "gy"), axis=0, tiled=True),
        lax.all_gather(w_value, ("gx", "gy"), axis=0, tiled=True),
        lax.all_gather(w_out, ("gx", "gy"), axis=0, tiled=True),
        lax.all_gather(w_up, ("gx", "gy"), axis=0, tiled=True),
        lax.all_gather(w_down, ("gx", "gy"), axis=0, tiled=True),
        lax.all_gather(media_gain, ("gx", "gy"), axis=0, tiled=True),
        lax.all_gather(latent_gain, ("gx", "gy"), axis=0, tiled=True),
        lax.all_gather(ffn_gain, ("gx", "gy"), axis=0, tiled=True),
        lax.all_gather(time_table, ("gx", "gy"), axis=1, tiled=True),
    )
    time_onehot = (
        time_index[:, None] == jnp.arange(full_time.shape[0], dtype=jnp.int32)[None, :]
    ).astype(jnp.float32)
    time_rows = product(time_onehot.astype(jnp.bfloat16), full_time)
    media_in = (
        media.astype(jnp.float32).reshape(frames, patches, model_width) + time_rows[:, None, :]
    ).reshape(-1, model_width)
    media_normed = layer_norm(media_in, full_media_gain.astype(jnp.float32)).astype(jnp.bfloat16)
    key_heads = (
        product(media_normed, full_key).astype(jnp.bfloat16).reshape(frames, patches, H, head_size)
    )
    value_heads = (
        product(media_normed, full_value)
        .astype(jnp.bfloat16)
        .reshape(frames, patches, H, head_size)
    )
    latent_in = latents.astype(jnp.float32)
    latent_normed = layer_norm(latent_in, full_latent_gain.astype(jnp.float32)).astype(jnp.bfloat16)
    own_query = product(latent_normed, full_query).astype(jnp.bfloat16)
    own_key = product(latent_normed, full_key).astype(jnp.bfloat16)
    own_value = product(latent_normed, full_value).astype(jnp.bfloat16)
    valid_total = lax.psum(jnp.sum(valid.astype(jnp.float32)), ("gx", "gy"))
    coefficient = ENTROPY_WEIGHT * (valid.shape[0] * lax.axis_size(("gx", "gy"))) / valid_total
    query_table = lax.all_gather(own_query, "gx", axis=0, tiled=True)
    picked = query_table.reshape(-1, latent_rows, H, head_size)[item_index]
    media_score = (
        jnp.einsum("flhd,fphd->flhp", picked, key_heads, preferred_element_type=jnp.float32)
        * score_scale
    )
    valid_mask = valid.reshape(frames, 1, 1, patches) > 0
    media_expo = jnp.where(valid_mask, jnp.exp(media_score), 0.0)
    expo_low = media_expo.astype(jnp.bfloat16)
    media_total = jnp.sum(media_expo, axis=-1)
    media_moment = jnp.sum(media_expo * media_score, axis=-1)
    media_weighted = jnp.einsum(
        "flhp,fphd->flhd", expo_low, value_heads, preferred_element_type=jnp.float32
    )
    dense_weighted = collect(item_onehot, media_weighted.reshape(frames, -1)).reshape(
        -1, model_width
    )
    dense_total = collect(item_onehot, media_total.reshape(frames, -1)).reshape(-1, H)
    dense_moment = collect(item_onehot, media_moment.reshape(frames, -1)).reshape(-1, H)
    got_weighted, got_total, got_moment = (
        lax.psum_scatter(dense_weighted, "gx", scatter_dimension=0, tiled=True),
        lax.psum_scatter(dense_total, "gx", scatter_dimension=0, tiled=True),
        lax.psum_scatter(dense_moment, "gx", scatter_dimension=0, tiled=True),
    )
    query_head_count = own_query.reshape(latent_rows, H, head_size)
    latent_key_rows = own_key.reshape(latent_rows, H, head_size)
    latent_value_rows = own_value.reshape(latent_rows, H, head_size)
    latent_score = (
        jnp.einsum(
            "uer,zer->uez", query_head_count, latent_key_rows, preferred_element_type=jnp.float32
        )
        * score_scale
    )
    latent_expo = jnp.exp(latent_score)
    latent_reduced_precision = latent_expo.astype(jnp.bfloat16)
    weighted = got_weighted.reshape(latent_rows, H, head_size) + jnp.einsum(
        "nwr,rwb->nwb",
        latent_reduced_precision,
        latent_value_rows,
        preferred_element_type=jnp.float32,
    )
    totals = got_total + jnp.sum(latent_expo, axis=-1)
    moment = got_moment + jnp.sum(latent_expo * latent_score, axis=-1)
    attention = weighted / totals[..., None]
    attn_low = attention.reshape(latent_rows, model_width).astype(jnp.bfloat16)
    middle = latent_in + product(attn_low, full_out)
    ffn_normed = layer_norm(middle, full_ffn_gain.astype(jnp.float32)).astype(jnp.bfloat16)
    up_rows = product(ffn_normed, full_up)
    hidden = jax.nn.gelu(up_rows, approximate=False).astype(jnp.bfloat16)
    new_latents = (middle + product(hidden, full_down)).astype(jnp.bfloat16)
    (
        back_query,
        back_key,
        back_value,
        back_out,
        back_up,
        back_down,
        back_media_gain,
        back_latent_gain,
        back_ffn_gain,
    ) = (
        lax.all_gather(w_query, ("gx", "gy"), axis=0, tiled=True),
        lax.all_gather(w_key, ("gx", "gy"), axis=0, tiled=True),
        lax.all_gather(w_value, ("gx", "gy"), axis=0, tiled=True),
        lax.all_gather(w_out, ("gx", "gy"), axis=0, tiled=True),
        lax.all_gather(w_up, ("gx", "gy"), axis=0, tiled=True),
        lax.all_gather(w_down, ("gx", "gy"), axis=0, tiled=True),
        lax.all_gather(media_gain, ("gx", "gy"), axis=0, tiled=True),
        lax.all_gather(latent_gain, ("gx", "gy"), axis=0, tiled=True),
        lax.all_gather(ffn_gain, ("gx", "gy"), axis=0, tiled=True),
    )
    owned_latent, owned_attn, owned_ffn, owned_hidden = (
        lax.all_to_all(latent_normed, ("gx", "gy"), split_axis=1, concat_axis=0, tiled=True),
        lax.all_to_all(attn_low, ("gx", "gy"), split_axis=1, concat_axis=0, tiled=True),
        lax.all_to_all(ffn_normed, ("gx", "gy"), split_axis=1, concat_axis=0, tiled=True),
        lax.all_to_all(hidden, ("gx", "gy"), split_axis=1, concat_axis=0, tiled=True),
    )
    hidden_grad = inner_last(cotangent, back_down)
    gelu_pull = jax.vjp(partial(jax.nn.gelu, approximate=False), up_rows)[1]
    up_grad = gelu_pull(hidden_grad)[0].astype(jnp.bfloat16)
    ffn_normed_grad = inner_last(up_grad, back_up)
    ffn_pull = jax.vjp(layer_norm, middle, back_ffn_gain.astype(jnp.float32))[1]
    middle_part, grad_ffn_gain = ffn_pull(ffn_normed_grad)
    middle_grad = cotangent.astype(jnp.float32) + middle_part
    middle_low = middle_grad.astype(jnp.bfloat16)
    attn_grad = inner_last(middle_low, back_out).reshape(latent_rows, H, head_size)
    weighted_sum_gradient = (attn_grad / totals[..., None]).astype(jnp.bfloat16)
    slope_term = -coefficient / totals
    shift_term = (
        -jnp.sum(attn_grad * attention, axis=-1) / totals
        + coefficient * (1.0 / totals + moment / (totals * totals))
        + slope_term
    )
    latent_mix = jnp.einsum(
        "uer,zer->uez", weighted_sum_gradient, latent_value_rows, preferred_element_type=jnp.float32
    )
    latent_sgrad = latent_expo * (
        latent_mix + shift_term[..., None] + slope_term[..., None] * latent_score
    )
    latent_residual_gradient = (latent_sgrad * score_scale).astype(jnp.bfloat16)
    query_part = jnp.einsum(
        "nwr,rwb->nwb",
        latent_residual_gradient,
        latent_key_rows,
        preferred_element_type=jnp.float32,
    )
    own_key_grad = (
        jnp.einsum(
            "zry,zrj->yrj",
            latent_residual_gradient,
            query_head_count,
            preferred_element_type=jnp.float32,
        )
        .astype(jnp.bfloat16)
        .reshape(latent_rows, model_width)
    )
    own_value_grad = (
        jnp.einsum(
            "zry,zrj->yrj",
            latent_reduced_precision,
            weighted_sum_gradient,
            preferred_element_type=jnp.float32,
        )
        .astype(jnp.bfloat16)
        .reshape(latent_rows, model_width)
    )
    grad_table = lax.all_gather(
        weighted_sum_gradient.reshape(latent_rows, model_width), "gx", axis=0, tiled=True
    )
    shift_table, slope_table = (
        lax.all_gather(shift_term, "gx", axis=0, tiled=True),
        lax.all_gather(slope_term, "gx", axis=0, tiled=True),
    )
    picked_grad = grad_table.reshape(-1, latent_rows, H, head_size)[item_index]
    picked_shift = shift_table.reshape(-1, latent_rows, H)[item_index]
    picked_slope = slope_table.reshape(-1, latent_rows, H)[item_index]
    media_mix = jnp.einsum(
        "flhd,fphd->flhp", picked_grad, value_heads, preferred_element_type=jnp.float32
    )
    media_sgrad = media_expo * (
        media_mix + picked_shift[..., None] + picked_slope[..., None] * media_score
    )
    media_rgrad = (media_sgrad * score_scale).astype(jnp.bfloat16)
    query_terms = jnp.einsum(
        "flhp,fphd->flhd", media_rgrad, key_heads, preferred_element_type=jnp.float32
    )
    dense_query = collect(item_onehot, query_terms.reshape(frames, -1)).reshape(-1, model_width)
    got_query = lax.psum_scatter(
        dense_query.astype(jnp.bfloat16), "gx", scatter_dimension=0, tiled=True
    ).astype(jnp.float32)
    media_key_grad = (
        jnp.einsum("flhp,flhd->fphd", media_rgrad, picked, preferred_element_type=jnp.float32)
        .astype(jnp.bfloat16)
        .reshape(-1, model_width)
    )
    media_value_grad = (
        jnp.einsum("flhp,flhd->fphd", expo_low, picked_grad, preferred_element_type=jnp.float32)
        .astype(jnp.bfloat16)
        .reshape(-1, model_width)
    )
    grad_key = inner_first(media_normed, media_key_grad) + inner_first(latent_normed, own_key_grad)
    grad_value = inner_first(media_normed, media_value_grad) + inner_first(
        latent_normed, own_value_grad
    )
    media_normed_grad = inner_last(media_key_grad, back_key) + inner_last(
        media_value_grad, back_value
    )
    media_pull = jax.vjp(layer_norm, media_in, back_media_gain.astype(jnp.float32))[1]
    media_grad, grad_media_gain = media_pull(media_normed_grad)
    frame_sums = jnp.sum(media_grad.reshape(frames, patches, model_width), axis=1)
    grad_time = collect(time_onehot, frame_sums)
    query_grad = (
        (got_query.reshape(latent_rows, H, head_size) + query_part)
        .astype(jnp.bfloat16)
        .reshape(latent_rows, model_width)
    )
    latent_normed_grad = (
        inner_last(query_grad, back_query)
        + inner_last(own_key_grad, back_key)
        + inner_last(own_value_grad, back_value)
    )
    latent_pull = jax.vjp(layer_norm, latent_in, back_latent_gain.astype(jnp.float32))[1]
    latent_part, grad_latent_gain = latent_pull(latent_normed_grad)
    latents_grad = middle_grad + latent_part
    piece_query = lax.all_gather(query_grad, ("gx", "gy"), axis=0, tiled=True)
    piece_middle = lax.all_gather(middle_low, ("gx", "gy"), axis=0, tiled=True)
    piece_up = lax.all_gather(up_grad, ("gx", "gy"), axis=0, tiled=True)
    piece_cot = lax.all_gather(cotangent, ("gx", "gy"), axis=0, tiled=True)
    shard_query = inner_first(owned_latent, piece_query)
    shard_out = inner_first(owned_attn, piece_middle)
    shard_up = inner_first(owned_ffn, piece_up)
    shard_down = inner_first(owned_hidden, piece_cot)
    shard_grads = (
        lax.psum_scatter(grad_key, ("gx", "gy"), scatter_dimension=0, tiled=True),
        lax.psum_scatter(grad_value, ("gx", "gy"), scatter_dimension=0, tiled=True),
        lax.psum_scatter(grad_media_gain, ("gx", "gy"), scatter_dimension=0, tiled=True),
        lax.psum_scatter(grad_latent_gain, ("gx", "gy"), scatter_dimension=0, tiled=True),
        lax.psum_scatter(grad_ffn_gain, ("gx", "gy"), scatter_dimension=0, tiled=True),
        lax.psum_scatter(grad_time, ("gx", "gy"), scatter_dimension=1, tiled=True),
    )
    return (
        new_latents,
        media_grad,
        latents_grad,
        shard_grads[5],
        shard_grads[2],
        shard_grads[3],
        shard_grads[4],
        shard_query,
        shard_grads[0],
        shard_grads[1],
        shard_out,
        shard_up,
        shard_down,
    )


GROUP = 4


def mates_of(z, chip, core):
    mates = []
    for j in range(1, 16):
        there = (4 * z + chip + j) % 16
        mates.append((there // 4, 2 * (there % 4) + core))
    return mates


class GiveBack:
    def __init__(self, wires, up_part, down_part, scratch, up_out, down_out):
        self.wires, self.up_part, self.down_part = wires, up_part, down_part
        self.up_out, self.down_out = up_out, down_out
        self.up_near, self.down_near, self.up_got = scratch
        self.z, self.g, self.chip, self.core = here()
        self.places = up_places(self.z, self.chip)

    def first(self):
        near = (self.z, sibling(self.g))
        theirs = 1 - self.core
        self.up = self.wires.send(self.up_part.at[:, :, theirs], self.up_near, near)
        self.down = self.wires.send(self.down_part.at[theirs], self.down_near, near)

    def columns(self):
        self.up.wait_recv()
        core = self.core

        @pl.loop(0, LINES)
        def _(n):
            for q in range(PLANE):
                self.up_part[n, q, core] = self.up_part[n, q, core] + self.up_near[n, q]

        self.moved = []
        for there, _ in self.places:
            self.moved.append(
                self.wires.send(
                    self.up_part.at[there[0], there[1], core],
                    self.up_got.at[self.z, self.chip],
                    (there[0], 2 * there[1] + core),
                )
            )
        self.up_got[self.z, self.chip] = self.up_part[self.z, self.chip, core]

    def rows(self):
        self.down.wait_recv()
        rows = self.down_out.shape[0] // 8
        core = self.core

        @pl.loop(0, 8)
        def _(n):
            block = pl.ds(pl.multiple_of(n * rows, 8), rows)
            self.down_out[block] = self.down_part[core, block] + self.down_near[block]

    def finish(self):
        for copy in self.moved:
            copy.wait_recv()
        width = self.up_got.shape[-1]
        for n in range(LINES):
            for q in range(PLANE):
                first = (n * PLANE + q) * width
                self.up_out[:, first : first + width] = self.up_got[n, q].astype(F32)


GIVE_SEMS = 17


class Total:
    def __init__(self, wires, mine, out, sums, got):
        self.wires, self.out, self.sums, self.got = wires, out, sums, got
        self.z, self.g, _, _ = here()
        self.source = mine
        self.step = 0

    def push(self):
        sides = [sibling(self.g), along_x(self.g), along_y(self.g)]
        if self.step < 3:
            self.copies = [
                self.wires.send(self.source, self.got.at[self.step], (self.z, sides[self.step]))
            ]
        else:
            self.copies = [
                self.wires.send(self.source, self.got.at[3 + k], device)
                for k, device in enumerate(line_of(self.z, self.g))
            ]

    def pull(self):
        for copy in self.copies:
            copy.wait_recv()
        if self.step < 3:
            self.sums[self.step] = self.source[...] + self.got[self.step]
            self.source = self.sums.at[self.step]
            self.step += 1
        else:
            self.out[...] = self.source[...] + self.got[3] + self.got[4] + self.got[5]


def head_masks(rows, width, head_size):
    lane = lax.broadcasted_iota(jnp.int32, (rows, width), 1)
    return [(lane >= h * head_size) & (lane < (h + 1) * head_size) for h in range(GROUP)]


def stacked(block, masks):
    zero = jnp.zeros_like(block)
    return jnp.concatenate([jnp.where(mask, block, zero) for mask in masks], axis=0)


def unstacked(block, masks):
    rows = block.shape[0] // GROUP
    total = jnp.where(masks[0], block[:rows], 0.0)
    for h in range(1, GROUP):
        total = jnp.where(masks[h], block[h * rows : (h + 1) * rows], total)
    return total


def dot_last(a, b):
    return lax.dot_general(a, b, (((1,), (1,)), ((), ())), preferred_element_type=F32)


def dot_first(a, b):
    return lax.dot_general(a, b, (((0,), (0,)), ((), ())), preferred_element_type=F32)


def spread_heads(columns, first, masks):
    out = jnp.where(masks[0], columns[:, first : first + 1], 0.0)
    for h in range(1, GROUP):
        out = jnp.where(masks[h], columns[:, first + h : first + h + 1], out)
    return out


def attend(queries, keys, values, valid, scale, masks):
    rows = queries.shape[0]
    score = dot_last(stacked(queries, masks), keys) * scale
    expo = jnp.exp(score)
    if valid is not None:
        expo = jnp.where(valid > 0, expo, 0.0)
    totals = jnp.sum(expo, axis=1, keepdims=True)
    moments = jnp.sum(expo * score, axis=1, keepdims=True)
    weighted = jnp.dot(expo.astype(BF16), values, preferred_element_type=F32)
    heads = [(totals[h * rows : (h + 1) * rows], moments[h * rows : (h + 1) * rows]) for h in range(GROUP)]
    return unstacked(weighted, masks), heads


def put_heads(heads, group, lane):
    out = jnp.zeros(lane.shape, F32)
    for h, (total, moment) in enumerate(heads):
        out = jnp.where(lane == group * GROUP + h, total, out)
        out = jnp.where(lane == H + group * GROUP + h, moment, out)
    return out


def multiply(left, right, out, tile):
    @pl.loop(0, right.shape[1] // tile)
    def _(n):
        cols = pl.ds(pl.multiple_of(n * tile, 128), tile)
        out[:, cols] = jnp.dot(left[...], right[:, cols], preferred_element_type=F32).astype(BF16)


def assemble(smalls, out):
    count, rows, lanes = smalls.shape
    shard = out.shape[1] // count
    block = 8
    row = lax.broadcasted_iota(jnp.int32, (block * lanes, block * shard), 0)
    col = lax.broadcasted_iota(jnp.int32, (block * lanes, block * shard), 1)
    lane = row % lanes
    chosen = ((row // lanes) * shard + lane == col) & (lane < shard)
    place = jnp.where(chosen, 1.0, 0.0).astype(BF16)
    for n in range(count // block):
        pieces = jnp.concatenate([smalls[n * block + d] for d in range(block)], axis=1)
        out[:, n * block * shard : (n + 1) * block * shard] = jnp.dot(
            pieces.astype(BF16), place, preferred_element_type=F32
        )


def up_places(z, chip):
    places = []
    for dz in range(LINES):
        for dx, dy in ((0, 0), (1, 0), (0, 1), (1, 1)):
            if dz or dx or dy:
                x, y = chip % 2, chip // 2
                there = (y + dy) % 2 * 2 + (x + dx) % 2
                places.append(((turn(z, dz), there), (turn(z, LINES - dz) if dz else z, there)))
    return places


def opening_kernel(scale, *refs):
    (
        small_ref,
        key_shard,
        value_shard,
        query_shard,
        out_shard,
        latents_ref,
        up_ref,
        down_ref,
        cot_ref,
        media_ref,
        valid_ref,
        times_ref,
        item_ref,
        tables_out,
        counts_out,
        key_weight_out,
        value_weight_out,
        query_weight_out,
        out_weight_out,
        up_out,
        down_out,
        cot_out,
        normed_out,
        keys_out,
        values_out,
        table_out,
        got_weighted,
        got_stats,
        own_weighted,
        own_stats,
        send_sems,
        recv_sems,
        local_sems,
        smalls,
        key_weight,
        value_weight,
        query_weight,
        line_latents,
        line_normed,
        normed,
        keys,
        values,
        table,
        time_rows,
        sums,
        weighted,
        stats,
    ) = refs
    z, g, chip, core = here()
    here_chip = 4 * z + chip
    me = 2 * here_chip + core
    items, rows, width = line_latents.shape
    frames, _, patches = valid_ref.shape
    shard = key_shard.shape[0]
    span = width // (H // GROUP)
    up_width = up_out.shape[-1]
    near = (z, sibling(g))
    places = up_places(z, chip)
    greet([(there[0], 2 * there[1] + core) for there, _ in places] + [near])
    wires = Wires(send_sems, recv_sems)
    masks = head_masks(rows, span, span // GROUP)
    lane = lax.broadcasted_iota(jnp.int32, (rows, 128), 1)
    local = []

    def keep(source, target):
        copy = pltpu.make_async_copy(source, target, local_sems.at[len(local)])
        copy.start()
        local.append(copy)
        return copy

    def rows_of(ref):
        return lambda zz, gg: ref.at[pl.ds(pl.multiple_of((zz * 8 + gg) * shard, 16), shard)]

    def piece(place):
        return up_ref.at[:, pl.ds(pl.multiple_of((4 * place[0] + place[1]) * up_width, 128), up_width)]

    def whole(source, slot):
        return Spread(wires, source, slot, columns_half, True), keep(source, slot(z, g))

    def small_slot(zz, gg):
        return smalls.at[zz * 8 + gg]

    small = Spread(wires, small_ref, small_slot, rows_half, True)
    small_kept = keep(small_ref, small_slot(z, g))
    key, key_kept = whole(key_shard, rows_of(key_weight))
    value, value_kept = whole(value_shard, rows_of(value_weight))
    query, query_kept = whole(query_shard, rows_of(query_weight))
    out, out_kept = whole(out_shard, rows_of(out_weight_out))
    cot = Spread(wires, cot_ref, lambda zz, gg: cot_out.at[zz * 4 + gg // 2], columns_half, False)
    line = Line(wires, latents_ref, lambda zz: line_latents.at[zz])
    exchange = Exchange(wires, [(weighted, got_weighted), (stats, got_stats)])
    line_kept = keep(latents_ref, line_latents.at[z])
    late = [
        out_kept,
        keep(cot_ref, cot_out.at[here_chip]),
        keep(piece((z, chip)), up_out.at[me]),
        keep(down_ref, down_out.at[core]),
    ]
    prompt = len(local)
    moved, given, down = [], [], []
    chunk = 32

    def normalise(first, last):
        @pl.loop(first, last)
        def _(n):
            block = pl.ds(pl.multiple_of(n * chunk, chunk), chunk)
            frame = n // (patches // chunk)
            row = media_ref[block].astype(F32) + time_rows[pl.ds(frame, 1)]
            normed[block] = layer_norm(row, tables_out[8:9]).astype(BF16)

    def normalise_latents():
        gain = tables_out[9:10]
        line_kept.wait()
        for item in range(items):

            @pl.loop(0, rows // chunk)
            def _(n):
                block = pl.ds(pl.multiple_of(n * chunk, chunk), chunk)
                row = line_latents[item, block].astype(F32)
                line_normed[item, block] = layer_norm(row, gain).astype(BF16)

        normed[frames * patches :] = line_normed[z]

    def tabulate():
        small_kept.wait()
        assemble(smalls, tables_out)
        counts = smalls[0, 8:]
        for n in range(1, smalls.shape[0]):
            counts = counts + smalls[n, 8:]
        counts_out[...] = counts
        time_rows[...] = jnp.dot(
            times_ref[...], tables_out[...].astype(BF16), preferred_element_type=F32
        )

    def project_keys():
        key_kept.wait()
        keep(key_weight, key_weight_out)
        keep(normed, normed_out)
        multiply(normed, key_weight, keys, span)
        keep(keys, keys_out)

    def project_values():
        value_kept.wait()
        keep(value_weight, value_weight_out)
        multiply(normed, value_weight, values, span)
        keep(values, values_out)

    def project_queries():
        query_kept.wait()
        keep(query_weight, query_weight_out)

        @pl.loop(0, width // span)
        def _(n):
            cols = pl.ds(pl.multiple_of(n * span, 128), span)
            for item in range(items):
                table[item, :, cols] = jnp.dot(
                    line_normed[item], query_weight[:, cols], preferred_element_type=F32
                ).astype(BF16)

        keep(table, table_out)

    def attend_own():
        sums[...] = jnp.zeros_like(sums)
        stats[...] = jnp.zeros_like(stats)
        last = slice(frames * patches, frames * patches + rows)
        own = jnp.zeros((rows, 128), F32)
        for group in range(H // GROUP):
            cols = slice(group * span, (group + 1) * span)
            part, heads = attend(
                table[z, :, cols], keys[last, cols], values[last, cols], None, scale, masks
            )
            own_weighted[:, cols] = part
            own = own + put_heads(heads, group, lane)
        own_stats[...] = own

    def attend_frames(first, last):
        @pl.loop(first, last)
        def _(frame):
            block = pl.ds(pl.multiple_of(frame * patches, patches), patches)
            valid = valid_ref[frame]
            found = jnp.zeros((rows, 128), F32)
            for group in range(H // GROUP):
                cols = slice(group * span, (group + 1) * span)
                chosen = item_ref[frame, 0] * table[0, :, cols].astype(F32)
                for item in range(1, items):
                    chosen = chosen + item_ref[frame, item] * table[item, :, cols].astype(F32)
                part, heads = attend(
                    chosen.astype(BF16), keys[block, cols], values[block, cols], valid, scale, masks
                )
                found = found + put_heads(heads, group, lane)
                for item in range(items):
                    sums[item, :, cols] += item_ref[frame, item] * part
            for item in range(items):
                stats[item] += item_ref[frame, item] * found

    def down_first():
        down.append(wires.send(down_ref, down_out.at[core], near))

    def up_first():
        given.append(wires.send(piece((z, chip)), up_out.at[me], near))
        for there, _ in places:
            moved.append(
                wires.send(piece(there), up_out.at[me], (there[0], 2 * there[1] + core))
            )

    def up_last():
        for n, (_, origin) in enumerate(places):
            moved[n].wait_recv()
            held = up_out.at[2 * (4 * origin[0] + origin[1]) + core]
            given.append(wires.send(held, held, near))
        for copy in given:
            copy.wait_recv()

    def sums_first():
        weighted[...] = sums[...].astype(BF16)
        exchange.first()

    key.first()
    small.first()
    query.first()
    key.column(0)
    small.corner_y(0)
    small.column(0)
    key.column(1)
    down_first()
    query.corner_x(0)
    value.first()
    query.column(0)
    query.column(1)
    key.corner_y(1)
    key.corner_x(1)
    value.column(0)
    key.column(2)
    small.corner_x(1)
    small.corner_y(1)
    value.corner_y(0)
    query.corner_y(2)
    line.first()
    small.corner_x(0)
    query.corner_y(0)
    value.corner_y(1)
    key.corner_y(0)
    query.corner_x(1)
    small.column(1)
    query.corner_y(1)
    small.column(2)
    key.corner_x(2)
    key.corner_x(0)
    cot.first()
    value.column(1)
    value.corner_x(0)
    key.corner_x(3)
    value.column(2)
    small.last(0)
    key.last(1)
    key.corner_y(3)
    small.corner_y(2)
    value.corner_x(1)
    query.last(0)
    query.corner_x(2)
    small.corner_x(2)
    key.last(0)
    small.corner_x(3)
    out.first()
    small.corner_y(3)
    query.last(1)
    value.corner_y(3)
    small.last(1)
    value.corner_x(2)
    small.last(2)
    key.corner_y(2)
    query.column(2)
    small.last(3)
    value.last(0)
    query.last(2)
    key.last(3)
    small.finish()
    line.take(0)
    down[0].wait_recv()
    value.last(1)
    tabulate()
    out.column(0)
    query.corner_x(3)
    query.corner_y(3)
    value.corner_x(3)
    value.corner_y(2)
    line.take(1)
    normalise(0, 8)
    cot.column(0)
    cot.corner_y(0)
    line.take(2)
    up_first()
    out.column(1)
    query.last(3)
    cot.column(1)
    out.corner_y(0)
    normalise_latents()
    query.finish()
    value.last(3)
    project_queries()
    value.last(2)
    key.last(2)
    cot.corner_x(0)
    normalise(8, 16)
    out.column(2)
    value.finish()
    cot.corner_y(1)
    project_values()
    key.finish()
    project_keys()
    cot.corner_x(1)
    attend_own()
    attend_frames(0, frames // 2)
    cot.corner_y(2)
    attend_frames(frames // 2, frames)
    sums_first()
    out.corner_y(2)
    out.corner_x(2)
    cot.corner_x(2)
    cot.column(2)
    exchange.finish()
    out.corner_y(3)
    out.corner_x(1)
    cot.corner_x(3)
    cot.last(2)
    cot.corner_y(3)
    cot.last(0)
    out.corner_y(1)
    cot.last(1)
    out.corner_x(3)
    out.last(1)
    cot.last(3)
    out.corner_x(0)
    out.last(2)
    out.last(0)
    up_last()
    out.last(3)
    out.finish()
    for copy in late + local[prompt:]:
        copy.wait()
    wires.drain()


def opening(scale, small, weights, latents, w_up, w_down, cotangent, media, valid, times, items):
    rows, width = latents.shape
    shard = weights[0].shape[0]
    up_rows, up_width = w_up.shape
    all_rows = media.shape[0] + rows
    wires = 5 * spread_sems(True) + spread_sems(False) + LINE_SEMS + 31 + 1 + 6
    square = jax.ShapeDtypeStruct((width, width), BF16)
    table = jax.ShapeDtypeStruct((LINES, rows, width), BF16)
    keys = jax.ShapeDtypeStruct((all_rows, width), BF16)
    return pl.pallas_call(
        partial(opening_kernel, scale),
        out_shape=[
            jax.ShapeDtypeStruct((16, width), F32),
            jax.ShapeDtypeStruct((8, 128), F32),
            square,
            square,
            square,
            square,
            jax.ShapeDtypeStruct((32, up_rows, up_width // 16), BF16),
            jax.ShapeDtypeStruct((2,) + w_down.shape, BF16),
            jax.ShapeDtypeStruct((16,) + cotangent.shape, BF16),
            keys,
            keys,
            keys,
            table,
            table,
            jax.ShapeDtypeStruct((LINES, rows, 128), F32),
            jax.ShapeDtypeStruct((rows, width), F32),
            jax.ShapeDtypeStruct((rows, 128), F32),
        ],
        in_specs=[LEFT] * 9 + [VMEM] * 3 + [pl.BlockSpec(memory_space=pltpu.SMEM)],
        out_specs=[VMEM] * 2 + [LEFT] * 11 + [VMEM] * 4,
        scratch_shapes=[
            sems(wires),
            sems(wires),
            sems(16),
            pltpu.VMEM((32,) + small.shape, F32),
            pltpu.VMEM((width, width), BF16),
            pltpu.VMEM((width, width), BF16),
            pltpu.VMEM((width, width), BF16),
            pltpu.VMEM((LINES, rows, width), BF16),
            pltpu.VMEM((LINES, rows, width), BF16),
            pltpu.VMEM((all_rows, width), BF16),
            pltpu.VMEM((all_rows, width), BF16),
            pltpu.VMEM((all_rows, width), BF16),
            pltpu.VMEM((LINES, rows, width), BF16),
            pltpu.VMEM((8, width), F32),
            pltpu.VMEM((LINES, rows, width), F32),
            pltpu.VMEM((LINES, rows, width), BF16),
            pltpu.VMEM((LINES, rows, 128), F32),
        ],
        compiler_params=params(0),
        name="opening",
    )(small, *weights, latents, w_up, w_down, cotangent, media, valid, times, items)


def repel(queries, grads, keys, values, valid, shift, slope, scale, masks):
    query_stack = stacked(queries, masks)
    grad_stack = stacked(grads, masks)
    score = dot_last(query_stack, keys) * scale
    expo = jnp.exp(score)
    if valid is not None:
        expo = jnp.where(valid > 0, expo, 0.0)
    mix = dot_last(grad_stack, values)
    raw = (expo * (mix + shift + slope * score) * scale).astype(BF16)
    query_grad = unstacked(jnp.dot(raw, keys, preferred_element_type=F32), masks)
    key_grad = dot_first(raw, query_stack).astype(BF16)
    value_grad = dot_first(expo.astype(BF16), grad_stack).astype(BF16)
    return query_grad, key_grad, value_grad


def stacked_columns(terms, first):
    return jnp.concatenate([terms[:, first + h : first + h + 1] for h in range(GROUP)], axis=0)


def closing_kernel(scale, *refs):
    (
        table_ref,
        grad_ref,
        terms_ref,
        keys_ref,
        values_ref,
        normed_ref,
        valid_ref,
        attn_ref,
        low_ref,
        own_grad_ref,
        own_terms_ref,
        key_weight_ref,
        value_weight_ref,
        query_weight_ref,
        media_ref,
        time_rows_ref,
        tables_ref,
        latents_ref,
        middle_grad_ref,
        ffn_gain_ref,
        item_ref,
        time_ref,
        media_grad_out,
        latents_grad_out,
        small_out,
        out_out,
        value_out,
        key_out,
        query_out,
        send_sems,
        recv_sems,
        local_sems,
        table,
        grads,
        keys,
        values,
        normed,
        key_grad,
        value_grad,
        weight_a,
        weight_b,
        sums,
        terms_query,
        got_query,
        query_grad,
        own_query_grad,
        media_grad,
        latent_grad,
        small,
        small_sums,
        small_got,
        part_a,
        part_b,
        part_c,
        *fold,
    ) = refs
    z, g, _, core = here()
    items, rows, width = table.shape
    frames, _, patches = valid_ref.shape
    media_rows = frames * patches
    shard = width // 32
    groups = H // GROUP
    span = width // groups
    masks = head_masks(rows, span, span // GROUP)
    greet(line_of(z, g) + sides_of(z, g, True))
    wires = Wires(send_sems, recv_sems)
    out = Fold(wires, part_a, True, fold[:FOLD], out_out)
    value = Fold(wires, part_b, True, fold[FOLD : 2 * FOLD], value_out)
    key = Fold(wires, part_c, True, fold[2 * FOLD : 3 * FOLD], key_out)
    query = Fold(wires, part_a, True, fold[3 * FOLD :], query_out)
    total = Total(wires, small, small_out, small_sums, small_got)
    exchange = Exchange(wires, [(terms_query, got_query)])
    local = []

    def load(source, target):
        copy = pltpu.make_async_copy(source, target, local_sems.at[len(local)])
        copy.start()
        local.append(copy)
        return copy

    loads = [
        load(table_ref, table),
        load(grad_ref, grads),
        load(keys_ref, keys),
        load(values_ref, values),
    ]
    normed_load = load(normed_ref, normed)
    key_load = load(key_weight_ref, weight_a)
    value_load = load(value_weight_ref, weight_b)
    stored = []

    def weight_part(part, left, right):
        @pl.loop(0, LINES)
        def _(n):
            cols = pl.ds(pl.multiple_of(n * span, 128), span)
            block = dot_first(left[:, cols], right[...]).astype(BF16)
            part[n] = block.reshape(PLANE, 2, shard, width)

    def out_part():
        weight_part(part_a, attn_ref, low_ref)
        out.start()

    def value_part():
        normed_load.wait()
        weight_part(part_b, normed, value_grad)
        value.start()

    def key_part():
        weight_part(part_c, normed, key_grad)
        key.start()

    def repel_own():
        for copy in loads:
            copy.wait()
        sums[...] = jnp.zeros_like(sums)
        own_terms = own_terms_ref[...]
        for group in range(groups):
            cols = slice(group * span, (group + 1) * span)
            (
                own_query_grad[:, cols],
                key_grad[media_rows:, cols],
                value_grad[media_rows:, cols],
            ) = repel(
                table[z, :, cols],
                own_grad_ref[:, cols],
                keys[media_rows:, cols],
                values[media_rows:, cols],
                None,
                stacked_columns(own_terms, group * GROUP),
                stacked_columns(own_terms, H + group * GROUP),
                scale,
                masks,
            )

    def repel_frames(first, last):
        @pl.loop(first, last)
        def _(frame):
            block = pl.ds(pl.multiple_of(frame * patches, patches), patches)
            valid = valid_ref[frame]
            share = [item_ref[frame, item] for item in range(items)]

            def pick(ref, cols):
                chosen = share[0] * ref[0, :, cols].astype(F32)
                for item in range(1, items):
                    chosen = chosen + share[item] * ref[item, :, cols].astype(F32)
                return chosen

            everything = slice(0, 128)
            terms = pick(terms_ref, everything)
            for group in range(groups):
                cols = slice(group * span, (group + 1) * span)
                query_part, key_grad[block, cols], value_grad[block, cols] = repel(
                    pick(table, cols).astype(BF16),
                    pick(grads, cols).astype(BF16),
                    keys[block, cols],
                    values[block, cols],
                    valid,
                    stacked_columns(terms, group * GROUP),
                    stacked_columns(terms, H + group * GROUP),
                    scale,
                    masks,
                )
                for item in range(items):
                    sums[item, :, cols] += share[item] * query_part

    def queries_first():
        terms_query[...] = sums[...].astype(BF16)
        exchange.first()

    def media_half(n):
        if n == 0:
            key_load.wait()
            value_load.wait()
            small[...] = jnp.zeros_like(small)
            small[10:11] = ffn_gain_ref[...]
        else:
            stored[-1].wait()
        count = media_rows // 2
        first = n * count
        block = slice(first, first + count)

        @pl.loop(0, groups)
        def _(t):
            cols = pl.ds(pl.multiple_of(t * span, 128), span)
            media_grad[:, cols] = dot_last(key_grad[block], weight_a[cols]) + dot_last(
                value_grad[block], weight_b[cols]
            )

        gain = tables_ref[8:9]
        chunk = 32
        per_frame = patches // chunk
        for f in range(count // patches):
            frame = n * (count // patches) + f
            moving = time_rows_ref[frame : frame + 1]

            def step(t, carry):
                gain_sum, row_sum = carry
                here_rows = pl.ds(pl.multiple_of(f * patches + t * chunk, chunk), chunk)
                there_rows = pl.ds(pl.multiple_of(first + f * patches + t * chunk, chunk), chunk)
                row = media_ref[there_rows].astype(F32) + moving
                pulled, summand = norm_pull(row, gain, media_grad[here_rows])
                media_grad[here_rows] = pulled
                return (
                    gain_sum + jnp.sum(summand, axis=0, keepdims=True),
                    row_sum + jnp.sum(pulled, axis=0, keepdims=True),
                )

            zero = jnp.zeros((1, width), F32)
            gain_sum, row_sum = lax.fori_loop(0, per_frame, step, (zero, zero))
            small[8:9] += gain_sum
            for t in range(8):
                small[t : t + 1] += time_ref[frame, t] * row_sum
        stored.append(load(media_grad, media_grad_out.at[pl.ds(first, count)]))

    def latents_side():
        @pl.loop(0, groups)
        def _(t):
            cols = pl.ds(pl.multiple_of(t * span, 128), span)
            latent_grad[:, cols] = dot_last(key_grad[media_rows:], weight_a[cols]) + dot_last(
                value_grad[media_rows:], weight_b[cols]
            )

        stored.append(load(query_weight_ref, weight_a))

    def query_part():
        found = own_query_grad[...]
        for item in range(items):
            found = found + got_query[item].astype(F32)
        query_grad[...] = found.astype(BF16)
        out.release()
        weight_part(part_a, normed.at[media_rows:], query_grad)
        query.start()

    def latents_end():
        stored[-1].wait()

        @pl.loop(0, groups)
        def _(t):
            cols = pl.ds(pl.multiple_of(t * span, 128), span)
            latent_grad[:, cols] += dot_last(query_grad[...], weight_a[cols])

        pulled, summand = norm_pull(
            latents_ref[...].astype(F32), tables_ref[9:10], latent_grad[...]
        )
        latents_grad_out[...] = middle_grad_ref[...] + pulled
        small[9:10] = jnp.sum(summand, axis=0, keepdims=True)
        total.push()

    def total_next():
        total.pull()
        total.push()

    out_part()
    repel_own()
    repel_frames(0, frames // 2)
    out.corner()
    repel_frames(frames // 2, frames)
    queries_first()
    out.side_x()
    out.side_y()
    value_part()
    key_part()
    value.corner()
    media_half(0)
    key.corner()
    value.side_x()
    value.side_y()
    out.line()
    media_half(1)
    key.side_x()
    exchange.finish()
    key.side_y()
    latents_side()
    query_part()
    value.line()
    latents_end()
    total_next()
    query.corner()
    key.line()
    total_next()
    query.side_x()
    value.finish()
    query.side_y()
    total_next()
    out.finish()
    query.line()
    key.finish()
    total.pull()
    query.finish()
    stored[1].wait()
    wires.drain()


def closing(scale, *args):
    (table, grads, terms, keys, values, normed) = args[:6]
    media, latents = args[14], args[17]
    rows, width = latents.shape
    shard = width // 32
    wires = 4 * fold_sems(True) + 6 + 3
    bf = [
        table.shape,
        table.shape,
        keys.shape,
        keys.shape,
        keys.shape,
        keys.shape,
        keys.shape,
        (width, width),
        (width, width),
    ]
    part = pltpu.VMEM((LINES, PLANE, 2, shard, width), BF16)
    small = (16, width)
    scratch = [pltpu.VMEM(shape, BF16) for shape in bf] + [
        pltpu.VMEM(table.shape, F32),
        pltpu.VMEM(table.shape, BF16),
        pltpu.VMEM(table.shape, BF16),
        pltpu.VMEM((rows, width), BF16),
        pltpu.VMEM((rows, width), F32),
        pltpu.VMEM((media.shape[0] // 2, width), F32),
        pltpu.VMEM((rows, width), F32),
        pltpu.VMEM(small, F32),
        pltpu.VMEM((3,) + small, F32),
        pltpu.VMEM((6,) + small, F32),
        part,
        part,
        part,
    ]
    for _ in range(4):
        scratch += fold_scratch(shard, width, True)
    smem = pl.BlockSpec(memory_space=pltpu.SMEM)
    return pl.pallas_call(
        partial(closing_kernel, scale),
        out_shape=[
            jax.ShapeDtypeStruct(media.shape, F32),
            jax.ShapeDtypeStruct(latents.shape, F32),
            jax.ShapeDtypeStruct(small, F32),
        ]
        + [jax.ShapeDtypeStruct((shard, width), F32)] * 4,
        in_specs=[LEFT, LEFT, VMEM, LEFT, LEFT, LEFT]
        + [VMEM] * 5
        + [LEFT] * 3
        + [VMEM] * 6
        + [smem] * 2,
        out_specs=[LEFT] + [VMEM] * 6,
        scratch_shapes=[sems(wires), sems(wires), sems(12)] + scratch,
        compiler_params=pltpu.CompilerParams(
            collective_id=3, has_side_effects=True, vmem_limit_bytes=67043328
        ),
        name="closing",
    )(*args)


def settle_kernel(
    weighted_ref,
    stats_ref,
    own_weighted_ref,
    own_stats_ref,
    out_ref,
    latents_ref,
    gain_ref,
    attention_ref,
    attn_ref,
    sums_ref,
    middle_ref,
    normed_ref,
    ready,
):
    rows, width = latents_ref.shape
    span = width // (H // GROUP)
    masks = head_masks(rows, span, span // GROUP)
    stats = own_stats_ref[...]
    for n in range(stats_ref.shape[0]):
        stats = stats + stats_ref[n]
    sums_ref[...] = stats
    for group in range(H // GROUP):
        cols = pl.ds(group * span, span)
        weighted = own_weighted_ref[:, cols]
        for n in range(weighted_ref.shape[0]):
            weighted = weighted + weighted_ref[n, :, cols].astype(F32)
        attention = weighted / spread_heads(stats, group * GROUP, masks)
        attention_ref[:, cols] = attention
        attn_ref[:, cols] = attention.astype(BF16)
    ready()
    middle = latents_ref[...].astype(F32) + jnp.dot(
        attn_ref[...], out_ref[...], preferred_element_type=F32
    )
    middle_ref[...] = middle
    normed_ref[...] = layer_norm(middle, gain_ref[...]).astype(BF16)


def norm_pull(rows, gain, grad):
    mean = jnp.mean(rows, axis=-1, keepdims=True)
    centred = rows - mean
    inverse = lax.rsqrt(jnp.mean(centred * centred, axis=-1, keepdims=True) + NORM_STABILIZER)
    xhat = centred * inverse
    t = grad * gain
    pulled = (
        t
        - jnp.mean(t, axis=-1, keepdims=True)
        - xhat * jnp.mean(t * xhat, axis=-1, keepdims=True)
    ) * inverse
    return pulled, grad * xhat


def unsettle_kernel(
    normed_grad_ref,
    middle_ref,
    gain_ref,
    cot_ref,
    out_ref,
    attention_ref,
    stats_ref,
    coef_ref,
    middle_grad_ref,
    low_ref,
    gain_grad_ref,
    weighted_grad_ref,
    terms_ref,
    attn_grad,
):
    rows, width = middle_ref.shape
    span = width // (H // GROUP)
    masks = head_masks(rows, span, span // GROUP)
    pulled, summand = norm_pull(middle_ref[...], gain_ref[...], normed_grad_ref[...])
    gain_grad_ref[...] = jnp.sum(summand, axis=0, keepdims=True)
    middle_grad = cot_ref[...].astype(F32) + pulled
    middle_grad_ref[...] = middle_grad
    low_ref[...] = middle_grad.astype(BF16)
    attn_grad[...] = dot_last(low_ref[...], out_ref[...])
    stats = stats_ref[...]
    coef = coef_ref[0, 0]
    lane = lax.broadcasted_iota(jnp.int32, (rows, 128), 1)
    terms = jnp.zeros((rows, 128), F32)
    for group in range(H // GROUP):
        cols = pl.ds(group * span, span)
        grad = attn_grad[:, cols]
        first = group * GROUP
        weighted_grad_ref[:, cols] = (grad / spread_heads(stats, first, masks)).astype(BF16)
        along = grad * attention_ref[:, cols]
        for h in range(GROUP):
            inner = jnp.sum(jnp.where(masks[h], along, 0.0), axis=1, keepdims=True)
            total = stats[:, first + h : first + h + 1]
            moment = stats[:, H + first + h : H + first + h + 1]
            slope = -coef / total
            shift = -inner / total + coef * (1.0 / total + moment / (total * total)) + slope
            terms = jnp.where(lane == first + h, shift, terms)
            terms = jnp.where(lane == H + first + h, slope, terms)
    terms_ref[...] = terms


def gelu_parts(rows):
    below = 0.5 * (1.0 + lax.erf(rows * (0.5**0.5)))
    density = jnp.exp(-0.5 * rows * rows) * ((0.5 / jnp.pi) ** 0.5)
    return rows * below, below + rows * density


def middle_kernel(*refs):
    (
        weighted_ref,
        stats_ref,
        own_weighted_ref,
        own_stats_ref,
        out_weight_ref,
        up_ref,
        down_ref,
        cot_rows_ref,
        latents_ref,
        gain_ref,
        cot_ref,
        coef_ref,
        attn_out,
        low_out,
        middle_grad_out,
        gain_grad_out,
        weighted_grad_out,
        terms_out,
        grad_table_out,
        terms_table_out,
        new_latents_out,
        up_grad_out,
        down_grad_out,
        send_sems,
        recv_sems,
        local_sems,
        out_weight,
        up_cols,
        down_rows,
        cot_rows,
        ffn_rows,
        attention,
        sums,
        middle,
        normed,
        hidden_grad,
        up_grad,
        hidden,
        normed_part,
        down_part,
        up_grad_part,
        down_grad_part,
        up_near,
        down_near,
        up_got,
        normed_grad,
        down_sum,
        attn_grad,
        *fold,
    ) = refs
    z, g, chip, core = here()
    rows, width = latents_ref.shape
    span = up_cols.shape[1]
    shard = width // 32
    block_rows = PLANE * rows
    near = (z, sibling(g))
    greet([(there[0], 2 * there[1] + core) for there, _ in up_places(z, chip)] + [near])
    wires = Wires(send_sems, recv_sems)
    gather = Spread(
        wires, normed, lambda zz, gg: ffn_rows.at[zz, gg // 2], columns_half, False
    )
    back = FoldSteps(wires, normed_part, fold[:FOLD], normed_grad)
    down = Fold(wires, down_part, False, fold[FOLD:], down_sum)
    give = GiveBack(
        wires,
        up_grad_part,
        down_grad_part,
        (up_near, down_near, up_got),
        up_grad_out,
        down_grad_out,
    )
    grad_line = Line(wires, weighted_grad_out, lambda zz: grad_table_out.at[zz])
    terms_line = Line(wires, terms_out, lambda zz: terms_table_out.at[zz])
    loads = [
        pltpu.make_async_copy(source, target, local_sems.at[n])
        for n, (source, target) in enumerate(
            (
                (out_weight_ref, out_weight),
                (down_ref, down_rows),
                (cot_rows_ref, cot_rows),
                (up_ref, up_cols),
            )
        )
    ]
    for load in loads:
        load.start()

    def settle():
        settle_kernel(
            weighted_ref,
            stats_ref,
            own_weighted_ref,
            own_stats_ref,
            out_weight,
            latents_ref,
            gain_ref,
            attention,
            attn_out,
            sums,
            middle,
            normed,
            loads[0].wait,
        )
        ffn_rows[z, chip] = normed[...]

    def hidden_back():
        loads[1].wait()
        loads[2].wait()
        loads[3].wait()

        @pl.loop(0, LINES)
        def _(n):
            block = cot_rows[n].reshape(block_rows, width)
            hidden_grad[n] = dot_last(block, down_rows[...])

    def group(n):
        place = gather.zs[n]
        block = ffn_rows[place].reshape(block_rows, width)
        value, slope = gelu_parts(jnp.dot(block, up_cols[...], preferred_element_type=F32))
        hidden[place] = value.astype(BF16)
        grad = (hidden_grad[place] * slope).astype(BF16)
        up_grad[place] = grad
        part = dot_last(grad, up_cols[...]).astype(BF16)
        normed_part[place] = part.reshape(PLANE, rows, width)

    def down_product():
        @pl.loop(0, LINES)
        def _(n):
            part = jnp.dot(hidden[n], down_rows[...], preferred_element_type=F32)
            down_part[n] = part.astype(BF16).reshape(PLANE, rows, width)

    def up_gradient():
        grads = up_grad[...].reshape(LINES * block_rows, span)

        @pl.loop(0, LINES)
        def _(n):
            cols = pl.ds(pl.multiple_of(n * span, 128), span)
            block = ffn_rows[:, :, :, cols].reshape(LINES * block_rows, span)
            part = dot_first(block, grads).astype(BF16)
            up_grad_part[n] = part.reshape(PLANE, 2, shard, span)

    def down_gradient():
        rows_up = hidden[...].reshape(LINES * block_rows, span)

        @pl.loop(0, width // span)
        def _(n):
            cols = pl.ds(pl.multiple_of(n * span, 128), span)
            block = cot_rows[:, :, :, cols].reshape(LINES * block_rows, span)
            part = dot_first(rows_up, block)
            down_grad_part[:, :, cols] = part.reshape(2, span // 2, span)

    def unsettle():
        unsettle_kernel(
            normed_grad,
            middle,
            gain_ref,
            cot_ref,
            out_weight,
            attention,
            sums,
            coef_ref,
            middle_grad_out,
            low_out,
            gain_grad_out,
            weighted_grad_out,
            terms_out,
            attn_grad,
        )
        grad_table_out[z] = weighted_grad_out[...]
        terms_table_out[z] = terms_out[...]

    def new_rows():
        new_latents_out[...] = (middle[...] + down_sum[...]).astype(BF16)

    settle()
    gather.first()
    gather.column(0)
    gather.column(1)
    gather.corner_y(1)
    gather.corner_y(0)
    gather.corner_x(1)
    hidden_back()
    gather.corner_x(0)
    gather.corner_x(2)
    gather.corner_y(2)
    gather.column(2)
    gather.last(1)
    gather.last(0)
    group(0)
    back.corner(0)
    gather.last(2)
    group(1)
    gather.corner_x(3)
    gather.corner_y(3)
    group(2)
    back.corner(2)
    back.corner(1)
    gather.last(3)
    back.side_y(2)
    back.side_x(2)
    group(3)
    back.corner(3)
    back.side_y(1)
    back.side_x(1)
    down_gradient()
    back.line(2)
    back.side_x(3)
    back.side_x(0)
    back.side_y(3)
    back.side_y(0)
    back.line(1)
    down_product()
    down.start()
    back.line(3)
    down.corner()
    up_gradient()
    give.first()
    give.columns()
    back.line(0)
    back.finish()
    down.side_x()
    down.side_y()
    unsettle()
    terms_line.first()
    grad_line.first()
    terms_line.take(0)
    grad_line.take(0)
    down.line()
    give.rows()
    give.finish()
    terms_line.take(1)
    grad_line.take(1)
    grad_line.take(2)
    terms_line.take(2)
    down.finish()
    new_rows()
    wires.drain()


def middle_part(
    weighted, stats, own_weighted, own_stats, w_out, up_cols, down_rows, cot_rows, latents, gain, cot, coef
):
    rows, width = latents.shape
    span = up_cols.shape[1]
    shard = width // 32
    plane = (LINES, PLANE, rows, width)
    block = (LINES, PLANE * rows, span)
    wires = spread_sems(False) + STEP_SEMS + fold_sems(False) + GIVE_SEMS + 2 * LINE_SEMS
    own = (rows, width)
    terms = own_stats.shape
    bf = [
        w_out.shape,
        up_cols.shape,
        down_rows.shape,
        plane,
        plane,
    ]
    scratch = [pltpu.VMEM(shape, BF16) for shape in bf] + [
        pltpu.VMEM(own, F32),
        pltpu.VMEM(terms, F32),
        pltpu.VMEM(own, F32),
        pltpu.VMEM(own, BF16),
        pltpu.VMEM(block, F32),
        pltpu.VMEM(block, BF16),
        pltpu.VMEM(block, BF16),
        pltpu.VMEM(plane, BF16),
        pltpu.VMEM(plane, BF16),
        pltpu.VMEM((LINES, PLANE, 2, shard, span), BF16),
        pltpu.VMEM((2, span // 2, width), F32),
        pltpu.VMEM((LINES, PLANE, shard, span), BF16),
        pltpu.VMEM((span // 2, width), F32),
        pltpu.VMEM((LINES, PLANE, shard, span), BF16),
        pltpu.VMEM(own, F32),
        pltpu.VMEM(own, F32),
        pltpu.VMEM(own, F32),
    ]
    scratch += fold_scratch(rows, width, False) * 2
    return pl.pallas_call(
        middle_kernel,
        out_shape=[
            jax.ShapeDtypeStruct(own, BF16),
            jax.ShapeDtypeStruct(own, BF16),
            jax.ShapeDtypeStruct(own, F32),
            jax.ShapeDtypeStruct((1, width), F32),
            jax.ShapeDtypeStruct(own, BF16),
            jax.ShapeDtypeStruct(terms, F32),
            jax.ShapeDtypeStruct((LINES,) + own, BF16),
            jax.ShapeDtypeStruct((LINES,) + terms, F32),
            jax.ShapeDtypeStruct(own, BF16),
            jax.ShapeDtypeStruct((shard, span * 16), F32),
            jax.ShapeDtypeStruct((span // 2, width), F32),
        ],
        in_specs=[VMEM] * 4 + [LEFT] * 4 + [VMEM] * 3 + [pl.BlockSpec(memory_space=pltpu.SMEM)],
        out_specs=[VMEM] * 11,
        scratch_shapes=[sems(wires), sems(wires), sems(4)] + scratch,
        compiler_params=params(1),
        name="middle",
    )(
        weighted,
        stats,
        own_weighted,
        own_stats,
        w_out,
        up_cols,
        down_rows,
        cot_rows.reshape(plane),
        latents,
        gain,
        cot,
        coef,
    )


def per_device(
    media,
    latents,
    frame_counts,
    time_index,
    valid,
    time_table,
    media_gain,
    latent_gain,
    ffn_gain,
    w_query,
    w_key,
    w_value,
    w_out,
    w_up,
    w_down,
    cotangent,
):
    frames = time_index.shape[0]
    patches = valid.shape[0] // frames
    latent_rows, width = latents.shape
    shard = media_gain.shape[0]
    scale = (width // H) ** (-0.5)
    column = lax.axis_index("gx")
    row_index = lax.axis_index("gy")
    frame_ends = jnp.cumsum(frame_counts[row_index])
    position = column * frames + jnp.arange(frames, dtype=jnp.int32)
    item_index = jnp.sum((frame_ends[None, :] <= position[:, None]).astype(jnp.int32), axis=1)
    item_index = jnp.clip(item_index, 0, LINES - 1).astype(jnp.int32)

    count = jnp.sum(valid.astype(F32))
    small = jnp.concatenate(
        [
            time_table.astype(F32),
            media_gain.astype(F32)[None],
            latent_gain.astype(F32)[None],
            ffn_gain.astype(F32)[None],
            jnp.full((1, shard), count, F32),
            jnp.zeros((4, shard), F32),
        ],
        axis=0,
    )
    small = jnp.pad(small, ((0, 0), (0, 128 - shard)))
    times = (time_index[:, None] == jnp.arange(16, dtype=jnp.int32)[None, :]).astype(BF16)
    times = jnp.pad(times, ((0, 8 - frames), (0, 0)))
    items = (item_index[:, None] == jnp.arange(LINES, dtype=jnp.int32)[None, :]).astype(F32)
    valid_rows = valid.reshape(frames, 1, patches)
    (
        tables,
        counts,
        full_key,
        full_value,
        full_query,
        full_out,
        up_cols,
        down_rows,
        cot_rows,
        normed,
        keys,
        values,
        table,
        got_weighted,
        got_stats,
        own_weighted,
        own_stats,
    ) = opening(
        scale,
        small,
        (w_key, w_value, w_query, w_out),
        latents,
        w_up,
        w_down,
        cotangent,
        media,
        valid_rows,
        times,
        items,
    )
    full_time = tables[:8].astype(BF16)
    full_media_gain, full_latent_gain, full_ffn_gain = tables[8:9], tables[9:10], tables[10:11]
    valid_total = counts[3, 0]
    coefficient = ENTROPY_WEIGHT * (valid.shape[0] * lax.axis_size(AXES)) / valid_total
    up_cols = up_cols.reshape(width, -1)
    down_rows = down_rows.reshape(-1, width)
    cot_rows = cot_rows.reshape(-1, width)
    time_rows = product(times[:frames, :8], full_time)
    (
        attn_low,
        middle_low,
        middle_grad,
        grad_ffn_gain,
        weighted_grad,
        terms,
        grad_table,
        terms_table,
        new_latents,
        shard_up,
        shard_down,
    ) = middle_part(
        got_weighted,
        got_stats,
        own_weighted,
        own_stats,
        full_out,
        up_cols,
        down_rows,
        cot_rows,
        latents,
        full_ffn_gain,
        cotangent,
        coefficient.reshape(1, 1),
    )
    (
        media_grad,
        latents_grad,
        smalls_grad,
        shard_out,
        shard_value,
        shard_key,
        shard_query,
    ) = closing(
        scale,
        table,
        grad_table,
        terms_table,
        keys,
        values,
        normed,
        valid_rows,
        attn_low,
        middle_low,
        weighted_grad,
        terms,
        full_key,
        full_value,
        full_query,
        media,
        jnp.pad(time_rows, ((0, 8 - frames), (0, 0))),
        tables,
        latents,
        middle_grad,
        grad_ffn_gain,
        items,
        times[:frames, :8].astype(F32),
    )
    place = (column * 8 + row_index) * shard
    mine = lax.dynamic_slice(smalls_grad, (0, place), (16, shard))
    return (
        new_latents,
        media_grad,
        latents_grad,
        mine[:8],
        mine[8],
        mine[9],
        mine[10],
        shard_query,
        shard_key,
        shard_value,
        shard_out,
        shard_up,
        shard_down,
    )


def solution(mesh):
    in_specs = (
        P(("gx", "gy"), None),
        P(("gx", "gy"), None),
        P(),
        P(("gx", "gy")),
        P(("gx", "gy")),
        P(None, ("gx", "gy")),
        P(("gx", "gy")),
        P(("gx", "gy")),
        P(("gx", "gy")),
        P(("gx", "gy"), None),
        P(("gx", "gy"), None),
        P(("gx", "gy"), None),
        P(("gx", "gy"), None),
        P(("gx", "gy"), None),
        P(("gx", "gy"), None),
        P(("gx", "gy"), None),
    )
    out_specs = (
        P(("gx", "gy"), None),
        P(("gx", "gy"), None),
        P(("gx", "gy"), None),
        P(None, ("gx", "gy")),
        P(("gx", "gy")),
        P(("gx", "gy")),
        P(("gx", "gy")),
        P(("gx", "gy"), None),
        P(("gx", "gy"), None),
        P(("gx", "gy"), None),
        P(("gx", "gy"), None),
        P(("gx", "gy"), None),
        P(("gx", "gy"), None),
    )
    return jax.shard_map(
        per_device if dict(mesh.shape) == {"gx": 4, "gy": 8} else plain_device,
        mesh=mesh, in_specs=in_specs, out_specs=out_specs, check_vma=False
    )
```

```python
from functools import partial

import jax
import jax.numpy as jnp
from jax import lax
from jax.experimental import pallas as pl
from jax.experimental.pallas import tpu as pltpu
from jax.sharding import PartitionSpec as P

H = 16


ENTROPY_WEIGHT = 4.0
NORM_STABILIZER = 1e-05
AXES = ("gx", "gy")
LINES = 4
PLANE = 4
HBM = pl.ANY
BF16 = jnp.bfloat16
F32 = jnp.float32


def here():
    z = lax.axis_index("gx")
    g = lax.axis_index("gy")
    return z, g, g // 2, g % 2


def sibling(g):
    return g + 1 - 2 * (g % 2)


def along_x(g):
    return g + 2 - 4 * ((g // 2) % 2)


def along_y(g):
    return (g + 4) % 8


def turn(z, k):
    return (z + k) % LINES


def greet(devices):
    barrier = pltpu.get_barrier_semaphore()
    for device in devices:
        pl.semaphore_signal(
            barrier, inc=1, device_id=device, device_id_type=pl.DeviceIdType.MESH
        )
    pl.semaphore_wait(barrier, len(devices))


def line_of(z, g):
    return [(turn(z, k), g) for k in (1, 2, 3)]


class Wires:
    def __init__(self, send_sems, recv_sems):
        self.send_sems, self.recv_sems, self.used, self.sent = send_sems, recv_sems, 0, []

    def reserve(self, count):
        first = self.used
        self.used += count
        return first

    def copy(self, source, target, device, send, recv):
        return pltpu.make_async_remote_copy(
            src_ref=source,
            dst_ref=target,
            send_sem=self.send_sems.at[send],
            recv_sem=self.recv_sems.at[recv],
            device_id=device,
            device_id_type=pl.DeviceIdType.MESH,
        )

    def send(self, source, target, device):
        n = self.reserve(1)
        copy = self.copy(source, target, device, n, n)
        copy.start()
        self.sent.append((None, copy))
        return copy

    def send_if(self, condition, source, target, device, send, recv):
        copy = self.copy(source, target, device, send, recv)
        self.sent.append((condition, copy))

        @pl.when(condition)
        def _():
            copy.start()

        return copy

    def drain(self):
        for condition, copy in self.sent:
            if condition is None:
                copy.wait_send()
            else:
                pl.when(condition)(copy.wait_send)


class Line:
    def __init__(self, wires, shard, slot):
        self.wires, self.shard, self.slot = wires, shard, slot
        self.z, self.g, _, _ = here()
        self.base = wires.reserve(4)
        low, high = (3 - self.z) // 3, self.z // 3
        self.order = (1 + 2 * low, 3 - low - high, 2 - low + high)

    def first(self):
        z, g = self.z, self.g
        own = self.slot(z)
        base = self.base
        self.wires.send_if(z < 3, self.shard, own, (turn(z, 1), g), base + 1, base + 1)
        self.wires.send_if(z > 0, self.shard, own, (turn(z, 3), g), base + 3, base + 3)
        self.across = self.wires.copy(self.shard, own, (turn(z, 2), g), base + 2, base + 2)
        self.across.start()
        self.wires.sent.append((None, self.across))

    def take(self, step):
        z, g = self.z, self.g
        k = self.order[step]
        origin = turn(z, LINES - k)
        held = self.slot(origin)
        self.wires.copy(held, held, (z, g), 0, self.base + k).wait_recv()
        if step == 2:
            self.relay(z == 2, 3, 3)
        if step == 2:
            self.relay(z == 1, 0, 1)
        return origin

    def relay(self, condition, there, k):
        held = self.slot(turn(self.z, 2))
        self.wires.send_if(
            condition, held, held, (there, self.g), self.base, self.base + k
        )


class LineSplit:
    def __init__(self, wires, shard, slot):
        self.wires, self.shard, self.slot = wires, shard, slot
        self.z, self.g, _, _ = here()
        self.base = wires.reserve(LINES)
        low, high = (3 - self.z) // 3, self.z // 3
        self.order = (1 + 2 * low, 3 - low - high, 2 - low + high)

    def first(self):
        for k in (2, 1, 3):
            there = turn(self.z, k)
            copy = self.wires.copy(
                piece_of(self.shard, there),
                self.slot(self.z),
                (there, self.g),
                self.base + k,
                self.base + k,
            )
            copy.start()
            self.wires.sent.append((None, copy))

    def take(self, step):
        k = self.order[step]
        origin = turn(self.z, LINES - k)
        held = self.slot(origin)
        self.wires.copy(held, held, (self.z, self.g), 0, self.base + k).wait_recv()
        return origin


def piece_of(shard, place):
    width = shard.shape[-1] // LINES
    return shard.at[:, pl.ds(pl.multiple_of(place * width, 128), width)]


class Spread:
    def __init__(self, wires, shard, slot, half, whole, split=False):
        self.wires, self.shard, self.slot, self.half, self.whole = wires, shard, slot, half, whole
        self.z, self.g, _, _ = here()
        self.line = (LineSplit if split else Line)(wires, shard, lambda z: slot(z, self.g))
        if split:
            self.shard = piece_of(shard, self.z)
        self.zs, self.x, self.y, self.dx, self.dy, self.sib = [self.z], [], [], {}, {}, []

    def side(self, gy):
        return (self.z, gy)

    def to_sibling(self, held):
        if self.whole:
            self.sib.append(self.wires.send(held, held, self.side(sibling(self.g))))

    def first(self):
        own = self.slot(self.z, self.g)
        self.line.first()
        self.x.append(self.wires.send(self.shard, own, self.side(along_x(self.g))))
        self.y.append(self.wires.send(self.shard, own, self.side(along_y(self.g))))
        if self.whole:
            self.sib.append(self.wires.send(self.shard, own, self.side(sibling(self.g))))

    def column(self, step):
        self.zs.append(self.line.take(step))
        held = self.slot(self.zs[-1], self.g)
        self.x.append(self.wires.send(held, held, self.side(along_x(self.g))))
        self.y.append(self.wires.send(held, held, self.side(along_y(self.g))))
        self.to_sibling(held)

    def corner(self, n):
        self.corner_x(n)
        self.corner_y(n)

    def corner_x(self, n):
        self.x[n].wait_recv()
        held = self.slot(self.zs[n], along_x(self.g))
        part = self.half(held, 0)
        self.dy[n] = self.wires.send(part, part, self.side(along_y(self.g)))
        self.to_sibling(held)

    def corner_y(self, n):
        self.y[n].wait_recv()
        held = self.slot(self.zs[n], along_y(self.g))
        part = self.half(held, 1)
        self.dx[n] = self.wires.send(part, part, self.side(along_x(self.g)))
        self.to_sibling(held)

    def last(self, n):
        self.dy[n].wait_recv()
        self.dx[n].wait_recv()
        self.to_sibling(self.slot(self.zs[n], along_y(along_x(self.g))))

    def finish(self):
        for copy in self.sib:
            copy.wait_recv()


def spread_all(flows):
    for flow in flows:
        flow.first()
    for flow in flows:
        flow.corner(0)
    for step in range(3):
        for flow in flows:
            flow.column(step)
        for flow in flows:
            flow.corner(step + 1)
    for n in range(4):
        for flow in flows:
            flow.last(n)
    for flow in flows:
        flow.finish()


LINE_SEMS = 4


def spread_sems(whole):
    return LINE_SEMS + 8 + 8 + (16 if whole else 0)


def columns_half(ref, which):
    width = ref.shape[-1] // 2
    return ref.at[..., pl.ds(which * width, width)]


def rows_half(ref, which):
    rows = ref.shape[0] // 2
    return ref.at[pl.ds(which * rows, rows)]


def rows_parts(ref, which):
    return ref.at[pl.ds(32, 16)] if which else ref.at[pl.ds(0, 32)]


def sides_of(z, g, whole):
    near = [(z, along_x(g)), (z, along_y(g))]
    return near + [(z, sibling(g))] if whole else near


def params(ident):
    return pltpu.CompilerParams(
        collective_id=ident, has_side_effects=True, vmem_limit_bytes=60 * 2**20
    )


def sems(count):
    return pltpu.SemaphoreType.DMA((count,))


VMEM = pl.BlockSpec(memory_space=pltpu.VMEM)
LEFT = pl.BlockSpec(memory_space=HBM)


class Exchange:
    def __init__(self, wires, pairs):
        self.wires, self.pairs = wires, pairs
        self.z, self.g, _, _ = here()

    def first(self):
        z = self.z
        self.copies = []
        for k in (2, 1, 3):
            there = turn(z, k)
            for source, out in self.pairs:
                self.copies.append(
                    self.wires.send(source.at[there], out.at[z], (there, self.g))
                )
        for source, out in self.pairs:
            out[z] = source[z]

    def finish(self):
        for copy in self.copies:
            copy.wait_recv()


def add_slots(target, source, count):
    @pl.loop(0, count)
    def _(n):
        target[n] = (target[n].astype(F32) + source[n].astype(F32)).astype(target.dtype)


class Fold:
    def __init__(self, wires, parts, whole, scratch, out):
        self.wires, self.parts, self.whole, self.out = wires, parts, whole, out
        self.from_sib, self.cx, self.cy, self.fx, self.fy, self.fz = scratch
        self.z, self.g, self.chip, self.core = here()
        self.cut = self.cy.shape[-1]

    def send(self, source, target, gy):
        return self.wires.send(source, target, (self.z, gy))

    def column(self, q):
        return self.parts.at[:, q, self.core] if self.whole else self.parts.at[:, q]

    def half(self, ref, which):
        if which:
            return ref.at[:, :, pl.ds(self.cut, ref.shape[-1] - self.cut)]
        return ref.at[:, :, pl.ds(0, self.cut)]

    def merge(self, q):
        if self.whole:
            core = self.core

            @pl.loop(0, LINES)
            def _(n):
                self.parts[n, q, core] = self.parts[n, q, core] + self.from_sib[n, q]

    def start(self):
        if self.whole:
            theirs = self.parts.at[:, :, 1 - self.core]
            self.sib = self.send(theirs, self.from_sib, sibling(self.g))

    def corner(self):
        if self.whole:
            self.sib.wait_recv()
        q = along_y(along_x(self.g)) // 2
        self.merge(q)
        far = self.column(q)
        self.to_y = self.send(self.half(far, 0), self.cy, along_y(self.g))
        self.to_x = self.send(self.half(far, 1), self.cx, along_x(self.g))

    def side(self, gy, came, corner, which, target):
        q = gy // 2
        self.merge(q)
        came.wait_recv()
        column = self.column(q)
        cols = slice(self.cut, None) if which else slice(0, self.cut)

        @pl.loop(0, LINES)
        def _(n):
            column[n, :, cols] = column[n, :, cols] + corner[n]

        return self.send(column, target, gy)

    def side_x(self):
        self.by_x = self.side(along_x(self.g), self.to_y, self.cy, 0, self.fx)

    def side_y(self):
        self.by_y = self.side(along_y(self.g), self.to_x, self.cx, 1, self.fy)

    def line(self):
        self.merge(self.chip)
        self.by_x.wait_recv()
        self.by_y.wait_recv()
        column = self.column(self.chip)
        self.zs = []
        for k in (2, 1, 3):
            there = turn(self.z, k)
            self.fx[there] = (
                column[there].astype(F32)
                + self.fx[there].astype(F32)
                + self.fy[there].astype(F32)
            ).astype(BF16)
            self.zs.append(
                self.wires.send(self.fx.at[there], self.fz.at[k - 1], (there, self.g))
            )
        z = self.z
        self.out[...] = column[z].astype(F32) + self.fx[z].astype(F32) + self.fy[z].astype(F32)

    def finish(self):
        for copy in self.zs:
            copy.wait_recv()
        self.out[...] += (
            self.fz[0].astype(F32) + self.fz[1].astype(F32) + self.fz[2].astype(F32)
        )


class FoldSplit(Fold):
    def line(self):
        self.merge(self.chip)
        self.by_x.wait_recv()
        self.by_y.wait_recv()
        column = self.column(self.chip)
        self.zs = []
        for k in (2, 1, 3, 0):
            there = turn(self.z, k) if k else self.z
            found = (
                column[there].astype(F32)
                + self.fx[there].astype(F32)
                + self.fy[there].astype(F32)
            ).astype(BF16)
            if k:
                self.fx[there] = found
                self.zs.append(
                    self.wires.send(self.fx.at[there], self.fz.at[self.z], (there, self.g))
                )
            else:
                self.fz[self.z] = found

    def finish(self):
        for copy in self.zs:
            copy.wait_recv()
        width = self.fz.shape[-1]
        for place in range(LINES):
            self.out[:, place * width : (place + 1) * width] = self.fz[place].astype(F32)


def fold_scratch(rows, cols, whole, split=False):
    cut = 256 if split else cols // 2
    return [
        pltpu.VMEM((LINES, PLANE, rows, cols) if whole else (1, 1, 16, 128), BF16),
        pltpu.VMEM((LINES, rows, cols - cut), BF16),
        pltpu.VMEM((LINES, rows, cut), BF16),
        pltpu.VMEM((LINES, rows, cols), BF16),
        pltpu.VMEM((LINES, rows, cols), BF16),
        pltpu.VMEM((LINES if split else LINES - 1, rows, cols), BF16),
    ]


FOLD = 6


def fold_sems(whole):
    return (1 if whole else 0) + 4 + 3


class FoldSteps:
    def __init__(self, wires, parts, scratch, out):
        self.wires, self.parts, self.out = wires, parts, out
        _, self.cx, self.cy, self.fx, self.fy, self.fz = scratch
        self.z, self.g, self.chip, _ = here()
        self.width = parts.shape[-1] // 2
        self.base = wires.reserve(LINES)
        low, high = (3 - self.z) // 3, self.z // 3
        back = (0, 1 + 2 * low, 3 - low - high, 2 - low + high)
        self.back = back
        self.zs = [turn(self.z, LINES - k) if n else self.z for n, k in enumerate(back)]
        self.to_x, self.to_y, self.by_x, self.by_y = {}, {}, {}, {}

    def half(self, n, q, which):
        return self.parts.at[self.zs[n], q, :, pl.ds(which * self.width, self.width)]

    def corner(self, n):
        far = along_y(along_x(self.g)) // 2
        place = self.zs[n]
        self.to_y[n] = self.wires.send(
            self.half(n, far, 0), self.cy.at[place], (self.z, along_y(self.g))
        )
        self.to_x[n] = self.wires.send(
            self.half(n, far, 1), self.cx.at[place], (self.z, along_x(self.g))
        )

    def side(self, n, gy, came, corner, which, target):
        came.wait_recv()
        q, place = gy // 2, self.zs[n]
        cols = slice(which * self.width, (which + 1) * self.width)
        self.parts[place, q, :, cols] = self.parts[place, q, :, cols] + corner[place]
        return self.wires.send(self.parts.at[place, q], target.at[place], (self.z, gy))

    def side_x(self, n):
        self.by_x[n] = self.side(n, along_x(self.g), self.to_y[n], self.cy, 0, self.fx)

    def side_y(self, n):
        self.by_y[n] = self.side(n, along_y(self.g), self.to_x[n], self.cx, 1, self.fy)

    def line(self, n):
        self.by_x[n].wait_recv()
        self.by_y[n].wait_recv()
        place = self.zs[n]
        found = (
            self.parts[place, self.chip].astype(F32)
            + self.fx[place].astype(F32)
            + self.fy[place].astype(F32)
        )
        if n == 0:
            self.out[...] = found
            return
        self.fx[place] = found.astype(BF16)
        k = LINES - self.back[n]
        copy = self.wires.copy(
            self.fx.at[place],
            self.fz.at[k - 1],
            (place, self.g),
            self.base + k,
            self.base + k,
        )
        copy.start()
        self.wires.sent.append((None, copy))

    def finish(self):
        for k in (1, 2, 3):
            held = self.fz.at[k - 1]
            self.wires.copy(held, held, (self.z, self.g), 0, self.base + k).wait_recv()
        self.out[...] += (
            self.fz[0].astype(F32) + self.fz[1].astype(F32) + self.fz[2].astype(F32)
        )


STEP_SEMS = 16 + LINES


def layer_norm(row_block, gain_row):
    row_mean = jnp.mean(row_block, axis=-1, keepdims=True)
    centred = row_block - row_mean
    variance = jnp.mean(centred * centred, axis=-1, keepdims=True)
    return centred * lax.rsqrt(variance + NORM_STABILIZER) * gain_row


def product(left_side, right_side):
    return jnp.dot(left_side, right_side, preferred_element_type=jnp.float32)


def inner_first(left_side, right_side):
    return lax.dot_general(
        left_side, right_side, (((0,), (0,)), ((), ())), preferred_element_type=jnp.float32
    )


def inner_last(left_side, right_side):
    return lax.dot_general(
        left_side, right_side, (((1,), (1,)), ((), ())), preferred_element_type=jnp.float32
    )


def collect(onehot_rows, value_rows):
    return lax.dot_general(
        onehot_rows,
        value_rows,
        (((0,), (0,)), ((), ())),
        precision=lax.Precision.HIGHEST,
        preferred_element_type=jnp.float32,
    )


def plain_device(
    media,
    latents,
    frame_counts,
    time_index,
    valid,
    time_table,
    media_gain,
    latent_gain,
    ffn_gain,
    w_query,
    w_key,
    w_value,
    w_out,
    w_up,
    w_down,
    cotangent,
):
    frames = time_index.shape[0]
    patches = valid.shape[0] // frames
    latent_rows = latents.shape[0]
    model_width = latents.shape[1]
    head_size = model_width // H
    score_scale = head_size ** (-0.5)
    across = lax.axis_size("gx")
    column = lax.axis_index("gx")
    row_index = lax.axis_index("gy")
    frame_ends = jnp.cumsum(frame_counts[row_index])
    position = column * frames + jnp.arange(frames, dtype=jnp.int32)
    item_index = jnp.sum((frame_ends[None, :] <= position[:, None]).astype(jnp.int32), axis=1)
    item_onehot = (item_index[:, None] == jnp.arange(across, dtype=jnp.int32)[None, :]).astype(
        jnp.float32
    )
    (
        full_query,
        full_key,
        full_value,
        full_out,
        full_up,
        full_down,
        full_media_gain,
        full_latent_gain,
        full_ffn_gain,
        full_time,
    ) = (
        lax.all_gather(w_query, ("gx", "gy"), axis=0, tiled=True),
        lax.all_gather(w_key, ("gx", "gy"), axis=0, tiled=True),
        lax.all_gather(w_value, ("gx", "gy"), axis=0, tiled=True),
        lax.all_gather(w_out, ("gx", "gy"), axis=0, tiled=True),
        lax.all_gather(w_up, ("gx", "gy"), axis=0, tiled=True),
        lax.all_gather(w_down, ("gx", "gy"), axis=0, tiled=True),
        lax.all_gather(media_gain, ("gx", "gy"), axis=0, tiled=True),
        lax.all_gather(latent_gain, ("gx", "gy"), axis=0, tiled=True),
        lax.all_gather(ffn_gain, ("gx", "gy"), axis=0, tiled=True),
        lax.all_gather(time_table, ("gx", "gy"), axis=1, tiled=True),
    )
    time_onehot = (
        time_index[:, None] == jnp.arange(full_time.shape[0], dtype=jnp.int32)[None, :]
    ).astype(jnp.float32)
    time_rows = product(time_onehot.astype(jnp.bfloat16), full_time)
    media_in = (
        media.astype(jnp.float32).reshape(frames, patches, model_width) + time_rows[:, None, :]
    ).reshape(-1, model_width)
    media_normed = layer_norm(media_in, full_media_gain.astype(jnp.float32)).astype(jnp.bfloat16)
    key_heads = (
        product(media_normed, full_key).astype(jnp.bfloat16).reshape(frames, patches, H, head_size)
    )
    value_heads = (
        product(media_normed, full_value)
        .astype(jnp.bfloat16)
        .reshape(frames, patches, H, head_size)
    )
    latent_in = latents.astype(jnp.float32)
    latent_normed = layer_norm(latent_in, full_latent_gain.astype(jnp.float32)).astype(jnp.bfloat16)
    own_query = product(latent_normed, full_query).astype(jnp.bfloat16)
    own_key = product(latent_normed, full_key).astype(jnp.bfloat16)
    own_value = product(latent_normed, full_value).astype(jnp.bfloat16)
    valid_total = lax.psum(jnp.sum(valid.astype(jnp.float32)), ("gx", "gy"))
    coefficient = ENTROPY_WEIGHT * (valid.shape[0] * lax.axis_size(("gx", "gy"))) / valid_total
    query_table = lax.all_gather(own_query, "gx", axis=0, tiled=True)
    picked = query_table.reshape(-1, latent_rows, H, head_size)[item_index]
    media_score = (
        jnp.einsum("flhd,fphd->flhp", picked, key_heads, preferred_element_type=jnp.float32)
        * score_scale
    )
    valid_mask = valid.reshape(frames, 1, 1, patches) > 0
    media_expo = jnp.where(valid_mask, jnp.exp(media_score), 0.0)
    expo_low = media_expo.astype(jnp.bfloat16)
    media_total = jnp.sum(media_expo, axis=-1)
    media_moment = jnp.sum(media_expo * media_score, axis=-1)
    media_weighted = jnp.einsum(
        "flhp,fphd->flhd", expo_low, value_heads, preferred_element_type=jnp.float32
    )
    dense_weighted = collect(item_onehot, media_weighted.reshape(frames, -1)).reshape(
        -1, model_width
    )
    dense_total = collect(item_onehot, media_total.reshape(frames, -1)).reshape(-1, H)
    dense_moment = collect(item_onehot, media_moment.reshape(frames, -1)).reshape(-1, H)
    got_weighted, got_total, got_moment = (
        lax.psum_scatter(dense_weighted, "gx", scatter_dimension=0, tiled=True),
        lax.psum_scatter(dense_total, "gx", scatter_dimension=0, tiled=True),
        lax.psum_scatter(dense_moment, "gx", scatter_dimension=0, tiled=True),
    )
    query_head_count = own_query.reshape(latent_rows, H, head_size)
    latent_key_rows = own_key.reshape(latent_rows, H, head_size)
    latent_value_rows = own_value.reshape(latent_rows, H, head_size)
    latent_score = (
        jnp.einsum(
            "uer,zer->uez", query_head_count, latent_key_rows, preferred_element_type=jnp.float32
        )
        * score_scale
    )
    latent_expo = jnp.exp(latent_score)
    latent_reduced_precision = latent_expo.astype(jnp.bfloat16)
    weighted = got_weighted.reshape(latent_rows, H, head_size) + jnp.einsum(
        "nwr,rwb->nwb",
        latent_reduced_precision,
        latent_value_rows,
        preferred_element_type=jnp.float32,
    )
    totals = got_total + jnp.sum(latent_expo, axis=-1)
    moment = got_moment + jnp.sum(latent_expo * latent_score, axis=-1)
    attention = weighted / totals[..., None]
    attn_low = attention.reshape(latent_rows, model_width).astype(jnp.bfloat16)
    middle = latent_in + product(attn_low, full_out)
    ffn_normed = layer_norm(middle, full_ffn_gain.astype(jnp.float32)).astype(jnp.bfloat16)
    up_rows = product(ffn_normed, full_up)
    hidden = jax.nn.gelu(up_rows, approximate=False).astype(jnp.bfloat16)
    new_latents = (middle + product(hidden, full_down)).astype(jnp.bfloat16)
    (
        back_query,
        back_key,
        back_value,
        back_out,
        back_up,
        back_down,
        back_media_gain,
        back_latent_gain,
        back_ffn_gain,
    ) = (
        lax.all_gather(w_query, ("gx", "gy"), axis=0, tiled=True),
        lax.all_gather(w_key, ("gx", "gy"), axis=0, tiled=True),
        lax.all_gather(w_value, ("gx", "gy"), axis=0, tiled=True),
        lax.all_gather(w_out, ("gx", "gy"), axis=0, tiled=True),
        lax.all_gather(w_up, ("gx", "gy"), axis=0, tiled=True),
        lax.all_gather(w_down, ("gx", "gy"), axis=0, tiled=True),
        lax.all_gather(media_gain, ("gx", "gy"), axis=0, tiled=True),
        lax.all_gather(latent_gain, ("gx", "gy"), axis=0, tiled=True),
        lax.all_gather(ffn_gain, ("gx", "gy"), axis=0, tiled=True),
    )
    owned_latent, owned_attn, owned_ffn, owned_hidden = (
        lax.all_to_all(latent_normed, ("gx", "gy"), split_axis=1, concat_axis=0, tiled=True),
        lax.all_to_all(attn_low, ("gx", "gy"), split_axis=1, concat_axis=0, tiled=True),
        lax.all_to_all(ffn_normed, ("gx", "gy"), split_axis=1, concat_axis=0, tiled=True),
        lax.all_to_all(hidden, ("gx", "gy"), split_axis=1, concat_axis=0, tiled=True),
    )
    hidden_grad = inner_last(cotangent, back_down)
    gelu_pull = jax.vjp(partial(jax.nn.gelu, approximate=False), up_rows)[1]
    up_grad = gelu_pull(hidden_grad)[0].astype(jnp.bfloat16)
    ffn_normed_grad = inner_last(up_grad, back_up)
    ffn_pull = jax.vjp(layer_norm, middle, back_ffn_gain.astype(jnp.float32))[1]
    middle_part, grad_ffn_gain = ffn_pull(ffn_normed_grad)
    middle_grad = cotangent.astype(jnp.float32) + middle_part
    middle_low = middle_grad.astype(jnp.bfloat16)
    attn_grad = inner_last(middle_low, back_out).reshape(latent_rows, H, head_size)
    weighted_sum_gradient = (attn_grad / totals[..., None]).astype(jnp.bfloat16)
    slope_term = -coefficient / totals
    shift_term = (
        -jnp.sum(attn_grad * attention, axis=-1) / totals
        + coefficient * (1.0 / totals + moment / (totals * totals))
        + slope_term
    )
    latent_mix = jnp.einsum(
        "uer,zer->uez", weighted_sum_gradient, latent_value_rows, preferred_element_type=jnp.float32
    )
    latent_sgrad = latent_expo * (
        latent_mix + shift_term[..., None] + slope_term[..., None] * latent_score
    )
    latent_residual_gradient = (latent_sgrad * score_scale).astype(jnp.bfloat16)
    query_part = jnp.einsum(
        "nwr,rwb->nwb",
        latent_residual_gradient,
        latent_key_rows,
        preferred_element_type=jnp.float32,
    )
    own_key_grad = (
        jnp.einsum(
            "zry,zrj->yrj",
            latent_residual_gradient,
            query_head_count,
            preferred_element_type=jnp.float32,
        )
        .astype(jnp.bfloat16)
        .reshape(latent_rows, model_width)
    )
    own_value_grad = (
        jnp.einsum(
            "zry,zrj->yrj",
            latent_reduced_precision,
            weighted_sum_gradient,
            preferred_element_type=jnp.float32,
        )
        .astype(jnp.bfloat16)
        .reshape(latent_rows, model_width)
    )
    grad_table = lax.all_gather(
        weighted_sum_gradient.reshape(latent_rows, model_width), "gx", axis=0, tiled=True
    )
    shift_table, slope_table = (
        lax.all_gather(shift_term, "gx", axis=0, tiled=True),
        lax.all_gather(slope_term, "gx", axis=0, tiled=True),
    )
    picked_grad = grad_table.reshape(-1, latent_rows, H, head_size)[item_index]
    picked_shift = shift_table.reshape(-1, latent_rows, H)[item_index]
    picked_slope = slope_table.reshape(-1, latent_rows, H)[item_index]
    media_mix = jnp.einsum(
        "flhd,fphd->flhp", picked_grad, value_heads, preferred_element_type=jnp.float32
    )
    media_sgrad = media_expo * (
        media_mix + picked_shift[..., None] + picked_slope[..., None] * media_score
    )
    media_rgrad = (media_sgrad * score_scale).astype(jnp.bfloat16)
    query_terms = jnp.einsum(
        "flhp,fphd->flhd", media_rgrad, key_heads, preferred_element_type=jnp.float32
    )
    dense_query = collect(item_onehot, query_terms.reshape(frames, -1)).reshape(-1, model_width)
    got_query = lax.psum_scatter(
        dense_query.astype(jnp.bfloat16), "gx", scatter_dimension=0, tiled=True
    ).astype(jnp.float32)
    media_key_grad = (
        jnp.einsum("flhp,flhd->fphd", media_rgrad, picked, preferred_element_type=jnp.float32)
        .astype(jnp.bfloat16)
        .reshape(-1, model_width)
    )
    media_value_grad = (
        jnp.einsum("flhp,flhd->fphd", expo_low, picked_grad, preferred_element_type=jnp.float32)
        .astype(jnp.bfloat16)
        .reshape(-1, model_width)
    )
    grad_key = inner_first(media_normed, media_key_grad) + inner_first(latent_normed, own_key_grad)
    grad_value = inner_first(media_normed, media_value_grad) + inner_first(
        latent_normed, own_value_grad
    )
    media_normed_grad = inner_last(media_key_grad, back_key) + inner_last(
        media_value_grad, back_value
    )
    media_pull = jax.vjp(layer_norm, media_in, back_media_gain.astype(jnp.float32))[1]
    media_grad, grad_media_gain = media_pull(media_normed_grad)
    frame_sums = jnp.sum(media_grad.reshape(frames, patches, model_width), axis=1)
    grad_time = collect(time_onehot, frame_sums)
    query_grad = (
        (got_query.reshape(latent_rows, H, head_size) + query_part)
        .astype(jnp.bfloat16)
        .reshape(latent_rows, model_width)
    )
    latent_normed_grad = (
        inner_last(query_grad, back_query)
        + inner_last(own_key_grad, back_key)
        + inner_last(own_value_grad, back_value)
    )
    latent_pull = jax.vjp(layer_norm, latent_in, back_latent_gain.astype(jnp.float32))[1]
    latent_part, grad_latent_gain = latent_pull(latent_normed_grad)
    latents_grad = middle_grad + latent_part
    piece_query = lax.all_gather(query_grad, ("gx", "gy"), axis=0, tiled=True)
    piece_middle = lax.all_gather(middle_low, ("gx", "gy"), axis=0, tiled=True)
    piece_up = lax.all_gather(up_grad, ("gx", "gy"), axis=0, tiled=True)
    piece_cot = lax.all_gather(cotangent, ("gx", "gy"), axis=0, tiled=True)
    shard_query = inner_first(owned_latent, piece_query)
    shard_out = inner_first(owned_attn, piece_middle)
    shard_up = inner_first(owned_ffn, piece_up)
    shard_down = inner_first(owned_hidden, piece_cot)
    shard_grads = (
        lax.psum_scatter(grad_key, ("gx", "gy"), scatter_dimension=0, tiled=True),
        lax.psum_scatter(grad_value, ("gx", "gy"), scatter_dimension=0, tiled=True),
        lax.psum_scatter(grad_media_gain, ("gx", "gy"), scatter_dimension=0, tiled=True),
        lax.psum_scatter(grad_latent_gain, ("gx", "gy"), scatter_dimension=0, tiled=True),
        lax.psum_scatter(grad_ffn_gain, ("gx", "gy"), scatter_dimension=0, tiled=True),
        lax.psum_scatter(grad_time, ("gx", "gy"), scatter_dimension=1, tiled=True),
    )
    return (
        new_latents,
        media_grad,
        latents_grad,
        shard_grads[5],
        shard_grads[2],
        shard_grads[3],
        shard_grads[4],
        shard_query,
        shard_grads[0],
        shard_grads[1],
        shard_out,
        shard_up,
        shard_down,
    )


GROUP = 4


def mates_of(z, chip, core):
    mates = []
    for j in range(1, 16):
        there = (4 * z + chip + j) % 16
        mates.append((there // 4, 2 * (there % 4) + core))
    return mates


class GiveBack:
    def __init__(self, wires, up_part, down_part, scratch, up_out, down_out):
        self.wires, self.up_part, self.down_part = wires, up_part, down_part
        self.up_out, self.down_out = up_out, down_out
        self.up_near, self.down_near, self.up_got = scratch
        self.z, self.g, self.chip, self.core = here()
        self.places = up_places(self.z, self.chip)

    def first(self):
        near = (self.z, sibling(self.g))
        theirs = 1 - self.core
        self.up = self.wires.send(self.up_part.at[:, :, theirs], self.up_near, near)
        self.down = self.wires.send(self.down_part.at[theirs], self.down_near, near)

    def columns(self):
        self.up.wait_recv()
        core = self.core

        @pl.loop(0, LINES)
        def _(n):
            for q in range(PLANE):
                self.up_part[n, q, core] = self.up_part[n, q, core] + self.up_near[n, q]

        self.moved = []
        for there, _ in self.places:
            self.moved.append(
                self.wires.send(
                    self.up_part.at[there[0], there[1], core],
                    self.up_got.at[self.z, self.chip],
                    (there[0], 2 * there[1] + core),
                )
            )
        self.up_got[self.z, self.chip] = self.up_part[self.z, self.chip, core]

    def rows(self):
        self.down.wait_recv()
        rows = self.down_out.shape[0] // 8
        core = self.core

        @pl.loop(0, 8)
        def _(n):
            block = pl.ds(pl.multiple_of(n * rows, 8), rows)
            self.down_out[block] = self.down_part[core, block] + self.down_near[block]

    def finish(self):
        for copy in self.moved:
            copy.wait_recv()
        width = self.up_got.shape[-1]
        for n in range(LINES):
            for q in range(PLANE):
                first = (n * PLANE + q) * width
                self.up_out[:, first : first + width] = self.up_got[n, q].astype(F32)


GIVE_SEMS = 17


class Total:
    def __init__(self, wires, mine, out, sums, got):
        self.wires, self.out, self.sums, self.got = wires, out, sums, got
        self.z, self.g, _, _ = here()
        self.source = mine
        self.step = 0

    def push(self):
        sides = [sibling(self.g), along_x(self.g), along_y(self.g)]
        if self.step < 3:
            self.copies = [
                self.wires.send(self.source, self.got.at[self.step], (self.z, sides[self.step]))
            ]
        else:
            self.copies = [
                self.wires.send(self.source, self.got.at[3 + k], device)
                for k, device in enumerate(line_of(self.z, self.g))
            ]

    def pull(self):
        for copy in self.copies:
            copy.wait_recv()
        if self.step < 3:
            self.sums[self.step] = self.source[...] + self.got[self.step]
            self.source = self.sums.at[self.step]
            self.step += 1
        else:
            self.out[...] = self.source[...] + self.got[3] + self.got[4] + self.got[5]


def head_masks(rows, width, head_size):
    lane = lax.broadcasted_iota(jnp.int32, (rows, width), 1)
    return [(lane >= h * head_size) & (lane < (h + 1) * head_size) for h in range(GROUP)]


def stacked(block, masks):
    zero = jnp.zeros_like(block)
    return jnp.concatenate([jnp.where(mask, block, zero) for mask in masks], axis=0)


def unstacked(block, masks):
    rows = block.shape[0] // GROUP
    total = jnp.where(masks[0], block[:rows], 0.0)
    for h in range(1, GROUP):
        total = jnp.where(masks[h], block[h * rows : (h + 1) * rows], total)
    return total


def dot_last(a, b):
    return lax.dot_general(a, b, (((1,), (1,)), ((), ())), preferred_element_type=F32)


def dot_first(a, b):
    return lax.dot_general(a, b, (((0,), (0,)), ((), ())), preferred_element_type=F32)


def spread_heads(columns, first, masks):
    out = jnp.where(masks[0], columns[:, first : first + 1], 0.0)
    for h in range(1, GROUP):
        out = jnp.where(masks[h], columns[:, first + h : first + h + 1], out)
    return out


def attend(queries, keys, values, valid, scale, masks):
    rows = queries.shape[0]
    score = dot_last(stacked(queries, masks), keys) * scale
    expo = jnp.exp(score)
    if valid is not None:
        expo = jnp.where(valid > 0, expo, 0.0)
    totals = jnp.sum(expo, axis=1, keepdims=True)
    moments = jnp.sum(expo * score, axis=1, keepdims=True)
    weighted = jnp.dot(expo.astype(BF16), values, preferred_element_type=F32)
    heads = [(totals[h * rows : (h + 1) * rows], moments[h * rows : (h + 1) * rows]) for h in range(GROUP)]
    return unstacked(weighted, masks), heads


def put_heads(heads, group, lane):
    out = jnp.zeros(lane.shape, F32)
    for h, (total, moment) in enumerate(heads):
        out = jnp.where(lane == group * GROUP + h, total, out)
        out = jnp.where(lane == H + group * GROUP + h, moment, out)
    return out


def assemble(smalls, out):
    count, rows, lanes = smalls.shape
    shard = out.shape[1] // count
    block = 8
    row = lax.broadcasted_iota(jnp.int32, (block * lanes, block * shard), 0)
    col = lax.broadcasted_iota(jnp.int32, (block * lanes, block * shard), 1)
    lane = row % lanes
    chosen = ((row // lanes) * shard + lane == col) & (lane < shard)
    place = jnp.where(chosen, 1.0, 0.0).astype(BF16)
    for n in range(count // block):
        pieces = jnp.concatenate([smalls[n * block + d] for d in range(block)], axis=1)
        out[:, n * block * shard : (n + 1) * block * shard] = jnp.dot(
            pieces.astype(BF16), place, preferred_element_type=F32
        )


def up_places(z, chip):
    places = []
    for dz in range(LINES):
        for dx, dy in ((0, 0), (1, 0), (0, 1), (1, 1)):
            if dz or dx or dy:
                x, y = chip % 2, chip // 2
                there = (y + dy) % 2 * 2 + (x + dx) % 2
                places.append(((turn(z, dz), there), (turn(z, LINES - dz) if dz else z, there)))
    return places


def shares(counts_ref, z, g, frame, frames, items):
    position = z * frames + frame
    end, slot = 0, 0
    for item in range(items):
        end = end + counts_ref[g, item]
        slot = slot + jnp.where(end <= position, 1, 0)
    return [jnp.where(slot == item, 1.0, 0.0) for item in range(items)]


def put_times(out, tables, times_ref, frames):
    for frame in range(frames):
        row = jnp.zeros((1, out.shape[1]), F32)
        for t in range(8):
            row = row + jnp.where(times_ref[frame] == t, 1.0, 0.0) * tables[t : t + 1]
        out[frame : frame + 1] = row


def opening_kernel(scale, *refs):
    (
        time_table_ref,
        media_gain_ref,
        latent_gain_ref,
        ffn_gain_ref,
        key_shard,
        value_shard,
        query_shard,
        out_shard,
        latents_ref,
        up_ref,
        down_ref,
        cot_ref,
        media_ref,
        valid_ref,
        counts_ref,
        times_ref,
        tables_out,
        counts_out,
        key_weight_out,
        value_weight_out,
        query_weight_out,
        out_weight_out,
        up_out,
        down_out,
        cot_out,
        normed_out,
        keys_out,
        values_out,
        table_out,
        line_normed_out,
        got_weighted,
        got_stats,
        own_weighted,
        own_stats,
        send_sems,
        recv_sems,
        local_sems,
        up_own,
        small_ref,
        smalls,
        key_weight,
        value_weight,
        query_weight,
        line_latents,
        line_normed,
        normed,
        keys,
        values,
        own_table,
        table,
        time_rows,
        sums,
        weighted,
        stats,
    ) = refs
    z, g, chip, core = here()
    here_chip = 4 * z + chip
    me = 2 * here_chip + core
    items, rows, width = line_latents.shape
    frames, _, patches = valid_ref.shape
    shard = key_shard.shape[0]
    span = width // (H // GROUP)
    up_width = up_out.shape[-1]
    near = (z, sibling(g))
    places = up_places(z, chip)
    greet([(there[0], 2 * there[1] + core) for there, _ in places] + [near])
    wires = Wires(send_sems, recv_sems)
    masks = head_masks(rows, span, span // GROUP)
    lane = lax.broadcasted_iota(jnp.int32, (rows, 128), 1)
    local = []
    small_ref[...] = jnp.zeros_like(small_ref)
    for place, source in (
        (slice(0, 8), time_table_ref),
        (slice(8, 9), media_gain_ref),
        (slice(9, 10), latent_gain_ref),
        (slice(10, 11), ffn_gain_ref),
    ):
        small_ref[place, :shard] = source[...].astype(F32)
    found = valid_ref[0].astype(F32)
    for n in range(1, frames):
        found = found + valid_ref[n].astype(F32)
    small_ref[11:12] = jnp.sum(found, axis=1, keepdims=True) + jnp.zeros((1, 128), F32)

    def keep(source, target):
        copy = pltpu.make_async_copy(source, target, local_sems.at[len(local)])
        copy.start()
        local.append(copy)
        return copy

    def rows_of(ref):
        return lambda zz, gg: ref.at[pl.ds(pl.multiple_of((zz * 8 + gg) * shard, 16), shard)]

    def piece(place):
        return up_ref.at[:, pl.ds(pl.multiple_of((4 * place[0] + place[1]) * up_width, 128), up_width)]

    def whole(source, slot):
        return Spread(wires, source, slot, columns_half, True), keep(source, slot(z, g))

    def small_slot(zz, gg):
        return smalls.at[zz * 8 + gg]

    small = Spread(wires, small_ref, small_slot, rows_half, True)
    small_kept = keep(small_ref, small_slot(z, g))
    key, key_kept = whole(key_shard, rows_of(key_weight))
    value, value_kept = whole(value_shard, rows_of(value_weight))
    query = Spread(wires, query_shard, rows_of(query_weight), rows_parts, True, True)
    query_kept = keep(piece_of(query_shard, z), rows_of(query_weight)(z, g))
    query_line = Line(wires, own_table, lambda zz: table.at[zz])
    out, out_kept = whole(out_shard, rows_of(out_weight_out))
    cot = Spread(wires, cot_ref, lambda zz, gg: cot_out.at[zz * 4 + gg // 2], columns_half, False)
    line = Line(wires, latents_ref, lambda zz: line_latents.at[zz])
    exchange = Exchange(wires, [(weighted, got_weighted), (stats, got_stats)])
    line_kept = keep(latents_ref, line_latents.at[z])
    up_load = keep(piece((z, chip)), up_own)
    late = [
        out_kept,
        keep(cot_ref, cot_out.at[here_chip]),
        keep(down_ref, down_out.at[core]),
    ]
    prompt = len(local)
    moved, given, down = [], [], []
    chunk = 32

    def normalise(first, last):
        @pl.loop(first, last)
        def _(n):
            block = pl.ds(pl.multiple_of(n * chunk, chunk), chunk)
            frame = n // (patches // chunk)
            row = media_ref[block].astype(F32) + time_rows[pl.ds(frame, 1)]
            normed[block] = layer_norm(row, tables_out[8:9]).astype(BF16)

    def normalise_latents():
        gain = tables_out[9:10]
        line_kept.wait()
        for item in range(items):

            @pl.loop(0, rows // chunk)
            def _(n):
                block = pl.ds(pl.multiple_of(n * chunk, chunk), chunk)
                row = line_latents[item, block].astype(F32)
                line_normed[item, block] = layer_norm(row, gain).astype(BF16)

        normed[frames * patches :] = line_normed[z]

    def tabulate():
        small_kept.wait()
        assemble(smalls, tables_out)
        counts = smalls[0, 8:]
        for n in range(1, smalls.shape[0]):
            counts = counts + smalls[n, 8:]
        counts_out[...] = counts
        put_times(time_rows, tables_out, times_ref, frames)

    def project(left, weight, out, n):
        cols = slice(n * span, (n + 1) * span)
        out[:, cols] = jnp.dot(left[...], weight[:, cols], preferred_element_type=F32).astype(BF16)

    def project_keys(n):
        if n == 0:
            key_kept.wait()
            keep(key_weight, key_weight_out)
            keep(normed, normed_out)
        project(normed, key_weight, keys, n)
        if n == 3:
            keep(keys, keys_out)

    def project_values(n):
        if n == 0:
            value_kept.wait()
            keep(value_weight, value_weight_out)
        project(normed, value_weight, values, n)
        if n == 3:
            keep(values, values_out)

    def project_queries():
        query_kept.wait()
        keep(query_weight, query_weight_out)
        for item in range(items):
            own_table[item] = jnp.dot(
                line_normed[item], query_weight[...], preferred_element_type=F32
            ).astype(BF16)
        table[z] = own_table[...]
        query_line.first()

    def attend_own():
        keep(table, table_out)
        keep(line_normed, line_normed_out)
        sums[...] = jnp.zeros_like(sums)
        stats[...] = jnp.zeros_like(stats)
        last = slice(frames * patches, frames * patches + rows)
        own = jnp.zeros((rows, 128), F32)
        for group in range(H // GROUP):
            cols = slice(group * span, (group + 1) * span)
            part, heads = attend(
                table[group, z], keys[last, cols], values[last, cols], None, scale, masks
            )
            own_weighted[:, cols] = part
            own = own + put_heads(heads, group, lane)
        own_stats[...] = own

    def attend_frames(first, last):
        @pl.loop(first, last)
        def _(frame):
            share = shares(counts_ref, z, g, frame, frames, items)
            block = pl.ds(pl.multiple_of(frame * patches, patches), patches)
            valid = valid_ref[frame]
            found = jnp.zeros((rows, 128), F32)
            for group in range(H // GROUP):
                cols = slice(group * span, (group + 1) * span)
                chosen = share[0] * table[group, 0].astype(F32)
                for item in range(1, items):
                    chosen = chosen + share[item] * table[group, item].astype(F32)
                part, heads = attend(
                    chosen.astype(BF16), keys[block, cols], values[block, cols], valid, scale, masks
                )
                found = found + put_heads(heads, group, lane)
                for item in range(items):
                    sums[item, :, cols] += share[item] * part
            for item in range(items):
                stats[item] += share[item] * found

    def down_first():
        down.append(wires.send(down_ref, down_out.at[core], near))

    def up_first():
        up_load.wait()
        keep(up_own, up_out.at[me])
        given.append(wires.send(up_own, up_out.at[me], near))
        for there, _ in places:
            moved.append(
                wires.send(piece(there), up_out.at[me], (there[0], 2 * there[1] + core))
            )

    def up_last():
        for n, (_, origin) in enumerate(places):
            moved[n].wait_recv()
            held = up_out.at[2 * (4 * origin[0] + origin[1]) + core]
            given.append(wires.send(held, held, near))
        for copy in given:
            copy.wait_recv()

    def sums_first():
        weighted[...] = sums[...].astype(BF16)
        exchange.first()

    small.first()
    out.first()
    small.column(0)
    key.first()
    out.column(0)
    query.first()
    small.column(1)
    value.first()
    small.corner_y(1)
    key.corner_x(0)
    key.column(0)
    small.corner_x(2)
    small.column(2)
    key.column(1)
    key.corner_y(0)
    query.column(0)
    line.first()
    value.column(0)
    cot.first()
    small.corner_y(2)
    query.corner_y(0)
    small.corner_x(0)
    out.column(1)
    query.column(1)
    small.corner_x(3)
    small.corner_y(0)
    out.corner_y(0)
    query.corner_x(0)
    value.column(1)
    key.column(2)
    line.take(0)
    small.corner_x(1)
    small.corner_y(3)
    query.corner_y(1)
    query.corner_x(1)
    value.corner_x(1)
    query.corner_x(2)
    out.corner_y(2)
    value.corner_x(2)
    key.corner_x(1)
    query.column(2)
    out.column(2)
    query.corner_y(2)
    value.corner_y(0)
    query.last(1)
    value.corner_y(2)
    small.last(3)
    small.last(0)
    small.last(1)
    key.last(0)
    small.last(2)
    key.corner_y(1)
    query.corner_x(3)
    cot.column(0)
    value.column(2)
    value.last(2)
    small.finish()
    query.corner_y(3)
    key.corner_y(3)
    value.corner_x(0)
    tabulate()
    line.take(1)
    key.corner_x(3)
    key.corner_y(2)
    key.corner_x(2)
    line.take(2)
    normalise(0, 4)
    value.corner_y(1)
    cot.column(1)
    normalise_latents()
    normalise(4, 8)
    down_first()
    query.last(2)
    normalise(8, 12)
    query.last(0)
    cot.corner_x(0)
    query.last(3)
    normalise(12, 16)
    value.corner_x(3)
    out.corner_x(1)
    key.last(3)
    value.corner_y(3)
    query.finish()
    project_queries()
    cot.corner_y(1)
    value.last(1)
    key.last(2)
    key.last(1)
    out.corner_x(2)
    out.corner_x(0)
    cot.corner_x(2)
    key.finish()
    out.corner_y(1)
    cot.column(2)
    value.last(0)
    up_first()
    out.corner_x(3)
    value.last(3)
    project_keys(0)
    project_keys(1)
    project_keys(2)
    project_keys(3)
    value.finish()
    project_values(0)
    cot.corner_x(1)
    query_line.take(0)
    project_values(1)
    out.last(0)
    cot.corner_x(3)
    project_values(2)
    project_values(3)
    query_line.take(1)
    query_line.take(2)
    down[0].wait_recv()
    attend_own()
    attend_frames(0, 1)
    attend_frames(1, 2)
    attend_frames(2, 3)
    attend_frames(3, 4)
    sums_first()
    cot.corner_y(2)
    cot.corner_y(0)
    cot.last(0)
    out.last(1)
    out.corner_y(3)
    cot.corner_y(3)
    out.last(3)
    out.last(2)
    cot.last(2)
    up_last()
    cot.last(3)
    out.finish()
    cot.last(1)
    exchange.finish()
    for copy in late + local[prompt:]:
        copy.wait()
    wires.drain()


def opening(scale, small, weights, latents, w_up, w_down, cotangent, media, valid, counts, times):
    rows, width = latents.shape
    shard = weights[0].shape[0]
    up_rows, up_width = w_up.shape
    all_rows = media.shape[0] + rows
    wires = 5 * spread_sems(True) + spread_sems(False) + 2 * LINE_SEMS + 31 + 1 + 6
    span = width // LINES
    square = jax.ShapeDtypeStruct((width, width), BF16)
    table = jax.ShapeDtypeStruct((LINES, rows, width), BF16)
    keys = jax.ShapeDtypeStruct((all_rows, width), BF16)
    smem = pl.BlockSpec(memory_space=pltpu.SMEM)
    return pl.pallas_call(
        partial(opening_kernel, scale),
        out_shape=[
            jax.ShapeDtypeStruct((16, width), F32),
            jax.ShapeDtypeStruct((8, 128), F32),
            square,
            square,
            jax.ShapeDtypeStruct((width, span), BF16),
            square,
            jax.ShapeDtypeStruct((32, up_rows, up_width // 16), BF16),
            jax.ShapeDtypeStruct((2,) + w_down.shape, BF16),
            jax.ShapeDtypeStruct((16,) + cotangent.shape, BF16),
            keys,
            keys,
            keys,
            jax.ShapeDtypeStruct((LINES, LINES, rows, span), BF16),
            table,
            table,
            jax.ShapeDtypeStruct((LINES, rows, 128), F32),
            jax.ShapeDtypeStruct((rows, width), F32),
            jax.ShapeDtypeStruct((rows, 128), F32),
        ],
        in_specs=[VMEM] * 8 + [LEFT] * 2 + [VMEM] * 4 + [smem] * 2,
        out_specs=[VMEM] * 2 + [LEFT] * 12 + [VMEM] * 4,
        scratch_shapes=[
            sems(wires),
            sems(wires),
            sems(24),
            pltpu.VMEM((up_rows, up_width // 16), BF16),
            pltpu.VMEM((16, 128), F32),
            pltpu.VMEM((32, 16, 128), F32),
            pltpu.VMEM((width, width), BF16),
            pltpu.VMEM((width, width), BF16),
            pltpu.VMEM((width, span), BF16),
            pltpu.VMEM((LINES, rows, width), BF16),
            pltpu.VMEM((LINES, rows, width), BF16),
            pltpu.VMEM((all_rows, width), BF16),
            pltpu.VMEM((all_rows, width), BF16),
            pltpu.VMEM((all_rows, width), BF16),
            pltpu.VMEM((LINES, rows, span), BF16),
            pltpu.VMEM((LINES, LINES, rows, span), BF16),
            pltpu.VMEM((8, width), F32),
            pltpu.VMEM((LINES, rows, width), F32),
            pltpu.VMEM((LINES, rows, width), BF16),
            pltpu.VMEM((LINES, rows, 128), F32),
        ],
        compiler_params=params(0),
        name="opening",
    )(*small, *weights, latents, w_up, w_down, cotangent, media, valid, counts, times)


def repel(queries, grads, keys, values, valid, shift, slope, scale, masks):
    query_stack = stacked(queries, masks)
    grad_stack = stacked(grads, masks)
    score = dot_last(query_stack, keys) * scale
    expo = jnp.exp(score)
    if valid is not None:
        expo = jnp.where(valid > 0, expo, 0.0)
    mix = dot_last(grad_stack, values)
    raw = (expo * (mix + shift + slope * score) * scale).astype(BF16)
    query_grad = unstacked(jnp.dot(raw, keys, preferred_element_type=F32), masks)
    key_grad = dot_first(raw, query_stack).astype(BF16)
    value_grad = dot_first(expo.astype(BF16), grad_stack).astype(BF16)
    return query_grad, key_grad, value_grad


def stacked_columns(terms, first):
    return jnp.concatenate([terms[:, first + h : first + h + 1] for h in range(GROUP)], axis=0)


def closing_kernel(scale, *refs):
    (
        table_ref,
        grad_ref,
        terms_ref,
        keys_ref,
        values_ref,
        normed_ref,
        valid_ref,
        attn_ref,
        low_ref,
        own_grad_ref,
        own_terms_ref,
        line_normed_ref,
        query_weight_ref,
        key_weight_ref,
        value_weight_ref,
        media_ref,
        tables_ref,
        latents_ref,
        middle_grad_ref,
        ffn_gain_ref,
        counts_ref,
        times_ref,
        media_grad_out,
        latents_grad_out,
        small_out,
        out_out,
        value_out,
        key_out,
        query_out,
        send_sems,
        recv_sems,
        local_sems,
        table,
        grads,
        keys,
        values,
        normed,
        key_grad,
        value_grad,
        weight_a,
        weight_b,
        sums,
        terms_query,
        got_query,
        query_grad,
        line_part,
        got_line,
        media_grad,
        latent_grad,
        small,
        small_sums,
        small_got,
        time_rows_ref,
        part_a,
        part_b,
        part_c,
        part_d,
        *fold,
    ) = refs
    z, g, _, core = here()
    items, rows, width = grads.shape
    frames, _, patches = valid_ref.shape
    media_rows = frames * patches
    shard = width // 32
    groups = H // GROUP
    span = width // groups
    masks = head_masks(rows, span, span // GROUP)
    greet(line_of(z, g) + sides_of(z, g, True))
    wires = Wires(send_sems, recv_sems)
    out = Fold(wires, part_a, True, fold[:FOLD], out_out)
    value = Fold(wires, part_b, True, fold[FOLD : 2 * FOLD], value_out)
    key = Fold(wires, part_c, True, fold[2 * FOLD : 3 * FOLD], key_out)
    query = FoldSplit(wires, part_d, True, fold[3 * FOLD :], query_out)
    total = Total(wires, small, small_out, small_sums, small_got)
    exchange = Exchange(wires, [(terms_query, got_query)])
    line_exchange = Exchange(wires, [(line_part, got_line)])
    local = []

    def load(source, target):
        copy = pltpu.make_async_copy(source, target, local_sems.at[len(local)])
        copy.start()
        local.append(copy)
        return copy

    loads = [
        load(table_ref, table),
        load(grad_ref, grads),
        load(keys_ref, keys),
        load(values_ref, values),
    ]
    normed_load = load(normed_ref, normed)
    key_load = load(key_weight_ref, weight_a)
    value_load = load(value_weight_ref, weight_b)
    stored = []

    def weight_part(part, left, right, first, last):
        @pl.loop(first, last)
        def _(n):
            cols = pl.ds(pl.multiple_of(n * span, 128), span)
            block = dot_first(left[:, cols], right[...]).astype(BF16)
            part[n] = block.reshape(PLANE, 2, shard, width)

    def out_part():
        weight_part(part_a, attn_ref, low_ref, 0, LINES)
        out.start()

    def value_part(n):
        if n == 0:
            normed_load.wait()
        weight_part(part_b, normed, value_grad, n, n + 1)
        if n == 3:
            value.start()

    def key_part(n):
        weight_part(part_c, normed, key_grad, n, n + 1)
        if n == 3:
            key.start()

    def repel_own():
        for copy in loads:
            copy.wait()
        sums[...] = jnp.zeros_like(sums)
        own_terms = own_terms_ref[...]
        for group in range(groups):
            cols = slice(group * span, (group + 1) * span)
            (
                sums[group, z],
                key_grad[media_rows:, cols],
                value_grad[media_rows:, cols],
            ) = repel(
                table[group, z],
                own_grad_ref[:, cols],
                keys[media_rows:, cols],
                values[media_rows:, cols],
                None,
                stacked_columns(own_terms, group * GROUP),
                stacked_columns(own_terms, H + group * GROUP),
                scale,
                masks,
            )

    def repel_frames(first, last):
        @pl.loop(first, last)
        def _(frame):
            block = pl.ds(pl.multiple_of(frame * patches, patches), patches)
            valid = valid_ref[frame]
            share = shares(counts_ref, z, g, frame, frames, items)

            def pick(ref, cols):
                chosen = share[0] * ref[0, :, cols].astype(F32)
                for item in range(1, items):
                    chosen = chosen + share[item] * ref[item, :, cols].astype(F32)
                return chosen

            everything = slice(None)
            terms = pick(terms_ref, everything)
            for group in range(groups):
                cols = slice(group * span, (group + 1) * span)
                query_part, key_grad[block, cols], value_grad[block, cols] = repel(
                    pick(table.at[group], everything).astype(BF16),
                    pick(grads, cols).astype(BF16),
                    keys[block, cols],
                    values[block, cols],
                    valid,
                    stacked_columns(terms, group * GROUP),
                    stacked_columns(terms, H + group * GROUP),
                    scale,
                    masks,
                )
                for item in range(items):
                    sums[group, item] += share[item] * query_part

    def queries_first():
        terms_query[...] = sums[...].astype(BF16)
        exchange.first()

    def media_product(n):
        if n == 0:
            key_load.wait()
            value_load.wait()
            small[...] = jnp.zeros_like(small)
            small[10:11] = ffn_gain_ref[...]
            put_times(time_rows_ref, tables_ref, times_ref, frames)
        if n == 2:
            stored[-1].wait()
        count = media_rows // 2
        block = slice(n // 2 * count, (n // 2 + 1) * count)

        @pl.loop(n % 2 * 2, n % 2 * 2 + 2)
        def _(t):
            cols = pl.ds(pl.multiple_of(t * span, 128), span)
            media_grad[:, cols] = dot_last(key_grad[block], weight_a[cols]) + dot_last(
                value_grad[block], weight_b[cols]
            )

    def media_pull(frame):
        count = media_rows // 2
        gain = tables_ref[8:9]
        chunk = 32
        f = frame % (frames // 2)
        moving = time_rows_ref[frame : frame + 1]

        def step(t, carry):
            gain_sum, row_sum = carry
            here_rows = pl.ds(pl.multiple_of(f * patches + t * chunk, chunk), chunk)
            there_rows = pl.ds(pl.multiple_of(frame * patches + t * chunk, chunk), chunk)
            row = media_ref[there_rows].astype(F32) + moving
            pulled, summand = norm_pull(row, gain, media_grad[here_rows])
            media_grad[here_rows] = pulled
            return (
                gain_sum + jnp.sum(summand, axis=0, keepdims=True),
                row_sum + jnp.sum(pulled, axis=0, keepdims=True),
            )

        zero = jnp.zeros((1, width), F32)
        gain_sum, row_sum = lax.fori_loop(0, patches // chunk, step, (zero, zero))
        small[8:9] += gain_sum
        for t in range(8):
            small[t : t + 1] += jnp.where(times_ref[frame] == t, 1.0, 0.0) * row_sum
        if f == frames // 2 - 1:
            first = frame // (frames // 2) * count
            stored.append(load(media_grad, media_grad_out.at[pl.ds(first, count)]))

    def latents_side(first):
        @pl.loop(first, first + 2)
        def _(t):
            cols = pl.ds(pl.multiple_of(t * span, 128), span)
            latent_grad[:, cols] = dot_last(key_grad[media_rows:], weight_a[cols]) + dot_last(
                value_grad[media_rows:], weight_b[cols]
            )

    def query_part():
        for item in range(items):
            found = got_query[0, item].astype(F32)
            for place in range(1, LINES):
                found = found + got_query[place, item].astype(F32)
            query_grad[item] = found.astype(BF16)
        grads_all = query_grad[...].reshape(items * rows, span)

        @pl.loop(0, LINES)
        def _(n):
            cols = pl.ds(pl.multiple_of(n * span, 128), span)
            left = line_normed_ref[:, :, cols].reshape(items * rows, span)
            block = dot_first(left, grads_all).astype(BF16)
            part_d[n] = block.reshape(PLANE, 2, shard, span)

        query.start()

    def line_first():
        for item in range(items):
            line_part[item] = dot_last(query_grad[item], query_weight_ref[...]).astype(BF16)
        line_exchange.first()

    def latents_end():
        for place in range(LINES):
            latent_grad[...] += got_line[place].astype(F32)
        pulled, summand = norm_pull(
            latents_ref[...].astype(F32), tables_ref[9:10], latent_grad[...]
        )
        latents_grad_out[...] = middle_grad_ref[...] + pulled
        small[9:10] = jnp.sum(summand, axis=0, keepdims=True)
        total.push()

    def total_next():
        total.pull()
        total.push()

    out_part()
    repel_own()
    repel_frames(0, 1)
    repel_frames(1, 2)
    repel_frames(2, 3)
    repel_frames(3, 4)
    out.corner()
    value_part(0)
    key_part(0)
    value_part(1)
    queries_first()
    key_part(1)
    key_part(2)
    key_part(3)
    value_part(2)
    out.side_x()
    out.side_y()
    key.corner()
    value_part(3)
    media_product(0)
    media_product(1)
    exchange.finish()
    query_part()
    line_first()
    media_pull(0)
    query.corner()
    value.corner()
    out.line()
    key.side_x()
    query.side_x()
    media_pull(1)
    key.side_y()
    query.side_y()
    value.side_x()
    media_product(2)
    media_product(3)
    media_pull(2)
    media_pull(3)
    value.side_y()
    latents_side(0)
    line_exchange.finish()
    key.line()
    latents_side(2)
    query.line()
    latents_end()
    total_next()
    value.line()
    total_next()
    key.finish()
    total_next()
    query.finish()
    out.finish()
    value.finish()
    total.pull()
    stored[1].wait()
    wires.drain()


def closing(scale, *args):
    (table, grads, terms, keys, values, normed) = args[:6]
    media, latents = args[15], args[17]
    span = table.shape[-1]
    rows, width = latents.shape
    shard = width // 32
    wires = 4 * fold_sems(True) + 6 + 6
    bf = [
        table.shape,
        grads.shape,
        keys.shape,
        keys.shape,
        keys.shape,
        keys.shape,
        keys.shape,
        (width, width),
        (width, width),
    ]
    part = pltpu.VMEM((LINES, PLANE, 2, shard, width), BF16)
    small = (16, width)
    scratch = [pltpu.VMEM(shape, BF16) for shape in bf] + [
        pltpu.VMEM(table.shape, F32),
        pltpu.VMEM(table.shape, BF16),
        pltpu.VMEM(table.shape, BF16),
        pltpu.VMEM(table.shape[1:], BF16),
        pltpu.VMEM(grads.shape, BF16),
        pltpu.VMEM(grads.shape, BF16),
        pltpu.VMEM((media.shape[0] // 2, width), F32),
        pltpu.VMEM((rows, width), F32),
        pltpu.VMEM(small, F32),
        pltpu.VMEM((3,) + small, F32),
        pltpu.VMEM((6,) + small, F32),
        pltpu.VMEM((8, width), F32),
        part,
        part,
        part,
        pltpu.VMEM((LINES, PLANE, 2, shard, span), BF16),
    ]
    scratch += fold_scratch(shard, width, True) * 3 + fold_scratch(shard, span, True, True)
    smem = pl.BlockSpec(memory_space=pltpu.SMEM)
    return pl.pallas_call(
        partial(closing_kernel, scale),
        out_shape=[
            jax.ShapeDtypeStruct(media.shape, F32),
            jax.ShapeDtypeStruct(latents.shape, F32),
            jax.ShapeDtypeStruct(small, F32),
        ]
        + [jax.ShapeDtypeStruct((shard, width), F32)] * 4,
        in_specs=[LEFT, LEFT, VMEM, LEFT, LEFT, LEFT]
        + [VMEM] * 7
        + [LEFT] * 2
        + [VMEM] * 5
        + [smem] * 2,
        out_specs=[LEFT] + [VMEM] * 6,
        scratch_shapes=[sems(wires), sems(wires), sems(12)] + scratch,
        compiler_params=pltpu.CompilerParams(
            collective_id=3, has_side_effects=True, vmem_limit_bytes=67043328
        ),
        name="closing",
    )(*args)


def settle_kernel(
    weighted_ref,
    stats_ref,
    own_weighted_ref,
    own_stats_ref,
    out_ref,
    latents_ref,
    gain_ref,
    attention_ref,
    attn_ref,
    sums_ref,
    middle_ref,
    normed_ref,
    ready,
):
    rows, width = latents_ref.shape
    span = width // (H // GROUP)
    masks = head_masks(rows, span, span // GROUP)
    stats = own_stats_ref[...]
    for n in range(stats_ref.shape[0]):
        stats = stats + stats_ref[n]
    sums_ref[...] = stats
    for group in range(H // GROUP):
        cols = pl.ds(group * span, span)
        weighted = own_weighted_ref[:, cols]
        for n in range(weighted_ref.shape[0]):
            weighted = weighted + weighted_ref[n, :, cols].astype(F32)
        attention = weighted / spread_heads(stats, group * GROUP, masks)
        attention_ref[:, cols] = attention
        attn_ref[:, cols] = attention.astype(BF16)
    ready()
    middle = latents_ref[...].astype(F32) + jnp.dot(
        attn_ref[...], out_ref[...], preferred_element_type=F32
    )
    middle_ref[...] = middle
    normed_ref[...] = layer_norm(middle, gain_ref[...]).astype(BF16)


def norm_pull(rows, gain, grad):
    mean = jnp.mean(rows, axis=-1, keepdims=True)
    centred = rows - mean
    inverse = lax.rsqrt(jnp.mean(centred * centred, axis=-1, keepdims=True) + NORM_STABILIZER)
    xhat = centred * inverse
    t = grad * gain
    pulled = (
        t
        - jnp.mean(t, axis=-1, keepdims=True)
        - xhat * jnp.mean(t * xhat, axis=-1, keepdims=True)
    ) * inverse
    return pulled, grad * xhat


def unsettle_kernel(
    normed_grad_ref,
    middle_ref,
    gain_ref,
    cot_ref,
    out_ref,
    attention_ref,
    stats_ref,
    coef,
    middle_grad_ref,
    low_ref,
    gain_grad_ref,
    weighted_grad_ref,
    terms_ref,
    attn_grad,
):
    rows, width = middle_ref.shape
    span = width // (H // GROUP)
    masks = head_masks(rows, span, span // GROUP)
    pulled, summand = norm_pull(middle_ref[...], gain_ref[...], normed_grad_ref[...])
    gain_grad_ref[...] = jnp.sum(summand, axis=0, keepdims=True)
    middle_grad = cot_ref[...].astype(F32) + pulled
    middle_grad_ref[...] = middle_grad
    low_ref[...] = middle_grad.astype(BF16)
    attn_grad[...] = dot_last(low_ref[...], out_ref[...])
    stats = stats_ref[...]
    lane = lax.broadcasted_iota(jnp.int32, (rows, 128), 1)
    terms = jnp.zeros((rows, 128), F32)
    for group in range(H // GROUP):
        cols = pl.ds(group * span, span)
        grad = attn_grad[:, cols]
        first = group * GROUP
        weighted_grad_ref[:, cols] = (grad / spread_heads(stats, first, masks)).astype(BF16)
        along = grad * attention_ref[:, cols]
        for h in range(GROUP):
            inner = jnp.sum(jnp.where(masks[h], along, 0.0), axis=1, keepdims=True)
            total = stats[:, first + h : first + h + 1]
            moment = stats[:, H + first + h : H + first + h + 1]
            slope = -coef / total
            shift = -inner / total + coef * (1.0 / total + moment / (total * total)) + slope
            terms = jnp.where(lane == first + h, shift, terms)
            terms = jnp.where(lane == H + first + h, slope, terms)
    terms_ref[...] = terms


def gelu_parts(rows):
    below = 0.5 * (1.0 + lax.erf(rows * (0.5**0.5)))
    density = jnp.exp(-0.5 * rows * rows) * ((0.5 / jnp.pi) ** 0.5)
    return rows * below, below + rows * density


def middle_kernel(patches, *refs):
    (
        weighted_ref,
        stats_ref,
        own_weighted_ref,
        own_stats_ref,
        out_weight_ref,
        up_ref,
        down_ref,
        cot_rows_ref,
        latents_ref,
        tables_ref,
        cot_ref,
        counts_ref,
        attn_out,
        low_out,
        middle_grad_out,
        gain_grad_out,
        weighted_grad_out,
        terms_out,
        grad_table_out,
        terms_table_out,
        new_latents_out,
        up_grad_out,
        down_grad_out,
        send_sems,
        recv_sems,
        local_sems,
        out_weight,
        up_cols,
        down_rows,
        cot_rows,
        ffn_rows,
        attention,
        sums,
        middle,
        normed,
        hidden_grad,
        up_grad,
        hidden,
        normed_part,
        down_part,
        up_grad_part,
        down_grad_part,
        up_near,
        down_near,
        up_got,
        normed_grad,
        down_sum,
        attn_grad,
        *fold,
    ) = refs
    z, g, chip, core = here()
    rows, width = latents_ref.shape
    span = up_cols.shape[1]
    shard = width // 32
    block_rows = PLANE * rows
    near = (z, sibling(g))
    gain_ref = tables_ref.at[10:11]
    greet([(there[0], 2 * there[1] + core) for there, _ in up_places(z, chip)] + [near])
    wires = Wires(send_sems, recv_sems)
    gather = Spread(
        wires, normed, lambda zz, gg: ffn_rows.at[zz, gg // 2], columns_half, False
    )
    back = FoldSteps(wires, normed_part, fold[:FOLD], normed_grad)
    down = Fold(wires, down_part, False, fold[FOLD:], down_sum)
    give = GiveBack(
        wires,
        up_grad_part,
        down_grad_part,
        (up_near, down_near, up_got),
        up_grad_out,
        down_grad_out,
    )
    grad_line = Line(wires, weighted_grad_out, lambda zz: grad_table_out.at[zz])
    terms_line = Line(wires, terms_out, lambda zz: terms_table_out.at[zz])
    loads = [
        pltpu.make_async_copy(source, target, local_sems.at[n])
        for n, (source, target) in enumerate(
            (
                (out_weight_ref, out_weight),
                (down_ref, down_rows),
                (cot_rows_ref, cot_rows),
                (up_ref, up_cols),
            )
        )
    ]
    for load in loads:
        load.start()

    def settle():
        settle_kernel(
            weighted_ref,
            stats_ref,
            own_weighted_ref,
            own_stats_ref,
            out_weight,
            latents_ref,
            gain_ref,
            attention,
            attn_out,
            sums,
            middle,
            normed,
            loads[0].wait,
        )
        ffn_rows[z, chip] = normed[...]

    def hidden_back(first):
        if first == 0:
            loads[1].wait()
            loads[2].wait()
            loads[3].wait()

        @pl.loop(first, first + 2)
        def _(n):
            block = cot_rows[n].reshape(block_rows, width)
            hidden_grad[n] = dot_last(block, down_rows[...])

    def group(n):
        place = gather.zs[n]
        block = ffn_rows[place].reshape(block_rows, width)
        value, slope = gelu_parts(jnp.dot(block, up_cols[...], preferred_element_type=F32))
        hidden[place] = value.astype(BF16)
        grad = (hidden_grad[place] * slope).astype(BF16)
        up_grad[place] = grad
        part = dot_last(grad, up_cols[...]).astype(BF16)
        normed_part[place] = part.reshape(PLANE, rows, width)

    def down_product(first):
        @pl.loop(first, first + 2)
        def _(n):
            part = jnp.dot(hidden[n], down_rows[...], preferred_element_type=F32)
            down_part[n] = part.astype(BF16).reshape(PLANE, rows, width)

    def up_gradient(first):
        grads = up_grad[...].reshape(LINES * block_rows, span)

        @pl.loop(first, first + 2)
        def _(n):
            cols = pl.ds(pl.multiple_of(n * span, 128), span)
            block = ffn_rows[:, :, :, cols].reshape(LINES * block_rows, span)
            part = dot_first(block, grads).astype(BF16)
            up_grad_part[n] = part.reshape(PLANE, 2, shard, span)

    def down_gradient(first):
        rows_up = hidden[...].reshape(LINES * block_rows, span)

        @pl.loop(first, first + 2)
        def _(n):
            cols = pl.ds(pl.multiple_of(n * span, 128), span)
            block = cot_rows[:, :, :, cols].reshape(LINES * block_rows, span)
            part = dot_first(rows_up, block)
            down_grad_part[:, :, cols] = part.reshape(2, span // 2, span)

    def unsettle():
        unsettle_kernel(
            normed_grad,
            middle,
            gain_ref,
            cot_ref,
            out_weight,
            attention,
            sums,
            ENTROPY_WEIGHT * patches / counts_ref[3:4, 0:1],
            middle_grad_out,
            low_out,
            gain_grad_out,
            weighted_grad_out,
            terms_out,
            attn_grad,
        )
        grad_table_out[z] = weighted_grad_out[...]
        terms_table_out[z] = terms_out[...]

    def new_rows():
        new_latents_out[...] = (middle[...] + down_sum[...]).astype(BF16)

    settle()
    gather.first()
    gather.column(0)
    gather.column(1)
    gather.corner_y(0)
    hidden_back(0)
    gather.corner_x(0)
    gather.corner_y(1)
    hidden_back(2)
    gather.corner_x(1)
    gather.column(2)
    gather.last(0)
    group(0)
    gather.corner_x(2)
    gather.corner_y(2)
    back.corner(0)
    gather.corner_y(3)
    gather.corner_x(3)
    gather.last(1)
    group(1)
    gather.last(2)
    group(2)
    back.corner(2)
    back.corner(1)
    back.side_x(2)
    back.side_y(2)
    gather.last(3)
    group(3)
    back.corner(3)
    back.side_x(1)
    up_gradient(0)
    down_product(0)
    down_gradient(0)
    down_product(2)
    down.start()
    back.side_y(1)
    back.line(2)
    up_gradient(2)
    back.side_y(3)
    down_gradient(2)
    back.side_y(0)
    back.side_x(3)
    back.line(1)
    give.first()
    back.side_x(0)
    back.line(3)
    down.corner()
    give.columns()
    back.line(0)
    down.side_x()
    down.side_y()
    back.finish()
    unsettle()
    grad_line.first()
    terms_line.first()
    terms_line.take(0)
    grad_line.take(0)
    grad_line.take(1)
    give.rows()
    down.line()
    terms_line.take(1)
    terms_line.take(2)
    grad_line.take(2)
    give.finish()
    down.finish()
    new_rows()
    wires.drain()


def middle_part(
    patches,
    weighted,
    stats,
    own_weighted,
    own_stats,
    w_out,
    up_cols,
    down_rows,
    cot_rows,
    latents,
    tables,
    cot,
    counts,
):
    rows, width = latents.shape
    span = up_cols.shape[1]
    shard = width // 32
    plane = (LINES, PLANE, rows, width)
    block = (LINES, PLANE * rows, span)
    wires = spread_sems(False) + STEP_SEMS + fold_sems(False) + GIVE_SEMS + 2 * LINE_SEMS
    own = (rows, width)
    terms = own_stats.shape
    bf = [
        w_out.shape,
        up_cols.shape,
        down_rows.shape,
        plane,
        plane,
    ]
    scratch = [pltpu.VMEM(shape, BF16) for shape in bf] + [
        pltpu.VMEM(own, F32),
        pltpu.VMEM(terms, F32),
        pltpu.VMEM(own, F32),
        pltpu.VMEM(own, BF16),
        pltpu.VMEM(block, F32),
        pltpu.VMEM(block, BF16),
        pltpu.VMEM(block, BF16),
        pltpu.VMEM(plane, BF16),
        pltpu.VMEM(plane, BF16),
        pltpu.VMEM((LINES, PLANE, 2, shard, span), BF16),
        pltpu.VMEM((2, span // 2, width), F32),
        pltpu.VMEM((LINES, PLANE, shard, span), BF16),
        pltpu.VMEM((span // 2, width), F32),
        pltpu.VMEM((LINES, PLANE, shard, span), BF16),
        pltpu.VMEM(own, F32),
        pltpu.VMEM(own, F32),
        pltpu.VMEM(own, F32),
    ]
    scratch += fold_scratch(rows, width, False) * 2
    return pl.pallas_call(
        partial(middle_kernel, patches),
        out_shape=[
            jax.ShapeDtypeStruct(own, BF16),
            jax.ShapeDtypeStruct(own, BF16),
            jax.ShapeDtypeStruct(own, F32),
            jax.ShapeDtypeStruct((1, width), F32),
            jax.ShapeDtypeStruct(own, BF16),
            jax.ShapeDtypeStruct(terms, F32),
            jax.ShapeDtypeStruct((LINES,) + own, BF16),
            jax.ShapeDtypeStruct((LINES,) + terms, F32),
            jax.ShapeDtypeStruct(own, BF16),
            jax.ShapeDtypeStruct((shard, span * 16), F32),
            jax.ShapeDtypeStruct((span // 2, width), F32),
        ],
        in_specs=[VMEM] * 4 + [LEFT] * 4 + [VMEM] * 4,
        out_specs=[VMEM] * 11,
        scratch_shapes=[sems(wires), sems(wires), sems(4)] + scratch,
        compiler_params=params(1),
        name="middle",
    )(
        weighted,
        stats,
        own_weighted,
        own_stats,
        w_out,
        up_cols,
        down_rows,
        cot_rows.reshape(plane),
        latents,
        tables,
        cot,
        counts,
    )


def ending_kernel(shard, *refs):
    count = (len(refs) - 6) // 3
    sources, small = refs[:count], refs[count]
    outs = refs[count + 1 : 2 * count + 1]
    small_outs = refs[2 * count + 1 : 2 * count + 5]
    held, arrive = refs[2 * count + 5 : 3 * count + 5], refs[3 * count + 5]
    loads, stores = [], []
    for n in range(count):
        loads.append(pltpu.make_async_copy(sources[n], held[n], arrive.at[n]))
        stores.append(pltpu.make_async_copy(held[n], outs[n], arrive.at[n]))
        loads[n].start()
    z, g, _, _ = here()
    width = small.shape[1]
    turned = pltpu.roll(small[...], width - (8 * z + g) * shard, 1)
    small_outs[0][...] = turned[:8, :shard]
    for n in range(3):
        small_outs[n + 1][...] = turned[8 + n : 9 + n, :shard]
    for n in range(count):
        loads[n].wait()
        stores[n].start()
    for n in range(count):
        stores[n].wait()


def ending(results, small, shard):
    count = len(results)
    return pl.pallas_call(
        partial(ending_kernel, shard),
        out_shape=[jax.ShapeDtypeStruct(r.shape, r.dtype) for r in results]
        + [jax.ShapeDtypeStruct((8, shard), F32)]
        + [jax.ShapeDtypeStruct((1, shard), F32)] * 3,
        in_specs=[LEFT] * count + [VMEM],
        out_specs=[LEFT] * count + [VMEM] * 4,
        scratch_shapes=[pltpu.VMEM(r.shape, r.dtype) for r in results] + [sems(count)],
        name="ending",
    )(*results, small)


def per_device(
    media,
    latents,
    frame_counts,
    time_index,
    valid,
    time_table,
    media_gain,
    latent_gain,
    ffn_gain,
    w_query,
    w_key,
    w_value,
    w_out,
    w_up,
    w_down,
    cotangent,
):
    frames = time_index.shape[0]
    patches = valid.shape[0] // frames
    width = latents.shape[1]
    shard = media_gain.shape[0]
    scale = (width // H) ** (-0.5)
    valid_rows = valid.reshape(frames, 1, patches)
    (
        tables,
        counts,
        full_key,
        full_value,
        full_query,
        full_out,
        up_cols,
        down_rows,
        cot_rows,
        normed,
        keys,
        values,
        table,
        line_normed,
        got_weighted,
        got_stats,
        own_weighted,
        own_stats,
    ) = opening(
        scale,
        (
            time_table,
            media_gain.reshape(1, shard),
            latent_gain.reshape(1, shard),
            ffn_gain.reshape(1, shard),
        ),
        (w_key, w_value, w_query, w_out),
        latents,
        w_up,
        w_down,
        cotangent,
        media,
        valid_rows,
        frame_counts,
        time_index,
    )
    (
        attn_low,
        middle_low,
        middle_grad,
        grad_ffn_gain,
        weighted_grad,
        terms,
        grad_table,
        terms_table,
        new_latents,
        shard_up,
        shard_down,
    ) = middle_part(
        valid.shape[0] * lax.axis_size(AXES),
        got_weighted,
        got_stats,
        own_weighted,
        own_stats,
        full_out,
        up_cols.reshape(width, -1),
        down_rows.reshape(-1, width),
        cot_rows,
        latents,
        tables,
        cotangent,
        counts,
    )
    (
        media_grad,
        latents_grad,
        smalls_grad,
        shard_out,
        shard_value,
        shard_key,
        shard_query,
    ) = closing(
        scale,
        table,
        grad_table,
        terms_table,
        keys,
        values,
        normed,
        valid_rows,
        attn_low,
        middle_low,
        weighted_grad,
        terms,
        line_normed,
        full_query,
        full_key,
        full_value,
        media,
        tables,
        latents,
        middle_grad,
        grad_ffn_gain,
        frame_counts,
        time_index,
    )
    results = ending(
        (
            new_latents,
            media_grad,
            latents_grad,
            shard_query,
            shard_key,
            shard_value,
            shard_out,
            shard_up,
            shard_down,
        ),
        smalls_grad,
        shard,
    )
    time_grad, *gains = results[9:]
    return (
        *results[:3],
        time_grad,
        *(gain.reshape(shard) for gain in gains),
        *results[3:9],
    )


def solution(mesh):
    in_specs = (
        P(("gx", "gy"), None),
        P(("gx", "gy"), None),
        P(),
        P(("gx", "gy")),
        P(("gx", "gy")),
        P(None, ("gx", "gy")),
        P(("gx", "gy")),
        P(("gx", "gy")),
        P(("gx", "gy")),
        P(("gx", "gy"), None),
        P(("gx", "gy"), None),
        P(("gx", "gy"), None),
        P(("gx", "gy"), None),
        P(("gx", "gy"), None),
        P(("gx", "gy"), None),
        P(("gx", "gy"), None),
    )
    out_specs = (
        P(("gx", "gy"), None),
        P(("gx", "gy"), None),
        P(("gx", "gy"), None),
        P(None, ("gx", "gy")),
        P(("gx", "gy")),
        P(("gx", "gy")),
        P(("gx", "gy")),
        P(("gx", "gy"), None),
        P(("gx", "gy"), None),
        P(("gx", "gy"), None),
        P(("gx", "gy"), None),
        P(("gx", "gy"), None),
        P(("gx", "gy"), None),
    )
    return jax.shard_map(
        per_device if dict(mesh.shape) == {"gx": 4, "gy": 8} else plain_device,
        mesh=mesh, in_specs=in_specs, out_specs=out_specs, check_vma=False
    )
```

```python
from functools import partial

import jax
import jax.numpy as jnp
from jax import lax
from jax.experimental import pallas as pl
from jax.experimental.pallas import tpu as pltpu
from jax.sharding import PartitionSpec as P

H = 16


ENTROPY_WEIGHT = 4.0
NORM_STABILIZER = 1e-05
AXES = ("gx", "gy")
LINES = 4
PLANE = 4
HBM = pl.ANY
BF16 = jnp.bfloat16
F32 = jnp.float32


def here():
    z = lax.axis_index("gx")
    g = lax.axis_index("gy")
    return z, g, g // 2, g % 2


def sibling(g):
    return g + 1 - 2 * (g % 2)


def along_x(g):
    return g + 2 - 4 * ((g // 2) % 2)


def along_y(g):
    return (g + 4) % 8


def turn(z, k):
    return (z + k) % LINES


def greet(devices):
    barrier = pltpu.get_barrier_semaphore()
    for device in devices:
        pl.semaphore_signal(
            barrier, inc=1, device_id=device, device_id_type=pl.DeviceIdType.MESH
        )
    pl.semaphore_wait(barrier, len(devices))


def line_of(z, g):
    return [(turn(z, k), g) for k in (1, 2, 3)]


class Wires:
    def __init__(self, send_sems, recv_sems):
        self.send_sems, self.recv_sems, self.used, self.sent = send_sems, recv_sems, 0, []

    def reserve(self, count):
        first = self.used
        self.used += count
        return first

    def copy(self, source, target, device, send, recv):
        return pltpu.make_async_remote_copy(
            src_ref=source,
            dst_ref=target,
            send_sem=self.send_sems.at[send],
            recv_sem=self.recv_sems.at[recv],
            device_id=device,
            device_id_type=pl.DeviceIdType.MESH,
        )

    def send(self, source, target, device):
        n = self.reserve(1)
        copy = self.copy(source, target, device, n, n)
        copy.start()
        self.sent.append((None, copy))
        return copy

    def send_if(self, condition, source, target, device, send, recv):
        copy = self.copy(source, target, device, send, recv)
        self.sent.append((condition, copy))

        @pl.when(condition)
        def _():
            copy.start()

        return copy

    def drain(self):
        for condition, copy in self.sent:
            if condition is None:
                copy.wait_send()
            else:
                pl.when(condition)(copy.wait_send)


class Line:
    def __init__(self, wires, shard, slot):
        self.wires, self.shard, self.slot = wires, shard, slot
        self.z, self.g, _, _ = here()
        self.base = wires.reserve(4)
        low, high = (3 - self.z) // 3, self.z // 3
        self.order = (1 + 2 * low, 3 - low - high, 2 - low + high)

    def first(self):
        z, g = self.z, self.g
        own = self.slot(z)
        base = self.base
        self.wires.send_if(z < 3, self.shard, own, (turn(z, 1), g), base + 1, base + 1)
        self.wires.send_if(z > 0, self.shard, own, (turn(z, 3), g), base + 3, base + 3)
        self.across = self.wires.copy(self.shard, own, (turn(z, 2), g), base + 2, base + 2)
        self.across.start()
        self.wires.sent.append((None, self.across))

    def take(self, step):
        z, g = self.z, self.g
        k = self.order[step]
        origin = turn(z, LINES - k)
        held = self.slot(origin)
        self.wires.copy(held, held, (z, g), 0, self.base + k).wait_recv()
        if step == 2:
            self.relay(z == 2, 3, 3)
        if step == 2:
            self.relay(z == 1, 0, 1)
        return origin

    def relay(self, condition, there, k):
        held = self.slot(turn(self.z, 2))
        self.wires.send_if(
            condition, held, held, (there, self.g), self.base, self.base + k
        )


class LineSplit:
    def __init__(self, wires, shard, slot):
        self.wires, self.shard, self.slot = wires, shard, slot
        self.z, self.g, _, _ = here()
        self.base = wires.reserve(LINES)
        low, high = (3 - self.z) // 3, self.z // 3
        self.order = (1 + 2 * low, 3 - low - high, 2 - low + high)

    def first(self):
        for k in (2, 1, 3):
            there = turn(self.z, k)
            copy = self.wires.copy(
                piece_of(self.shard, there),
                self.slot(self.z),
                (there, self.g),
                self.base + k,
                self.base + k,
            )
            copy.start()
            self.wires.sent.append((None, copy))

    def take(self, step):
        k = self.order[step]
        origin = turn(self.z, LINES - k)
        held = self.slot(origin)
        self.wires.copy(held, held, (self.z, self.g), 0, self.base + k).wait_recv()
        return origin


def piece_of(shard, place):
    width = shard.shape[-1] // LINES
    return shard.at[:, pl.ds(pl.multiple_of(place * width, 128), width)]


class Spread:
    def __init__(self, wires, shard, slot, half, whole, split=False):
        self.wires, self.shard, self.slot, self.half, self.whole = wires, shard, slot, half, whole
        self.z, self.g, _, _ = here()
        self.line = (LineSplit if split else Line)(wires, shard, lambda z: slot(z, self.g))
        if split:
            self.shard = piece_of(shard, self.z)
        self.zs, self.x, self.y, self.dx, self.dy, self.sib = [self.z], [], [], {}, {}, []

    def side(self, gy):
        return (self.z, gy)

    def to_sibling(self, held):
        if self.whole:
            self.sib.append(self.wires.send(held, held, self.side(sibling(self.g))))

    def first(self):
        own = self.slot(self.z, self.g)
        self.line.first()
        self.x.append(self.wires.send(self.shard, own, self.side(along_x(self.g))))
        self.y.append(self.wires.send(self.shard, own, self.side(along_y(self.g))))
        if self.whole:
            self.sib.append(self.wires.send(self.shard, own, self.side(sibling(self.g))))

    def column(self, step):
        self.zs.append(self.line.take(step))
        held = self.slot(self.zs[-1], self.g)
        self.x.append(self.wires.send(held, held, self.side(along_x(self.g))))
        self.y.append(self.wires.send(held, held, self.side(along_y(self.g))))
        self.to_sibling(held)

    def corner(self, n):
        self.corner_x(n)
        self.corner_y(n)

    def corner_x(self, n):
        self.x[n].wait_recv()
        held = self.slot(self.zs[n], along_x(self.g))
        part = self.half(held, 0)
        self.dy[n] = self.wires.send(part, part, self.side(along_y(self.g)))
        self.to_sibling(held)

    def corner_y(self, n):
        self.y[n].wait_recv()
        held = self.slot(self.zs[n], along_y(self.g))
        part = self.half(held, 1)
        self.dx[n] = self.wires.send(part, part, self.side(along_x(self.g)))
        self.to_sibling(held)

    def last(self, n):
        self.dy[n].wait_recv()
        self.dx[n].wait_recv()
        self.to_sibling(self.slot(self.zs[n], along_y(along_x(self.g))))

    def finish(self):
        for copy in self.sib:
            copy.wait_recv()


def spread_all(flows):
    for flow in flows:
        flow.first()
    for flow in flows:
        flow.corner(0)
    for step in range(3):
        for flow in flows:
            flow.column(step)
        for flow in flows:
            flow.corner(step + 1)
    for n in range(4):
        for flow in flows:
            flow.last(n)
    for flow in flows:
        flow.finish()


LINE_SEMS = 4


def spread_sems(whole):
    return LINE_SEMS + 8 + 8 + (16 if whole else 0)


def columns_half(ref, which):
    width = ref.shape[-1] // 2
    return ref.at[..., pl.ds(which * width, width)]


def rows_half(ref, which):
    rows = ref.shape[0] // 2
    return ref.at[pl.ds(which * rows, rows)]


def rows_parts(ref, which):
    return ref.at[pl.ds(32, 16)] if which else ref.at[pl.ds(0, 32)]


def sides_of(z, g, whole):
    near = [(z, along_x(g)), (z, along_y(g))]
    return near + [(z, sibling(g))] if whole else near


def params(ident):
    return pltpu.CompilerParams(
        collective_id=ident, has_side_effects=True, vmem_limit_bytes=60 * 2**20
    )


def sems(count):
    return pltpu.SemaphoreType.DMA((count,))


VMEM = pl.BlockSpec(memory_space=pltpu.VMEM)
LEFT = pl.BlockSpec(memory_space=HBM)


class SumLine:
    def __init__(self, wires, source, out, relayed=None):
        self.wires, self.source, self.out, self.relayed = wires, source, out, relayed
        self.z, self.g, _, _ = here()
        self.base = wires.reserve(LINES)
        low, high = (3 - self.z) // 3, self.z // 3
        self.back = (0, 1 + 2 * low, 3 - low - high, 2 - low + high)
        self.places = [turn(self.z, LINES - k) if n else self.z for n, k in enumerate(self.back)]
        self.end = low + high > 0
        self.inner = low + high < 1
        self.beside = 1 + high

    def step(self, n):
        place = self.places[n]
        if n < 3 or self.relayed is None:
            k = LINES - self.back[n]
            copy = self.wires.copy(
                self.source.at[place],
                self.out.at[self.z],
                (place, self.g),
                self.base + k,
                self.base + k,
            )
            copy.start()
            self.wires.sent.append((None, copy))
        else:
            self.wires.send_if(
                self.end,
                self.source.at[place],
                self.relayed,
                (self.beside, self.g),
                self.base,
                self.base,
            )

    def first(self):
        for n in (2, 1, 3):
            self.step(n)
        self.clear()
        self.out[self.z] = self.source[self.z]

    def clear(self):
        if self.relayed is None:
            return

        @pl.when(self.end)
        def _():
            self.out[3 - self.z] = jnp.zeros(self.out.shape[1:], self.out.dtype)

    def relay(self):
        place = self.places[3]
        held = self.source.at[place]
        across = self.wires.copy(
            held, self.out.at[self.z], (place, self.g), self.base + 2, self.base + 2
        )
        came = self.wires.copy(
            self.relayed, self.relayed, (self.z, self.g), self.base, self.base
        )
        self.wires.sent.append((self.inner, across))

        @pl.when(self.inner)
        def _():
            came.wait_recv()
            held[...] = held[...] + self.relayed[...]
            across.start()

    def finish(self):
        for k, condition in ((1, self.z > 0), (3, self.z < 3), (2, None)):
            if self.relayed is None:
                condition = None
            held = self.out.at[turn(self.z, LINES - k)]
            copy = self.wires.copy(held, held, (self.z, self.g), 0, self.base + k)
            if condition is None:
                copy.wait_recv()
            else:
                pl.when(condition)(copy.wait_recv)


class Exchange:
    def __init__(self, wires, arrays):
        self.lines = [SumLine(wires, *array) for array in arrays]

    def first(self):
        for line in self.lines:
            line.first()

    def relay(self):
        for line in self.lines:
            line.relay()

    def finish(self):
        for line in self.lines:
            line.finish()


def add_slots(target, source, count):
    @pl.loop(0, count)
    def _(n):
        target[n] = (target[n].astype(F32) + source[n].astype(F32)).astype(target.dtype)


def sum_slots(ref):
    found = ref[0].astype(F32)
    for n in range(1, LINES):
        found = found + ref[n].astype(F32)
    return found


class Fold:
    summed = True

    def __init__(self, wires, parts, whole, scratch, out):
        self.wires, self.parts, self.whole, self.out = wires, parts, whole, out
        self.from_sib, self.cx, self.cy, self.fx, self.fy, self.fz, self.relayed = scratch
        self.z, self.g, self.chip, self.core = here()
        self.cut = self.cy.shape[-1]
        self.lines = SumLine(wires, self.fx, self.fz, self.relayed) if self.summed else None

    def send(self, source, target, gy):
        return self.wires.send(source, target, (self.z, gy))

    def column(self, q):
        return self.parts.at[:, q, self.core] if self.whole else self.parts.at[:, q]

    def half(self, ref, which):
        if which:
            return ref.at[:, :, pl.ds(self.cut, ref.shape[-1] - self.cut)]
        return ref.at[:, :, pl.ds(0, self.cut)]

    def merge(self, q):
        if self.whole:
            core = self.core

            @pl.loop(0, LINES)
            def _(n):
                self.parts[n, q, core] = self.parts[n, q, core] + self.from_sib[n, q]

    def start(self):
        if self.whole:
            theirs = self.parts.at[:, :, 1 - self.core]
            self.sib = self.send(theirs, self.from_sib, sibling(self.g))

    def corner(self):
        if self.whole:
            self.sib.wait_recv()
        q = along_y(along_x(self.g)) // 2
        self.merge(q)
        far = self.column(q)
        self.to_y = self.send(self.half(far, 0), self.cy, along_y(self.g))
        self.to_x = self.send(self.half(far, 1), self.cx, along_x(self.g))

    def side(self, gy, came, corner, which, target):
        q = gy // 2
        self.merge(q)
        came.wait_recv()
        column = self.column(q)
        cols = slice(self.cut, None) if which else slice(0, self.cut)

        @pl.loop(0, LINES)
        def _(n):
            column[n, :, cols] = column[n, :, cols] + corner[n]

        return self.send(column, target, gy)

    def side_x(self):
        self.by_x = self.side(along_x(self.g), self.to_y, self.cy, 0, self.fx)

    def side_y(self):
        self.by_y = self.side(along_y(self.g), self.to_x, self.cx, 1, self.fy)

    def line(self):
        self.merge(self.chip)
        self.by_x.wait_recv()
        self.by_y.wait_recv()
        column = self.column(self.chip)
        for n in (3, 2, 1):
            there = self.lines.places[n]
            self.fx[there] = (
                column[there].astype(F32)
                + self.fx[there].astype(F32)
                + self.fy[there].astype(F32)
            ).astype(BF16)
            self.lines.step(n)
        z = self.z
        self.lines.clear()
        self.fz[z] = jnp.zeros(self.fz.shape[1:], BF16)
        self.out[...] = column[z].astype(F32) + self.fx[z].astype(F32) + self.fy[z].astype(F32)

    def relay(self):
        self.lines.relay()

    def finish(self):
        self.lines.finish()
        self.out[...] += sum_slots(self.fz)


class FoldSplit(Fold):
    summed = False

    def line(self):
        self.merge(self.chip)
        self.by_x.wait_recv()
        self.by_y.wait_recv()
        column = self.column(self.chip)
        self.zs = []
        for k in (2, 1, 3, 0):
            there = turn(self.z, k) if k else self.z
            found = (
                column[there].astype(F32)
                + self.fx[there].astype(F32)
                + self.fy[there].astype(F32)
            ).astype(BF16)
            if k:
                self.fx[there] = found
                self.zs.append(
                    self.wires.send(self.fx.at[there], self.fz.at[self.z], (there, self.g))
                )
            else:
                self.fz[self.z] = found

    def finish(self):
        for copy in self.zs:
            copy.wait_recv()
        width = self.fz.shape[-1]
        for place in range(LINES):
            self.out[:, place * width : (place + 1) * width] = self.fz[place].astype(F32)


def fold_scratch(rows, cols, whole, split=False):
    cut = 256 if split else cols // 2
    return [
        pltpu.VMEM((LINES, PLANE, rows, cols) if whole else (1, 1, 16, 128), BF16),
        pltpu.VMEM((LINES, rows, cols - cut), BF16),
        pltpu.VMEM((LINES, rows, cut), BF16),
        pltpu.VMEM((LINES, rows, cols), BF16),
        pltpu.VMEM((LINES, rows, cols), BF16),
        pltpu.VMEM((LINES, rows, cols), BF16),
        pltpu.VMEM((rows, cols), BF16),
    ]


FOLD = 7


def fold_sems(whole):
    return (1 if whole else 0) + 4 + LINES


class FoldSteps:
    def __init__(self, wires, parts, scratch, out):
        self.wires, self.parts, self.out = wires, parts, out
        _, self.cx, self.cy, self.fx, self.fy, self.fz, relayed = scratch
        self.z, self.g, self.chip, _ = here()
        self.width = parts.shape[-1] // 2
        self.lines = SumLine(wires, self.fx, self.fz, relayed)
        self.zs = self.lines.places
        self.to_x, self.to_y, self.by_x, self.by_y = {}, {}, {}, {}

    def half(self, n, q, which):
        return self.parts.at[self.zs[n], q, :, pl.ds(which * self.width, self.width)]

    def corner(self, n):
        far = along_y(along_x(self.g)) // 2
        place = self.zs[n]
        self.to_y[n] = self.wires.send(
            self.half(n, far, 0), self.cy.at[place], (self.z, along_y(self.g))
        )
        self.to_x[n] = self.wires.send(
            self.half(n, far, 1), self.cx.at[place], (self.z, along_x(self.g))
        )

    def side(self, n, gy, came, corner, which, target):
        came.wait_recv()
        q, place = gy // 2, self.zs[n]
        cols = slice(which * self.width, (which + 1) * self.width)
        self.parts[place, q, :, cols] = self.parts[place, q, :, cols] + corner[place]
        return self.wires.send(self.parts.at[place, q], target.at[place], (self.z, gy))

    def side_x(self, n):
        self.by_x[n] = self.side(n, along_x(self.g), self.to_y[n], self.cy, 0, self.fx)

    def side_y(self, n):
        self.by_y[n] = self.side(n, along_y(self.g), self.to_x[n], self.cx, 1, self.fy)

    def line(self, n):
        self.by_x[n].wait_recv()
        self.by_y[n].wait_recv()
        place = self.zs[n]
        found = (
            self.parts[place, self.chip].astype(F32)
            + self.fx[place].astype(F32)
            + self.fy[place].astype(F32)
        )
        if n == 0:
            self.out[...] = found
            self.lines.clear()
            self.fz[self.z] = jnp.zeros(self.fz.shape[1:], BF16)
        else:
            self.fx[place] = found.astype(BF16)
            self.lines.step(n)

    def relay(self):
        self.lines.relay()

    def finish(self):
        self.lines.finish()
        self.out[...] += sum_slots(self.fz)


STEP_SEMS = 16 + LINES


def layer_norm(row_block, gain_row):
    row_mean = jnp.mean(row_block, axis=-1, keepdims=True)
    centred = row_block - row_mean
    variance = jnp.mean(centred * centred, axis=-1, keepdims=True)
    return centred * lax.rsqrt(variance + NORM_STABILIZER) * gain_row


def product(left_side, right_side):
    return jnp.dot(left_side, right_side, preferred_element_type=jnp.float32)


def inner_first(left_side, right_side):
    return lax.dot_general(
        left_side, right_side, (((0,), (0,)), ((), ())), preferred_element_type=jnp.float32
    )


def inner_last(left_side, right_side):
    return lax.dot_general(
        left_side, right_side, (((1,), (1,)), ((), ())), preferred_element_type=jnp.float32
    )


def collect(onehot_rows, value_rows):
    return lax.dot_general(
        onehot_rows,
        value_rows,
        (((0,), (0,)), ((), ())),
        precision=lax.Precision.HIGHEST,
        preferred_element_type=jnp.float32,
    )


def plain_device(
    media,
    latents,
    frame_counts,
    time_index,
    valid,
    time_table,
    media_gain,
    latent_gain,
    ffn_gain,
    w_query,
    w_key,
    w_value,
    w_out,
    w_up,
    w_down,
    cotangent,
):
    frames = time_index.shape[0]
    patches = valid.shape[0] // frames
    latent_rows = latents.shape[0]
    model_width = latents.shape[1]
    head_size = model_width // H
    score_scale = head_size ** (-0.5)
    across = lax.axis_size("gx")
    column = lax.axis_index("gx")
    row_index = lax.axis_index("gy")
    frame_ends = jnp.cumsum(frame_counts[row_index])
    position = column * frames + jnp.arange(frames, dtype=jnp.int32)
    item_index = jnp.sum((frame_ends[None, :] <= position[:, None]).astype(jnp.int32), axis=1)
    item_onehot = (item_index[:, None] == jnp.arange(across, dtype=jnp.int32)[None, :]).astype(
        jnp.float32
    )
    (
        full_query,
        full_key,
        full_value,
        full_out,
        full_up,
        full_down,
        full_media_gain,
        full_latent_gain,
        full_ffn_gain,
        full_time,
    ) = (
        lax.all_gather(w_query, ("gx", "gy"), axis=0, tiled=True),
        lax.all_gather(w_key, ("gx", "gy"), axis=0, tiled=True),
        lax.all_gather(w_value, ("gx", "gy"), axis=0, tiled=True),
        lax.all_gather(w_out, ("gx", "gy"), axis=0, tiled=True),
        lax.all_gather(w_up, ("gx", "gy"), axis=0, tiled=True),
        lax.all_gather(w_down, ("gx", "gy"), axis=0, tiled=True),
        lax.all_gather(media_gain, ("gx", "gy"), axis=0, tiled=True),
        lax.all_gather(latent_gain, ("gx", "gy"), axis=0, tiled=True),
        lax.all_gather(ffn_gain, ("gx", "gy"), axis=0, tiled=True),
        lax.all_gather(time_table, ("gx", "gy"), axis=1, tiled=True),
    )
    time_onehot = (
        time_index[:, None] == jnp.arange(full_time.shape[0], dtype=jnp.int32)[None, :]
    ).astype(jnp.float32)
    time_rows = product(time_onehot.astype(jnp.bfloat16), full_time)
    media_in = (
        media.astype(jnp.float32).reshape(frames, patches, model_width) + time_rows[:, None, :]
    ).reshape(-1, model_width)
    media_normed = layer_norm(media_in, full_media_gain.astype(jnp.float32)).astype(jnp.bfloat16)
    key_heads = (
        product(media_normed, full_key).astype(jnp.bfloat16).reshape(frames, patches, H, head_size)
    )
    value_heads = (
        product(media_normed, full_value)
        .astype(jnp.bfloat16)
        .reshape(frames, patches, H, head_size)
    )
    latent_in = latents.astype(jnp.float32)
    latent_normed = layer_norm(latent_in, full_latent_gain.astype(jnp.float32)).astype(jnp.bfloat16)
    own_query = product(latent_normed, full_query).astype(jnp.bfloat16)
    own_key = product(latent_normed, full_key).astype(jnp.bfloat16)
    own_value = product(latent_normed, full_value).astype(jnp.bfloat16)
    valid_total = lax.psum(jnp.sum(valid.astype(jnp.float32)), ("gx", "gy"))
    coefficient = ENTROPY_WEIGHT * (valid.shape[0] * lax.axis_size(("gx", "gy"))) / valid_total
    query_table = lax.all_gather(own_query, "gx", axis=0, tiled=True)
    picked = query_table.reshape(-1, latent_rows, H, head_size)[item_index]
    media_score = (
        jnp.einsum("flhd,fphd->flhp", picked, key_heads, preferred_element_type=jnp.float32)
        * score_scale
    )
    valid_mask = valid.reshape(frames, 1, 1, patches) > 0
    media_expo = jnp.where(valid_mask, jnp.exp(media_score), 0.0)
    expo_low = media_expo.astype(jnp.bfloat16)
    media_total = jnp.sum(media_expo, axis=-1)
    media_moment = jnp.sum(media_expo * media_score, axis=-1)
    media_weighted = jnp.einsum(
        "flhp,fphd->flhd", expo_low, value_heads, preferred_element_type=jnp.float32
    )
    dense_weighted = collect(item_onehot, media_weighted.reshape(frames, -1)).reshape(
        -1, model_width
    )
    dense_total = collect(item_onehot, media_total.reshape(frames, -1)).reshape(-1, H)
    dense_moment = collect(item_onehot, media_moment.reshape(frames, -1)).reshape(-1, H)
    got_weighted, got_total, got_moment = (
        lax.psum_scatter(dense_weighted, "gx", scatter_dimension=0, tiled=True),
        lax.psum_scatter(dense_total, "gx", scatter_dimension=0, tiled=True),
        lax.psum_scatter(dense_moment, "gx", scatter_dimension=0, tiled=True),
    )
    query_head_count = own_query.reshape(latent_rows, H, head_size)
    latent_key_rows = own_key.reshape(latent_rows, H, head_size)
    latent_value_rows = own_value.reshape(latent_rows, H, head_size)
    latent_score = (
        jnp.einsum(
            "uer,zer->uez", query_head_count, latent_key_rows, preferred_element_type=jnp.float32
        )
        * score_scale
    )
    latent_expo = jnp.exp(latent_score)
    latent_reduced_precision = latent_expo.astype(jnp.bfloat16)
    weighted = got_weighted.reshape(latent_rows, H, head_size) + jnp.einsum(
        "nwr,rwb->nwb",
        latent_reduced_precision,
        latent_value_rows,
        preferred_element_type=jnp.float32,
    )
    totals = got_total + jnp.sum(latent_expo, axis=-1)
    moment = got_moment + jnp.sum(latent_expo * latent_score, axis=-1)
    attention = weighted / totals[..., None]
    attn_low = attention.reshape(latent_rows, model_width).astype(jnp.bfloat16)
    middle = latent_in + product(attn_low, full_out)
    ffn_normed = layer_norm(middle, full_ffn_gain.astype(jnp.float32)).astype(jnp.bfloat16)
    up_rows = product(ffn_normed, full_up)
    hidden = jax.nn.gelu(up_rows, approximate=False).astype(jnp.bfloat16)
    new_latents = (middle + product(hidden, full_down)).astype(jnp.bfloat16)
    (
        back_query,
        back_key,
        back_value,
        back_out,
        back_up,
        back_down,
        back_media_gain,
        back_latent_gain,
        back_ffn_gain,
    ) = (
        lax.all_gather(w_query, ("gx", "gy"), axis=0, tiled=True),
        lax.all_gather(w_key, ("gx", "gy"), axis=0, tiled=True),
        lax.all_gather(w_value, ("gx", "gy"), axis=0, tiled=True),
        lax.all_gather(w_out, ("gx", "gy"), axis=0, tiled=True),
        lax.all_gather(w_up, ("gx", "gy"), axis=0, tiled=True),
        lax.all_gather(w_down, ("gx", "gy"), axis=0, tiled=True),
        lax.all_gather(media_gain, ("gx", "gy"), axis=0, tiled=True),
        lax.all_gather(latent_gain, ("gx", "gy"), axis=0, tiled=True),
        lax.all_gather(ffn_gain, ("gx", "gy"), axis=0, tiled=True),
    )
    owned_latent, owned_attn, owned_ffn, owned_hidden = (
        lax.all_to_all(latent_normed, ("gx", "gy"), split_axis=1, concat_axis=0, tiled=True),
        lax.all_to_all(attn_low, ("gx", "gy"), split_axis=1, concat_axis=0, tiled=True),
        lax.all_to_all(ffn_normed, ("gx", "gy"), split_axis=1, concat_axis=0, tiled=True),
        lax.all_to_all(hidden, ("gx", "gy"), split_axis=1, concat_axis=0, tiled=True),
    )
    hidden_grad = inner_last(cotangent, back_down)
    gelu_pull = jax.vjp(partial(jax.nn.gelu, approximate=False), up_rows)[1]
    up_grad = gelu_pull(hidden_grad)[0].astype(jnp.bfloat16)
    ffn_normed_grad = inner_last(up_grad, back_up)
    ffn_pull = jax.vjp(layer_norm, middle, back_ffn_gain.astype(jnp.float32))[1]
    middle_part, grad_ffn_gain = ffn_pull(ffn_normed_grad)
    middle_grad = cotangent.astype(jnp.float32) + middle_part
    middle_low = middle_grad.astype(jnp.bfloat16)
    attn_grad = inner_last(middle_low, back_out).reshape(latent_rows, H, head_size)
    weighted_sum_gradient = (attn_grad / totals[..., None]).astype(jnp.bfloat16)
    slope_term = -coefficient / totals
    shift_term = (
        -jnp.sum(attn_grad * attention, axis=-1) / totals
        + coefficient * (1.0 / totals + moment / (totals * totals))
        + slope_term
    )
    latent_mix = jnp.einsum(
        "uer,zer->uez", weighted_sum_gradient, latent_value_rows, preferred_element_type=jnp.float32
    )
    latent_sgrad = latent_expo * (
        latent_mix + shift_term[..., None] + slope_term[..., None] * latent_score
    )
    latent_residual_gradient = (latent_sgrad * score_scale).astype(jnp.bfloat16)
    query_part = jnp.einsum(
        "nwr,rwb->nwb",
        latent_residual_gradient,
        latent_key_rows,
        preferred_element_type=jnp.float32,
    )
    own_key_grad = (
        jnp.einsum(
            "zry,zrj->yrj",
            latent_residual_gradient,
            query_head_count,
            preferred_element_type=jnp.float32,
        )
        .astype(jnp.bfloat16)
        .reshape(latent_rows, model_width)
    )
    own_value_grad = (
        jnp.einsum(
            "zry,zrj->yrj",
            latent_reduced_precision,
            weighted_sum_gradient,
            preferred_element_type=jnp.float32,
        )
        .astype(jnp.bfloat16)
        .reshape(latent_rows, model_width)
    )
    grad_table = lax.all_gather(
        weighted_sum_gradient.reshape(latent_rows, model_width), "gx", axis=0, tiled=True
    )
    shift_table, slope_table = (
        lax.all_gather(shift_term, "gx", axis=0, tiled=True),
        lax.all_gather(slope_term, "gx", axis=0, tiled=True),
    )
    picked_grad = grad_table.reshape(-1, latent_rows, H, head_size)[item_index]
    picked_shift = shift_table.reshape(-1, latent_rows, H)[item_index]
    picked_slope = slope_table.reshape(-1, latent_rows, H)[item_index]
    media_mix = jnp.einsum(
        "flhd,fphd->flhp", picked_grad, value_heads, preferred_element_type=jnp.float32
    )
    media_sgrad = media_expo * (
        media_mix + picked_shift[..., None] + picked_slope[..., None] * media_score
    )
    media_rgrad = (media_sgrad * score_scale).astype(jnp.bfloat16)
    query_terms = jnp.einsum(
        "flhp,fphd->flhd", media_rgrad, key_heads, preferred_element_type=jnp.float32
    )
    dense_query = collect(item_onehot, query_terms.reshape(frames, -1)).reshape(-1, model_width)
    got_query = lax.psum_scatter(
        dense_query.astype(jnp.bfloat16), "gx", scatter_dimension=0, tiled=True
    ).astype(jnp.float32)
    media_key_grad = (
        jnp.einsum("flhp,flhd->fphd", media_rgrad, picked, preferred_element_type=jnp.float32)
        .astype(jnp.bfloat16)
        .reshape(-1, model_width)
    )
    media_value_grad = (
        jnp.einsum("flhp,flhd->fphd", expo_low, picked_grad, preferred_element_type=jnp.float32)
        .astype(jnp.bfloat16)
        .reshape(-1, model_width)
    )
    grad_key = inner_first(media_normed, media_key_grad) + inner_first(latent_normed, own_key_grad)
    grad_value = inner_first(media_normed, media_value_grad) + inner_first(
        latent_normed, own_value_grad
    )
    media_normed_grad = inner_last(media_key_grad, back_key) + inner_last(
        media_value_grad, back_value
    )
    media_pull = jax.vjp(layer_norm, media_in, back_media_gain.astype(jnp.float32))[1]
    media_grad, grad_media_gain = media_pull(media_normed_grad)
    frame_sums = jnp.sum(media_grad.reshape(frames, patches, model_width), axis=1)
    grad_time = collect(time_onehot, frame_sums)
    query_grad = (
        (got_query.reshape(latent_rows, H, head_size) + query_part)
        .astype(jnp.bfloat16)
        .reshape(latent_rows, model_width)
    )
    latent_normed_grad = (
        inner_last(query_grad, back_query)
        + inner_last(own_key_grad, back_key)
        + inner_last(own_value_grad, back_value)
    )
    latent_pull = jax.vjp(layer_norm, latent_in, back_latent_gain.astype(jnp.float32))[1]
    latent_part, grad_latent_gain = latent_pull(latent_normed_grad)
    latents_grad = middle_grad + latent_part
    piece_query = lax.all_gather(query_grad, ("gx", "gy"), axis=0, tiled=True)
    piece_middle = lax.all_gather(middle_low, ("gx", "gy"), axis=0, tiled=True)
    piece_up = lax.all_gather(up_grad, ("gx", "gy"), axis=0, tiled=True)
    piece_cot = lax.all_gather(cotangent, ("gx", "gy"), axis=0, tiled=True)
    shard_query = inner_first(owned_latent, piece_query)
    shard_out = inner_first(owned_attn, piece_middle)
    shard_up = inner_first(owned_ffn, piece_up)
    shard_down = inner_first(owned_hidden, piece_cot)
    shard_grads = (
        lax.psum_scatter(grad_key, ("gx", "gy"), scatter_dimension=0, tiled=True),
        lax.psum_scatter(grad_value, ("gx", "gy"), scatter_dimension=0, tiled=True),
        lax.psum_scatter(grad_media_gain, ("gx", "gy"), scatter_dimension=0, tiled=True),
        lax.psum_scatter(grad_latent_gain, ("gx", "gy"), scatter_dimension=0, tiled=True),
        lax.psum_scatter(grad_ffn_gain, ("gx", "gy"), scatter_dimension=0, tiled=True),
        lax.psum_scatter(grad_time, ("gx", "gy"), scatter_dimension=1, tiled=True),
    )
    return (
        new_latents,
        media_grad,
        latents_grad,
        shard_grads[5],
        shard_grads[2],
        shard_grads[3],
        shard_grads[4],
        shard_query,
        shard_grads[0],
        shard_grads[1],
        shard_out,
        shard_up,
        shard_down,
    )


GROUP = 4


def mates_of(z, chip, core):
    mates = []
    for j in range(1, 16):
        there = (4 * z + chip + j) % 16
        mates.append((there // 4, 2 * (there % 4) + core))
    return mates


class GiveBack:
    def __init__(self, wires, up_part, down_part, scratch, up_out, down_out):
        self.wires, self.up_part, self.down_part = wires, up_part, down_part
        self.up_out, self.down_out = up_out, down_out
        self.up_near, self.down_near, self.up_got = scratch
        self.z, self.g, self.chip, self.core = here()
        self.places = up_places(self.z, self.chip)

    def first(self):
        near = (self.z, sibling(self.g))
        theirs = 1 - self.core
        self.up = self.wires.send(self.up_part.at[:, :, theirs], self.up_near, near)
        self.down = self.wires.send(self.down_part.at[theirs], self.down_near, near)

    def columns(self):
        self.up.wait_recv()
        core = self.core

        @pl.loop(0, LINES)
        def _(n):
            for q in range(PLANE):
                self.up_part[n, q, core] = self.up_part[n, q, core] + self.up_near[n, q]

        self.moved = []
        for there, _ in self.places:
            self.moved.append(
                self.wires.send(
                    self.up_part.at[there[0], there[1], core],
                    self.up_got.at[self.z, self.chip],
                    (there[0], 2 * there[1] + core),
                )
            )
        self.up_got[self.z, self.chip] = self.up_part[self.z, self.chip, core]

    def rows(self):
        self.down.wait_recv()
        rows = self.down_out.shape[0] // 8
        core = self.core

        @pl.loop(0, 8)
        def _(n):
            block = pl.ds(pl.multiple_of(n * rows, 8), rows)
            self.down_out[block] = self.down_part[core, block] + self.down_near[block]

    def finish(self):
        for copy in self.moved:
            copy.wait_recv()
        width = self.up_got.shape[-1]
        for n in range(LINES):
            for q in range(PLANE):
                first = (n * PLANE + q) * width
                self.up_out[:, first : first + width] = self.up_got[n, q].astype(F32)


GIVE_SEMS = 17


class Total:
    def __init__(self, wires, mine, out, sums, got):
        self.wires, self.out, self.sums, self.got = wires, out, sums, got
        self.z, self.g, _, _ = here()
        self.source = mine
        self.step = 0

    def push(self):
        sides = [sibling(self.g), along_x(self.g), along_y(self.g)]
        if self.step < 3:
            self.copies = [
                self.wires.send(self.source, self.got.at[self.step], (self.z, sides[self.step]))
            ]
        else:
            self.copies = [
                self.wires.send(self.source, self.got.at[3 + k], device)
                for k, device in enumerate(line_of(self.z, self.g))
            ]

    def pull(self):
        for copy in self.copies:
            copy.wait_recv()
        if self.step < 3:
            self.sums[self.step] = self.source[...] + self.got[self.step]
            self.source = self.sums.at[self.step]
            self.step += 1
        else:
            self.out[...] = self.source[...] + self.got[3] + self.got[4] + self.got[5]


def head_masks(rows, width, head_size):
    lane = lax.broadcasted_iota(jnp.int32, (rows, width), 1)
    return [(lane >= h * head_size) & (lane < (h + 1) * head_size) for h in range(GROUP)]


def stacked(block, masks):
    zero = jnp.zeros_like(block)
    return jnp.concatenate([jnp.where(mask, block, zero) for mask in masks], axis=0)


def unstacked(block, masks):
    rows = block.shape[0] // GROUP
    total = jnp.where(masks[0], block[:rows], 0.0)
    for h in range(1, GROUP):
        total = jnp.where(masks[h], block[h * rows : (h + 1) * rows], total)
    return total


def dot_last(a, b):
    return lax.dot_general(a, b, (((1,), (1,)), ((), ())), preferred_element_type=F32)


def dot_first(a, b):
    return lax.dot_general(a, b, (((0,), (0,)), ((), ())), preferred_element_type=F32)


def spread_heads(columns, first, masks):
    out = jnp.where(masks[0], columns[:, first : first + 1], 0.0)
    for h in range(1, GROUP):
        out = jnp.where(masks[h], columns[:, first + h : first + h + 1], out)
    return out


def attend(queries, keys, values, valid, scale, masks):
    rows = queries.shape[0]
    score = dot_last(stacked(queries, masks), keys) * scale
    expo = jnp.exp(score)
    if valid is not None:
        expo = jnp.where(valid > 0, expo, 0.0)
    totals = jnp.sum(expo, axis=1, keepdims=True)
    moments = jnp.sum(expo * score, axis=1, keepdims=True)
    weighted = jnp.dot(expo.astype(BF16), values, preferred_element_type=F32)
    heads = [(totals[h * rows : (h + 1) * rows], moments[h * rows : (h + 1) * rows]) for h in range(GROUP)]
    return unstacked(weighted, masks), heads


def put_heads(heads, group, lane):
    out = jnp.zeros(lane.shape, F32)
    for h, (total, moment) in enumerate(heads):
        out = jnp.where(lane == group * GROUP + h, total, out)
        out = jnp.where(lane == H + group * GROUP + h, moment, out)
    return out


def assemble(smalls, out):
    count, rows, lanes = smalls.shape
    shard = out.shape[1] // count
    block = 8
    row = lax.broadcasted_iota(jnp.int32, (block * lanes, block * shard), 0)
    col = lax.broadcasted_iota(jnp.int32, (block * lanes, block * shard), 1)
    lane = row % lanes
    chosen = ((row // lanes) * shard + lane == col) & (lane < shard)
    place = jnp.where(chosen, 1.0, 0.0).astype(BF16)
    for n in range(count // block):
        pieces = jnp.concatenate([smalls[n * block + d] for d in range(block)], axis=1)
        out[:, n * block * shard : (n + 1) * block * shard] = jnp.dot(
            pieces.astype(BF16), place, preferred_element_type=F32
        )


def up_places(z, chip):
    places = []
    for dz in range(LINES):
        for dx, dy in ((0, 0), (1, 0), (0, 1), (1, 1)):
            if dz or dx or dy:
                x, y = chip % 2, chip // 2
                there = (y + dy) % 2 * 2 + (x + dx) % 2
                places.append(((turn(z, dz), there), (turn(z, LINES - dz) if dz else z, there)))
    return places


def shares(counts_ref, z, g, frame, frames, items):
    position = z * frames + frame
    end, slot = 0, 0
    for item in range(items):
        end = end + counts_ref[g, item]
        slot = slot + jnp.where(end <= position, 1, 0)
    return [jnp.where(slot == item, 1.0, 0.0) for item in range(items)]


def put_times(out, tables, times_ref, frames):
    for frame in range(frames):
        row = jnp.zeros((1, out.shape[1]), F32)
        for t in range(8):
            row = row + jnp.where(times_ref[frame] == t, 1.0, 0.0) * tables[t : t + 1]
        out[frame : frame + 1] = row


def opening_kernel(scale, *refs):
    (
        time_table_ref,
        media_gain_ref,
        latent_gain_ref,
        ffn_gain_ref,
        key_shard,
        value_shard,
        query_shard,
        out_shard,
        latents_ref,
        up_ref,
        down_ref,
        cot_ref,
        media_ref,
        valid_ref,
        counts_ref,
        times_ref,
        tables_out,
        counts_out,
        key_weight_out,
        value_weight_out,
        query_weight_out,
        out_weight_out,
        up_out,
        down_out,
        cot_out,
        normed_out,
        keys_out,
        values_out,
        table_out,
        line_normed_out,
        got_weighted,
        got_stats,
        own_weighted,
        own_stats,
        send_sems,
        recv_sems,
        local_sems,
        up_own,
        small_ref,
        smalls,
        key_weight,
        value_weight,
        query_weight,
        line_latents,
        line_normed,
        normed,
        keys,
        values,
        own_table,
        table,
        time_rows,
        sums,
        weighted,
        stats,
    ) = refs
    z, g, chip, core = here()
    here_chip = 4 * z + chip
    me = 2 * here_chip + core
    items, rows, width = line_latents.shape
    frames, _, patches = valid_ref.shape
    shard = key_shard.shape[0]
    span = width // (H // GROUP)
    up_width = up_out.shape[-1]
    near = (z, sibling(g))
    places = up_places(z, chip)
    greet([(there[0], 2 * there[1] + core) for there, _ in places] + [near])
    wires = Wires(send_sems, recv_sems)
    masks = head_masks(rows, span, span // GROUP)
    lane = lax.broadcasted_iota(jnp.int32, (rows, 128), 1)
    local = []
    small_ref[...] = jnp.zeros_like(small_ref)
    for place, source in (
        (slice(0, 8), time_table_ref),
        (slice(8, 9), media_gain_ref),
        (slice(9, 10), latent_gain_ref),
        (slice(10, 11), ffn_gain_ref),
    ):
        small_ref[place, :shard] = source[...].astype(F32)
    found = valid_ref[0].astype(F32)
    for n in range(1, frames):
        found = found + valid_ref[n].astype(F32)
    small_ref[11:12] = jnp.sum(found, axis=1, keepdims=True) + jnp.zeros((1, 128), F32)

    def keep(source, target):
        copy = pltpu.make_async_copy(source, target, local_sems.at[len(local)])
        copy.start()
        local.append(copy)
        return copy

    def rows_of(ref):
        return lambda zz, gg: ref.at[pl.ds(pl.multiple_of((zz * 8 + gg) * shard, 16), shard)]

    def piece(place):
        return up_ref.at[:, pl.ds(pl.multiple_of((4 * place[0] + place[1]) * up_width, 128), up_width)]

    def whole(source, slot):
        return Spread(wires, source, slot, columns_half, True), keep(source, slot(z, g))

    def small_slot(zz, gg):
        return smalls.at[zz * 8 + gg]

    small = Spread(wires, small_ref, small_slot, rows_half, True)
    small_kept = keep(small_ref, small_slot(z, g))
    key, key_kept = whole(key_shard, rows_of(key_weight))
    value, value_kept = whole(value_shard, rows_of(value_weight))
    query = Spread(wires, query_shard, rows_of(query_weight), rows_parts, True, True)
    query_kept = keep(piece_of(query_shard, z), rows_of(query_weight)(z, g))
    query_line = Line(wires, own_table, lambda zz: table.at[zz])
    out, out_kept = whole(out_shard, rows_of(out_weight_out))
    cot = Spread(wires, cot_ref, lambda zz, gg: cot_out.at[zz * 4 + gg // 2], columns_half, False)
    line = Line(wires, latents_ref, lambda zz: line_latents.at[zz])
    exchange = Exchange(
        wires,
        [(weighted, got_weighted), (stats, got_stats)],
    )
    line_kept = keep(latents_ref, line_latents.at[z])
    up_load = keep(piece((z, chip)), up_own)
    late = [
        out_kept,
        keep(cot_ref, cot_out.at[here_chip]),
        keep(down_ref, down_out.at[core]),
    ]
    prompt = len(local)
    moved, given, down = [], [], []
    chunk = 32

    def normalise(first, last):
        @pl.loop(first, last)
        def _(n):
            block = pl.ds(pl.multiple_of(n * chunk, chunk), chunk)
            frame = n // (patches // chunk)
            row = media_ref[block].astype(F32) + time_rows[pl.ds(frame, 1)]
            normed[block] = layer_norm(row, tables_out[8:9]).astype(BF16)

    def normalise_latents():
        gain = tables_out[9:10]
        line_kept.wait()
        for item in range(items):

            @pl.loop(0, rows // chunk)
            def _(n):
                block = pl.ds(pl.multiple_of(n * chunk, chunk), chunk)
                row = line_latents[item, block].astype(F32)
                line_normed[item, block] = layer_norm(row, gain).astype(BF16)

        normed[frames * patches :] = line_normed[z]

    def tabulate():
        small_kept.wait()
        assemble(smalls, tables_out)
        counts = smalls[0, 8:]
        for n in range(1, smalls.shape[0]):
            counts = counts + smalls[n, 8:]
        counts_out[...] = counts
        put_times(time_rows, tables_out, times_ref, frames)

    def project(left, weight, out, first):
        @pl.loop(first, first + 2)
        def _(n):
            cols = pl.ds(pl.multiple_of(n * span, 128), span)
            out[:, cols] = jnp.dot(
                left[...], weight[:, cols], preferred_element_type=F32
            ).astype(BF16)

    def project_keys(first):
        if first == 0:
            key_kept.wait()
            keep(key_weight, key_weight_out)
            keep(normed, normed_out)
        project(normed, key_weight, keys, first)
        if first > 0:
            keep(keys, keys_out)

    def project_values(first):
        if first == 0:
            value_kept.wait()
            keep(value_weight, value_weight_out)
        project(normed, value_weight, values, first)
        if first > 0:
            keep(values, values_out)

    def project_queries():
        query_kept.wait()
        keep(query_weight, query_weight_out)
        for item in range(items):
            own_table[item] = jnp.dot(
                line_normed[item], query_weight[...], preferred_element_type=F32
            ).astype(BF16)
        table[z] = own_table[...]
        query_line.first()

    def attend_own():
        keep(table, table_out)
        keep(line_normed, line_normed_out)
        sums[...] = jnp.zeros_like(sums)
        stats[...] = jnp.zeros_like(stats)
        last = slice(frames * patches, frames * patches + rows)
        own = jnp.zeros((rows, 128), F32)
        for group in range(H // GROUP):
            cols = slice(group * span, (group + 1) * span)
            part, heads = attend(
                table[group, z], keys[last, cols], values[last, cols], None, scale, masks
            )
            own_weighted[:, cols] = part
            own = own + put_heads(heads, group, lane)
        own_stats[...] = own

    def attend_frames(first, last):
        @pl.loop(first, last)
        def _(frame):
            share = shares(counts_ref, z, g, frame, frames, items)
            block = pl.ds(pl.multiple_of(frame * patches, patches), patches)
            valid = valid_ref[frame]
            found = jnp.zeros((rows, 128), F32)
            for group in range(H // GROUP):
                cols = slice(group * span, (group + 1) * span)
                chosen = share[0] * table[group, 0].astype(F32)
                for item in range(1, items):
                    chosen = chosen + share[item] * table[group, item].astype(F32)
                part, heads = attend(
                    chosen.astype(BF16), keys[block, cols], values[block, cols], valid, scale, masks
                )
                found = found + put_heads(heads, group, lane)
                for item in range(items):
                    sums[item, :, cols] += share[item] * part
            for item in range(items):
                stats[item] += share[item] * found

    def down_first():
        down.append(wires.send(down_ref, down_out.at[core], near))

    def up_first():
        up_load.wait()
        keep(up_own, up_out.at[me])
        given.append(wires.send(up_own, up_out.at[me], near))
        for there, _ in places:
            moved.append(
                wires.send(piece(there), up_out.at[me], (there[0], 2 * there[1] + core))
            )

    def up_last():
        for n, (_, origin) in enumerate(places):
            moved[n].wait_recv()
            held = up_out.at[2 * (4 * origin[0] + origin[1]) + core]
            given.append(wires.send(held, held, near))
        for copy in given:
            copy.wait_recv()

    def sums_first():
        weighted[...] = sums[...].astype(BF16)
        exchange.first()

    small.first()
    out.first()
    small.column(0)
    key.first()
    out.column(0)
    query.first()
    small.column(1)
    value.first()
    small.corner_y(1)
    key.corner_x(0)
    key.column(0)
    small.corner_x(2)
    small.column(2)
    key.column(1)
    key.corner_y(0)
    query.column(0)
    line.first()
    value.column(0)
    cot.first()
    small.corner_y(2)
    query.corner_y(0)
    small.corner_x(0)
    out.column(1)
    query.column(1)
    small.corner_x(3)
    small.corner_y(0)
    out.corner_y(0)
    query.corner_x(0)
    value.column(1)
    key.column(2)
    line.take(0)
    small.corner_x(1)
    small.corner_y(3)
    query.corner_y(1)
    query.corner_x(1)
    value.corner_x(1)
    query.corner_x(2)
    out.corner_y(2)
    value.corner_x(2)
    key.corner_x(1)
    query.column(2)
    out.column(2)
    query.corner_y(2)
    value.corner_y(0)
    query.last(1)
    value.corner_y(2)
    small.last(3)
    small.last(0)
    small.last(1)
    key.last(0)
    small.last(2)
    key.corner_y(1)
    query.corner_x(3)
    cot.column(0)
    value.column(2)
    value.last(2)
    small.finish()
    query.corner_y(3)
    key.corner_y(3)
    value.corner_x(0)
    tabulate()
    line.take(1)
    key.corner_x(3)
    key.corner_y(2)
    key.corner_x(2)
    line.take(2)
    value.corner_y(1)
    cot.column(1)
    normalise_latents()
    normalise(0, 8)
    down_first()
    query.last(2)
    query.last(0)
    cot.corner_x(0)
    query.last(3)
    normalise(8, 16)
    value.corner_x(3)
    out.corner_x(1)
    key.last(3)
    value.corner_y(3)
    query.finish()
    project_queries()
    cot.corner_y(1)
    value.last(1)
    key.last(2)
    key.last(1)
    out.corner_x(2)
    out.corner_x(0)
    cot.corner_x(2)
    key.finish()
    out.corner_y(1)
    cot.column(2)
    value.last(0)
    up_first()
    out.corner_x(3)
    value.last(3)
    project_keys(0)
    project_keys(2)
    value.finish()
    cot.corner_x(1)
    query_line.take(0)
    project_values(0)
    out.last(0)
    cot.corner_x(3)
    project_values(2)
    query_line.take(1)
    query_line.take(2)
    down[0].wait_recv()
    attend_own()
    attend_frames(0, 2)
    attend_frames(2, 4)
    sums_first()
    cot.corner_y(2)
    cot.corner_y(0)
    cot.last(0)
    out.last(1)
    out.corner_y(3)
    cot.corner_y(3)
    out.last(3)
    out.last(2)
    cot.last(2)
    up_last()
    cot.last(3)
    out.finish()
    cot.last(1)
    exchange.finish()
    for copy in late + local[prompt:]:
        copy.wait()
    wires.drain()


def opening(scale, small, weights, latents, w_up, w_down, cotangent, media, valid, counts, times):
    rows, width = latents.shape
    shard = weights[0].shape[0]
    up_rows, up_width = w_up.shape
    all_rows = media.shape[0] + rows
    wires = 5 * spread_sems(True) + spread_sems(False) + 2 * LINE_SEMS + 31 + 1 + 2 * LINES
    span = width // LINES
    square = jax.ShapeDtypeStruct((width, width), BF16)
    table = jax.ShapeDtypeStruct((LINES, rows, width), BF16)
    keys = jax.ShapeDtypeStruct((all_rows, width), BF16)
    smem = pl.BlockSpec(memory_space=pltpu.SMEM)
    return pl.pallas_call(
        partial(opening_kernel, scale),
        out_shape=[
            jax.ShapeDtypeStruct((16, width), F32),
            jax.ShapeDtypeStruct((8, 128), F32),
            square,
            square,
            jax.ShapeDtypeStruct((width, span), BF16),
            square,
            jax.ShapeDtypeStruct((32, up_rows, up_width // 16), BF16),
            jax.ShapeDtypeStruct((2,) + w_down.shape, BF16),
            jax.ShapeDtypeStruct((16,) + cotangent.shape, BF16),
            keys,
            keys,
            keys,
            jax.ShapeDtypeStruct((LINES, LINES, rows, span), BF16),
            table,
            table,
            jax.ShapeDtypeStruct((LINES, rows, 128), F32),
            jax.ShapeDtypeStruct((rows, width), F32),
            jax.ShapeDtypeStruct((rows, 128), F32),
        ],
        in_specs=[VMEM] * 8 + [LEFT] * 2 + [VMEM] * 4 + [smem] * 2,
        out_specs=[VMEM] * 2 + [LEFT] * 12 + [VMEM] * 4,
        scratch_shapes=[
            sems(wires),
            sems(wires),
            sems(24),
            pltpu.VMEM((up_rows, up_width // 16), BF16),
            pltpu.VMEM((16, 128), F32),
            pltpu.VMEM((32, 16, 128), F32),
            pltpu.VMEM((width, width), BF16),
            pltpu.VMEM((width, width), BF16),
            pltpu.VMEM((width, span), BF16),
            pltpu.VMEM((LINES, rows, width), BF16),
            pltpu.VMEM((LINES, rows, width), BF16),
            pltpu.VMEM((all_rows, width), BF16),
            pltpu.VMEM((all_rows, width), BF16),
            pltpu.VMEM((all_rows, width), BF16),
            pltpu.VMEM((LINES, rows, span), BF16),
            pltpu.VMEM((LINES, LINES, rows, span), BF16),
            pltpu.VMEM((8, width), F32),
            pltpu.VMEM((LINES, rows, width), F32),
            pltpu.VMEM((LINES, rows, width), BF16),
            pltpu.VMEM((LINES, rows, 128), F32),
        ],
        compiler_params=params(0),
        name="opening",
    )(*small, *weights, latents, w_up, w_down, cotangent, media, valid, counts, times)


def repel(queries, grads, keys, values, valid, shift, slope, scale, masks):
    query_stack = stacked(queries, masks)
    grad_stack = stacked(grads, masks)
    score = dot_last(query_stack, keys) * scale
    expo = jnp.exp(score)
    if valid is not None:
        expo = jnp.where(valid > 0, expo, 0.0)
    mix = dot_last(grad_stack, values)
    raw = (expo * (mix + shift + slope * score) * scale).astype(BF16)
    query_grad = unstacked(jnp.dot(raw, keys, preferred_element_type=F32), masks)
    key_grad = dot_first(raw, query_stack).astype(BF16)
    value_grad = dot_first(expo.astype(BF16), grad_stack).astype(BF16)
    return query_grad, key_grad, value_grad


def stacked_columns(terms, first):
    return jnp.concatenate([terms[:, first + h : first + h + 1] for h in range(GROUP)], axis=0)


def closing_kernel(scale, *refs):
    (
        table_ref,
        grad_ref,
        terms_ref,
        keys_ref,
        values_ref,
        normed_ref,
        valid_ref,
        attn_ref,
        low_ref,
        own_grad_ref,
        own_terms_ref,
        line_normed_ref,
        query_weight_ref,
        key_weight_ref,
        value_weight_ref,
        media_ref,
        tables_ref,
        latents_ref,
        middle_grad_ref,
        ffn_gain_ref,
        counts_ref,
        times_ref,
        media_grad_out,
        latents_grad_out,
        small_out,
        out_out,
        value_out,
        key_out,
        query_out,
        send_sems,
        recv_sems,
        local_sems,
        table,
        grads,
        keys,
        values,
        normed,
        key_grad,
        value_grad,
        weight_a,
        weight_b,
        sums,
        terms_query,
        got_query,
        query_grad,
        got_line,
        media_grad,
        latent_grad,
        small,
        small_sums,
        small_got,
        time_rows_ref,
        part_a,
        part_b,
        part_c,
        part_d,
        query_relay,
        line_relay,
        *fold,
    ) = refs
    z, g, _, core = here()
    items, rows, width = grads.shape
    frames, _, patches = valid_ref.shape
    media_rows = frames * patches
    shard = width // 32
    groups = H // GROUP
    span = width // groups
    masks = head_masks(rows, span, span // GROUP)
    greet(line_of(z, g) + sides_of(z, g, True))
    wires = Wires(send_sems, recv_sems)
    out = Fold(wires, part_a, True, fold[:FOLD], out_out)
    value = Fold(wires, part_b, True, fold[FOLD : 2 * FOLD], value_out)
    key = Fold(wires, part_c, True, fold[2 * FOLD : 3 * FOLD], key_out)
    query = FoldSplit(wires, part_d, True, fold[3 * FOLD :], query_out)
    total = Total(wires, small, small_out, small_sums, small_got)
    exchange = SumLine(wires, terms_query, got_query, query_relay)
    line_exchange = SumLine(wires, grads, got_line, line_relay)
    local = []

    def load(source, target):
        copy = pltpu.make_async_copy(source, target, local_sems.at[len(local)])
        copy.start()
        local.append(copy)
        return copy

    loads = [
        load(table_ref, table),
        load(grad_ref, grads),
        load(keys_ref, keys),
        load(values_ref, values),
    ]
    normed_load = load(normed_ref, normed)
    key_load = load(key_weight_ref, weight_a)
    value_load = load(value_weight_ref, weight_b)
    stored = []

    def weight_part(part, left, right, first, last):
        @pl.loop(first, last)
        def _(n):
            cols = pl.ds(pl.multiple_of(n * span, 128), span)
            block = dot_first(left[:, cols], right[...]).astype(BF16)
            part[n] = block.reshape(PLANE, 2, shard, width)

    def out_part():
        weight_part(part_a, attn_ref, low_ref, 0, LINES)
        out.start()

    def value_part(first):
        if first == 0:
            normed_load.wait()
        weight_part(part_b, normed, value_grad, first, first + 2)
        if first > 0:
            value.start()

    def key_part(first):
        weight_part(part_c, normed, key_grad, first, first + 2)
        if first > 0:
            key.start()

    def repel_own():
        for copy in loads:
            copy.wait()
        sums[...] = jnp.zeros_like(sums)
        own_terms = own_terms_ref[...]
        for group in range(groups):
            cols = slice(group * span, (group + 1) * span)
            (
                sums[group, z],
                key_grad[media_rows:, cols],
                value_grad[media_rows:, cols],
            ) = repel(
                table[group, z],
                own_grad_ref[:, cols],
                keys[media_rows:, cols],
                values[media_rows:, cols],
                None,
                stacked_columns(own_terms, group * GROUP),
                stacked_columns(own_terms, H + group * GROUP),
                scale,
                masks,
            )

    def repel_frames(first, last):
        @pl.loop(first, last)
        def _(frame):
            block = pl.ds(pl.multiple_of(frame * patches, patches), patches)
            valid = valid_ref[frame]
            share = shares(counts_ref, z, g, frame, frames, items)

            def pick(ref, cols):
                chosen = share[0] * ref[0, :, cols].astype(F32)
                for item in range(1, items):
                    chosen = chosen + share[item] * ref[item, :, cols].astype(F32)
                return chosen

            everything = slice(None)
            terms = pick(terms_ref, everything)
            for group in range(groups):
                cols = slice(group * span, (group + 1) * span)
                query_part, key_grad[block, cols], value_grad[block, cols] = repel(
                    pick(table.at[group], everything).astype(BF16),
                    pick(grads, cols).astype(BF16),
                    keys[block, cols],
                    values[block, cols],
                    valid,
                    stacked_columns(terms, group * GROUP),
                    stacked_columns(terms, H + group * GROUP),
                    scale,
                    masks,
                )
                for item in range(items):
                    sums[group, item] += share[item] * query_part

    def queries_first():
        terms_query[...] = sums[...].astype(BF16)
        exchange.first()

    def media_product(n):
        if n == 0:
            key_load.wait()
            value_load.wait()
            small[...] = jnp.zeros_like(small)
            small[10:11] = ffn_gain_ref[...]
            put_times(time_rows_ref, tables_ref, times_ref, frames)
        if n == 2:
            stored[-1].wait()
        count = media_rows // 2
        block = slice(n // 2 * count, (n // 2 + 1) * count)

        @pl.loop(n % 2 * 2, n % 2 * 2 + 2)
        def _(t):
            cols = pl.ds(pl.multiple_of(t * span, 128), span)
            media_grad[:, cols] = dot_last(key_grad[block], weight_a[cols]) + dot_last(
                value_grad[block], weight_b[cols]
            )

    def media_pull(frame):
        count = media_rows // 2
        gain = tables_ref[8:9]
        chunk = 32
        f = frame % (frames // 2)
        moving = time_rows_ref[frame : frame + 1]

        def step(t, carry):
            gain_sum, row_sum = carry
            here_rows = pl.ds(pl.multiple_of(f * patches + t * chunk, chunk), chunk)
            there_rows = pl.ds(pl.multiple_of(frame * patches + t * chunk, chunk), chunk)
            row = media_ref[there_rows].astype(F32) + moving
            pulled, summand = norm_pull(row, gain, media_grad[here_rows])
            media_grad[here_rows] = pulled
            return (
                gain_sum + jnp.sum(summand, axis=0, keepdims=True),
                row_sum + jnp.sum(pulled, axis=0, keepdims=True),
            )

        zero = jnp.zeros((1, width), F32)
        gain_sum, row_sum = lax.fori_loop(0, patches // chunk, step, (zero, zero))
        small[8:9] += gain_sum
        for t in range(8):
            small[t : t + 1] += jnp.where(times_ref[frame] == t, 1.0, 0.0) * row_sum
        if f == frames // 2 - 1:
            first = frame // (frames // 2) * count
            stored.append(load(media_grad, media_grad_out.at[pl.ds(first, count)]))

    def latents_side():
        @pl.loop(0, groups)
        def _(t):
            cols = pl.ds(pl.multiple_of(t * span, 128), span)
            latent_grad[:, cols] = dot_last(key_grad[media_rows:], weight_a[cols]) + dot_last(
                value_grad[media_rows:], weight_b[cols]
            )

    def query_part():
        for item in range(items):
            found = got_query[0, item].astype(F32)
            for place in range(1, LINES):
                found = found + got_query[place, item].astype(F32)
            query_grad[item] = found.astype(BF16)
        grads_all = query_grad[...].reshape(items * rows, span)

        @pl.loop(0, LINES)
        def _(n):
            cols = pl.ds(pl.multiple_of(n * span, 128), span)
            left = line_normed_ref[:, :, cols].reshape(items * rows, span)
            block = dot_first(left, grads_all).astype(BF16)
            part_d[n] = block.reshape(PLANE, 2, shard, span)

        query.start()

    def line_first():
        for item in range(items):
            grads[item] = dot_last(query_grad[item], query_weight_ref[...]).astype(BF16)
        line_exchange.first()

    def latents_end():
        for place in range(LINES):
            latent_grad[...] += got_line[place].astype(F32)
        pulled, summand = norm_pull(
            latents_ref[...].astype(F32), tables_ref[9:10], latent_grad[...]
        )
        latents_grad_out[...] = middle_grad_ref[...] + pulled
        small[9:10] = jnp.sum(summand, axis=0, keepdims=True)
        total.push()

    def total_next():
        total.pull()
        total.push()

    out_part()
    repel_own()
    repel_frames(0, 2)
    repel_frames(2, 4)
    queries_first()
    out.corner()
    media_product(0)
    value_part(0)
    value_part(2)
    out.side_x()
    out.side_y()
    key_part(0)
    exchange.relay()
    media_product(1)
    value.corner()
    key_part(2)
    media_pull(0)
    media_pull(1)
    exchange.finish()
    query_part()
    key.corner()
    line_first()
    value.side_x()
    value.side_y()
    key.side_x()
    out.line()
    line_exchange.relay()
    media_product(2)
    media_product(3)
    key.side_y()
    media_pull(2)
    out.relay()
    value.line()
    media_pull(3)
    line_exchange.finish()
    query.corner()
    latents_side()
    value.relay()
    latents_end()
    key.line()
    total_next()
    query.side_x()
    query.side_y()
    total_next()
    key.relay()
    out.finish()
    query.line()
    value.finish()
    total_next()
    query.finish()
    key.finish()
    total.pull()
    stored[1].wait()
    wires.drain()


def closing(scale, *args):
    (table, grads, terms, keys, values, normed) = args[:6]
    media, latents = args[15], args[17]
    span = table.shape[-1]
    rows, width = latents.shape
    shard = width // 32
    wires = 4 * fold_sems(True) + 6 + 2 * LINES
    bf = [
        table.shape,
        grads.shape,
        keys.shape,
        keys.shape,
        keys.shape,
        keys.shape,
        keys.shape,
        (width, width),
        (width, width),
    ]
    part = pltpu.VMEM((LINES, PLANE, 2, shard, width), BF16)
    small = (16, width)
    scratch = [pltpu.VMEM(shape, BF16) for shape in bf] + [
        pltpu.VMEM(table.shape, F32),
        pltpu.VMEM(table.shape, BF16),
        pltpu.VMEM(table.shape, BF16),
        pltpu.VMEM(table.shape[1:], BF16),
        pltpu.VMEM(grads.shape, BF16),
        pltpu.VMEM((media.shape[0] // 2, width), F32),
        pltpu.VMEM((rows, width), F32),
        pltpu.VMEM(small, F32),
        pltpu.VMEM((3,) + small, F32),
        pltpu.VMEM((6,) + small, F32),
        pltpu.VMEM((8, width), F32),
        part,
        part,
        part,
        pltpu.VMEM((LINES, PLANE, 2, shard, span), BF16),
        pltpu.VMEM(table.shape[1:], BF16),
        pltpu.VMEM((rows, width), BF16),
    ]
    scratch += fold_scratch(shard, width, True) * 3 + fold_scratch(shard, span, True, True)
    smem = pl.BlockSpec(memory_space=pltpu.SMEM)
    return pl.pallas_call(
        partial(closing_kernel, scale),
        out_shape=[
            jax.ShapeDtypeStruct(media.shape, F32),
            jax.ShapeDtypeStruct(latents.shape, F32),
            jax.ShapeDtypeStruct(small, F32),
        ]
        + [jax.ShapeDtypeStruct((shard, width), F32)] * 4,
        in_specs=[LEFT, LEFT, VMEM, LEFT, LEFT, LEFT]
        + [VMEM] * 7
        + [LEFT] * 2
        + [VMEM] * 5
        + [smem] * 2,
        out_specs=[LEFT] + [VMEM] * 6,
        scratch_shapes=[sems(wires), sems(wires), sems(12)] + scratch,
        compiler_params=pltpu.CompilerParams(
            collective_id=3, has_side_effects=True, vmem_limit_bytes=67043328
        ),
        name="closing",
    )(*args)


def settle_kernel(
    weighted_ref,
    stats_ref,
    own_weighted_ref,
    own_stats_ref,
    out_ref,
    latents_ref,
    gain_ref,
    attention_ref,
    attn_ref,
    sums_ref,
    middle_ref,
    normed_ref,
    ready,
):
    rows, width = latents_ref.shape
    span = width // (H // GROUP)
    masks = head_masks(rows, span, span // GROUP)
    stats = own_stats_ref[...]
    for n in range(stats_ref.shape[0]):
        stats = stats + stats_ref[n]
    sums_ref[...] = stats
    for group in range(H // GROUP):
        cols = pl.ds(group * span, span)
        weighted = own_weighted_ref[:, cols]
        for n in range(weighted_ref.shape[0]):
            weighted = weighted + weighted_ref[n, :, cols].astype(F32)
        attention = weighted / spread_heads(stats, group * GROUP, masks)
        attention_ref[:, cols] = attention
        attn_ref[:, cols] = attention.astype(BF16)
    ready()
    middle = latents_ref[...].astype(F32) + jnp.dot(
        attn_ref[...], out_ref[...], preferred_element_type=F32
    )
    middle_ref[...] = middle
    normed_ref[...] = layer_norm(middle, gain_ref[...]).astype(BF16)


def norm_pull(rows, gain, grad):
    mean = jnp.mean(rows, axis=-1, keepdims=True)
    centred = rows - mean
    inverse = lax.rsqrt(jnp.mean(centred * centred, axis=-1, keepdims=True) + NORM_STABILIZER)
    xhat = centred * inverse
    t = grad * gain
    pulled = (
        t
        - jnp.mean(t, axis=-1, keepdims=True)
        - xhat * jnp.mean(t * xhat, axis=-1, keepdims=True)
    ) * inverse
    return pulled, grad * xhat


def unsettle_kernel(
    normed_grad_ref,
    middle_ref,
    gain_ref,
    cot_ref,
    out_ref,
    attention_ref,
    stats_ref,
    coef,
    middle_grad_ref,
    low_ref,
    gain_grad_ref,
    weighted_grad_ref,
    terms_ref,
    attn_grad,
):
    rows, width = middle_ref.shape
    span = width // (H // GROUP)
    masks = head_masks(rows, span, span // GROUP)
    pulled, summand = norm_pull(middle_ref[...], gain_ref[...], normed_grad_ref[...])
    gain_grad_ref[...] = jnp.sum(summand, axis=0, keepdims=True)
    middle_grad = cot_ref[...].astype(F32) + pulled
    middle_grad_ref[...] = middle_grad
    low_ref[...] = middle_grad.astype(BF16)
    attn_grad[...] = dot_last(low_ref[...], out_ref[...])
    stats = stats_ref[...]
    lane = lax.broadcasted_iota(jnp.int32, (rows, 128), 1)
    terms = jnp.zeros((rows, 128), F32)
    for group in range(H // GROUP):
        cols = pl.ds(group * span, span)
        grad = attn_grad[:, cols]
        first = group * GROUP
        weighted_grad_ref[:, cols] = (grad / spread_heads(stats, first, masks)).astype(BF16)
        along = grad * attention_ref[:, cols]
        for h in range(GROUP):
            inner = jnp.sum(jnp.where(masks[h], along, 0.0), axis=1, keepdims=True)
            total = stats[:, first + h : first + h + 1]
            moment = stats[:, H + first + h : H + first + h + 1]
            slope = -coef / total
            shift = -inner / total + coef * (1.0 / total + moment / (total * total)) + slope
            terms = jnp.where(lane == first + h, shift, terms)
            terms = jnp.where(lane == H + first + h, slope, terms)
    terms_ref[...] = terms


def gelu_parts(rows):
    below = 0.5 * (1.0 + lax.erf(rows * (0.5**0.5)))
    density = jnp.exp(-0.5 * rows * rows) * ((0.5 / jnp.pi) ** 0.5)
    return rows * below, below + rows * density


def middle_kernel(patches, *refs):
    (
        weighted_ref,
        stats_ref,
        own_weighted_ref,
        own_stats_ref,
        out_weight_ref,
        up_ref,
        down_ref,
        cot_rows_ref,
        latents_ref,
        tables_ref,
        cot_ref,
        counts_ref,
        attn_out,
        low_out,
        middle_grad_out,
        gain_grad_out,
        weighted_grad_out,
        terms_out,
        grad_table_out,
        terms_table_out,
        new_latents_out,
        up_grad_out,
        down_grad_out,
        send_sems,
        recv_sems,
        local_sems,
        out_weight,
        up_cols,
        down_rows,
        cot_rows,
        ffn_rows,
        attention,
        sums,
        middle,
        normed,
        hidden_grad,
        up_grad,
        hidden,
        normed_part,
        down_part,
        up_grad_part,
        down_grad_part,
        up_near,
        down_near,
        up_got,
        normed_grad,
        down_sum,
        attn_grad,
        *fold,
    ) = refs
    z, g, chip, core = here()
    rows, width = latents_ref.shape
    span = up_cols.shape[1]
    shard = width // 32
    block_rows = PLANE * rows
    near = (z, sibling(g))
    gain_ref = tables_ref.at[10:11]
    greet([(there[0], 2 * there[1] + core) for there, _ in up_places(z, chip)] + [near])
    wires = Wires(send_sems, recv_sems)
    gather = Spread(
        wires, normed, lambda zz, gg: ffn_rows.at[zz, gg // 2], columns_half, False
    )
    back = FoldSteps(wires, normed_part, fold[:FOLD], normed_grad)
    down = Fold(wires, down_part, False, fold[FOLD:], down_sum)
    give = GiveBack(
        wires,
        up_grad_part,
        down_grad_part,
        (up_near, down_near, up_got),
        up_grad_out,
        down_grad_out,
    )
    grad_line = Line(wires, weighted_grad_out, lambda zz: grad_table_out.at[zz])
    terms_line = Line(wires, terms_out, lambda zz: terms_table_out.at[zz])
    loads = [
        pltpu.make_async_copy(source, target, local_sems.at[n])
        for n, (source, target) in enumerate(
            (
                (out_weight_ref, out_weight),
                (down_ref, down_rows),
                (cot_rows_ref, cot_rows),
                (up_ref, up_cols),
            )
        )
    ]
    for load in loads:
        load.start()

    def settle():
        settle_kernel(
            weighted_ref,
            stats_ref,
            own_weighted_ref,
            own_stats_ref,
            out_weight,
            latents_ref,
            gain_ref,
            attention,
            attn_out,
            sums,
            middle,
            normed,
            loads[0].wait,
        )
        ffn_rows[z, chip] = normed[...]

    def hidden_back():
        loads[1].wait()
        loads[2].wait()
        loads[3].wait()

        @pl.loop(0, LINES)
        def _(n):
            block = cot_rows[n].reshape(block_rows, width)
            hidden_grad[n] = dot_last(block, down_rows[...])

    def group(n):
        place = gather.zs[n]
        block = ffn_rows[place].reshape(block_rows, width)
        value, slope = gelu_parts(jnp.dot(block, up_cols[...], preferred_element_type=F32))
        hidden[place] = value.astype(BF16)
        grad = (hidden_grad[place] * slope).astype(BF16)
        up_grad[place] = grad
        part = dot_last(grad, up_cols[...]).astype(BF16)
        normed_part[place] = part.reshape(PLANE, rows, width)

    def down_product():
        @pl.loop(0, LINES)
        def _(n):
            part = jnp.dot(hidden[n], down_rows[...], preferred_element_type=F32)
            down_part[n] = part.astype(BF16).reshape(PLANE, rows, width)

    def up_gradient():
        grads = up_grad[...].reshape(LINES * block_rows, span)

        @pl.loop(0, LINES)
        def _(n):
            cols = pl.ds(pl.multiple_of(n * span, 128), span)
            block = ffn_rows[:, :, :, cols].reshape(LINES * block_rows, span)
            part = dot_first(block, grads).astype(BF16)
            up_grad_part[n] = part.reshape(PLANE, 2, shard, span)

    def down_gradient():
        rows_up = hidden[...].reshape(LINES * block_rows, span)

        @pl.loop(0, LINES)
        def _(n):
            cols = pl.ds(pl.multiple_of(n * span, 128), span)
            block = cot_rows[:, :, :, cols].reshape(LINES * block_rows, span)
            part = dot_first(rows_up, block)
            down_grad_part[:, :, cols] = part.reshape(2, span // 2, span)

    def unsettle():
        unsettle_kernel(
            normed_grad,
            middle,
            gain_ref,
            cot_ref,
            out_weight,
            attention,
            sums,
            ENTROPY_WEIGHT * patches / counts_ref[3:4, 0:1],
            middle_grad_out,
            low_out,
            gain_grad_out,
            weighted_grad_out,
            terms_out,
            attn_grad,
        )
        grad_table_out[z] = weighted_grad_out[...]
        terms_table_out[z] = terms_out[...]

    def new_rows():
        new_latents_out[...] = (middle[...] + down_sum[...]).astype(BF16)

    settle()
    gather.first()
    gather.column(0)
    gather.column(1)
    gather.corner_x(1)
    gather.corner_y(0)
    gather.corner_x(0)
    gather.corner_y(1)
    gather.column(2)
    gather.last(0)
    gather.corner_x(2)
    hidden_back()
    gather.last(1)
    gather.corner_y(2)
    gather.corner_x(3)
    gather.corner_y(3)
    group(0)
    back.corner(0)
    group(1)
    back.corner(1)
    gather.last(2)
    group(2)
    gather.last(3)
    back.corner(2)
    group(3)
    back.corner(3)
    down_product()
    back.side_y(1)
    back.side_x(1)
    back.side_y(3)
    back.side_x(3)
    back.line(1)
    back.side_y(2)
    back.side_x(2)
    down.start()
    back.side_y(0)
    back.side_x(0)
    back.line(3)
    up_gradient()
    back.line(2)
    down.corner()
    down_gradient()
    back.line(0)
    back.relay()
    give.first()
    give.columns()
    down.side_x()
    back.finish()
    give.rows()
    down.side_y()
    unsettle()
    terms_line.first()
    grad_line.first()
    down.line()
    grad_line.take(0)
    grad_line.take(1)
    grad_line.take(2)
    down.relay()
    terms_line.take(0)
    terms_line.take(1)
    terms_line.take(2)
    give.finish()
    down.finish()
    new_rows()
    wires.drain()


def middle_part(
    patches,
    weighted,
    stats,
    own_weighted,
    own_stats,
    w_out,
    up_cols,
    down_rows,
    cot_rows,
    latents,
    tables,
    cot,
    counts,
):
    rows, width = latents.shape
    span = up_cols.shape[1]
    shard = width // 32
    plane = (LINES, PLANE, rows, width)
    block = (LINES, PLANE * rows, span)
    wires = spread_sems(False) + STEP_SEMS + fold_sems(False) + GIVE_SEMS + 2 * LINE_SEMS
    own = (rows, width)
    terms = own_stats.shape
    bf = [
        w_out.shape,
        up_cols.shape,
        down_rows.shape,
        plane,
        plane,
    ]
    scratch = [pltpu.VMEM(shape, BF16) for shape in bf] + [
        pltpu.VMEM(own, F32),
        pltpu.VMEM(terms, F32),
        pltpu.VMEM(own, F32),
        pltpu.VMEM(own, BF16),
        pltpu.VMEM(block, F32),
        pltpu.VMEM(block, BF16),
        pltpu.VMEM(block, BF16),
        pltpu.VMEM(plane, BF16),
        pltpu.VMEM(plane, BF16),
        pltpu.VMEM((LINES, PLANE, 2, shard, span), BF16),
        pltpu.VMEM((2, span // 2, width), F32),
        pltpu.VMEM((LINES, PLANE, shard, span), BF16),
        pltpu.VMEM((span // 2, width), F32),
        pltpu.VMEM((LINES, PLANE, shard, span), BF16),
        pltpu.VMEM(own, F32),
        pltpu.VMEM(own, F32),
        pltpu.VMEM(own, F32),
    ]
    scratch += fold_scratch(rows, width, False) * 2
    return pl.pallas_call(
        partial(middle_kernel, patches),
        out_shape=[
            jax.ShapeDtypeStruct(own, BF16),
            jax.ShapeDtypeStruct(own, BF16),
            jax.ShapeDtypeStruct(own, F32),
            jax.ShapeDtypeStruct((1, width), F32),
            jax.ShapeDtypeStruct(own, BF16),
            jax.ShapeDtypeStruct(terms, F32),
            jax.ShapeDtypeStruct((LINES,) + own, BF16),
            jax.ShapeDtypeStruct((LINES,) + terms, F32),
            jax.ShapeDtypeStruct(own, BF16),
            jax.ShapeDtypeStruct((shard, span * 16), F32),
            jax.ShapeDtypeStruct((span // 2, width), F32),
        ],
        in_specs=[VMEM] * 4 + [LEFT] * 4 + [VMEM] * 4,
        out_specs=[VMEM] * 11,
        scratch_shapes=[sems(wires), sems(wires), sems(4)] + scratch,
        compiler_params=params(1),
        name="middle",
    )(
        weighted,
        stats,
        own_weighted,
        own_stats,
        w_out,
        up_cols,
        down_rows,
        cot_rows.reshape(plane),
        latents,
        tables,
        cot,
        counts,
    )


def ending_kernel(shard, *refs):
    count = (len(refs) - 6) // 3
    sources, small = refs[:count], refs[count]
    outs = refs[count + 1 : 2 * count + 1]
    small_outs = refs[2 * count + 1 : 2 * count + 5]
    held, arrive = refs[2 * count + 5 : 3 * count + 5], refs[3 * count + 5]
    loads, stores = [], []
    for n in range(count):
        loads.append(pltpu.make_async_copy(sources[n], held[n], arrive.at[n]))
        stores.append(pltpu.make_async_copy(held[n], outs[n], arrive.at[n]))
        loads[n].start()
    z, g, _, _ = here()
    width = small.shape[1]
    turned = pltpu.roll(small[...], width - (8 * z + g) * shard, 1)
    small_outs[0][...] = turned[:8, :shard]
    for n in range(3):
        small_outs[n + 1][...] = turned[8 + n : 9 + n, :shard]
    for n in range(count):
        loads[n].wait()
        stores[n].start()
    for n in range(count):
        stores[n].wait()


def ending(results, small, shard):
    count = len(results)
    return pl.pallas_call(
        partial(ending_kernel, shard),
        out_shape=[jax.ShapeDtypeStruct(r.shape, r.dtype) for r in results]
        + [jax.ShapeDtypeStruct((8, shard), F32)]
        + [jax.ShapeDtypeStruct((1, shard), F32)] * 3,
        in_specs=[LEFT] * count + [VMEM],
        out_specs=[LEFT] * count + [VMEM] * 4,
        scratch_shapes=[pltpu.VMEM(r.shape, r.dtype) for r in results] + [sems(count)],
        name="ending",
    )(*results, small)


def per_device(
    media,
    latents,
    frame_counts,
    time_index,
    valid,
    time_table,
    media_gain,
    latent_gain,
    ffn_gain,
    w_query,
    w_key,
    w_value,
    w_out,
    w_up,
    w_down,
    cotangent,
):
    frames = time_index.shape[0]
    patches = valid.shape[0] // frames
    width = latents.shape[1]
    shard = media_gain.shape[0]
    scale = (width // H) ** (-0.5)
    valid_rows = valid.reshape(frames, 1, patches)
    (
        tables,
        counts,
        full_key,
        full_value,
        full_query,
        full_out,
        up_cols,
        down_rows,
        cot_rows,
        normed,
        keys,
        values,
        table,
        line_normed,
        got_weighted,
        got_stats,
        own_weighted,
        own_stats,
    ) = opening(
        scale,
        (
            time_table,
            media_gain.reshape(1, shard),
            latent_gain.reshape(1, shard),
            ffn_gain.reshape(1, shard),
        ),
        (w_key, w_value, w_query, w_out),
        latents,
        w_up,
        w_down,
        cotangent,
        media,
        valid_rows,
        frame_counts,
        time_index,
    )
    (
        attn_low,
        middle_low,
        middle_grad,
        grad_ffn_gain,
        weighted_grad,
        terms,
        grad_table,
        terms_table,
        new_latents,
        shard_up,
        shard_down,
    ) = middle_part(
        valid.shape[0] * lax.axis_size(AXES),
        got_weighted,
        got_stats,
        own_weighted,
        own_stats,
        full_out,
        up_cols.reshape(width, -1),
        down_rows.reshape(-1, width),
        cot_rows,
        latents,
        tables,
        cotangent,
        counts,
    )
    (
        media_grad,
        latents_grad,
        smalls_grad,
        shard_out,
        shard_value,
        shard_key,
        shard_query,
    ) = closing(
        scale,
        table,
        grad_table,
        terms_table,
        keys,
        values,
        normed,
        valid_rows,
        attn_low,
        middle_low,
        weighted_grad,
        terms,
        line_normed,
        full_query,
        full_key,
        full_value,
        media,
        tables,
        latents,
        middle_grad,
        grad_ffn_gain,
        frame_counts,
        time_index,
    )
    results = ending(
        (
            new_latents,
            media_grad,
            latents_grad,
            shard_query,
            shard_key,
            shard_value,
            shard_out,
            shard_up,
            shard_down,
        ),
        smalls_grad,
        shard,
    )
    time_grad, *gains = results[9:]
    return (
        *results[:3],
        time_grad,
        *(gain.reshape(shard) for gain in gains),
        *results[3:9],
    )


def solution(mesh):
    in_specs = (
        P(("gx", "gy"), None),
        P(("gx", "gy"), None),
        P(),
        P(("gx", "gy")),
        P(("gx", "gy")),
        P(None, ("gx", "gy")),
        P(("gx", "gy")),
        P(("gx", "gy")),
        P(("gx", "gy")),
        P(("gx", "gy"), None),
        P(("gx", "gy"), None),
        P(("gx", "gy"), None),
        P(("gx", "gy"), None),
        P(("gx", "gy"), None),
        P(("gx", "gy"), None),
        P(("gx", "gy"), None),
    )
    out_specs = (
        P(("gx", "gy"), None),
        P(("gx", "gy"), None),
        P(("gx", "gy"), None),
        P(None, ("gx", "gy")),
        P(("gx", "gy")),
        P(("gx", "gy")),
        P(("gx", "gy")),
        P(("gx", "gy"), None),
        P(("gx", "gy"), None),
        P(("gx", "gy"), None),
        P(("gx", "gy"), None),
        P(("gx", "gy"), None),
        P(("gx", "gy"), None),
    )
    return jax.shard_map(
        per_device if dict(mesh.shape) == {"gx": 4, "gy": 8} else plain_device,
        mesh=mesh, in_specs=in_specs, out_specs=out_specs, check_vma=False
    )
```

```python
from functools import partial

import jax
import jax.numpy as jnp
from jax import lax
from jax.experimental import pallas as pl
from jax.experimental.pallas import tpu as pltpu
from jax.sharding import PartitionSpec as P

H = 16


ENTROPY_WEIGHT = 4.0
NORM_STABILIZER = 1e-05
AXES = ("gx", "gy")
LINES = 4
PLANE = 4
HBM = pl.ANY
BF16 = jnp.bfloat16
F32 = jnp.float32


def here():
    z = lax.axis_index("gx")
    g = lax.axis_index("gy")
    return z, g, g // 2, g % 2


def sibling(g):
    return g + 1 - 2 * (g % 2)


def along_x(g):
    return g + 2 - 4 * ((g // 2) % 2)


def along_y(g):
    return (g + 4) % 8


def turn(z, k):
    return (z + k) % LINES


def greet(devices):
    barrier = pltpu.get_barrier_semaphore()
    for device in devices:
        pl.semaphore_signal(
            barrier, inc=1, device_id=device, device_id_type=pl.DeviceIdType.MESH
        )
    pl.semaphore_wait(barrier, len(devices))


def line_of(z, g):
    return [(turn(z, k), g) for k in (1, 2, 3)]


class Wires:
    def __init__(self, send_sems, recv_sems):
        self.send_sems, self.recv_sems, self.used, self.sent = send_sems, recv_sems, 0, []

    def reserve(self, count):
        first = self.used
        self.used += count
        return first

    def copy(self, source, target, device, send, recv):
        return pltpu.make_async_remote_copy(
            src_ref=source,
            dst_ref=target,
            send_sem=self.send_sems.at[send],
            recv_sem=self.recv_sems.at[recv],
            device_id=device,
            device_id_type=pl.DeviceIdType.MESH,
        )

    def send(self, source, target, device):
        n = self.reserve(1)
        copy = self.copy(source, target, device, n, n)
        copy.start()
        self.sent.append((None, copy))
        return copy

    def send_if(self, condition, source, target, device, send, recv):
        copy = self.copy(source, target, device, send, recv)
        self.sent.append((condition, copy))

        @pl.when(condition)
        def _():
            copy.start()

        return copy

    def drain(self):
        for condition, copy in self.sent:
            if condition is None:
                copy.wait_send()
            else:
                pl.when(condition)(copy.wait_send)


class Line:
    def __init__(self, wires, shard, slot):
        self.wires, self.shard, self.slot = wires, shard, slot
        self.z, self.g, _, _ = here()
        self.base = wires.reserve(4)
        low, high = (3 - self.z) // 3, self.z // 3
        self.order = (1 + 2 * low, 3 - low - high, 2 - low + high)

    def first(self):
        z, g = self.z, self.g
        own = self.slot(z)
        base = self.base
        self.wires.send_if(z < 3, self.shard, own, (turn(z, 1), g), base + 1, base + 1)
        self.wires.send_if(z > 0, self.shard, own, (turn(z, 3), g), base + 3, base + 3)
        self.across = self.wires.copy(self.shard, own, (turn(z, 2), g), base + 2, base + 2)
        self.across.start()
        self.wires.sent.append((None, self.across))

    def take(self, step):
        z, g = self.z, self.g
        k = self.order[step]
        origin = turn(z, LINES - k)
        held = self.slot(origin)
        self.wires.copy(held, held, (z, g), 0, self.base + k).wait_recv()
        if step == 2:
            self.relay(z == 2, 3, 3)
        if step == 2:
            self.relay(z == 1, 0, 1)
        return origin

    def relay(self, condition, there, k):
        held = self.slot(turn(self.z, 2))
        self.wires.send_if(
            condition, held, held, (there, self.g), self.base, self.base + k
        )


class LineSplit:
    def __init__(self, wires, shard, slot):
        self.wires, self.shard, self.slot = wires, shard, slot
        self.z, self.g, _, _ = here()
        self.base = wires.reserve(LINES)
        low, high = (3 - self.z) // 3, self.z // 3
        self.order = (1 + 2 * low, 3 - low - high, 2 - low + high)

    def first(self):
        for k in (2, 1, 3):
            there = turn(self.z, k)
            copy = self.wires.copy(
                piece_of(self.shard, there),
                self.slot(self.z),
                (there, self.g),
                self.base + k,
                self.base + k,
            )
            copy.start()
            self.wires.sent.append((None, copy))

    def take(self, step):
        k = self.order[step]
        origin = turn(self.z, LINES - k)
        held = self.slot(origin)
        self.wires.copy(held, held, (self.z, self.g), 0, self.base + k).wait_recv()
        return origin


def piece_of(shard, place):
    width = shard.shape[-1] // LINES
    return shard.at[:, pl.ds(pl.multiple_of(place * width, 128), width)]


class Spread:
    def __init__(self, wires, shard, slot, half, whole, split=False):
        self.wires, self.shard, self.slot, self.half, self.whole = wires, shard, slot, half, whole
        self.z, self.g, _, _ = here()
        self.line = (LineSplit if split else Line)(wires, shard, lambda z: slot(z, self.g))
        if split:
            self.shard = piece_of(shard, self.z)
        self.zs, self.x, self.y, self.dx, self.dy, self.sib = [self.z], [], [], {}, {}, []

    def side(self, gy):
        return (self.z, gy)

    def to_sibling(self, held):
        if self.whole:
            self.sib.append(self.wires.send(held, held, self.side(sibling(self.g))))

    def first(self):
        own = self.slot(self.z, self.g)
        self.line.first()
        self.x.append(self.wires.send(self.shard, own, self.side(along_x(self.g))))
        self.y.append(self.wires.send(self.shard, own, self.side(along_y(self.g))))
        if self.whole:
            self.sib.append(self.wires.send(self.shard, own, self.side(sibling(self.g))))

    def column(self, step):
        self.zs.append(self.line.take(step))
        held = self.slot(self.zs[-1], self.g)
        self.x.append(self.wires.send(held, held, self.side(along_x(self.g))))
        self.y.append(self.wires.send(held, held, self.side(along_y(self.g))))
        self.to_sibling(held)

    def corner(self, n):
        self.corner_x(n)
        self.corner_y(n)

    def corner_x(self, n):
        self.x[n].wait_recv()
        held = self.slot(self.zs[n], along_x(self.g))
        part = self.half(held, 0)
        self.dy[n] = self.wires.send(part, part, self.side(along_y(self.g)))
        self.to_sibling(held)

    def corner_y(self, n):
        self.y[n].wait_recv()
        held = self.slot(self.zs[n], along_y(self.g))
        part = self.half(held, 1)
        self.dx[n] = self.wires.send(part, part, self.side(along_x(self.g)))
        self.to_sibling(held)

    def last(self, n):
        self.dy[n].wait_recv()
        self.dx[n].wait_recv()
        self.to_sibling(self.slot(self.zs[n], along_y(along_x(self.g))))

    def finish(self):
        for copy in self.sib:
            copy.wait_recv()


def spread_all(flows):
    for flow in flows:
        flow.first()
    for flow in flows:
        flow.corner(0)
    for step in range(3):
        for flow in flows:
            flow.column(step)
        for flow in flows:
            flow.corner(step + 1)
    for n in range(4):
        for flow in flows:
            flow.last(n)
    for flow in flows:
        flow.finish()


LINE_SEMS = 4


def spread_sems(whole):
    return LINE_SEMS + 8 + 8 + (16 if whole else 0)


def columns_half(ref, which):
    width = ref.shape[-1] // 2
    return ref.at[..., pl.ds(which * width, width)]


def rows_half(ref, which):
    rows = ref.shape[0] // 2
    return ref.at[pl.ds(which * rows, rows)]


def rows_parts(ref, which):
    return ref.at[pl.ds(32, 16)] if which else ref.at[pl.ds(0, 32)]


def sides_of(z, g, whole):
    near = [(z, along_x(g)), (z, along_y(g))]
    return near + [(z, sibling(g))] if whole else near


def params(ident):
    return pltpu.CompilerParams(
        collective_id=ident, has_side_effects=True, vmem_limit_bytes=60 * 2**20
    )


def sems(count):
    return pltpu.SemaphoreType.DMA((count,))


VMEM = pl.BlockSpec(memory_space=pltpu.VMEM)
LEFT = pl.BlockSpec(memory_space=HBM)


class SumLine:
    def __init__(self, wires, source, out, relayed=None):
        self.wires, self.source, self.out, self.relayed = wires, source, out, relayed
        self.z, self.g, _, _ = here()
        self.base = wires.reserve(LINES)
        low, high = (3 - self.z) // 3, self.z // 3
        self.back = (0, 1 + 2 * low, 3 - low - high, 2 - low + high)
        self.places = [turn(self.z, LINES - k) if n else self.z for n, k in enumerate(self.back)]
        self.end = low + high > 0
        self.inner = low + high < 1
        self.beside = 1 + high

    def step(self, n):
        place = self.places[n]
        if n < 3 or self.relayed is None:
            k = LINES - self.back[n]
            copy = self.wires.copy(
                self.source.at[place],
                self.out.at[self.z],
                (place, self.g),
                self.base + k,
                self.base + k,
            )
            copy.start()
            self.wires.sent.append((None, copy))
        else:
            self.wires.send_if(
                self.end,
                self.source.at[place],
                self.relayed,
                (self.beside, self.g),
                self.base,
                self.base,
            )

    def first(self):
        for n in (2, 1, 3):
            self.step(n)
        self.clear()
        self.out[self.z] = self.source[self.z]

    def clear(self):
        if self.relayed is None:
            return

        @pl.when(self.end)
        def _():
            self.out[3 - self.z] = jnp.zeros(self.out.shape[1:], self.out.dtype)

    def relay(self):
        place = self.places[3]
        held = self.source.at[place]
        across = self.wires.copy(
            held, self.out.at[self.z], (place, self.g), self.base + 2, self.base + 2
        )
        came = self.wires.copy(
            self.relayed, self.relayed, (self.z, self.g), self.base, self.base
        )
        self.wires.sent.append((self.inner, across))

        @pl.when(self.inner)
        def _():
            came.wait_recv()
            held[...] = held[...] + self.relayed[...]
            across.start()

    def finish(self):
        for k, condition in ((1, self.z > 0), (3, self.z < 3), (2, None)):
            if self.relayed is None:
                condition = None
            held = self.out.at[turn(self.z, LINES - k)]
            copy = self.wires.copy(held, held, (self.z, self.g), 0, self.base + k)
            if condition is None:
                copy.wait_recv()
            else:
                pl.when(condition)(copy.wait_recv)


class Exchange:
    def __init__(self, wires, arrays):
        self.lines = [SumLine(wires, *array) for array in arrays]

    def first(self):
        for line in self.lines:
            line.first()

    def relay(self):
        for line in self.lines:
            line.relay()

    def finish(self):
        for line in self.lines:
            line.finish()


def add_slots(target, source, count):
    @pl.loop(0, count)
    def _(n):
        target[n] = (target[n].astype(F32) + source[n].astype(F32)).astype(target.dtype)


def sum_slots(ref):
    found = ref[0].astype(F32)
    for n in range(1, LINES):
        found = found + ref[n].astype(F32)
    return found


class Fold:
    summed = True

    def __init__(self, wires, parts, whole, scratch, out):
        self.wires, self.parts, self.whole, self.out = wires, parts, whole, out
        self.from_sib, self.cx, self.cy, self.fx, self.fy, self.fz, self.relayed = scratch
        self.z, self.g, self.chip, self.core = here()
        self.cut = self.cy.shape[-1]
        self.lines = SumLine(wires, self.fx, self.fz, self.relayed) if self.summed else None

    def send(self, source, target, gy):
        return self.wires.send(source, target, (self.z, gy))

    def column(self, q):
        return self.parts.at[:, q, self.core] if self.whole else self.parts.at[:, q]

    def half(self, ref, which):
        if which:
            return ref.at[:, :, pl.ds(self.cut, ref.shape[-1] - self.cut)]
        return ref.at[:, :, pl.ds(0, self.cut)]

    def merge(self, q):
        if self.whole:
            core = self.core

            @pl.loop(0, LINES)
            def _(n):
                self.parts[n, q, core] = self.parts[n, q, core] + self.from_sib[n, q]

    def start(self):
        if self.whole:
            theirs = self.parts.at[:, :, 1 - self.core]
            self.sib = self.send(theirs, self.from_sib, sibling(self.g))

    def corner(self):
        if self.whole:
            self.sib.wait_recv()
        q = along_y(along_x(self.g)) // 2
        self.merge(q)
        far = self.column(q)
        self.to_y = self.send(self.half(far, 0), self.cy, along_y(self.g))
        self.to_x = self.send(self.half(far, 1), self.cx, along_x(self.g))

    def side(self, gy, came, corner, which, target):
        q = gy // 2
        self.merge(q)
        came.wait_recv()
        column = self.column(q)
        cols = slice(self.cut, None) if which else slice(0, self.cut)

        @pl.loop(0, LINES)
        def _(n):
            column[n, :, cols] = column[n, :, cols] + corner[n]

        return self.send(column, target, gy)

    def side_x(self):
        self.by_x = self.side(along_x(self.g), self.to_y, self.cy, 0, self.fx)

    def side_y(self):
        self.by_y = self.side(along_y(self.g), self.to_x, self.cx, 1, self.fy)

    def line(self):
        self.merge(self.chip)
        self.by_x.wait_recv()
        self.by_y.wait_recv()
        column = self.column(self.chip)
        for n in (3, 2, 1):
            there = self.lines.places[n]
            self.fx[there] = (
                column[there].astype(F32)
                + self.fx[there].astype(F32)
                + self.fy[there].astype(F32)
            ).astype(BF16)
            self.lines.step(n)
        z = self.z
        self.lines.clear()
        self.fz[z] = jnp.zeros(self.fz.shape[1:], BF16)
        self.out[...] = column[z].astype(F32) + self.fx[z].astype(F32) + self.fy[z].astype(F32)

    def relay(self):
        self.lines.relay()

    def finish(self):
        self.lines.finish()
        self.out[...] += sum_slots(self.fz)


class FoldSplit(Fold):
    summed = False

    def line(self):
        self.merge(self.chip)
        self.by_x.wait_recv()
        self.by_y.wait_recv()
        column = self.column(self.chip)
        self.zs = []
        for k in (2, 1, 3, 0):
            there = turn(self.z, k) if k else self.z
            found = (
                column[there].astype(F32)
                + self.fx[there].astype(F32)
                + self.fy[there].astype(F32)
            ).astype(BF16)
            if k:
                self.fx[there] = found
                self.zs.append(
                    self.wires.send(self.fx.at[there], self.fz.at[self.z], (there, self.g))
                )
            else:
                self.fz[self.z] = found

    def finish(self):
        for copy in self.zs:
            copy.wait_recv()
        width = self.fz.shape[-1]
        for place in range(LINES):
            self.out[:, place * width : (place + 1) * width] = self.fz[place].astype(F32)


def fold_scratch(rows, cols, whole, split=False):
    cut = 256 if split else cols // 2
    return [
        pltpu.VMEM((LINES, PLANE, rows, cols) if whole else (1, 1, 16, 128), BF16),
        pltpu.VMEM((LINES, rows, cols - cut), BF16),
        pltpu.VMEM((LINES, rows, cut), BF16),
        pltpu.VMEM((LINES, rows, cols), BF16),
        pltpu.VMEM((LINES, rows, cols), BF16),
        pltpu.VMEM((LINES, rows, cols), BF16),
        pltpu.VMEM((rows, cols), BF16),
    ]


FOLD = 7


def fold_sems(whole):
    return (1 if whole else 0) + 4 + LINES


class FoldSteps:
    def __init__(self, wires, parts, scratch, out):
        self.wires, self.parts, self.out = wires, parts, out
        _, self.cx, self.cy, self.fx, self.fy, self.fz, relayed = scratch
        self.z, self.g, self.chip, _ = here()
        self.width = parts.shape[-1] // 2
        self.lines = SumLine(wires, self.fx, self.fz, relayed)
        self.zs = self.lines.places
        self.to_x, self.to_y, self.by_x, self.by_y = {}, {}, {}, {}

    def half(self, n, q, which):
        return self.parts.at[self.zs[n], q, :, pl.ds(which * self.width, self.width)]

    def corner(self, n):
        far = along_y(along_x(self.g)) // 2
        place = self.zs[n]
        self.to_y[n] = self.wires.send(
            self.half(n, far, 0), self.cy.at[place], (self.z, along_y(self.g))
        )
        self.to_x[n] = self.wires.send(
            self.half(n, far, 1), self.cx.at[place], (self.z, along_x(self.g))
        )

    def side(self, n, gy, came, corner, which, target):
        came.wait_recv()
        q, place = gy // 2, self.zs[n]
        cols = slice(which * self.width, (which + 1) * self.width)
        self.parts[place, q, :, cols] = self.parts[place, q, :, cols] + corner[place]
        return self.wires.send(self.parts.at[place, q], target.at[place], (self.z, gy))

    def side_x(self, n):
        self.by_x[n] = self.side(n, along_x(self.g), self.to_y[n], self.cy, 0, self.fx)

    def side_y(self, n):
        self.by_y[n] = self.side(n, along_y(self.g), self.to_x[n], self.cx, 1, self.fy)

    def line(self, n):
        self.by_x[n].wait_recv()
        self.by_y[n].wait_recv()
        place = self.zs[n]
        found = (
            self.parts[place, self.chip].astype(F32)
            + self.fx[place].astype(F32)
            + self.fy[place].astype(F32)
        )
        if n == 0:
            self.out[...] = found
            self.lines.clear()
            self.fz[self.z] = jnp.zeros(self.fz.shape[1:], BF16)
        else:
            self.fx[place] = found.astype(BF16)
            self.lines.step(n)

    def relay(self):
        self.lines.relay()

    def finish(self):
        self.lines.finish()
        self.out[...] += sum_slots(self.fz)


STEP_SEMS = 16 + LINES


def layer_norm(row_block, gain_row):
    row_mean = jnp.mean(row_block, axis=-1, keepdims=True)
    centred = row_block - row_mean
    variance = jnp.mean(centred * centred, axis=-1, keepdims=True)
    return centred * lax.rsqrt(variance + NORM_STABILIZER) * gain_row


def product(left_side, right_side):
    return jnp.dot(left_side, right_side, preferred_element_type=jnp.float32)


def inner_first(left_side, right_side):
    return lax.dot_general(
        left_side, right_side, (((0,), (0,)), ((), ())), preferred_element_type=jnp.float32
    )


def inner_last(left_side, right_side):
    return lax.dot_general(
        left_side, right_side, (((1,), (1,)), ((), ())), preferred_element_type=jnp.float32
    )


def collect(onehot_rows, value_rows):
    return lax.dot_general(
        onehot_rows,
        value_rows,
        (((0,), (0,)), ((), ())),
        precision=lax.Precision.HIGHEST,
        preferred_element_type=jnp.float32,
    )


def plain_device(
    media,
    latents,
    frame_counts,
    time_index,
    valid,
    time_table,
    media_gain,
    latent_gain,
    ffn_gain,
    w_query,
    w_key,
    w_value,
    w_out,
    w_up,
    w_down,
    cotangent,
):
    frames = time_index.shape[0]
    patches = valid.shape[0] // frames
    latent_rows = latents.shape[0]
    model_width = latents.shape[1]
    head_size = model_width // H
    score_scale = head_size ** (-0.5)
    across = lax.axis_size("gx")
    column = lax.axis_index("gx")
    row_index = lax.axis_index("gy")
    frame_ends = jnp.cumsum(frame_counts[row_index])
    position = column * frames + jnp.arange(frames, dtype=jnp.int32)
    item_index = jnp.sum((frame_ends[None, :] <= position[:, None]).astype(jnp.int32), axis=1)
    item_onehot = (item_index[:, None] == jnp.arange(across, dtype=jnp.int32)[None, :]).astype(
        jnp.float32
    )
    (
        full_query,
        full_key,
        full_value,
        full_out,
        full_up,
        full_down,
        full_media_gain,
        full_latent_gain,
        full_ffn_gain,
        full_time,
    ) = (
        lax.all_gather(w_query, ("gx", "gy"), axis=0, tiled=True),
        lax.all_gather(w_key, ("gx", "gy"), axis=0, tiled=True),
        lax.all_gather(w_value, ("gx", "gy"), axis=0, tiled=True),
        lax.all_gather(w_out, ("gx", "gy"), axis=0, tiled=True),
        lax.all_gather(w_up, ("gx", "gy"), axis=0, tiled=True),
        lax.all_gather(w_down, ("gx", "gy"), axis=0, tiled=True),
        lax.all_gather(media_gain, ("gx", "gy"), axis=0, tiled=True),
        lax.all_gather(latent_gain, ("gx", "gy"), axis=0, tiled=True),
        lax.all_gather(ffn_gain, ("gx", "gy"), axis=0, tiled=True),
        lax.all_gather(time_table, ("gx", "gy"), axis=1, tiled=True),
    )
    time_onehot = (
        time_index[:, None] == jnp.arange(full_time.shape[0], dtype=jnp.int32)[None, :]
    ).astype(jnp.float32)
    time_rows = product(time_onehot.astype(jnp.bfloat16), full_time)
    media_in = (
        media.astype(jnp.float32).reshape(frames, patches, model_width) + time_rows[:, None, :]
    ).reshape(-1, model_width)
    media_normed = layer_norm(media_in, full_media_gain.astype(jnp.float32)).astype(jnp.bfloat16)
    key_heads = (
        product(media_normed, full_key).astype(jnp.bfloat16).reshape(frames, patches, H, head_size)
    )
    value_heads = (
        product(media_normed, full_value)
        .astype(jnp.bfloat16)
        .reshape(frames, patches, H, head_size)
    )
    latent_in = latents.astype(jnp.float32)
    latent_normed = layer_norm(latent_in, full_latent_gain.astype(jnp.float32)).astype(jnp.bfloat16)
    own_query = product(latent_normed, full_query).astype(jnp.bfloat16)
    own_key = product(latent_normed, full_key).astype(jnp.bfloat16)
    own_value = product(latent_normed, full_value).astype(jnp.bfloat16)
    valid_total = lax.psum(jnp.sum(valid.astype(jnp.float32)), ("gx", "gy"))
    coefficient = ENTROPY_WEIGHT * (valid.shape[0] * lax.axis_size(("gx", "gy"))) / valid_total
    query_table = lax.all_gather(own_query, "gx", axis=0, tiled=True)
    picked = query_table.reshape(-1, latent_rows, H, head_size)[item_index]
    media_score = (
        jnp.einsum("flhd,fphd->flhp", picked, key_heads, preferred_element_type=jnp.float32)
        * score_scale
    )
    valid_mask = valid.reshape(frames, 1, 1, patches) > 0
    media_expo = jnp.where(valid_mask, jnp.exp(media_score), 0.0)
    expo_low = media_expo.astype(jnp.bfloat16)
    media_total = jnp.sum(media_expo, axis=-1)
    media_moment = jnp.sum(media_expo * media_score, axis=-1)
    media_weighted = jnp.einsum(
        "flhp,fphd->flhd", expo_low, value_heads, preferred_element_type=jnp.float32
    )
    dense_weighted = collect(item_onehot, media_weighted.reshape(frames, -1)).reshape(
        -1, model_width
    )
    dense_total = collect(item_onehot, media_total.reshape(frames, -1)).reshape(-1, H)
    dense_moment = collect(item_onehot, media_moment.reshape(frames, -1)).reshape(-1, H)
    got_weighted, got_total, got_moment = (
        lax.psum_scatter(dense_weighted, "gx", scatter_dimension=0, tiled=True),
        lax.psum_scatter(dense_total, "gx", scatter_dimension=0, tiled=True),
        lax.psum_scatter(dense_moment, "gx", scatter_dimension=0, tiled=True),
    )
    query_head_count = own_query.reshape(latent_rows, H, head_size)
    latent_key_rows = own_key.reshape(latent_rows, H, head_size)
    latent_value_rows = own_value.reshape(latent_rows, H, head_size)
    latent_score = (
        jnp.einsum(
            "uer,zer->uez", query_head_count, latent_key_rows, preferred_element_type=jnp.float32
        )
        * score_scale
    )
    latent_expo = jnp.exp(latent_score)
    latent_reduced_precision = latent_expo.astype(jnp.bfloat16)
    weighted = got_weighted.reshape(latent_rows, H, head_size) + jnp.einsum(
        "nwr,rwb->nwb",
        latent_reduced_precision,
        latent_value_rows,
        preferred_element_type=jnp.float32,
    )
    totals = got_total + jnp.sum(latent_expo, axis=-1)
    moment = got_moment + jnp.sum(latent_expo * latent_score, axis=-1)
    attention = weighted / totals[..., None]
    attn_low = attention.reshape(latent_rows, model_width).astype(jnp.bfloat16)
    middle = latent_in + product(attn_low, full_out)
    ffn_normed = layer_norm(middle, full_ffn_gain.astype(jnp.float32)).astype(jnp.bfloat16)
    up_rows = product(ffn_normed, full_up)
    hidden = jax.nn.gelu(up_rows, approximate=False).astype(jnp.bfloat16)
    new_latents = (middle + product(hidden, full_down)).astype(jnp.bfloat16)
    (
        back_query,
        back_key,
        back_value,
        back_out,
        back_up,
        back_down,
        back_media_gain,
        back_latent_gain,
        back_ffn_gain,
    ) = (
        lax.all_gather(w_query, ("gx", "gy"), axis=0, tiled=True),
        lax.all_gather(w_key, ("gx", "gy"), axis=0, tiled=True),
        lax.all_gather(w_value, ("gx", "gy"), axis=0, tiled=True),
        lax.all_gather(w_out, ("gx", "gy"), axis=0, tiled=True),
        lax.all_gather(w_up, ("gx", "gy"), axis=0, tiled=True),
        lax.all_gather(w_down, ("gx", "gy"), axis=0, tiled=True),
        lax.all_gather(media_gain, ("gx", "gy"), axis=0, tiled=True),
        lax.all_gather(latent_gain, ("gx", "gy"), axis=0, tiled=True),
        lax.all_gather(ffn_gain, ("gx", "gy"), axis=0, tiled=True),
    )
    owned_latent, owned_attn, owned_ffn, owned_hidden = (
        lax.all_to_all(latent_normed, ("gx", "gy"), split_axis=1, concat_axis=0, tiled=True),
        lax.all_to_all(attn_low, ("gx", "gy"), split_axis=1, concat_axis=0, tiled=True),
        lax.all_to_all(ffn_normed, ("gx", "gy"), split_axis=1, concat_axis=0, tiled=True),
        lax.all_to_all(hidden, ("gx", "gy"), split_axis=1, concat_axis=0, tiled=True),
    )
    hidden_grad = inner_last(cotangent, back_down)
    gelu_pull = jax.vjp(partial(jax.nn.gelu, approximate=False), up_rows)[1]
    up_grad = gelu_pull(hidden_grad)[0].astype(jnp.bfloat16)
    ffn_normed_grad = inner_last(up_grad, back_up)
    ffn_pull = jax.vjp(layer_norm, middle, back_ffn_gain.astype(jnp.float32))[1]
    middle_part, grad_ffn_gain = ffn_pull(ffn_normed_grad)
    middle_grad = cotangent.astype(jnp.float32) + middle_part
    middle_low = middle_grad.astype(jnp.bfloat16)
    attn_grad = inner_last(middle_low, back_out).reshape(latent_rows, H, head_size)
    weighted_sum_gradient = (attn_grad / totals[..., None]).astype(jnp.bfloat16)
    slope_term = -coefficient / totals
    shift_term = (
        -jnp.sum(attn_grad * attention, axis=-1) / totals
        + coefficient * (1.0 / totals + moment / (totals * totals))
        + slope_term
    )
    latent_mix = jnp.einsum(
        "uer,zer->uez", weighted_sum_gradient, latent_value_rows, preferred_element_type=jnp.float32
    )
    latent_sgrad = latent_expo * (
        latent_mix + shift_term[..., None] + slope_term[..., None] * latent_score
    )
    latent_residual_gradient = (latent_sgrad * score_scale).astype(jnp.bfloat16)
    query_part = jnp.einsum(
        "nwr,rwb->nwb",
        latent_residual_gradient,
        latent_key_rows,
        preferred_element_type=jnp.float32,
    )
    own_key_grad = (
        jnp.einsum(
            "zry,zrj->yrj",
            latent_residual_gradient,
            query_head_count,
            preferred_element_type=jnp.float32,
        )
        .astype(jnp.bfloat16)
        .reshape(latent_rows, model_width)
    )
    own_value_grad = (
        jnp.einsum(
            "zry,zrj->yrj",
            latent_reduced_precision,
            weighted_sum_gradient,
            preferred_element_type=jnp.float32,
        )
        .astype(jnp.bfloat16)
        .reshape(latent_rows, model_width)
    )
    grad_table = lax.all_gather(
        weighted_sum_gradient.reshape(latent_rows, model_width), "gx", axis=0, tiled=True
    )
    shift_table, slope_table = (
        lax.all_gather(shift_term, "gx", axis=0, tiled=True),
        lax.all_gather(slope_term, "gx", axis=0, tiled=True),
    )
    picked_grad = grad_table.reshape(-1, latent_rows, H, head_size)[item_index]
    picked_shift = shift_table.reshape(-1, latent_rows, H)[item_index]
    picked_slope = slope_table.reshape(-1, latent_rows, H)[item_index]
    media_mix = jnp.einsum(
        "flhd,fphd->flhp", picked_grad, value_heads, preferred_element_type=jnp.float32
    )
    media_sgrad = media_expo * (
        media_mix + picked_shift[..., None] + picked_slope[..., None] * media_score
    )
    media_rgrad = (media_sgrad * score_scale).astype(jnp.bfloat16)
    query_terms = jnp.einsum(
        "flhp,fphd->flhd", media_rgrad, key_heads, preferred_element_type=jnp.float32
    )
    dense_query = collect(item_onehot, query_terms.reshape(frames, -1)).reshape(-1, model_width)
    got_query = lax.psum_scatter(
        dense_query.astype(jnp.bfloat16), "gx", scatter_dimension=0, tiled=True
    ).astype(jnp.float32)
    media_key_grad = (
        jnp.einsum("flhp,flhd->fphd", media_rgrad, picked, preferred_element_type=jnp.float32)
        .astype(jnp.bfloat16)
        .reshape(-1, model_width)
    )
    media_value_grad = (
        jnp.einsum("flhp,flhd->fphd", expo_low, picked_grad, preferred_element_type=jnp.float32)
        .astype(jnp.bfloat16)
        .reshape(-1, model_width)
    )
    grad_key = inner_first(media_normed, media_key_grad) + inner_first(latent_normed, own_key_grad)
    grad_value = inner_first(media_normed, media_value_grad) + inner_first(
        latent_normed, own_value_grad
    )
    media_normed_grad = inner_last(media_key_grad, back_key) + inner_last(
        media_value_grad, back_value
    )
    media_pull = jax.vjp(layer_norm, media_in, back_media_gain.astype(jnp.float32))[1]
    media_grad, grad_media_gain = media_pull(media_normed_grad)
    frame_sums = jnp.sum(media_grad.reshape(frames, patches, model_width), axis=1)
    grad_time = collect(time_onehot, frame_sums)
    query_grad = (
        (got_query.reshape(latent_rows, H, head_size) + query_part)
        .astype(jnp.bfloat16)
        .reshape(latent_rows, model_width)
    )
    latent_normed_grad = (
        inner_last(query_grad, back_query)
        + inner_last(own_key_grad, back_key)
        + inner_last(own_value_grad, back_value)
    )
    latent_pull = jax.vjp(layer_norm, latent_in, back_latent_gain.astype(jnp.float32))[1]
    latent_part, grad_latent_gain = latent_pull(latent_normed_grad)
    latents_grad = middle_grad + latent_part
    piece_query = lax.all_gather(query_grad, ("gx", "gy"), axis=0, tiled=True)
    piece_middle = lax.all_gather(middle_low, ("gx", "gy"), axis=0, tiled=True)
    piece_up = lax.all_gather(up_grad, ("gx", "gy"), axis=0, tiled=True)
    piece_cot = lax.all_gather(cotangent, ("gx", "gy"), axis=0, tiled=True)
    shard_query = inner_first(owned_latent, piece_query)
    shard_out = inner_first(owned_attn, piece_middle)
    shard_up = inner_first(owned_ffn, piece_up)
    shard_down = inner_first(owned_hidden, piece_cot)
    shard_grads = (
        lax.psum_scatter(grad_key, ("gx", "gy"), scatter_dimension=0, tiled=True),
        lax.psum_scatter(grad_value, ("gx", "gy"), scatter_dimension=0, tiled=True),
        lax.psum_scatter(grad_media_gain, ("gx", "gy"), scatter_dimension=0, tiled=True),
        lax.psum_scatter(grad_latent_gain, ("gx", "gy"), scatter_dimension=0, tiled=True),
        lax.psum_scatter(grad_ffn_gain, ("gx", "gy"), scatter_dimension=0, tiled=True),
        lax.psum_scatter(grad_time, ("gx", "gy"), scatter_dimension=1, tiled=True),
    )
    return (
        new_latents,
        media_grad,
        latents_grad,
        shard_grads[5],
        shard_grads[2],
        shard_grads[3],
        shard_grads[4],
        shard_query,
        shard_grads[0],
        shard_grads[1],
        shard_out,
        shard_up,
        shard_down,
    )


GROUP = 4


def mates_of(z, chip, core):
    mates = []
    for j in range(1, 16):
        there = (4 * z + chip + j) % 16
        mates.append((there // 4, 2 * (there % 4) + core))
    return mates


class GiveBack:
    def __init__(self, wires, up_part, down_part, scratch, up_out, down_out):
        self.wires, self.up_part, self.down_part = wires, up_part, down_part
        self.up_out, self.down_out = up_out, down_out
        self.up_near, self.down_near, self.up_got = scratch
        self.z, self.g, self.chip, self.core = here()
        self.places = up_places(self.z, self.chip)

    def first(self):
        near = (self.z, sibling(self.g))
        theirs = 1 - self.core
        self.up = self.wires.send(self.up_part.at[:, :, theirs], self.up_near, near)
        self.down = self.wires.send(self.down_part.at[theirs], self.down_near, near)

    def columns(self):
        self.up.wait_recv()
        core = self.core

        @pl.loop(0, LINES)
        def _(n):
            for q in range(PLANE):
                self.up_part[n, q, core] = self.up_part[n, q, core] + self.up_near[n, q]

        self.moved = []
        for there, _ in self.places:
            self.moved.append(
                self.wires.send(
                    self.up_part.at[there[0], there[1], core],
                    self.up_got.at[self.z, self.chip],
                    (there[0], 2 * there[1] + core),
                )
            )
        self.up_got[self.z, self.chip] = self.up_part[self.z, self.chip, core]

    def rows(self):
        self.down.wait_recv()
        rows = self.down_out.shape[0] // 8
        core = self.core

        @pl.loop(0, 8)
        def _(n):
            block = pl.ds(pl.multiple_of(n * rows, 8), rows)
            self.down_out[block] = self.down_part[core, block] + self.down_near[block]

    def finish(self):
        for copy in self.moved:
            copy.wait_recv()
        width = self.up_got.shape[-1]
        for n in range(LINES):
            for q in range(PLANE):
                first = (n * PLANE + q) * width
                self.up_out[:, first : first + width] = self.up_got[n, q].astype(F32)


GIVE_SEMS = 17


class Total:
    def __init__(self, wires, mine, out, sums, got):
        self.wires, self.out, self.sums, self.got = wires, out, sums, got
        self.z, self.g, _, _ = here()
        self.source = mine
        self.step = 0

    def push(self):
        sides = [sibling(self.g), along_x(self.g), along_y(self.g)]
        if self.step < 3:
            self.copies = [
                self.wires.send(self.source, self.got.at[self.step], (self.z, sides[self.step]))
            ]
        else:
            self.copies = [
                self.wires.send(self.source, self.got.at[3 + k], device)
                for k, device in enumerate(line_of(self.z, self.g))
            ]

    def pull(self):
        for copy in self.copies:
            copy.wait_recv()
        if self.step < 3:
            self.sums[self.step] = self.source[...] + self.got[self.step]
            self.source = self.sums.at[self.step]
            self.step += 1
        else:
            self.out[...] = self.source[...] + self.got[3] + self.got[4] + self.got[5]


def head_masks(rows, width, head_size):
    lane = lax.broadcasted_iota(jnp.int32, (rows, width), 1)
    return [(lane >= h * head_size) & (lane < (h + 1) * head_size) for h in range(GROUP)]


def stacked(block, masks):
    zero = jnp.zeros_like(block)
    return jnp.concatenate([jnp.where(mask, block, zero) for mask in masks], axis=0)


def unstacked(block, masks):
    rows = block.shape[0] // GROUP
    total = jnp.where(masks[0], block[:rows], 0.0)
    for h in range(1, GROUP):
        total = jnp.where(masks[h], block[h * rows : (h + 1) * rows], total)
    return total


def dot_last(a, b):
    return lax.dot_general(a, b, (((1,), (1,)), ((), ())), preferred_element_type=F32)


def dot_first(a, b):
    return lax.dot_general(a, b, (((0,), (0,)), ((), ())), preferred_element_type=F32)


def spread_heads(columns, first, masks):
    out = jnp.where(masks[0], columns[:, first : first + 1], 0.0)
    for h in range(1, GROUP):
        out = jnp.where(masks[h], columns[:, first + h : first + h + 1], out)
    return out


def attend(queries, keys, values, valid, scale, masks):
    rows = queries.shape[0]
    score = dot_last(stacked(queries, masks), keys) * scale
    expo = jnp.exp(score)
    if valid is not None:
        expo = jnp.where(valid > 0, expo, 0.0)
    totals = jnp.sum(expo, axis=1, keepdims=True)
    moments = jnp.sum(expo * score, axis=1, keepdims=True)
    weighted = jnp.dot(expo.astype(BF16), values, preferred_element_type=F32)
    heads = [(totals[h * rows : (h + 1) * rows], moments[h * rows : (h + 1) * rows]) for h in range(GROUP)]
    return unstacked(weighted, masks), heads


def pack_rows(terms):
    part = terms.shape[0] // 4
    out = terms[:part]
    for k in range(1, 4):
        out = out + pltpu.roll(terms[k * part : (k + 1) * part], 32 * k, 1)
    return out


def unpack_rows(packed):
    turned = [pltpu.roll(packed, 128 - 32 * k, 1) for k in range(1, 4)]
    return jnp.concatenate([packed] + turned, axis=0)


def put_heads(heads, group, lane):
    out = jnp.zeros(lane.shape, F32)
    for h, (total, moment) in enumerate(heads):
        out = jnp.where(lane == group * GROUP + h, total, out)
        out = jnp.where(lane == H + group * GROUP + h, moment, out)
    return out


def assemble(smalls, out):
    count, rows, lanes = smalls.shape
    shard = out.shape[1] // count
    block = 8
    row = lax.broadcasted_iota(jnp.int32, (block * lanes, block * shard), 0)
    col = lax.broadcasted_iota(jnp.int32, (block * lanes, block * shard), 1)
    lane = row % lanes
    chosen = ((row // lanes) * shard + lane == col) & (lane < shard)
    place = jnp.where(chosen, 1.0, 0.0).astype(BF16)
    for n in range(count // block):
        pieces = jnp.concatenate([smalls[n * block + d] for d in range(block)], axis=1)
        out[:, n * block * shard : (n + 1) * block * shard] = jnp.dot(
            pieces.astype(BF16), place, preferred_element_type=F32
        )


def up_places(z, chip):
    places = []
    for dz in range(LINES):
        for dx, dy in ((0, 0), (1, 0), (0, 1), (1, 1)):
            if dz or dx or dy:
                x, y = chip % 2, chip // 2
                there = (y + dy) % 2 * 2 + (x + dx) % 2
                places.append(((turn(z, dz), there), (turn(z, LINES - dz) if dz else z, there)))
    return places


def shares(counts_ref, z, g, frame, frames, items):
    position = z * frames + frame
    end, slot = 0, 0
    for item in range(items):
        end = end + counts_ref[g, item]
        slot = slot + jnp.where(end <= position, 1, 0)
    return [jnp.where(slot == item, 1.0, 0.0) for item in range(items)]


def put_times(out, tables, times_ref, frames):
    for frame in range(frames):
        row = jnp.zeros((1, out.shape[1]), F32)
        for t in range(8):
            row = row + jnp.where(times_ref[frame] == t, 1.0, 0.0) * tables[t : t + 1]
        out[frame : frame + 1] = row


def opening_kernel(scale, *refs):
    (
        time_table_ref,
        media_gain_ref,
        latent_gain_ref,
        ffn_gain_ref,
        key_shard,
        value_shard,
        query_shard,
        out_shard,
        latents_ref,
        up_ref,
        down_ref,
        cot_ref,
        media_ref,
        valid_ref,
        counts_ref,
        times_ref,
        tables_out,
        counts_out,
        key_weight_out,
        value_weight_out,
        query_weight_out,
        out_weight_out,
        up_out,
        down_out,
        cot_out,
        normed_out,
        keys_out,
        values_out,
        table_out,
        line_normed_out,
        got_weighted,
        got_stats,
        own_weighted,
        own_stats,
        send_sems,
        recv_sems,
        local_sems,
        up_own,
        small_ref,
        smalls,
        key_weight,
        value_weight,
        query_weight,
        line_latents,
        line_normed,
        normed,
        keys,
        values,
        own_table,
        table,
        time_rows,
        sums,
        weighted,
        stats,
        packed,
    ) = refs
    z, g, chip, core = here()
    here_chip = 4 * z + chip
    me = 2 * here_chip + core
    items, rows, width = line_latents.shape
    frames, _, patches = valid_ref.shape
    shard = key_shard.shape[0]
    span = width // (H // GROUP)
    up_width = up_out.shape[-1]
    near = (z, sibling(g))
    places = up_places(z, chip)
    greet([(there[0], 2 * there[1] + core) for there, _ in places] + [near])
    wires = Wires(send_sems, recv_sems)
    masks = head_masks(rows, span, span // GROUP)
    lane = lax.broadcasted_iota(jnp.int32, (rows, 128), 1)
    local = []
    small_ref[...] = jnp.zeros_like(small_ref)
    for place, source in (
        (slice(0, 8), time_table_ref),
        (slice(8, 9), media_gain_ref),
        (slice(9, 10), latent_gain_ref),
        (slice(10, 11), ffn_gain_ref),
    ):
        small_ref[place, :shard] = source[...].astype(F32)
    found = valid_ref[0].astype(F32)
    for n in range(1, frames):
        found = found + valid_ref[n].astype(F32)
    small_ref[11:12] = jnp.sum(found, axis=1, keepdims=True) + jnp.zeros((1, 128), F32)

    def keep(source, target):
        copy = pltpu.make_async_copy(source, target, local_sems.at[len(local)])
        copy.start()
        local.append(copy)
        return copy

    def rows_of(ref):
        return lambda zz, gg: ref.at[pl.ds(pl.multiple_of((zz * 8 + gg) * shard, 16), shard)]

    def piece(place):
        return up_ref.at[:, pl.ds(pl.multiple_of((4 * place[0] + place[1]) * up_width, 128), up_width)]

    def whole(source, slot):
        return Spread(wires, source, slot, columns_half, True), keep(source, slot(z, g))

    def small_slot(zz, gg):
        return smalls.at[zz * 8 + gg]

    small = Spread(wires, small_ref, small_slot, rows_half, True)
    small_kept = keep(small_ref, small_slot(z, g))
    key, key_kept = whole(key_shard, rows_of(key_weight))
    value, value_kept = whole(value_shard, rows_of(value_weight))
    query = Spread(wires, query_shard, rows_of(query_weight), rows_parts, True, True)
    query_kept = keep(piece_of(query_shard, z), rows_of(query_weight)(z, g))
    query_line = Line(wires, own_table, lambda zz: table.at[zz])
    out, out_kept = whole(out_shard, rows_of(out_weight_out))
    cot = Spread(wires, cot_ref, lambda zz, gg: cot_out.at[zz * 4 + gg // 2], columns_half, False)
    line = Line(wires, latents_ref, lambda zz: line_latents.at[zz])
    exchange = Exchange(
        wires,
        [(weighted, got_weighted), (packed, got_stats)],
    )
    line_kept = keep(latents_ref, line_latents.at[z])
    up_load = keep(piece((z, chip)), up_own)
    late = [
        out_kept,
        keep(cot_ref, cot_out.at[here_chip]),
        keep(down_ref, down_out.at[core]),
    ]
    prompt = len(local)
    moved, given, down = [], [], []
    chunk = 32

    def normalise(first, last):
        @pl.loop(first, last)
        def _(n):
            block = pl.ds(pl.multiple_of(n * chunk, chunk), chunk)
            frame = n // (patches // chunk)
            row = media_ref[block].astype(F32) + time_rows[pl.ds(frame, 1)]
            normed[block] = layer_norm(row, tables_out[8:9]).astype(BF16)

    def normalise_latents():
        gain = tables_out[9:10]
        line_kept.wait()
        for item in range(items):

            @pl.loop(0, rows // chunk)
            def _(n):
                block = pl.ds(pl.multiple_of(n * chunk, chunk), chunk)
                row = line_latents[item, block].astype(F32)
                line_normed[item, block] = layer_norm(row, gain).astype(BF16)

        normed[frames * patches :] = line_normed[z]

    def tabulate():
        small_kept.wait()
        assemble(smalls, tables_out)
        counts = smalls[0, 8:]
        for n in range(1, smalls.shape[0]):
            counts = counts + smalls[n, 8:]
        counts_out[...] = counts
        put_times(time_rows, tables_out, times_ref, frames)

    def project(left, weight, out, first):
        @pl.loop(first, first + 2)
        def _(n):
            cols = pl.ds(pl.multiple_of(n * span, 128), span)
            out[:, cols] = jnp.dot(
                left[...], weight[:, cols], preferred_element_type=F32
            ).astype(BF16)

    def project_keys(first):
        if first == 0:
            key_kept.wait()
            keep(key_weight, key_weight_out)
            keep(normed, normed_out)
        project(normed, key_weight, keys, first)
        if first > 0:
            keep(keys, keys_out)

    def project_values(first):
        if first == 0:
            value_kept.wait()
            keep(value_weight, value_weight_out)
        project(normed, value_weight, values, first)
        if first > 0:
            keep(values, values_out)

    def project_queries():
        query_kept.wait()
        keep(query_weight, query_weight_out)
        for item in range(items):
            own_table[item] = jnp.dot(
                line_normed[item], query_weight[...], preferred_element_type=F32
            ).astype(BF16)
        table[z] = own_table[...]
        query_line.first()

    def attend_own():
        keep(table, table_out)
        keep(line_normed, line_normed_out)
        sums[...] = jnp.zeros_like(sums)
        stats[...] = jnp.zeros_like(stats)
        last = slice(frames * patches, frames * patches + rows)
        own = jnp.zeros((rows, 128), F32)
        for group in range(H // GROUP):
            cols = slice(group * span, (group + 1) * span)
            part, heads = attend(
                table[group, z], keys[last, cols], values[last, cols], None, scale, masks
            )
            own_weighted[:, cols] = part
            own = own + put_heads(heads, group, lane)
        own_stats[...] = own

    def attend_frames(first, last):
        @pl.loop(first, last)
        def _(frame):
            share = shares(counts_ref, z, g, frame, frames, items)
            block = pl.ds(pl.multiple_of(frame * patches, patches), patches)
            valid = valid_ref[frame]
            found = jnp.zeros((rows, 128), F32)
            for group in range(H // GROUP):
                cols = slice(group * span, (group + 1) * span)
                chosen = share[0] * table[group, 0].astype(F32)
                for item in range(1, items):
                    chosen = chosen + share[item] * table[group, item].astype(F32)
                part, heads = attend(
                    chosen.astype(BF16), keys[block, cols], values[block, cols], valid, scale, masks
                )
                found = found + put_heads(heads, group, lane)
                for item in range(items):
                    sums[item, :, cols] += share[item] * part
            for item in range(items):
                stats[item] += share[item] * found

    def down_first():
        down.append(wires.send(down_ref, down_out.at[core], near))

    def up_first():
        up_load.wait()
        keep(up_own, up_out.at[me])
        given.append(wires.send(up_own, up_out.at[me], near))
        for there, _ in places:
            moved.append(
                wires.send(piece(there), up_out.at[me], (there[0], 2 * there[1] + core))
            )

    def up_last():
        for n, (_, origin) in enumerate(places):
            moved[n].wait_recv()
            held = up_out.at[2 * (4 * origin[0] + origin[1]) + core]
            given.append(wires.send(held, held, near))
        for copy in given:
            copy.wait_recv()

    def sums_first():
        weighted[...] = sums[...].astype(BF16)
        for item in range(items):
            packed[item] = pack_rows(stats[item])
        exchange.first()

    small.first()
    value.first()
    small.corner_y(0)
    small.column(0)
    query.first()
    down_first()
    small.column(1)
    key.first()
    small.corner_x(1)
    value.column(0)
    key.corner_y(0)
    line.first()
    small.corner_y(2)
    query.column(0)
    value.column(1)
    query.column(1)
    small.corner_x(2)
    small.column(2)
    query.corner_y(0)
    key.column(0)
    query.corner_y(2)
    small.corner_y(1)
    small.corner_x(3)
    value.corner_y(0)
    query.corner_x(0)
    value.corner_x(1)
    query.corner_y(1)
    value.corner_x(0)
    small.corner_x(0)
    query.corner_x(1)
    small.corner_y(3)
    query.column(2)
    value.corner_y(1)
    key.column(1)
    value.corner_x(2)
    query.corner_x(2)
    value.column(2)
    small.last(1)
    line.take(0)
    small.last(0)
    line.take(1)
    out.first()
    key.corner_y(1)
    query.corner_y(3)
    small.last(3)
    value.corner_y(2)
    small.last(2)
    query.last(1)
    small.finish()
    tabulate()
    query.corner_x(3)
    key.column(2)
    value.last(0)
    normalise(0, 8)
    key.corner_x(1)
    query.last(0)
    query.last(2)
    value.corner_y(3)
    normalise(8, 16)
    line.take(2)
    query.last(3)
    key.corner_x(2)
    value.corner_x(3)
    value.last(1)
    key.corner_x(0)
    cot.first()
    key.corner_y(3)
    down[0].wait_recv()
    query.finish()
    normalise_latents()
    project_queries()
    value.last(2)
    key.corner_x(3)
    value.last(3)
    key.corner_y(2)
    out.column(0)
    value.finish()
    key.last(1)
    out.column(1)
    out.corner_x(1)
    key.last(3)
    key.last(0)
    out.corner_y(0)
    cot.corner_x(0)
    out.column(2)
    cot.corner_y(0)
    key.last(2)
    project_values(0)
    project_values(2)
    up_first()
    key.finish()
    project_keys(0)
    out.corner_y(1)
    query_line.take(0)
    out.corner_y(3)
    out.corner_x(3)
    project_keys(2)
    cot.last(0)
    cot.column(0)
    query_line.take(1)
    query_line.take(2)
    cot.column(1)
    out.corner_y(2)
    attend_own()
    attend_frames(0, 2)
    out.corner_x(2)
    attend_frames(2, 4)
    sums_first()
    out.corner_x(0)
    out.last(1)
    cot.column(2)
    cot.corner_y(2)
    cot.corner_x(1)
    cot.corner_y(1)
    cot.corner_x(2)
    cot.corner_y(3)
    cot.corner_x(3)
    out.last(3)
    up_last()
    out.last(0)
    out.last(2)
    out.finish()
    exchange.finish()
    cot.last(2)
    cot.last(3)
    cot.last(1)
    for copy in late + local[prompt:]:
        copy.wait()
    wires.drain()


def opening(scale, small, weights, latents, w_up, w_down, cotangent, media, valid, counts, times):
    rows, width = latents.shape
    shard = weights[0].shape[0]
    up_rows, up_width = w_up.shape
    all_rows = media.shape[0] + rows
    wires = 5 * spread_sems(True) + spread_sems(False) + 2 * LINE_SEMS + 31 + 1 + 2 * LINES
    span = width // LINES
    square = jax.ShapeDtypeStruct((width, width), BF16)
    table = jax.ShapeDtypeStruct((LINES, rows, width), BF16)
    keys = jax.ShapeDtypeStruct((all_rows, width), BF16)
    smem = pl.BlockSpec(memory_space=pltpu.SMEM)
    return pl.pallas_call(
        partial(opening_kernel, scale),
        out_shape=[
            jax.ShapeDtypeStruct((16, width), F32),
            jax.ShapeDtypeStruct((8, 128), F32),
            square,
            square,
            jax.ShapeDtypeStruct((width, span), BF16),
            square,
            jax.ShapeDtypeStruct((32, up_rows, up_width // 16), BF16),
            jax.ShapeDtypeStruct((2,) + w_down.shape, BF16),
            jax.ShapeDtypeStruct((16,) + cotangent.shape, BF16),
            keys,
            keys,
            keys,
            jax.ShapeDtypeStruct((LINES, LINES, rows, span), BF16),
            table,
            table,
            jax.ShapeDtypeStruct((LINES, rows // 4, 128), F32),
            jax.ShapeDtypeStruct((rows, width), F32),
            jax.ShapeDtypeStruct((rows, 128), F32),
        ],
        in_specs=[VMEM] * 8 + [LEFT] * 2 + [VMEM] * 4 + [smem] * 2,
        out_specs=[VMEM] * 2 + [LEFT] * 12 + [VMEM] * 4,
        scratch_shapes=[
            sems(wires),
            sems(wires),
            sems(24),
            pltpu.VMEM((up_rows, up_width // 16), BF16),
            pltpu.VMEM((16, 128), F32),
            pltpu.VMEM((32, 16, 128), F32),
            pltpu.VMEM((width, width), BF16),
            pltpu.VMEM((width, width), BF16),
            pltpu.VMEM((width, span), BF16),
            pltpu.VMEM((LINES, rows, width), BF16),
            pltpu.VMEM((LINES, rows, width), BF16),
            pltpu.VMEM((all_rows, width), BF16),
            pltpu.VMEM((all_rows, width), BF16),
            pltpu.VMEM((all_rows, width), BF16),
            pltpu.VMEM((LINES, rows, span), BF16),
            pltpu.VMEM((LINES, LINES, rows, span), BF16),
            pltpu.VMEM((8, width), F32),
            pltpu.VMEM((LINES, rows, width), F32),
            pltpu.VMEM((LINES, rows, width), BF16),
            pltpu.VMEM((LINES, rows, 128), F32),
            pltpu.VMEM((LINES, rows // 4, 128), F32),
        ],
        compiler_params=params(0),
        name="opening",
    )(*small, *weights, latents, w_up, w_down, cotangent, media, valid, counts, times)


def repel(queries, grads, keys, values, valid, shift, slope, scale, masks):
    query_stack = stacked(queries, masks)
    grad_stack = stacked(grads, masks)
    score = dot_last(query_stack, keys) * scale
    expo = jnp.exp(score)
    if valid is not None:
        expo = jnp.where(valid > 0, expo, 0.0)
    mix = dot_last(grad_stack, values)
    raw = (expo * (mix + shift + slope * score) * scale).astype(BF16)
    query_grad = unstacked(jnp.dot(raw, keys, preferred_element_type=F32), masks)
    key_grad = dot_first(raw, query_stack).astype(BF16)
    value_grad = dot_first(expo.astype(BF16), grad_stack).astype(BF16)
    return query_grad, key_grad, value_grad


def stacked_columns(terms, first):
    return jnp.concatenate([terms[:, first + h : first + h + 1] for h in range(GROUP)], axis=0)


def closing_kernel(scale, *refs):
    (
        table_ref,
        grad_ref,
        terms_ref,
        keys_ref,
        values_ref,
        normed_ref,
        valid_ref,
        attn_ref,
        low_ref,
        own_grad_ref,
        own_terms_ref,
        line_normed_ref,
        query_weight_ref,
        key_weight_ref,
        value_weight_ref,
        media_ref,
        tables_ref,
        latents_ref,
        middle_grad_ref,
        ffn_gain_ref,
        counts_ref,
        times_ref,
        media_grad_out,
        latents_grad_out,
        small_out,
        out_out,
        value_out,
        key_out,
        query_out,
        send_sems,
        recv_sems,
        local_sems,
        table,
        grads,
        keys,
        values,
        normed,
        key_grad,
        value_grad,
        weight_a,
        weight_b,
        sums,
        terms_query,
        got_query,
        query_grad,
        got_line,
        media_grad,
        latent_grad,
        small,
        small_sums,
        small_got,
        time_rows_ref,
        part_a,
        part_b,
        part_c,
        part_d,
        query_relay,
        line_relay,
        *fold,
    ) = refs
    z, g, _, core = here()
    items, rows, width = grads.shape
    frames, _, patches = valid_ref.shape
    media_rows = frames * patches
    shard = width // 32
    groups = H // GROUP
    span = width // groups
    masks = head_masks(rows, span, span // GROUP)
    greet(line_of(z, g) + sides_of(z, g, True))
    wires = Wires(send_sems, recv_sems)
    out = Fold(wires, part_a, True, fold[:FOLD], out_out)
    value = Fold(wires, part_b, True, fold[FOLD : 2 * FOLD], value_out)
    key = Fold(wires, part_c, True, fold[2 * FOLD : 3 * FOLD], key_out)
    query = FoldSplit(wires, part_d, True, fold[3 * FOLD :], query_out)
    total = Total(wires, small, small_out, small_sums, small_got)
    exchange = SumLine(wires, terms_query, got_query, query_relay)
    line_exchange = SumLine(wires, grads, got_line, line_relay)
    local = []

    def load(source, target):
        copy = pltpu.make_async_copy(source, target, local_sems.at[len(local)])
        copy.start()
        local.append(copy)
        return copy

    loads = [
        load(table_ref, table),
        load(grad_ref, grads),
        load(keys_ref, keys),
        load(values_ref, values),
    ]
    normed_load = load(normed_ref, normed)
    key_load = load(key_weight_ref, weight_a)
    value_load = load(value_weight_ref, weight_b)
    stored = []

    def weight_part(part, left, right, first, last):
        @pl.loop(first, last)
        def _(n):
            cols = pl.ds(pl.multiple_of(n * span, 128), span)
            block = dot_first(left[:, cols], right[...]).astype(BF16)
            part[n] = block.reshape(PLANE, 2, shard, width)

    def out_part():
        weight_part(part_a, attn_ref, low_ref, 0, LINES)
        out.start()

    def value_part(first):
        if first == 0:
            normed_load.wait()
        weight_part(part_b, normed, value_grad, first, first + 2)
        if first > 0:
            value.start()

    def key_part(first):
        weight_part(part_c, normed, key_grad, first, first + 2)
        if first > 0:
            key.start()

    def repel_own():
        for copy in loads:
            copy.wait()
        sums[...] = jnp.zeros_like(sums)
        own_terms = own_terms_ref[...]
        for group in range(groups):
            cols = slice(group * span, (group + 1) * span)
            (
                sums[group, z],
                key_grad[media_rows:, cols],
                value_grad[media_rows:, cols],
            ) = repel(
                table[group, z],
                own_grad_ref[:, cols],
                keys[media_rows:, cols],
                values[media_rows:, cols],
                None,
                stacked_columns(own_terms, group * GROUP),
                stacked_columns(own_terms, H + group * GROUP),
                scale,
                masks,
            )

    def repel_frames(first, last):
        @pl.loop(first, last)
        def _(frame):
            block = pl.ds(pl.multiple_of(frame * patches, patches), patches)
            valid = valid_ref[frame]
            share = shares(counts_ref, z, g, frame, frames, items)

            def pick(ref, cols):
                chosen = share[0] * ref[0, :, cols].astype(F32)
                for item in range(1, items):
                    chosen = chosen + share[item] * ref[item, :, cols].astype(F32)
                return chosen

            everything = slice(None)
            terms = unpack_rows(pick(terms_ref, everything))
            for group in range(groups):
                cols = slice(group * span, (group + 1) * span)
                query_part, key_grad[block, cols], value_grad[block, cols] = repel(
                    pick(table.at[group], everything).astype(BF16),
                    pick(grads, cols).astype(BF16),
                    keys[block, cols],
                    values[block, cols],
                    valid,
                    stacked_columns(terms, group * GROUP),
                    stacked_columns(terms, H + group * GROUP),
                    scale,
                    masks,
                )
                for item in range(items):
                    sums[group, item] += share[item] * query_part

    def queries_first():
        terms_query[...] = sums[...].astype(BF16)
        exchange.first()

    def media_product(n):
        if n == 0:
            key_load.wait()
            value_load.wait()
            small[...] = jnp.zeros_like(small)
            small[10:11] = ffn_gain_ref[...]
            put_times(time_rows_ref, tables_ref, times_ref, frames)
        if n == 2:
            stored[-1].wait()
        count = media_rows // 2
        block = slice(n // 2 * count, (n // 2 + 1) * count)

        @pl.loop(n % 2 * 2, n % 2 * 2 + 2)
        def _(t):
            cols = pl.ds(pl.multiple_of(t * span, 128), span)
            media_grad[:, cols] = dot_last(key_grad[block], weight_a[cols]) + dot_last(
                value_grad[block], weight_b[cols]
            )

    def media_pull(frame):
        count = media_rows // 2
        gain = tables_ref[8:9]
        chunk = 32
        f = frame % (frames // 2)
        moving = time_rows_ref[frame : frame + 1]

        def step(t, carry):
            gain_sum, row_sum = carry
            here_rows = pl.ds(pl.multiple_of(f * patches + t * chunk, chunk), chunk)
            there_rows = pl.ds(pl.multiple_of(frame * patches + t * chunk, chunk), chunk)
            row = media_ref[there_rows].astype(F32) + moving
            pulled, summand = norm_pull(row, gain, media_grad[here_rows])
            media_grad[here_rows] = pulled
            return (
                gain_sum + jnp.sum(summand, axis=0, keepdims=True),
                row_sum + jnp.sum(pulled, axis=0, keepdims=True),
            )

        zero = jnp.zeros((1, width), F32)
        gain_sum, row_sum = lax.fori_loop(0, patches // chunk, step, (zero, zero))
        small[8:9] += gain_sum
        for t in range(8):
            small[t : t + 1] += jnp.where(times_ref[frame] == t, 1.0, 0.0) * row_sum
        if f == frames // 2 - 1:
            first = frame // (frames // 2) * count
            stored.append(load(media_grad, media_grad_out.at[pl.ds(first, count)]))

    def latents_side():
        @pl.loop(0, groups)
        def _(t):
            cols = pl.ds(pl.multiple_of(t * span, 128), span)
            latent_grad[:, cols] = dot_last(key_grad[media_rows:], weight_a[cols]) + dot_last(
                value_grad[media_rows:], weight_b[cols]
            )

    def query_part():
        for item in range(items):
            found = got_query[0, item].astype(F32)
            for place in range(1, LINES):
                found = found + got_query[place, item].astype(F32)
            query_grad[item] = found.astype(BF16)
        grads_all = query_grad[...].reshape(items * rows, span)

        @pl.loop(0, LINES)
        def _(n):
            cols = pl.ds(pl.multiple_of(n * span, 128), span)
            left = line_normed_ref[:, :, cols].reshape(items * rows, span)
            block = dot_first(left, grads_all).astype(BF16)
            part_d[n] = block.reshape(PLANE, 2, shard, span)

        query.start()

    def line_first():
        for item in range(items):
            grads[item] = dot_last(query_grad[item], query_weight_ref[...]).astype(BF16)
        line_exchange.first()

    def latents_end():
        for place in range(LINES):
            latent_grad[...] += got_line[place].astype(F32)
        pulled, summand = norm_pull(
            latents_ref[...].astype(F32), tables_ref[9:10], latent_grad[...]
        )
        latents_grad_out[...] = middle_grad_ref[...] + pulled
        small[9:10] = jnp.sum(summand, axis=0, keepdims=True)
        total.push()

    def total_next():
        total.pull()
        total.push()

    out_part()
    repel_own()
    repel_frames(0, 2)
    repel_frames(2, 4)
    queries_first()
    out.corner()
    media_product(0)
    value_part(0)
    value_part(2)
    out.side_x()
    out.side_y()
    key_part(0)
    exchange.relay()
    media_product(1)
    value.corner()
    key_part(2)
    media_pull(0)
    media_pull(1)
    exchange.finish()
    query_part()
    key.corner()
    line_first()
    value.side_x()
    value.side_y()
    key.side_x()
    out.line()
    line_exchange.relay()
    media_product(2)
    media_product(3)
    key.side_y()
    media_pull(2)
    out.relay()
    value.line()
    media_pull(3)
    line_exchange.finish()
    query.corner()
    latents_side()
    value.relay()
    latents_end()
    key.line()
    total_next()
    query.side_x()
    query.side_y()
    total_next()
    key.relay()
    out.finish()
    query.line()
    value.finish()
    total_next()
    query.finish()
    key.finish()
    total.pull()
    stored[1].wait()
    wires.drain()


def closing(scale, *args):
    (table, grads, terms, keys, values, normed) = args[:6]
    media, latents = args[15], args[17]
    span = table.shape[-1]
    rows, width = latents.shape
    shard = width // 32
    wires = 4 * fold_sems(True) + 6 + 2 * LINES
    bf = [
        table.shape,
        grads.shape,
        keys.shape,
        keys.shape,
        keys.shape,
        keys.shape,
        keys.shape,
        (width, width),
        (width, width),
    ]
    part = pltpu.VMEM((LINES, PLANE, 2, shard, width), BF16)
    small = (16, width)
    scratch = [pltpu.VMEM(shape, BF16) for shape in bf] + [
        pltpu.VMEM(table.shape, F32),
        pltpu.VMEM(table.shape, BF16),
        pltpu.VMEM(table.shape, BF16),
        pltpu.VMEM(table.shape[1:], BF16),
        pltpu.VMEM(grads.shape, BF16),
        pltpu.VMEM((media.shape[0] // 2, width), F32),
        pltpu.VMEM((rows, width), F32),
        pltpu.VMEM(small, F32),
        pltpu.VMEM((3,) + small, F32),
        pltpu.VMEM((6,) + small, F32),
        pltpu.VMEM((8, width), F32),
        part,
        part,
        part,
        pltpu.VMEM((LINES, PLANE, 2, shard, span), BF16),
        pltpu.VMEM(table.shape[1:], BF16),
        pltpu.VMEM((rows, width), BF16),
    ]
    scratch += fold_scratch(shard, width, True) * 3 + fold_scratch(shard, span, True, True)
    smem = pl.BlockSpec(memory_space=pltpu.SMEM)
    return pl.pallas_call(
        partial(closing_kernel, scale),
        out_shape=[
            jax.ShapeDtypeStruct(media.shape, F32),
            jax.ShapeDtypeStruct(latents.shape, F32),
            jax.ShapeDtypeStruct(small, F32),
        ]
        + [jax.ShapeDtypeStruct((shard, width), F32)] * 4,
        in_specs=[LEFT, LEFT, VMEM, LEFT, LEFT, LEFT]
        + [VMEM] * 7
        + [LEFT] * 2
        + [VMEM] * 5
        + [smem] * 2,
        out_specs=[LEFT] + [VMEM] * 6,
        scratch_shapes=[sems(wires), sems(wires), sems(12)] + scratch,
        compiler_params=pltpu.CompilerParams(
            collective_id=3, has_side_effects=True, vmem_limit_bytes=67043328
        ),
        name="closing",
    )(*args)


def settle_kernel(
    weighted_ref,
    stats_ref,
    own_weighted_ref,
    own_stats_ref,
    out_ref,
    latents_ref,
    gain_ref,
    attention_ref,
    attn_ref,
    sums_ref,
    middle_ref,
    normed_ref,
    ready,
):
    rows, width = latents_ref.shape
    span = width // (H // GROUP)
    masks = head_masks(rows, span, span // GROUP)
    found = stats_ref[0]
    for n in range(1, stats_ref.shape[0]):
        found = found + stats_ref[n]
    stats = own_stats_ref[...] + unpack_rows(found)
    sums_ref[...] = stats
    for group in range(H // GROUP):
        cols = pl.ds(group * span, span)
        weighted = own_weighted_ref[:, cols]
        for n in range(weighted_ref.shape[0]):
            weighted = weighted + weighted_ref[n, :, cols].astype(F32)
        attention = weighted / spread_heads(stats, group * GROUP, masks)
        attention_ref[:, cols] = attention
        attn_ref[:, cols] = attention.astype(BF16)
    ready()
    middle = latents_ref[...].astype(F32) + jnp.dot(
        attn_ref[...], out_ref[...], preferred_element_type=F32
    )
    middle_ref[...] = middle
    normed_ref[...] = layer_norm(middle, gain_ref[...]).astype(BF16)


def norm_pull(rows, gain, grad):
    mean = jnp.mean(rows, axis=-1, keepdims=True)
    centred = rows - mean
    inverse = lax.rsqrt(jnp.mean(centred * centred, axis=-1, keepdims=True) + NORM_STABILIZER)
    xhat = centred * inverse
    t = grad * gain
    pulled = (
        t
        - jnp.mean(t, axis=-1, keepdims=True)
        - xhat * jnp.mean(t * xhat, axis=-1, keepdims=True)
    ) * inverse
    return pulled, grad * xhat


def unsettle_kernel(
    normed_grad_ref,
    middle_ref,
    gain_ref,
    cot_ref,
    out_ref,
    attention_ref,
    stats_ref,
    coef,
    middle_grad_ref,
    low_ref,
    gain_grad_ref,
    weighted_grad_ref,
    terms_ref,
    attn_grad,
):
    rows, width = middle_ref.shape
    span = width // (H // GROUP)
    masks = head_masks(rows, span, span // GROUP)
    pulled, summand = norm_pull(middle_ref[...], gain_ref[...], normed_grad_ref[...])
    gain_grad_ref[...] = jnp.sum(summand, axis=0, keepdims=True)
    middle_grad = cot_ref[...].astype(F32) + pulled
    middle_grad_ref[...] = middle_grad
    low_ref[...] = middle_grad.astype(BF16)
    attn_grad[...] = dot_last(low_ref[...], out_ref[...])
    stats = stats_ref[...]
    lane = lax.broadcasted_iota(jnp.int32, (rows, 128), 1)
    terms = jnp.zeros((rows, 128), F32)
    for group in range(H // GROUP):
        cols = pl.ds(group * span, span)
        grad = attn_grad[:, cols]
        first = group * GROUP
        weighted_grad_ref[:, cols] = (grad / spread_heads(stats, first, masks)).astype(BF16)
        along = grad * attention_ref[:, cols]
        for h in range(GROUP):
            inner = jnp.sum(jnp.where(masks[h], along, 0.0), axis=1, keepdims=True)
            total = stats[:, first + h : first + h + 1]
            moment = stats[:, H + first + h : H + first + h + 1]
            slope = -coef / total
            shift = -inner / total + coef * (1.0 / total + moment / (total * total)) + slope
            terms = jnp.where(lane == first + h, shift, terms)
            terms = jnp.where(lane == H + first + h, slope, terms)
    terms_ref[...] = terms


def gelu_parts(rows):
    below = 0.5 * (1.0 + lax.erf(rows * (0.5**0.5)))
    density = jnp.exp(-0.5 * rows * rows) * ((0.5 / jnp.pi) ** 0.5)
    return rows * below, below + rows * density


def middle_kernel(patches, *refs):
    (
        weighted_ref,
        stats_ref,
        own_weighted_ref,
        own_stats_ref,
        out_weight_ref,
        up_ref,
        down_ref,
        cot_rows_ref,
        latents_ref,
        tables_ref,
        cot_ref,
        counts_ref,
        attn_out,
        low_out,
        middle_grad_out,
        gain_grad_out,
        weighted_grad_out,
        terms_out,
        grad_table_out,
        terms_table_out,
        new_latents_out,
        up_grad_out,
        down_grad_out,
        send_sems,
        recv_sems,
        local_sems,
        out_weight,
        up_cols,
        down_rows,
        cot_rows,
        ffn_rows,
        attention,
        sums,
        middle,
        normed,
        hidden_grad,
        up_grad,
        hidden,
        normed_part,
        down_part,
        up_grad_part,
        down_grad_part,
        up_near,
        down_near,
        up_got,
        normed_grad,
        down_sum,
        attn_grad,
        packed,
        *fold,
    ) = refs
    z, g, chip, core = here()
    rows, width = latents_ref.shape
    span = up_cols.shape[1]
    shard = width // 32
    block_rows = PLANE * rows
    near = (z, sibling(g))
    gain_ref = tables_ref.at[10:11]
    greet([(there[0], 2 * there[1] + core) for there, _ in up_places(z, chip)] + [near])
    wires = Wires(send_sems, recv_sems)
    gather = Spread(
        wires, normed, lambda zz, gg: ffn_rows.at[zz, gg // 2], columns_half, False
    )
    back = FoldSteps(wires, normed_part, fold[:FOLD], normed_grad)
    down = Fold(wires, down_part, False, fold[FOLD:], down_sum)
    give = GiveBack(
        wires,
        up_grad_part,
        down_grad_part,
        (up_near, down_near, up_got),
        up_grad_out,
        down_grad_out,
    )
    grad_line = Line(wires, weighted_grad_out, lambda zz: grad_table_out.at[zz])
    terms_line = Line(wires, packed, lambda zz: terms_table_out.at[zz])
    loads = [
        pltpu.make_async_copy(source, target, local_sems.at[n])
        for n, (source, target) in enumerate(
            (
                (out_weight_ref, out_weight),
                (down_ref, down_rows),
                (cot_rows_ref, cot_rows),
                (up_ref, up_cols),
            )
        )
    ]
    for load in loads:
        load.start()

    def settle():
        settle_kernel(
            weighted_ref,
            stats_ref,
            own_weighted_ref,
            own_stats_ref,
            out_weight,
            latents_ref,
            gain_ref,
            attention,
            attn_out,
            sums,
            middle,
            normed,
            loads[0].wait,
        )
        ffn_rows[z, chip] = normed[...]

    def hidden_back():
        loads[1].wait()
        loads[2].wait()
        loads[3].wait()

        @pl.loop(0, LINES)
        def _(n):
            block = cot_rows[n].reshape(block_rows, width)
            hidden_grad[n] = dot_last(block, down_rows[...])

    def group(n):
        place = gather.zs[n]
        block = ffn_rows[place].reshape(block_rows, width)
        value, slope = gelu_parts(jnp.dot(block, up_cols[...], preferred_element_type=F32))
        hidden[place] = value.astype(BF16)
        grad = (hidden_grad[place] * slope).astype(BF16)
        up_grad[place] = grad
        part = dot_last(grad, up_cols[...]).astype(BF16)
        normed_part[place] = part.reshape(PLANE, rows, width)

    def down_product():
        @pl.loop(0, LINES)
        def _(n):
            part = jnp.dot(hidden[n], down_rows[...], preferred_element_type=F32)
            down_part[n] = part.astype(BF16).reshape(PLANE, rows, width)

    def up_gradient():
        grads = up_grad[...].reshape(LINES * block_rows, span)

        @pl.loop(0, LINES)
        def _(n):
            cols = pl.ds(pl.multiple_of(n * span, 128), span)
            block = ffn_rows[:, :, :, cols].reshape(LINES * block_rows, span)
            part = dot_first(block, grads).astype(BF16)
            up_grad_part[n] = part.reshape(PLANE, 2, shard, span)

    def down_gradient():
        rows_up = hidden[...].reshape(LINES * block_rows, span)

        @pl.loop(0, LINES)
        def _(n):
            cols = pl.ds(pl.multiple_of(n * span, 128), span)
            block = cot_rows[:, :, :, cols].reshape(LINES * block_rows, span)
            part = dot_first(rows_up, block)
            down_grad_part[:, :, cols] = part.reshape(2, span // 2, span)

    def unsettle():
        unsettle_kernel(
            normed_grad,
            middle,
            gain_ref,
            cot_ref,
            out_weight,
            attention,
            sums,
            ENTROPY_WEIGHT * patches / counts_ref[3:4, 0:1],
            middle_grad_out,
            low_out,
            gain_grad_out,
            weighted_grad_out,
            terms_out,
            attn_grad,
        )
        grad_table_out[z] = weighted_grad_out[...]
        packed[...] = pack_rows(terms_out[...])
        terms_table_out[z] = packed[...]

    def new_rows():
        new_latents_out[...] = (middle[...] + down_sum[...]).astype(BF16)

    settle()
    gather.first()
    gather.column(0)
    gather.column(1)
    gather.corner_y(0)
    gather.corner_x(1)
    gather.corner_x(0)
    gather.corner_y(1)
    gather.column(2)
    gather.last(0)
    gather.corner_x(2)
    hidden_back()
    gather.corner_y(2)
    group(0)
    back.corner(0)
    gather.corner_y(3)
    gather.corner_x(3)
    gather.last(1)
    group(1)
    gather.last(2)
    back.corner(1)
    group(2)
    back.corner(2)
    gather.last(3)
    back.side_x(0)
    group(3)
    back.corner(3)
    back.side_y(2)
    back.side_y(1)
    up_gradient()
    back.side_x(2)
    down_product()
    back.side_y(3)
    back.side_x(3)
    back.side_y(0)
    back.side_x(1)
    down_gradient()
    give.first()
    down.start()
    back.line(2)
    down.corner()
    back.line(3)
    give.columns()
    back.line(1)
    back.line(0)
    back.relay()
    down.side_x()
    down.side_y()
    back.finish()
    unsettle()
    grad_line.first()
    terms_line.first()
    grad_line.take(0)
    grad_line.take(1)
    down.line()
    grad_line.take(2)
    terms_line.take(0)
    terms_line.take(1)
    give.rows()
    down.relay()
    give.finish()
    terms_line.take(2)
    down.finish()
    new_rows()
    wires.drain()


def middle_part(
    patches,
    weighted,
    stats,
    own_weighted,
    own_stats,
    w_out,
    up_cols,
    down_rows,
    cot_rows,
    latents,
    tables,
    cot,
    counts,
):
    rows, width = latents.shape
    span = up_cols.shape[1]
    shard = width // 32
    plane = (LINES, PLANE, rows, width)
    block = (LINES, PLANE * rows, span)
    wires = spread_sems(False) + STEP_SEMS + fold_sems(False) + GIVE_SEMS + 2 * LINE_SEMS
    own = (rows, width)
    terms = own_stats.shape
    bf = [
        w_out.shape,
        up_cols.shape,
        down_rows.shape,
        plane,
        plane,
    ]
    scratch = [pltpu.VMEM(shape, BF16) for shape in bf] + [
        pltpu.VMEM(own, F32),
        pltpu.VMEM(terms, F32),
        pltpu.VMEM(own, F32),
        pltpu.VMEM(own, BF16),
        pltpu.VMEM(block, F32),
        pltpu.VMEM(block, BF16),
        pltpu.VMEM(block, BF16),
        pltpu.VMEM(plane, BF16),
        pltpu.VMEM(plane, BF16),
        pltpu.VMEM((LINES, PLANE, 2, shard, span), BF16),
        pltpu.VMEM((2, span // 2, width), F32),
        pltpu.VMEM((LINES, PLANE, shard, span), BF16),
        pltpu.VMEM((span // 2, width), F32),
        pltpu.VMEM((LINES, PLANE, shard, span), BF16),
        pltpu.VMEM(own, F32),
        pltpu.VMEM(own, F32),
        pltpu.VMEM(own, F32),
        pltpu.VMEM((rows // 4, 128), F32),
    ]
    scratch += fold_scratch(rows, width, False) * 2
    return pl.pallas_call(
        partial(middle_kernel, patches),
        out_shape=[
            jax.ShapeDtypeStruct(own, BF16),
            jax.ShapeDtypeStruct(own, BF16),
            jax.ShapeDtypeStruct(own, F32),
            jax.ShapeDtypeStruct((1, width), F32),
            jax.ShapeDtypeStruct(own, BF16),
            jax.ShapeDtypeStruct(terms, F32),
            jax.ShapeDtypeStruct((LINES,) + own, BF16),
            jax.ShapeDtypeStruct((LINES, rows // 4, 128), F32),
            jax.ShapeDtypeStruct(own, BF16),
            jax.ShapeDtypeStruct((shard, span * 16), F32),
            jax.ShapeDtypeStruct((span // 2, width), F32),
        ],
        in_specs=[VMEM] * 4 + [LEFT] * 4 + [VMEM] * 4,
        out_specs=[VMEM] * 11,
        scratch_shapes=[sems(wires), sems(wires), sems(4)] + scratch,
        compiler_params=params(1),
        name="middle",
    )(
        weighted,
        stats,
        own_weighted,
        own_stats,
        w_out,
        up_cols,
        down_rows,
        cot_rows.reshape(plane),
        latents,
        tables,
        cot,
        counts,
    )


def ending_kernel(shard, *refs):
    count = (len(refs) - 6) // 3
    sources, small = refs[:count], refs[count]
    outs = refs[count + 1 : 2 * count + 1]
    small_outs = refs[2 * count + 1 : 2 * count + 5]
    held, arrive = refs[2 * count + 5 : 3 * count + 5], refs[3 * count + 5]
    loads, stores = [], []
    for n in range(count):
        loads.append(pltpu.make_async_copy(sources[n], held[n], arrive.at[n]))
        stores.append(pltpu.make_async_copy(held[n], outs[n], arrive.at[n]))
        loads[n].start()
    z, g, _, _ = here()
    width = small.shape[1]
    turned = pltpu.roll(small[...], width - (8 * z + g) * shard, 1)
    small_outs[0][...] = turned[:8, :shard]
    for n in range(3):
        small_outs[n + 1][...] = turned[8 + n : 9 + n, :shard]
    for n in range(count):
        loads[n].wait()
        stores[n].start()
    for n in range(count):
        stores[n].wait()


def ending(results, small, shard):
    count = len(results)
    return pl.pallas_call(
        partial(ending_kernel, shard),
        out_shape=[jax.ShapeDtypeStruct(r.shape, r.dtype) for r in results]
        + [jax.ShapeDtypeStruct((8, shard), F32)]
        + [jax.ShapeDtypeStruct((1, shard), F32)] * 3,
        in_specs=[LEFT] * count + [VMEM],
        out_specs=[LEFT] * count + [VMEM] * 4,
        scratch_shapes=[pltpu.VMEM(r.shape, r.dtype) for r in results] + [sems(count)],
        name="ending",
    )(*results, small)


def per_device(
    media,
    latents,
    frame_counts,
    time_index,
    valid,
    time_table,
    media_gain,
    latent_gain,
    ffn_gain,
    w_query,
    w_key,
    w_value,
    w_out,
    w_up,
    w_down,
    cotangent,
):
    frames = time_index.shape[0]
    patches = valid.shape[0] // frames
    width = latents.shape[1]
    shard = media_gain.shape[0]
    scale = (width // H) ** (-0.5)
    valid_rows = valid.reshape(frames, 1, patches)
    (
        tables,
        counts,
        full_key,
        full_value,
        full_query,
        full_out,
        up_cols,
        down_rows,
        cot_rows,
        normed,
        keys,
        values,
        table,
        line_normed,
        got_weighted,
        got_stats,
        own_weighted,
        own_stats,
    ) = opening(
        scale,
        (
            time_table,
            media_gain.reshape(1, shard),
            latent_gain.reshape(1, shard),
            ffn_gain.reshape(1, shard),
        ),
        (w_key, w_value, w_query, w_out),
        latents,
        w_up,
        w_down,
        cotangent,
        media,
        valid_rows,
        frame_counts,
        time_index,
    )
    (
        attn_low,
        middle_low,
        middle_grad,
        grad_ffn_gain,
        weighted_grad,
        terms,
        grad_table,
        terms_table,
        new_latents,
        shard_up,
        shard_down,
    ) = middle_part(
        valid.shape[0] * lax.axis_size(AXES),
        got_weighted,
        got_stats,
        own_weighted,
        own_stats,
        full_out,
        up_cols.reshape(width, -1),
        down_rows.reshape(-1, width),
        cot_rows,
        latents,
        tables,
        cotangent,
        counts,
    )
    (
        media_grad,
        latents_grad,
        smalls_grad,
        shard_out,
        shard_value,
        shard_key,
        shard_query,
    ) = closing(
        scale,
        table,
        grad_table,
        terms_table,
        keys,
        values,
        normed,
        valid_rows,
        attn_low,
        middle_low,
        weighted_grad,
        terms,
        line_normed,
        full_query,
        full_key,
        full_value,
        media,
        tables,
        latents,
        middle_grad,
        grad_ffn_gain,
        frame_counts,
        time_index,
    )
    results = ending(
        (
            new_latents,
            media_grad,
            latents_grad,
            shard_query,
            shard_key,
            shard_value,
            shard_out,
            shard_up,
            shard_down,
        ),
        smalls_grad,
        shard,
    )
    time_grad, *gains = results[9:]
    return (
        *results[:3],
        time_grad,
        *(gain.reshape(shard) for gain in gains),
        *results[3:9],
    )


def solution(mesh):
    in_specs = (
        P(("gx", "gy"), None),
        P(("gx", "gy"), None),
        P(),
        P(("gx", "gy")),
        P(("gx", "gy")),
        P(None, ("gx", "gy")),
        P(("gx", "gy")),
        P(("gx", "gy")),
        P(("gx", "gy")),
        P(("gx", "gy"), None),
        P(("gx", "gy"), None),
        P(("gx", "gy"), None),
        P(("gx", "gy"), None),
        P(("gx", "gy"), None),
        P(("gx", "gy"), None),
        P(("gx", "gy"), None),
    )
    out_specs = (
        P(("gx", "gy"), None),
        P(("gx", "gy"), None),
        P(("gx", "gy"), None),
        P(None, ("gx", "gy")),
        P(("gx", "gy")),
        P(("gx", "gy")),
        P(("gx", "gy")),
        P(("gx", "gy"), None),
        P(("gx", "gy"), None),
        P(("gx", "gy"), None),
        P(("gx", "gy"), None),
        P(("gx", "gy"), None),
        P(("gx", "gy"), None),
    )
    return jax.shard_map(
        per_device if dict(mesh.shape) == {"gx": 4, "gy": 8} else plain_device,
        mesh=mesh, in_specs=in_specs, out_specs=out_specs, check_vma=False
    )
```

```python
from functools import partial

import jax
import jax.numpy as jnp
from jax import lax
from jax.experimental import pallas as pl
from jax.experimental.pallas import tpu as pltpu
from jax.sharding import PartitionSpec as P

H = 16


ENTROPY_WEIGHT = 4.0
NORM_STABILIZER = 1e-05
AXES = ("gx", "gy")
LINES = 4
PLANE = 4
HBM = pl.ANY
BF16 = jnp.bfloat16
F32 = jnp.float32


def here():
    z = lax.axis_index("gx")
    g = lax.axis_index("gy")
    return z, g, g // 2, g % 2


def sibling(g):
    return g + 1 - 2 * (g % 2)


def along_x(g):
    return g + 2 - 4 * ((g // 2) % 2)


def along_y(g):
    return (g + 4) % 8


def turn(z, k):
    return (z + k) % LINES


def greet(devices):
    barrier = pltpu.get_barrier_semaphore()
    for device in devices:
        pl.semaphore_signal(
            barrier, inc=1, device_id=device, device_id_type=pl.DeviceIdType.MESH
        )
    pl.semaphore_wait(barrier, len(devices))


def line_of(z, g):
    return [(turn(z, k), g) for k in (1, 2, 3)]


class Wires:
    def __init__(self, send_sems, recv_sems):
        self.send_sems, self.recv_sems, self.used, self.sent = send_sems, recv_sems, 0, []

    def reserve(self, count):
        first = self.used
        self.used += count
        return first

    def copy(self, source, target, device, send, recv):
        return pltpu.make_async_remote_copy(
            src_ref=source,
            dst_ref=target,
            send_sem=self.send_sems.at[send],
            recv_sem=self.recv_sems.at[recv],
            device_id=device,
            device_id_type=pl.DeviceIdType.MESH,
        )

    def send(self, source, target, device):
        n = self.reserve(1)
        copy = self.copy(source, target, device, n, n)
        copy.start()
        self.sent.append((None, copy))
        return copy

    def send_if(self, condition, source, target, device, send, recv):
        copy = self.copy(source, target, device, send, recv)
        self.sent.append((condition, copy))

        @pl.when(condition)
        def _():
            copy.start()

        return copy

    def drain(self):
        for condition, copy in self.sent:
            if condition is None:
                copy.wait_send()
            else:
                pl.when(condition)(copy.wait_send)


class Line:
    def __init__(self, wires, shard, slot):
        self.wires, self.shard, self.slot = wires, shard, slot
        self.z, self.g, _, _ = here()
        self.base = wires.reserve(4)
        low, high = (3 - self.z) // 3, self.z // 3
        self.order = (1 + 2 * low, 3 - low - high, 2 - low + high)

    def first(self):
        z, g = self.z, self.g
        own = self.slot(z)
        base = self.base
        self.wires.send_if(z < 3, self.shard, own, (turn(z, 1), g), base + 1, base + 1)
        self.wires.send_if(z > 0, self.shard, own, (turn(z, 3), g), base + 3, base + 3)
        self.across = self.wires.copy(self.shard, own, (turn(z, 2), g), base + 2, base + 2)
        self.across.start()
        self.wires.sent.append((None, self.across))

    def take(self, step):
        z, g = self.z, self.g
        k = self.order[step]
        origin = turn(z, LINES - k)
        held = self.slot(origin)
        self.wires.copy(held, held, (z, g), 0, self.base + k).wait_recv()
        if step == 2:
            self.relay(z == 2, 3, 3)
        if step == 2:
            self.relay(z == 1, 0, 1)
        return origin

    def relay(self, condition, there, k):
        held = self.slot(turn(self.z, 2))
        self.wires.send_if(
            condition, held, held, (there, self.g), self.base, self.base + k
        )


class LineSplit:
    def __init__(self, wires, shard, slot):
        self.wires, self.shard, self.slot = wires, shard, slot
        self.z, self.g, _, _ = here()
        self.base = wires.reserve(LINES)
        low, high = (3 - self.z) // 3, self.z // 3
        self.order = (1 + 2 * low, 3 - low - high, 2 - low + high)

    def first(self):
        for k in (2, 1, 3):
            there = turn(self.z, k)
            copy = self.wires.copy(
                piece_of(self.shard, there),
                self.slot(self.z),
                (there, self.g),
                self.base + k,
                self.base + k,
            )
            copy.start()
            self.wires.sent.append((None, copy))

    def take(self, step):
        k = self.order[step]
        origin = turn(self.z, LINES - k)
        held = self.slot(origin)
        self.wires.copy(held, held, (self.z, self.g), 0, self.base + k).wait_recv()
        return origin


def piece_of(shard, place):
    width = shard.shape[-1] // LINES
    return shard.at[:, pl.ds(pl.multiple_of(place * width, 128), width)]


class Spread:
    def __init__(self, wires, shard, slot, half, whole, split=False):
        self.wires, self.shard, self.slot, self.half, self.whole = wires, shard, slot, half, whole
        self.z, self.g, _, _ = here()
        self.line = (LineSplit if split else Line)(wires, shard, lambda z: slot(z, self.g))
        if split:
            self.shard = piece_of(shard, self.z)
        self.zs, self.x, self.y, self.dx, self.dy, self.sib = [self.z], [], [], {}, {}, []

    def side(self, gy):
        return (self.z, gy)

    def to_sibling(self, held):
        if self.whole:
            self.sib.append(self.wires.send(held, held, self.side(sibling(self.g))))

    def first(self):
        own = self.slot(self.z, self.g)
        self.line.first()
        self.x.append(self.wires.send(self.shard, own, self.side(along_x(self.g))))
        self.y.append(self.wires.send(self.shard, own, self.side(along_y(self.g))))
        if self.whole:
            self.sib.append(self.wires.send(self.shard, own, self.side(sibling(self.g))))

    def column(self, step):
        self.zs.append(self.line.take(step))
        held = self.slot(self.zs[-1], self.g)
        self.x.append(self.wires.send(held, held, self.side(along_x(self.g))))
        self.y.append(self.wires.send(held, held, self.side(along_y(self.g))))
        self.to_sibling(held)

    def corner(self, n):
        self.corner_x(n)
        self.corner_y(n)

    def corner_x(self, n):
        self.x[n].wait_recv()
        held = self.slot(self.zs[n], along_x(self.g))
        part = self.half(held, 0)
        self.dy[n] = self.wires.send(part, part, self.side(along_y(self.g)))
        self.to_sibling(held)

    def corner_y(self, n):
        self.y[n].wait_recv()
        held = self.slot(self.zs[n], along_y(self.g))
        part = self.half(held, 1)
        self.dx[n] = self.wires.send(part, part, self.side(along_x(self.g)))
        self.to_sibling(held)

    def last(self, n):
        self.dy[n].wait_recv()
        self.dx[n].wait_recv()
        self.to_sibling(self.slot(self.zs[n], along_y(along_x(self.g))))

    def finish(self):
        for copy in self.sib:
            copy.wait_recv()


def spread_all(flows):
    for flow in flows:
        flow.first()
    for flow in flows:
        flow.corner(0)
    for step in range(3):
        for flow in flows:
            flow.column(step)
        for flow in flows:
            flow.corner(step + 1)
    for n in range(4):
        for flow in flows:
            flow.last(n)
    for flow in flows:
        flow.finish()


LINE_SEMS = 4


def spread_sems(whole):
    return LINE_SEMS + 8 + 8 + (16 if whole else 0)


def columns_half(ref, which):
    width = ref.shape[-1] // 2
    return ref.at[..., pl.ds(which * width, width)]


def rows_half(ref, which):
    rows = ref.shape[0] // 2
    return ref.at[pl.ds(which * rows, rows)]


def rows_parts(ref, which):
    return ref.at[pl.ds(32, 16)] if which else ref.at[pl.ds(0, 32)]


def sides_of(z, g, whole):
    near = [(z, along_x(g)), (z, along_y(g))]
    return near + [(z, sibling(g))] if whole else near


def params(ident):
    return pltpu.CompilerParams(
        collective_id=ident, has_side_effects=True, vmem_limit_bytes=60 * 2**20
    )


def sems(count):
    return pltpu.SemaphoreType.DMA((count,))


VMEM = pl.BlockSpec(memory_space=pltpu.VMEM)
LEFT = pl.BlockSpec(memory_space=HBM)


class SumLine:
    def __init__(self, wires, source, out, relayed=None):
        self.wires, self.source, self.out, self.relayed = wires, source, out, relayed
        self.z, self.g, _, _ = here()
        self.base = wires.reserve(LINES)
        low, high = (3 - self.z) // 3, self.z // 3
        self.back = (0, 1 + 2 * low, 3 - low - high, 2 - low + high)
        self.places = [turn(self.z, LINES - k) if n else self.z for n, k in enumerate(self.back)]
        self.end = low + high > 0
        self.inner = low + high < 1
        self.beside = 1 + high

    def step(self, n):
        place = self.places[n]
        if n < 3 or self.relayed is None:
            k = LINES - self.back[n]
            copy = self.wires.copy(
                self.source.at[place],
                self.out.at[self.z],
                (place, self.g),
                self.base + k,
                self.base + k,
            )
            copy.start()
            self.wires.sent.append((None, copy))
        else:
            self.wires.send_if(
                self.end,
                self.source.at[place],
                self.relayed,
                (self.beside, self.g),
                self.base,
                self.base,
            )

    def first(self):
        for n in (2, 1, 3):
            self.step(n)
        self.clear()
        self.out[self.z] = self.source[self.z]

    def clear(self):
        if self.relayed is None:
            return

        @pl.when(self.end)
        def _():
            self.out[3 - self.z] = jnp.zeros(self.out.shape[1:], self.out.dtype)

    def relay(self):
        place = self.places[3]
        held = self.source.at[place]
        across = self.wires.copy(
            held, self.out.at[self.z], (place, self.g), self.base + 2, self.base + 2
        )
        came = self.wires.copy(
            self.relayed, self.relayed, (self.z, self.g), self.base, self.base
        )
        self.wires.sent.append((self.inner, across))

        @pl.when(self.inner)
        def _():
            came.wait_recv()
            held[...] = held[...] + self.relayed[...]
            across.start()

    def finish(self):
        for k, condition in ((1, self.z > 0), (3, self.z < 3), (2, None)):
            if self.relayed is None:
                condition = None
            held = self.out.at[turn(self.z, LINES - k)]
            copy = self.wires.copy(held, held, (self.z, self.g), 0, self.base + k)
            if condition is None:
                copy.wait_recv()
            else:
                pl.when(condition)(copy.wait_recv)


class Exchange:
    def __init__(self, wires, arrays):
        self.lines = [SumLine(wires, *array) for array in arrays]

    def first(self):
        for line in self.lines:
            line.first()

    def relay(self):
        for line in self.lines:
            line.relay()

    def finish(self):
        for line in self.lines:
            line.finish()


def add_slots(target, source, count):
    @pl.loop(0, count)
    def _(n):
        target[n] = (target[n].astype(F32) + source[n].astype(F32)).astype(target.dtype)


def sum_slots(ref):
    found = ref[0].astype(F32)
    for n in range(1, LINES):
        found = found + ref[n].astype(F32)
    return found


class Fold:
    summed = True

    def __init__(self, wires, parts, whole, scratch, out):
        self.wires, self.parts, self.whole, self.out = wires, parts, whole, out
        self.from_sib, self.cx, self.cy, self.fx, self.fy, self.fz, self.relayed = scratch
        self.z, self.g, self.chip, self.core = here()
        self.cut = self.cy.shape[-1]
        self.lines = SumLine(wires, self.fx, self.fz, self.relayed) if self.summed else None

    def send(self, source, target, gy):
        return self.wires.send(source, target, (self.z, gy))

    def column(self, q):
        return self.parts.at[:, q, self.core] if self.whole else self.parts.at[:, q]

    def half(self, ref, which):
        if which:
            return ref.at[:, :, pl.ds(self.cut, ref.shape[-1] - self.cut)]
        return ref.at[:, :, pl.ds(0, self.cut)]

    def merge(self, q):
        if self.whole:
            core = self.core

            @pl.loop(0, LINES)
            def _(n):
                self.parts[n, q, core] = self.parts[n, q, core] + self.from_sib[n, q]

    def start(self):
        if self.whole:
            theirs = self.parts.at[:, :, 1 - self.core]
            self.sib = self.send(theirs, self.from_sib, sibling(self.g))

    def corner(self):
        if self.whole:
            self.sib.wait_recv()
        q = along_y(along_x(self.g)) // 2
        self.merge(q)
        far = self.column(q)
        self.to_y = self.send(self.half(far, 0), self.cy, along_y(self.g))
        self.to_x = self.send(self.half(far, 1), self.cx, along_x(self.g))

    def side(self, gy, came, corner, which, target):
        q = gy // 2
        self.merge(q)
        came.wait_recv()
        column = self.column(q)
        cols = slice(self.cut, None) if which else slice(0, self.cut)

        @pl.loop(0, LINES)
        def _(n):
            column[n, :, cols] = column[n, :, cols] + corner[n]

        return self.send(column, target, gy)

    def side_x(self):
        self.by_x = self.side(along_x(self.g), self.to_y, self.cy, 0, self.fx)

    def side_y(self):
        self.by_y = self.side(along_y(self.g), self.to_x, self.cx, 1, self.fy)

    def line(self):
        self.merge(self.chip)
        self.by_x.wait_recv()
        self.by_y.wait_recv()
        column = self.column(self.chip)
        for n in (3, 2, 1):
            there = self.lines.places[n]
            self.fx[there] = (
                column[there].astype(F32)
                + self.fx[there].astype(F32)
                + self.fy[there].astype(F32)
            ).astype(BF16)
            self.lines.step(n)
        z = self.z
        self.lines.clear()
        self.fz[z] = jnp.zeros(self.fz.shape[1:], BF16)
        self.out[...] = column[z].astype(F32) + self.fx[z].astype(F32) + self.fy[z].astype(F32)

    def relay(self):
        self.lines.relay()

    def finish(self):
        self.lines.finish()
        self.out[...] += sum_slots(self.fz)


class FoldSplit(Fold):
    summed = False

    def line(self):
        self.merge(self.chip)
        self.by_x.wait_recv()
        self.by_y.wait_recv()
        column = self.column(self.chip)
        self.zs = []
        for k in (2, 1, 3, 0):
            there = turn(self.z, k) if k else self.z
            found = (
                column[there].astype(F32)
                + self.fx[there].astype(F32)
                + self.fy[there].astype(F32)
            ).astype(BF16)
            if k:
                self.fx[there] = found
                self.zs.append(
                    self.wires.send(self.fx.at[there], self.fz.at[self.z], (there, self.g))
                )
            else:
                self.fz[self.z] = found

    def finish(self):
        for copy in self.zs:
            copy.wait_recv()
        width = self.fz.shape[-1]
        for place in range(LINES):
            self.out[:, place * width : (place + 1) * width] = self.fz[place].astype(F32)


def fold_scratch(rows, cols, whole, split=False):
    cut = 256 if split else cols // 2
    return [
        pltpu.VMEM((LINES, PLANE, rows, cols) if whole else (1, 1, 16, 128), BF16),
        pltpu.VMEM((LINES, rows, cols - cut), BF16),
        pltpu.VMEM((LINES, rows, cut), BF16),
        pltpu.VMEM((LINES, rows, cols), BF16),
        pltpu.VMEM((LINES, rows, cols), BF16),
        pltpu.VMEM((LINES, rows, cols), BF16),
        pltpu.VMEM((rows, cols), BF16),
    ]


FOLD = 7


def fold_sems(whole):
    return (1 if whole else 0) + 4 + LINES


class FoldSteps:
    def __init__(self, wires, parts, scratch, out):
        self.wires, self.parts, self.out = wires, parts, out
        _, self.cx, self.cy, self.fx, self.fy, self.fz, relayed = scratch
        self.z, self.g, self.chip, _ = here()
        self.width = parts.shape[-1] // 2
        self.lines = SumLine(wires, self.fx, self.fz, relayed)
        self.zs = self.lines.places
        self.to_x, self.to_y, self.by_x, self.by_y = {}, {}, {}, {}

    def half(self, n, q, which):
        return self.parts.at[self.zs[n], q, :, pl.ds(which * self.width, self.width)]

    def corner(self, n):
        far = along_y(along_x(self.g)) // 2
        place = self.zs[n]
        self.to_y[n] = self.wires.send(
            self.half(n, far, 0), self.cy.at[place], (self.z, along_y(self.g))
        )
        self.to_x[n] = self.wires.send(
            self.half(n, far, 1), self.cx.at[place], (self.z, along_x(self.g))
        )

    def side(self, n, gy, came, corner, which, target):
        came.wait_recv()
        q, place = gy // 2, self.zs[n]
        cols = slice(which * self.width, (which + 1) * self.width)
        self.parts[place, q, :, cols] = self.parts[place, q, :, cols] + corner[place]
        return self.wires.send(self.parts.at[place, q], target.at[place], (self.z, gy))

    def side_x(self, n):
        self.by_x[n] = self.side(n, along_x(self.g), self.to_y[n], self.cy, 0, self.fx)

    def side_y(self, n):
        self.by_y[n] = self.side(n, along_y(self.g), self.to_x[n], self.cx, 1, self.fy)

    def line(self, n):
        self.by_x[n].wait_recv()
        self.by_y[n].wait_recv()
        place = self.zs[n]
        found = (
            self.parts[place, self.chip].astype(F32)
            + self.fx[place].astype(F32)
            + self.fy[place].astype(F32)
        )
        if n == 0:
            self.out[...] = found
            self.lines.clear()
            self.fz[self.z] = jnp.zeros(self.fz.shape[1:], BF16)
        else:
            self.fx[place] = found.astype(BF16)
            self.lines.step(n)

    def relay(self):
        self.lines.relay()

    def finish(self):
        self.lines.finish()
        self.out[...] += sum_slots(self.fz)


STEP_SEMS = 16 + LINES


def layer_norm(row_block, gain_row):
    row_mean = jnp.mean(row_block, axis=-1, keepdims=True)
    centred = row_block - row_mean
    variance = jnp.mean(centred * centred, axis=-1, keepdims=True)
    return centred * lax.rsqrt(variance + NORM_STABILIZER) * gain_row


def product(left_side, right_side):
    return jnp.dot(left_side, right_side, preferred_element_type=jnp.float32)


def inner_first(left_side, right_side):
    return lax.dot_general(
        left_side, right_side, (((0,), (0,)), ((), ())), preferred_element_type=jnp.float32
    )


def inner_last(left_side, right_side):
    return lax.dot_general(
        left_side, right_side, (((1,), (1,)), ((), ())), preferred_element_type=jnp.float32
    )


def collect(onehot_rows, value_rows):
    return lax.dot_general(
        onehot_rows,
        value_rows,
        (((0,), (0,)), ((), ())),
        precision=lax.Precision.HIGHEST,
        preferred_element_type=jnp.float32,
    )


def plain_device(
    media,
    latents,
    frame_counts,
    time_index,
    valid,
    time_table,
    media_gain,
    latent_gain,
    ffn_gain,
    w_query,
    w_key,
    w_value,
    w_out,
    w_up,
    w_down,
    cotangent,
):
    frames = time_index.shape[0]
    patches = valid.shape[0] // frames
    latent_rows = latents.shape[0]
    model_width = latents.shape[1]
    head_size = model_width // H
    score_scale = head_size ** (-0.5)
    across = lax.axis_size("gx")
    column = lax.axis_index("gx")
    row_index = lax.axis_index("gy")
    frame_ends = jnp.cumsum(frame_counts[row_index])
    position = column * frames + jnp.arange(frames, dtype=jnp.int32)
    item_index = jnp.sum((frame_ends[None, :] <= position[:, None]).astype(jnp.int32), axis=1)
    item_onehot = (item_index[:, None] == jnp.arange(across, dtype=jnp.int32)[None, :]).astype(
        jnp.float32
    )
    (
        full_query,
        full_key,
        full_value,
        full_out,
        full_up,
        full_down,
        full_media_gain,
        full_latent_gain,
        full_ffn_gain,
        full_time,
    ) = (
        lax.all_gather(w_query, ("gx", "gy"), axis=0, tiled=True),
        lax.all_gather(w_key, ("gx", "gy"), axis=0, tiled=True),
        lax.all_gather(w_value, ("gx", "gy"), axis=0, tiled=True),
        lax.all_gather(w_out, ("gx", "gy"), axis=0, tiled=True),
        lax.all_gather(w_up, ("gx", "gy"), axis=0, tiled=True),
        lax.all_gather(w_down, ("gx", "gy"), axis=0, tiled=True),
        lax.all_gather(media_gain, ("gx", "gy"), axis=0, tiled=True),
        lax.all_gather(latent_gain, ("gx", "gy"), axis=0, tiled=True),
        lax.all_gather(ffn_gain, ("gx", "gy"), axis=0, tiled=True),
        lax.all_gather(time_table, ("gx", "gy"), axis=1, tiled=True),
    )
    time_onehot = (
        time_index[:, None] == jnp.arange(full_time.shape[0], dtype=jnp.int32)[None, :]
    ).astype(jnp.float32)
    time_rows = product(time_onehot.astype(jnp.bfloat16), full_time)
    media_in = (
        media.astype(jnp.float32).reshape(frames, patches, model_width) + time_rows[:, None, :]
    ).reshape(-1, model_width)
    media_normed = layer_norm(media_in, full_media_gain.astype(jnp.float32)).astype(jnp.bfloat16)
    key_heads = (
        product(media_normed, full_key).astype(jnp.bfloat16).reshape(frames, patches, H, head_size)
    )
    value_heads = (
        product(media_normed, full_value)
        .astype(jnp.bfloat16)
        .reshape(frames, patches, H, head_size)
    )
    latent_in = latents.astype(jnp.float32)
    latent_normed = layer_norm(latent_in, full_latent_gain.astype(jnp.float32)).astype(jnp.bfloat16)
    own_query = product(latent_normed, full_query).astype(jnp.bfloat16)
    own_key = product(latent_normed, full_key).astype(jnp.bfloat16)
    own_value = product(latent_normed, full_value).astype(jnp.bfloat16)
    valid_total = lax.psum(jnp.sum(valid.astype(jnp.float32)), ("gx", "gy"))
    coefficient = ENTROPY_WEIGHT * (valid.shape[0] * lax.axis_size(("gx", "gy"))) / valid_total
    query_table = lax.all_gather(own_query, "gx", axis=0, tiled=True)
    picked = query_table.reshape(-1, latent_rows, H, head_size)[item_index]
    media_score = (
        jnp.einsum("flhd,fphd->flhp", picked, key_heads, preferred_element_type=jnp.float32)
        * score_scale
    )
    valid_mask = valid.reshape(frames, 1, 1, patches) > 0
    media_expo = jnp.where(valid_mask, jnp.exp(media_score), 0.0)
    expo_low = media_expo.astype(jnp.bfloat16)
    media_total = jnp.sum(media_expo, axis=-1)
    media_moment = jnp.sum(media_expo * media_score, axis=-1)
    media_weighted = jnp.einsum(
        "flhp,fphd->flhd", expo_low, value_heads, preferred_element_type=jnp.float32
    )
    dense_weighted = collect(item_onehot, media_weighted.reshape(frames, -1)).reshape(
        -1, model_width
    )
    dense_total = collect(item_onehot, media_total.reshape(frames, -1)).reshape(-1, H)
    dense_moment = collect(item_onehot, media_moment.reshape(frames, -1)).reshape(-1, H)
    got_weighted, got_total, got_moment = (
        lax.psum_scatter(dense_weighted, "gx", scatter_dimension=0, tiled=True),
        lax.psum_scatter(dense_total, "gx", scatter_dimension=0, tiled=True),
        lax.psum_scatter(dense_moment, "gx", scatter_dimension=0, tiled=True),
    )
    query_head_count = own_query.reshape(latent_rows, H, head_size)
    latent_key_rows = own_key.reshape(latent_rows, H, head_size)
    latent_value_rows = own_value.reshape(latent_rows, H, head_size)
    latent_score = (
        jnp.einsum(
            "uer,zer->uez", query_head_count, latent_key_rows, preferred_element_type=jnp.float32
        )
        * score_scale
    )
    latent_expo = jnp.exp(latent_score)
    latent_reduced_precision = latent_expo.astype(jnp.bfloat16)
    weighted = got_weighted.reshape(latent_rows, H, head_size) + jnp.einsum(
        "nwr,rwb->nwb",
        latent_reduced_precision,
        latent_value_rows,
        preferred_element_type=jnp.float32,
    )
    totals = got_total + jnp.sum(latent_expo, axis=-1)
    moment = got_moment + jnp.sum(latent_expo * latent_score, axis=-1)
    attention = weighted / totals[..., None]
    attn_low = attention.reshape(latent_rows, model_width).astype(jnp.bfloat16)
    middle = latent_in + product(attn_low, full_out)
    ffn_normed = layer_norm(middle, full_ffn_gain.astype(jnp.float32)).astype(jnp.bfloat16)
    up_rows = product(ffn_normed, full_up)
    hidden = jax.nn.gelu(up_rows, approximate=False).astype(jnp.bfloat16)
    new_latents = (middle + product(hidden, full_down)).astype(jnp.bfloat16)
    (
        back_query,
        back_key,
        back_value,
        back_out,
        back_up,
        back_down,
        back_media_gain,
        back_latent_gain,
        back_ffn_gain,
    ) = (
        lax.all_gather(w_query, ("gx", "gy"), axis=0, tiled=True),
        lax.all_gather(w_key, ("gx", "gy"), axis=0, tiled=True),
        lax.all_gather(w_value, ("gx", "gy"), axis=0, tiled=True),
        lax.all_gather(w_out, ("gx", "gy"), axis=0, tiled=True),
        lax.all_gather(w_up, ("gx", "gy"), axis=0, tiled=True),
        lax.all_gather(w_down, ("gx", "gy"), axis=0, tiled=True),
        lax.all_gather(media_gain, ("gx", "gy"), axis=0, tiled=True),
        lax.all_gather(latent_gain, ("gx", "gy"), axis=0, tiled=True),
        lax.all_gather(ffn_gain, ("gx", "gy"), axis=0, tiled=True),
    )
    owned_latent, owned_attn, owned_ffn, owned_hidden = (
        lax.all_to_all(latent_normed, ("gx", "gy"), split_axis=1, concat_axis=0, tiled=True),
        lax.all_to_all(attn_low, ("gx", "gy"), split_axis=1, concat_axis=0, tiled=True),
        lax.all_to_all(ffn_normed, ("gx", "gy"), split_axis=1, concat_axis=0, tiled=True),
        lax.all_to_all(hidden, ("gx", "gy"), split_axis=1, concat_axis=0, tiled=True),
    )
    hidden_grad = inner_last(cotangent, back_down)
    gelu_pull = jax.vjp(partial(jax.nn.gelu, approximate=False), up_rows)[1]
    up_grad = gelu_pull(hidden_grad)[0].astype(jnp.bfloat16)
    ffn_normed_grad = inner_last(up_grad, back_up)
    ffn_pull = jax.vjp(layer_norm, middle, back_ffn_gain.astype(jnp.float32))[1]
    middle_part, grad_ffn_gain = ffn_pull(ffn_normed_grad)
    middle_grad = cotangent.astype(jnp.float32) + middle_part
    middle_low = middle_grad.astype(jnp.bfloat16)
    attn_grad = inner_last(middle_low, back_out).reshape(latent_rows, H, head_size)
    weighted_sum_gradient = (attn_grad / totals[..., None]).astype(jnp.bfloat16)
    slope_term = -coefficient / totals
    shift_term = (
        -jnp.sum(attn_grad * attention, axis=-1) / totals
        + coefficient * (1.0 / totals + moment / (totals * totals))
        + slope_term
    )
    latent_mix = jnp.einsum(
        "uer,zer->uez", weighted_sum_gradient, latent_value_rows, preferred_element_type=jnp.float32
    )
    latent_sgrad = latent_expo * (
        latent_mix + shift_term[..., None] + slope_term[..., None] * latent_score
    )
    latent_residual_gradient = (latent_sgrad * score_scale).astype(jnp.bfloat16)
    query_part = jnp.einsum(
        "nwr,rwb->nwb",
        latent_residual_gradient,
        latent_key_rows,
        preferred_element_type=jnp.float32,
    )
    own_key_grad = (
        jnp.einsum(
            "zry,zrj->yrj",
            latent_residual_gradient,
            query_head_count,
            preferred_element_type=jnp.float32,
        )
        .astype(jnp.bfloat16)
        .reshape(latent_rows, model_width)
    )
    own_value_grad = (
        jnp.einsum(
            "zry,zrj->yrj",
            latent_reduced_precision,
            weighted_sum_gradient,
            preferred_element_type=jnp.float32,
        )
        .astype(jnp.bfloat16)
        .reshape(latent_rows, model_width)
    )
    grad_table = lax.all_gather(
        weighted_sum_gradient.reshape(latent_rows, model_width), "gx", axis=0, tiled=True
    )
    shift_table, slope_table = (
        lax.all_gather(shift_term, "gx", axis=0, tiled=True),
        lax.all_gather(slope_term, "gx", axis=0, tiled=True),
    )
    picked_grad = grad_table.reshape(-1, latent_rows, H, head_size)[item_index]
    picked_shift = shift_table.reshape(-1, latent_rows, H)[item_index]
    picked_slope = slope_table.reshape(-1, latent_rows, H)[item_index]
    media_mix = jnp.einsum(
        "flhd,fphd->flhp", picked_grad, value_heads, preferred_element_type=jnp.float32
    )
    media_sgrad = media_expo * (
        media_mix + picked_shift[..., None] + picked_slope[..., None] * media_score
    )
    media_rgrad = (media_sgrad * score_scale).astype(jnp.bfloat16)
    query_terms = jnp.einsum(
        "flhp,fphd->flhd", media_rgrad, key_heads, preferred_element_type=jnp.float32
    )
    dense_query = collect(item_onehot, query_terms.reshape(frames, -1)).reshape(-1, model_width)
    got_query = lax.psum_scatter(
        dense_query.astype(jnp.bfloat16), "gx", scatter_dimension=0, tiled=True
    ).astype(jnp.float32)
    media_key_grad = (
        jnp.einsum("flhp,flhd->fphd", media_rgrad, picked, preferred_element_type=jnp.float32)
        .astype(jnp.bfloat16)
        .reshape(-1, model_width)
    )
    media_value_grad = (
        jnp.einsum("flhp,flhd->fphd", expo_low, picked_grad, preferred_element_type=jnp.float32)
        .astype(jnp.bfloat16)
        .reshape(-1, model_width)
    )
    grad_key = inner_first(media_normed, media_key_grad) + inner_first(latent_normed, own_key_grad)
    grad_value = inner_first(media_normed, media_value_grad) + inner_first(
        latent_normed, own_value_grad
    )
    media_normed_grad = inner_last(media_key_grad, back_key) + inner_last(
        media_value_grad, back_value
    )
    media_pull = jax.vjp(layer_norm, media_in, back_media_gain.astype(jnp.float32))[1]
    media_grad, grad_media_gain = media_pull(media_normed_grad)
    frame_sums = jnp.sum(media_grad.reshape(frames, patches, model_width), axis=1)
    grad_time = collect(time_onehot, frame_sums)
    query_grad = (
        (got_query.reshape(latent_rows, H, head_size) + query_part)
        .astype(jnp.bfloat16)
        .reshape(latent_rows, model_width)
    )
    latent_normed_grad = (
        inner_last(query_grad, back_query)
        + inner_last(own_key_grad, back_key)
        + inner_last(own_value_grad, back_value)
    )
    latent_pull = jax.vjp(layer_norm, latent_in, back_latent_gain.astype(jnp.float32))[1]
    latent_part, grad_latent_gain = latent_pull(latent_normed_grad)
    latents_grad = middle_grad + latent_part
    piece_query = lax.all_gather(query_grad, ("gx", "gy"), axis=0, tiled=True)
    piece_middle = lax.all_gather(middle_low, ("gx", "gy"), axis=0, tiled=True)
    piece_up = lax.all_gather(up_grad, ("gx", "gy"), axis=0, tiled=True)
    piece_cot = lax.all_gather(cotangent, ("gx", "gy"), axis=0, tiled=True)
    shard_query = inner_first(owned_latent, piece_query)
    shard_out = inner_first(owned_attn, piece_middle)
    shard_up = inner_first(owned_ffn, piece_up)
    shard_down = inner_first(owned_hidden, piece_cot)
    shard_grads = (
        lax.psum_scatter(grad_key, ("gx", "gy"), scatter_dimension=0, tiled=True),
        lax.psum_scatter(grad_value, ("gx", "gy"), scatter_dimension=0, tiled=True),
        lax.psum_scatter(grad_media_gain, ("gx", "gy"), scatter_dimension=0, tiled=True),
        lax.psum_scatter(grad_latent_gain, ("gx", "gy"), scatter_dimension=0, tiled=True),
        lax.psum_scatter(grad_ffn_gain, ("gx", "gy"), scatter_dimension=0, tiled=True),
        lax.psum_scatter(grad_time, ("gx", "gy"), scatter_dimension=1, tiled=True),
    )
    return (
        new_latents,
        media_grad,
        latents_grad,
        shard_grads[5],
        shard_grads[2],
        shard_grads[3],
        shard_grads[4],
        shard_query,
        shard_grads[0],
        shard_grads[1],
        shard_out,
        shard_up,
        shard_down,
    )


GROUP = 4


def mates_of(z, chip, core):
    mates = []
    for j in range(1, 16):
        there = (4 * z + chip + j) % 16
        mates.append((there // 4, 2 * (there % 4) + core))
    return mates


class GiveBack:
    def __init__(self, wires, up_part, down_part, scratch, up_out, down_out):
        self.wires, self.up_part, self.down_part = wires, up_part, down_part
        self.up_out, self.down_out = up_out, down_out
        self.up_near, self.down_near, self.up_got = scratch
        self.z, self.g, self.chip, self.core = here()
        self.places = up_places(self.z, self.chip)

    def first(self):
        near = (self.z, sibling(self.g))
        theirs = 1 - self.core
        self.up = self.wires.send(self.up_part.at[:, :, theirs], self.up_near, near)
        self.down = self.wires.send(self.down_part.at[theirs], self.down_near, near)

    def columns(self):
        self.up.wait_recv()
        core = self.core

        @pl.loop(0, LINES)
        def _(n):
            for q in range(PLANE):
                self.up_part[n, q, core] = self.up_part[n, q, core] + self.up_near[n, q]

        self.moved = []
        for there, _ in self.places:
            self.moved.append(
                self.wires.send(
                    self.up_part.at[there[0], there[1], core],
                    self.up_got.at[self.z, self.chip],
                    (there[0], 2 * there[1] + core),
                )
            )
        self.up_got[self.z, self.chip] = self.up_part[self.z, self.chip, core]

    def rows(self):
        self.down.wait_recv()
        rows = self.down_out.shape[0] // 8
        core = self.core

        @pl.loop(0, 8)
        def _(n):
            block = pl.ds(pl.multiple_of(n * rows, 8), rows)
            self.down_out[block] = self.down_part[core, block] + self.down_near[block]

    def finish(self):
        for copy in self.moved:
            copy.wait_recv()
        width = self.up_got.shape[-1]
        for n in range(LINES):
            for q in range(PLANE):
                first = (n * PLANE + q) * width
                self.up_out[:, first : first + width] = self.up_got[n, q].astype(F32)


GIVE_SEMS = 17


class Total:
    def __init__(self, wires, mine, out, sums, got):
        self.wires, self.out, self.sums, self.got = wires, out, sums, got
        self.z, self.g, _, _ = here()
        self.source = mine
        self.step = 0

    def push(self):
        sides = [sibling(self.g), along_x(self.g), along_y(self.g)]
        if self.step < 3:
            self.copies = [
                self.wires.send(self.source, self.got.at[self.step], (self.z, sides[self.step]))
            ]
        else:
            self.copies = [
                self.wires.send(self.source, self.got.at[3 + k], device)
                for k, device in enumerate(line_of(self.z, self.g))
            ]

    def pull(self):
        for copy in self.copies:
            copy.wait_recv()
        if self.step < 3:
            self.sums[self.step] = self.source[...] + self.got[self.step]
            self.source = self.sums.at[self.step]
            self.step += 1
        else:
            self.out[...] = self.source[...] + self.got[3] + self.got[4] + self.got[5]


def head_masks(rows, width, head_size):
    lane = lax.broadcasted_iota(jnp.int32, (rows, width), 1)
    return [(lane >= h * head_size) & (lane < (h + 1) * head_size) for h in range(GROUP)]


def stacked(block, masks):
    zero = jnp.zeros_like(block)
    return jnp.concatenate([jnp.where(mask, block, zero) for mask in masks], axis=0)


def unstacked(block, masks):
    rows = block.shape[0] // GROUP
    total = jnp.where(masks[0], block[:rows], 0.0)
    for h in range(1, GROUP):
        total = jnp.where(masks[h], block[h * rows : (h + 1) * rows], total)
    return total


def dot_last(a, b):
    return lax.dot_general(a, b, (((1,), (1,)), ((), ())), preferred_element_type=F32)


def dot_first(a, b):
    return lax.dot_general(a, b, (((0,), (0,)), ((), ())), preferred_element_type=F32)


def spread_heads(columns, first, masks):
    out = jnp.where(masks[0], columns[:, first : first + 1], 0.0)
    for h in range(1, GROUP):
        out = jnp.where(masks[h], columns[:, first + h : first + h + 1], out)
    return out


def attend(queries, keys, values, valid, scale, masks):
    rows = queries.shape[0]
    score = dot_last(stacked(queries, masks), keys) * scale
    expo = jnp.exp(score)
    if valid is not None:
        expo = jnp.where(valid > 0, expo, 0.0)
    totals = jnp.sum(expo, axis=1, keepdims=True)
    moments = jnp.sum(expo * score, axis=1, keepdims=True)
    weighted = jnp.dot(expo.astype(BF16), values, preferred_element_type=F32)
    heads = [(totals[h * rows : (h + 1) * rows], moments[h * rows : (h + 1) * rows]) for h in range(GROUP)]
    return unstacked(weighted, masks), heads


def pack_rows(terms):
    part = terms.shape[0] // 4
    out = terms[:part]
    for k in range(1, 4):
        out = out + pltpu.roll(terms[k * part : (k + 1) * part], 32 * k, 1)
    return out


def unpack_rows(packed):
    turned = [pltpu.roll(packed, 128 - 32 * k, 1) for k in range(1, 4)]
    return jnp.concatenate([packed] + turned, axis=0)


def put_heads(heads, group, lane):
    out = jnp.zeros(lane.shape, F32)
    for h, (total, moment) in enumerate(heads):
        out = jnp.where(lane == group * GROUP + h, total, out)
        out = jnp.where(lane == H + group * GROUP + h, moment, out)
    return out


def assemble(smalls, out):
    count, rows, lanes = smalls.shape
    shard = out.shape[1] // count
    block = 8
    row = lax.broadcasted_iota(jnp.int32, (block * lanes, block * shard), 0)
    col = lax.broadcasted_iota(jnp.int32, (block * lanes, block * shard), 1)
    lane = row % lanes
    chosen = ((row // lanes) * shard + lane == col) & (lane < shard)
    place = jnp.where(chosen, 1.0, 0.0).astype(BF16)
    for n in range(count // block):
        pieces = jnp.concatenate([smalls[n * block + d] for d in range(block)], axis=1)
        out[:, n * block * shard : (n + 1) * block * shard] = jnp.dot(
            pieces.astype(BF16), place, preferred_element_type=F32
        )


def up_places(z, chip):
    places = []
    for dz in range(LINES):
        for dx, dy in ((0, 0), (1, 0), (0, 1), (1, 1)):
            if dz or dx or dy:
                x, y = chip % 2, chip // 2
                there = (y + dy) % 2 * 2 + (x + dx) % 2
                places.append(((turn(z, dz), there), (turn(z, LINES - dz) if dz else z, there)))
    return places


def shares(counts_ref, z, g, frame, frames, items):
    position = z * frames + frame
    end, slot = 0, 0
    for item in range(items):
        end = end + counts_ref[g, item]
        slot = slot + jnp.where(end <= position, 1, 0)
    return [jnp.where(slot == item, 1.0, 0.0) for item in range(items)]


def put_times(out, tables, times_ref, frames):
    for frame in range(frames):
        row = jnp.zeros((1, out.shape[1]), F32)
        for t in range(8):
            row = row + jnp.where(times_ref[frame] == t, 1.0, 0.0) * tables[t : t + 1]
        out[frame : frame + 1] = row


def opening_kernel(scale, *refs):
    (
        time_table_ref,
        media_gain_ref,
        latent_gain_ref,
        ffn_gain_ref,
        key_shard,
        value_shard,
        query_shard,
        out_shard,
        latents_ref,
        up_ref,
        down_ref,
        cot_ref,
        media_ref,
        valid_ref,
        counts_ref,
        times_ref,
        tables_out,
        counts_out,
        key_weight_out,
        value_weight_out,
        query_weight_out,
        out_weight_out,
        up_out,
        down_out,
        cot_out,
        normed_out,
        keys_out,
        values_out,
        table_out,
        line_normed_out,
        got_weighted,
        got_stats,
        own_weighted,
        own_stats,
        send_sems,
        recv_sems,
        local_sems,
        up_own,
        small_ref,
        smalls,
        key_weight,
        value_weight,
        query_weight,
        line_latents,
        line_normed,
        normed,
        keys,
        values,
        own_table,
        table,
        time_rows,
        sums,
        weighted,
        stats,
        packed,
    ) = refs
    z, g, chip, core = here()
    here_chip = 4 * z + chip
    me = 2 * here_chip + core
    items, rows, width = line_latents.shape
    frames, _, patches = valid_ref.shape
    shard = key_shard.shape[0]
    span = width // (H // GROUP)
    up_width = up_out.shape[-1]
    near = (z, sibling(g))
    places = up_places(z, chip)
    greet([(there[0], 2 * there[1] + core) for there, _ in places] + [near])
    wires = Wires(send_sems, recv_sems)
    masks = head_masks(rows, span, span // GROUP)
    lane = lax.broadcasted_iota(jnp.int32, (rows, 128), 1)
    local = []
    small_ref[...] = jnp.zeros_like(small_ref)
    for place, source in (
        (slice(0, 8), time_table_ref),
        (slice(8, 9), media_gain_ref),
        (slice(9, 10), latent_gain_ref),
        (slice(10, 11), ffn_gain_ref),
    ):
        small_ref[place, :shard] = source[...].astype(F32)
    found = valid_ref[0].astype(F32)
    for n in range(1, frames):
        found = found + valid_ref[n].astype(F32)
    small_ref[11:12] = jnp.sum(found, axis=1, keepdims=True) + jnp.zeros((1, 128), F32)

    def keep(source, target):
        copy = pltpu.make_async_copy(source, target, local_sems.at[len(local)])
        copy.start()
        local.append(copy)
        return copy

    def rows_of(ref):
        return lambda zz, gg: ref.at[pl.ds(pl.multiple_of((zz * 8 + gg) * shard, 16), shard)]

    def piece(place):
        return up_ref.at[:, pl.ds(pl.multiple_of((4 * place[0] + place[1]) * up_width, 128), up_width)]

    def whole(source, slot):
        return Spread(wires, source, slot, columns_half, True), keep(source, slot(z, g))

    def small_slot(zz, gg):
        return smalls.at[zz * 8 + gg]

    small = Spread(wires, small_ref, small_slot, rows_half, True)
    small_kept = keep(small_ref, small_slot(z, g))
    key, key_kept = whole(key_shard, rows_of(key_weight))
    value, value_kept = whole(value_shard, rows_of(value_weight))
    query = Spread(wires, query_shard, rows_of(query_weight), rows_parts, True, True)
    query_kept = keep(piece_of(query_shard, z), rows_of(query_weight)(z, g))
    query_line = Line(wires, own_table, lambda zz: table.at[zz])
    out, out_kept = whole(out_shard, rows_of(out_weight_out))
    cot = Spread(wires, cot_ref, lambda zz, gg: cot_out.at[zz * 4 + gg // 2], columns_half, False)
    line = Line(wires, latents_ref, lambda zz: line_latents.at[zz])
    exchange = Exchange(
        wires,
        [(weighted, got_weighted), (packed, got_stats)],
    )
    line_kept = keep(latents_ref, line_latents.at[z])
    up_load = keep(piece((z, chip)), up_own)
    late = [
        out_kept,
        keep(cot_ref, cot_out.at[here_chip]),
        keep(down_ref, down_out.at[core]),
    ]
    prompt = len(local)
    moved, given, down = [], [], []
    chunk = 32

    def normalise(first, last):
        @pl.loop(first, last)
        def _(n):
            block = pl.ds(pl.multiple_of(n * chunk, chunk), chunk)
            frame = n // (patches // chunk)
            row = media_ref[block].astype(F32) + time_rows[pl.ds(frame, 1)]
            normed[block] = layer_norm(row, tables_out[8:9]).astype(BF16)

    def normalise_latents():
        gain = tables_out[9:10]
        line_kept.wait()
        for item in range(items):

            @pl.loop(0, rows // chunk)
            def _(n):
                block = pl.ds(pl.multiple_of(n * chunk, chunk), chunk)
                row = line_latents[item, block].astype(F32)
                line_normed[item, block] = layer_norm(row, gain).astype(BF16)

        normed[frames * patches :] = line_normed[z]

    def tabulate():
        small_kept.wait()
        assemble(smalls, tables_out)
        counts = smalls[0, 8:]
        for n in range(1, smalls.shape[0]):
            counts = counts + smalls[n, 8:]
        counts_out[...] = counts
        put_times(time_rows, tables_out, times_ref, frames)

    def project(left, weight, out, first):
        @pl.loop(first, first + 2)
        def _(n):
            cols = pl.ds(pl.multiple_of(n * span, 128), span)
            out[:, cols] = jnp.dot(
                left[...], weight[:, cols], preferred_element_type=F32
            ).astype(BF16)

    def project_keys(first):
        if first == 0:
            key_kept.wait()
            keep(key_weight, key_weight_out)
            keep(normed, normed_out)
        project(normed, key_weight, keys, first)
        if first > 0:
            keep(keys, keys_out)

    def project_values(first):
        if first == 0:
            value_kept.wait()
            keep(value_weight, value_weight_out)
        project(normed, value_weight, values, first)
        if first > 0:
            keep(values, values_out)

    def project_queries():
        query_kept.wait()
        keep(query_weight, query_weight_out)
        for item in range(items):
            own_table[item] = jnp.dot(
                line_normed[item], query_weight[...], preferred_element_type=F32
            ).astype(BF16)
        table[z] = own_table[...]
        query_line.first()

    def attend_own():
        keep(table, table_out)
        keep(line_normed, line_normed_out)
        sums[...] = jnp.zeros_like(sums)
        stats[...] = jnp.zeros_like(stats)
        last = slice(frames * patches, frames * patches + rows)
        own = jnp.zeros((rows, 128), F32)
        for group in range(H // GROUP):
            cols = slice(group * span, (group + 1) * span)
            part, heads = attend(
                table[group, z], keys[last, cols], values[last, cols], None, scale, masks
            )
            own_weighted[:, cols] = part
            own = own + put_heads(heads, group, lane)
        own_stats[...] = own

    def attend_frames(first, last):
        @pl.loop(first, last)
        def _(frame):
            share = shares(counts_ref, z, g, frame, frames, items)
            block = pl.ds(pl.multiple_of(frame * patches, patches), patches)
            valid = valid_ref[frame]
            found = jnp.zeros((rows, 128), F32)
            for group in range(H // GROUP):
                cols = slice(group * span, (group + 1) * span)
                chosen = share[0] * table[group, 0].astype(F32)
                for item in range(1, items):
                    chosen = chosen + share[item] * table[group, item].astype(F32)
                part, heads = attend(
                    chosen.astype(BF16), keys[block, cols], values[block, cols], valid, scale, masks
                )
                found = found + put_heads(heads, group, lane)
                for item in range(items):
                    sums[item, :, cols] += share[item] * part
            for item in range(items):
                stats[item] += share[item] * found

    def down_first():
        down.append(wires.send(down_ref, down_out.at[core], near))

    def up_first():
        up_load.wait()
        keep(up_own, up_out.at[me])
        given.append(wires.send(up_own, up_out.at[me], near))
        for there, _ in places:
            moved.append(
                wires.send(piece(there), up_out.at[me], (there[0], 2 * there[1] + core))
            )

    def up_last():
        for n, (_, origin) in enumerate(places):
            moved[n].wait_recv()
            held = up_out.at[2 * (4 * origin[0] + origin[1]) + core]
            given.append(wires.send(held, held, near))
        for copy in given:
            copy.wait_recv()

    def sums_first():
        weighted[...] = sums[...].astype(BF16)
        for item in range(items):
            packed[item] = pack_rows(stats[item])
        exchange.first()

    small.first()
    query.first()
    value.first()
    key.first()
    query.column(0)
    small.column(0)
    small.column(1)
    small.column(2)
    query.column(1)
    down_first()
    value.column(0)
    small.corner_x(0)
    small.corner_y(2)
    small.corner_y(3)
    query.corner_y(2)
    value.column(1)
    small.corner_x(1)
    key.column(0)
    small.corner_y(0)
    small.corner_y(1)
    value.corner_x(1)
    small.corner_x(3)
    small.corner_x(2)
    value.corner_y(2)
    value.corner_y(1)
    key.column(1)
    line.first()
    query.corner_x(0)
    query.corner_x(2)
    value.corner_y(0)
    query.corner_y(0)
    small.last(1)
    query.column(2)
    value.column(2)
    small.last(3)
    query.corner_x(1)
    small.last(0)
    small.last(2)
    query.corner_y(1)
    key.corner_x(2)
    small.finish()
    value.corner_x(0)
    query.corner_x(3)
    query.corner_y(3)
    key.corner_x(1)
    line.take(0)
    cot.first()
    tabulate()
    line.take(1)
    key.corner_y(1)
    value.corner_x(3)
    value.corner_x(2)
    query.last(2)
    normalise(0, 8)
    key.corner_y(2)
    value.last(0)
    query.last(0)
    query.last(1)
    value.corner_y(3)
    key.column(2)
    value.last(1)
    key.corner_y(0)
    normalise(8, 16)
    query.last(3)
    line.take(2)
    key.corner_x(0)
    cot.corner_y(0)
    normalise_latents()
    cot.column(0)
    key.last(1)
    value.last(3)
    cot.corner_x(0)
    value.last(2)
    query.finish()
    project_queries()
    value.finish()
    key.corner_x(3)
    cot.column(1)
    project_values(0)
    key.last(2)
    key.corner_y(3)
    out.first()
    cot.corner_y(1)
    up_first()
    project_values(2)
    cot.column(2)
    query_line.take(0)
    key.last(0)
    key.last(3)
    cot.corner_x(1)
    key.finish()
    project_keys(0)
    out.column(0)
    query_line.take(1)
    out.column(1)
    out.corner_x(0)
    cot.last(0)
    out.corner_y(0)
    project_keys(2)
    query_line.take(2)
    attend_own()
    attend_frames(0, 2)
    attend_frames(2, 4)
    out.column(2)
    cot.corner_x(2)
    out.corner_x(1)
    out.corner_y(1)
    cot.corner_y(3)
    sums_first()
    cot.corner_x(3)
    out.corner_y(3)
    out.corner_x(2)
    down[0].wait_recv()
    out.last(0)
    out.corner_x(3)
    out.corner_y(2)
    cot.last(3)
    up_last()
    cot.last(1)
    cot.corner_y(2)
    out.last(1)
    out.last(2)
    out.last(3)
    cot.last(2)
    out.finish()
    exchange.finish()
    for copy in late + local[prompt:]:
        copy.wait()
    wires.drain()


def opening(scale, small, weights, latents, w_up, w_down, cotangent, media, valid, counts, times):
    rows, width = latents.shape
    shard = weights[0].shape[0]
    up_rows, up_width = w_up.shape
    all_rows = media.shape[0] + rows
    wires = 5 * spread_sems(True) + spread_sems(False) + 2 * LINE_SEMS + 31 + 1 + 2 * LINES
    span = width // LINES
    square = jax.ShapeDtypeStruct((width, width), BF16)
    table = jax.ShapeDtypeStruct((LINES, rows, width), BF16)
    keys = jax.ShapeDtypeStruct((all_rows, width), BF16)
    smem = pl.BlockSpec(memory_space=pltpu.SMEM)
    return pl.pallas_call(
        partial(opening_kernel, scale),
        out_shape=[
            jax.ShapeDtypeStruct((16, width), F32),
            jax.ShapeDtypeStruct((8, 128), F32),
            square,
            square,
            jax.ShapeDtypeStruct((width, span), BF16),
            square,
            jax.ShapeDtypeStruct((32, up_rows, up_width // 16), BF16),
            jax.ShapeDtypeStruct((2,) + w_down.shape, BF16),
            jax.ShapeDtypeStruct((16,) + cotangent.shape, BF16),
            keys,
            keys,
            keys,
            jax.ShapeDtypeStruct((LINES, LINES, rows, span), BF16),
            table,
            table,
            jax.ShapeDtypeStruct((LINES, rows // 4, 128), F32),
            jax.ShapeDtypeStruct((rows, width), F32),
            jax.ShapeDtypeStruct((rows, 128), F32),
        ],
        in_specs=[VMEM] * 8 + [LEFT] * 2 + [VMEM] * 4 + [smem] * 2,
        out_specs=[VMEM] * 2 + [LEFT] * 12 + [VMEM] * 4,
        scratch_shapes=[
            sems(wires),
            sems(wires),
            sems(24),
            pltpu.VMEM((up_rows, up_width // 16), BF16),
            pltpu.VMEM((16, 128), F32),
            pltpu.VMEM((32, 16, 128), F32),
            pltpu.VMEM((width, width), BF16),
            pltpu.VMEM((width, width), BF16),
            pltpu.VMEM((width, span), BF16),
            pltpu.VMEM((LINES, rows, width), BF16),
            pltpu.VMEM((LINES, rows, width), BF16),
            pltpu.VMEM((all_rows, width), BF16),
            pltpu.VMEM((all_rows, width), BF16),
            pltpu.VMEM((all_rows, width), BF16),
            pltpu.VMEM((LINES, rows, span), BF16),
            pltpu.VMEM((LINES, LINES, rows, span), BF16),
            pltpu.VMEM((8, width), F32),
            pltpu.VMEM((LINES, rows, width), F32),
            pltpu.VMEM((LINES, rows, width), BF16),
            pltpu.VMEM((LINES, rows, 128), F32),
            pltpu.VMEM((LINES, rows // 4, 128), F32),
        ],
        compiler_params=params(0),
        name="opening",
    )(*small, *weights, latents, w_up, w_down, cotangent, media, valid, counts, times)


def repel(queries, grads, keys, values, valid, shift, slope, scale, masks):
    query_stack = stacked(queries, masks)
    grad_stack = stacked(grads, masks)
    score = dot_last(query_stack, keys) * scale
    expo = jnp.exp(score)
    if valid is not None:
        expo = jnp.where(valid > 0, expo, 0.0)
    mix = dot_last(grad_stack, values)
    raw = (expo * (mix + shift + slope * score) * scale).astype(BF16)
    query_grad = unstacked(jnp.dot(raw, keys, preferred_element_type=F32), masks)
    key_grad = dot_first(raw, query_stack).astype(BF16)
    value_grad = dot_first(expo.astype(BF16), grad_stack).astype(BF16)
    return query_grad, key_grad, value_grad


def stacked_columns(terms, first):
    return jnp.concatenate([terms[:, first + h : first + h + 1] for h in range(GROUP)], axis=0)


def closing_kernel(scale, *refs):
    (
        table_ref,
        grad_ref,
        terms_ref,
        keys_ref,
        values_ref,
        normed_ref,
        valid_ref,
        attn_ref,
        low_ref,
        own_grad_ref,
        own_terms_ref,
        line_normed_ref,
        query_weight_ref,
        key_weight_ref,
        value_weight_ref,
        media_ref,
        tables_ref,
        latents_ref,
        middle_grad_ref,
        ffn_gain_ref,
        counts_ref,
        times_ref,
        media_grad_out,
        latents_grad_out,
        small_out,
        out_out,
        value_out,
        key_out,
        query_out,
        send_sems,
        recv_sems,
        local_sems,
        table,
        grads,
        keys,
        values,
        normed,
        key_grad,
        value_grad,
        weight_a,
        weight_b,
        sums,
        terms_query,
        got_query,
        query_grad,
        got_line,
        media_grad,
        latent_grad,
        small,
        small_sums,
        small_got,
        time_rows_ref,
        part_a,
        part_b,
        part_c,
        part_d,
        query_relay,
        line_relay,
        *fold,
    ) = refs
    z, g, _, core = here()
    items, rows, width = grads.shape
    frames, _, patches = valid_ref.shape
    media_rows = frames * patches
    shard = width // 32
    groups = H // GROUP
    span = width // groups
    masks = head_masks(rows, span, span // GROUP)
    greet(line_of(z, g) + sides_of(z, g, True))
    wires = Wires(send_sems, recv_sems)
    out = Fold(wires, part_a, True, fold[:FOLD], out_out)
    value = Fold(wires, part_b, True, fold[FOLD : 2 * FOLD], value_out)
    key = Fold(wires, part_c, True, fold[2 * FOLD : 3 * FOLD], key_out)
    query = FoldSplit(wires, part_d, True, fold[3 * FOLD :], query_out)
    total = Total(wires, small, small_out, small_sums, small_got)
    exchange = SumLine(wires, terms_query, got_query, query_relay)
    line_exchange = SumLine(wires, grads, got_line, line_relay)
    local = []

    def load(source, target):
        copy = pltpu.make_async_copy(source, target, local_sems.at[len(local)])
        copy.start()
        local.append(copy)
        return copy

    loads = [
        load(table_ref, table),
        load(grad_ref, grads),
        load(keys_ref, keys),
        load(values_ref, values),
    ]
    normed_load = load(normed_ref, normed)
    key_load = load(key_weight_ref, weight_a)
    value_load = load(value_weight_ref, weight_b)
    stored = []

    def weight_part(part, left, right, first, last):
        @pl.loop(first, last)
        def _(n):
            cols = pl.ds(pl.multiple_of(n * span, 128), span)
            block = dot_first(left[:, cols], right[...]).astype(BF16)
            part[n] = block.reshape(PLANE, 2, shard, width)

    def out_part():
        weight_part(part_a, attn_ref, low_ref, 0, LINES)
        out.start()

    def value_part(first):
        weight_part(part_b, normed, value_grad, first, first + 2)
        if first > 0:
            value.start()

    def key_part(first):
        weight_part(part_c, normed, key_grad, first, first + 2)
        if first > 0:
            key.start()

    def repel_own():
        for copy in loads:
            copy.wait()
        normed_load.wait()
        sums[...] = jnp.zeros_like(sums)
        own_terms = own_terms_ref[...]
        for group in range(groups):
            cols = slice(group * span, (group + 1) * span)
            (
                sums[group, z],
                key_grad[media_rows:, cols],
                value_grad[media_rows:, cols],
            ) = repel(
                table[group, z],
                own_grad_ref[:, cols],
                keys[media_rows:, cols],
                values[media_rows:, cols],
                None,
                stacked_columns(own_terms, group * GROUP),
                stacked_columns(own_terms, H + group * GROUP),
                scale,
                masks,
            )

    def repel_frames(first, last):
        @pl.loop(first, last)
        def _(frame):
            block = pl.ds(pl.multiple_of(frame * patches, patches), patches)
            valid = valid_ref[frame]
            share = shares(counts_ref, z, g, frame, frames, items)

            def pick(ref, cols):
                chosen = share[0] * ref[0, :, cols].astype(F32)
                for item in range(1, items):
                    chosen = chosen + share[item] * ref[item, :, cols].astype(F32)
                return chosen

            everything = slice(None)
            terms = unpack_rows(pick(terms_ref, everything))
            for group in range(groups):
                cols = slice(group * span, (group + 1) * span)
                query_part, key_grad[block, cols], value_grad[block, cols] = repel(
                    pick(table.at[group], everything).astype(BF16),
                    pick(grads, cols).astype(BF16),
                    keys[block, cols],
                    values[block, cols],
                    valid,
                    stacked_columns(terms, group * GROUP),
                    stacked_columns(terms, H + group * GROUP),
                    scale,
                    masks,
                )
                for item in range(items):
                    sums[group, item] += share[item] * query_part

    def queries_first():
        terms_query[...] = sums[...].astype(BF16)
        exchange.first()

    def media_product(n):
        if n == 0:
            key_load.wait()
            value_load.wait()
            small[...] = jnp.zeros_like(small)
            small[10:11] = ffn_gain_ref[...]
            put_times(time_rows_ref, tables_ref, times_ref, frames)
        if n == 2:
            stored[-1].wait()
        count = media_rows // 2
        block = slice(n // 2 * count, (n // 2 + 1) * count)

        @pl.loop(n % 2 * 2, n % 2 * 2 + 2)
        def _(t):
            cols = pl.ds(pl.multiple_of(t * span, 128), span)
            media_grad[:, cols] = dot_last(key_grad[block], weight_a[cols]) + dot_last(
                value_grad[block], weight_b[cols]
            )

    def media_pull(frame):
        count = media_rows // 2
        gain = tables_ref[8:9]
        chunk = 32
        f = frame % (frames // 2)
        moving = time_rows_ref[frame : frame + 1]

        def step(t, carry):
            gain_sum, row_sum = carry
            here_rows = pl.ds(pl.multiple_of(f * patches + t * chunk, chunk), chunk)
            there_rows = pl.ds(pl.multiple_of(frame * patches + t * chunk, chunk), chunk)
            row = media_ref[there_rows].astype(F32) + moving
            pulled, summand = norm_pull(row, gain, media_grad[here_rows])
            media_grad[here_rows] = pulled
            return (
                gain_sum + jnp.sum(summand, axis=0, keepdims=True),
                row_sum + jnp.sum(pulled, axis=0, keepdims=True),
            )

        zero = jnp.zeros((1, width), F32)
        gain_sum, row_sum = lax.fori_loop(0, patches // chunk, step, (zero, zero))
        small[8:9] += gain_sum
        for t in range(8):
            small[t : t + 1] += jnp.where(times_ref[frame] == t, 1.0, 0.0) * row_sum
        if f == frames // 2 - 1:
            first = frame // (frames // 2) * count
            stored.append(load(media_grad, media_grad_out.at[pl.ds(first, count)]))

    def latents_side():
        @pl.loop(0, groups)
        def _(t):
            cols = pl.ds(pl.multiple_of(t * span, 128), span)
            latent_grad[:, cols] = dot_last(key_grad[media_rows:], weight_a[cols]) + dot_last(
                value_grad[media_rows:], weight_b[cols]
            )

    def query_part():
        for item in range(items):
            found = got_query[0, item].astype(F32)
            for place in range(1, LINES):
                found = found + got_query[place, item].astype(F32)
            query_grad[item] = found.astype(BF16)
        grads_all = query_grad[...].reshape(items * rows, span)

        @pl.loop(0, LINES)
        def _(n):
            cols = pl.ds(pl.multiple_of(n * span, 128), span)
            left = line_normed_ref[:, :, cols].reshape(items * rows, span)
            block = dot_first(left, grads_all).astype(BF16)
            part_d[n] = block.reshape(PLANE, 2, shard, span)

        query.start()

    def line_first():
        for item in range(items):
            grads[item] = dot_last(query_grad[item], query_weight_ref[...]).astype(BF16)
        line_exchange.first()

    def latents_end():
        for place in range(LINES):
            latent_grad[...] += got_line[place].astype(F32)
        pulled, summand = norm_pull(
            latents_ref[...].astype(F32), tables_ref[9:10], latent_grad[...]
        )
        latents_grad_out[...] = middle_grad_ref[...] + pulled
        small[9:10] = jnp.sum(summand, axis=0, keepdims=True)
        total.push()

    def total_next():
        total.pull()
        total.push()

    out_part()
    repel_own()
    repel_frames(0, 2)
    repel_frames(2, 4)
    out.corner()
    queries_first()
    media_product(0)
    key_part(0)
    key_part(2)
    out.side_x()
    out.side_y()
    media_product(1)
    media_pull(0)
    exchange.relay()
    key.corner()
    value_part(0)
    value_part(2)
    media_pull(1)
    exchange.finish()
    query_part()
    line_first()
    value.corner()
    media_product(2)
    media_product(3)
    key.side_x()
    key.side_y()
    media_pull(2)
    value.side_x()
    out.line()
    line_exchange.relay()
    value.side_y()
    media_pull(3)
    key.line()
    out.relay()
    line_exchange.finish()
    key.relay()
    query.corner()
    latents_side()
    latents_end()
    value.line()
    total_next()
    out.finish()
    query.side_x()
    query.side_y()
    key.finish()
    value.relay()
    total_next()
    query.line()
    total_next()
    query.finish()
    value.finish()
    total.pull()
    stored[1].wait()
    wires.drain()


def closing(scale, *args):
    (table, grads, terms, keys, values, normed) = args[:6]
    media, latents = args[15], args[17]
    span = table.shape[-1]
    rows, width = latents.shape
    shard = width // 32
    wires = 4 * fold_sems(True) + 6 + 2 * LINES
    bf = [
        table.shape,
        grads.shape,
        keys.shape,
        keys.shape,
        keys.shape,
        keys.shape,
        keys.shape,
        (width, width),
        (width, width),
    ]
    part = pltpu.VMEM((LINES, PLANE, 2, shard, width), BF16)
    small = (16, width)
    scratch = [pltpu.VMEM(shape, BF16) for shape in bf] + [
        pltpu.VMEM(table.shape, F32),
        pltpu.VMEM(table.shape, BF16),
        pltpu.VMEM(table.shape, BF16),
        pltpu.VMEM(table.shape[1:], BF16),
        pltpu.VMEM(grads.shape, BF16),
        pltpu.VMEM((media.shape[0] // 2, width), F32),
        pltpu.VMEM((rows, width), F32),
        pltpu.VMEM(small, F32),
        pltpu.VMEM((3,) + small, F32),
        pltpu.VMEM((6,) + small, F32),
        pltpu.VMEM((8, width), F32),
        part,
        part,
        part,
        pltpu.VMEM((LINES, PLANE, 2, shard, span), BF16),
        pltpu.VMEM(table.shape[1:], BF16),
        pltpu.VMEM((rows, width), BF16),
    ]
    scratch += fold_scratch(shard, width, True) * 3 + fold_scratch(shard, span, True, True)
    smem = pl.BlockSpec(memory_space=pltpu.SMEM)
    return pl.pallas_call(
        partial(closing_kernel, scale),
        out_shape=[
            jax.ShapeDtypeStruct(media.shape, F32),
            jax.ShapeDtypeStruct(latents.shape, F32),
            jax.ShapeDtypeStruct(small, F32),
        ]
        + [jax.ShapeDtypeStruct((shard, width), F32)] * 4,
        in_specs=[LEFT, LEFT, VMEM, LEFT, LEFT, LEFT]
        + [VMEM] * 7
        + [LEFT] * 2
        + [VMEM] * 5
        + [smem] * 2,
        out_specs=[LEFT] + [VMEM] * 6,
        scratch_shapes=[sems(wires), sems(wires), sems(12)] + scratch,
        compiler_params=pltpu.CompilerParams(
            collective_id=3, has_side_effects=True, vmem_limit_bytes=67043328
        ),
        name="closing",
    )(*args)


def settle_kernel(
    weighted_ref,
    stats_ref,
    own_weighted_ref,
    own_stats_ref,
    out_ref,
    latents_ref,
    gain_ref,
    attention_ref,
    attn_ref,
    sums_ref,
    middle_ref,
    normed_ref,
    ready,
):
    rows, width = latents_ref.shape
    span = width // (H // GROUP)
    masks = head_masks(rows, span, span // GROUP)
    found = stats_ref[0]
    for n in range(1, stats_ref.shape[0]):
        found = found + stats_ref[n]
    stats = own_stats_ref[...] + unpack_rows(found)
    sums_ref[...] = stats
    for group in range(H // GROUP):
        cols = pl.ds(group * span, span)
        weighted = own_weighted_ref[:, cols]
        for n in range(weighted_ref.shape[0]):
            weighted = weighted + weighted_ref[n, :, cols].astype(F32)
        attention = weighted / spread_heads(stats, group * GROUP, masks)
        attention_ref[:, cols] = attention
        attn_ref[:, cols] = attention.astype(BF16)
    ready()
    middle = latents_ref[...].astype(F32) + jnp.dot(
        attn_ref[...], out_ref[...], preferred_element_type=F32
    )
    middle_ref[...] = middle
    normed_ref[...] = layer_norm(middle, gain_ref[...]).astype(BF16)


def norm_pull(rows, gain, grad):
    mean = jnp.mean(rows, axis=-1, keepdims=True)
    centred = rows - mean
    inverse = lax.rsqrt(jnp.mean(centred * centred, axis=-1, keepdims=True) + NORM_STABILIZER)
    xhat = centred * inverse
    t = grad * gain
    pulled = (
        t
        - jnp.mean(t, axis=-1, keepdims=True)
        - xhat * jnp.mean(t * xhat, axis=-1, keepdims=True)
    ) * inverse
    return pulled, grad * xhat


def unsettle_kernel(
    normed_grad_ref,
    middle_ref,
    gain_ref,
    cot_ref,
    out_ref,
    attention_ref,
    stats_ref,
    coef,
    middle_grad_ref,
    low_ref,
    gain_grad_ref,
    weighted_grad_ref,
    terms_ref,
    attn_grad,
):
    rows, width = middle_ref.shape
    span = width // (H // GROUP)
    masks = head_masks(rows, span, span // GROUP)
    pulled, summand = norm_pull(middle_ref[...], gain_ref[...], normed_grad_ref[...])
    gain_grad_ref[...] = jnp.sum(summand, axis=0, keepdims=True)
    middle_grad = cot_ref[...].astype(F32) + pulled
    middle_grad_ref[...] = middle_grad
    low_ref[...] = middle_grad.astype(BF16)
    attn_grad[...] = dot_last(low_ref[...], out_ref[...])
    stats = stats_ref[...]
    lane = lax.broadcasted_iota(jnp.int32, (rows, 128), 1)
    terms = jnp.zeros((rows, 128), F32)
    for group in range(H // GROUP):
        cols = pl.ds(group * span, span)
        grad = attn_grad[:, cols]
        first = group * GROUP
        weighted_grad_ref[:, cols] = (grad / spread_heads(stats, first, masks)).astype(BF16)
        along = grad * attention_ref[:, cols]
        for h in range(GROUP):
            inner = jnp.sum(jnp.where(masks[h], along, 0.0), axis=1, keepdims=True)
            total = stats[:, first + h : first + h + 1]
            moment = stats[:, H + first + h : H + first + h + 1]
            slope = -coef / total
            shift = -inner / total + coef * (1.0 / total + moment / (total * total)) + slope
            terms = jnp.where(lane == first + h, shift, terms)
            terms = jnp.where(lane == H + first + h, slope, terms)
    terms_ref[...] = terms


def gelu_parts(rows):
    below = 0.5 * (1.0 + lax.erf(rows * (0.5**0.5)))
    density = jnp.exp(-0.5 * rows * rows) * ((0.5 / jnp.pi) ** 0.5)
    return rows * below, below + rows * density


def middle_kernel(patches, *refs):
    (
        weighted_ref,
        stats_ref,
        own_weighted_ref,
        own_stats_ref,
        out_weight_ref,
        up_ref,
        down_ref,
        cot_rows_ref,
        latents_ref,
        tables_ref,
        cot_ref,
        counts_ref,
        attn_out,
        low_out,
        middle_grad_out,
        gain_grad_out,
        weighted_grad_out,
        terms_out,
        grad_table_out,
        terms_table_out,
        new_latents_out,
        up_grad_out,
        down_grad_out,
        send_sems,
        recv_sems,
        local_sems,
        out_weight,
        up_cols,
        down_rows,
        cot_rows,
        ffn_rows,
        attention,
        sums,
        middle,
        normed,
        hidden_grad,
        up_grad,
        hidden,
        normed_part,
        down_part,
        up_grad_part,
        down_grad_part,
        up_near,
        down_near,
        up_got,
        normed_grad,
        down_sum,
        attn_grad,
        packed,
        *fold,
    ) = refs
    z, g, chip, core = here()
    rows, width = latents_ref.shape
    span = up_cols.shape[1]
    shard = width // 32
    block_rows = PLANE * rows
    near = (z, sibling(g))
    gain_ref = tables_ref.at[10:11]
    greet([(there[0], 2 * there[1] + core) for there, _ in up_places(z, chip)] + [near])
    wires = Wires(send_sems, recv_sems)
    gather = Spread(
        wires, normed, lambda zz, gg: ffn_rows.at[zz, gg // 2], columns_half, False
    )
    back = FoldSteps(wires, normed_part, fold[:FOLD], normed_grad)
    down = Fold(wires, down_part, False, fold[FOLD:], down_sum)
    give = GiveBack(
        wires,
        up_grad_part,
        down_grad_part,
        (up_near, down_near, up_got),
        up_grad_out,
        down_grad_out,
    )
    grad_line = Line(wires, weighted_grad_out, lambda zz: grad_table_out.at[zz])
    terms_line = Line(wires, packed, lambda zz: terms_table_out.at[zz])
    loads = [
        pltpu.make_async_copy(source, target, local_sems.at[n])
        for n, (source, target) in enumerate(
            (
                (out_weight_ref, out_weight),
                (down_ref, down_rows),
                (cot_rows_ref, cot_rows),
                (up_ref, up_cols),
            )
        )
    ]
    for load in loads:
        load.start()

    def settle():
        settle_kernel(
            weighted_ref,
            stats_ref,
            own_weighted_ref,
            own_stats_ref,
            out_weight,
            latents_ref,
            gain_ref,
            attention,
            attn_out,
            sums,
            middle,
            normed,
            loads[0].wait,
        )
        ffn_rows[z, chip] = normed[...]

    def hidden_back():
        loads[1].wait()
        loads[2].wait()
        loads[3].wait()

        @pl.loop(0, LINES)
        def _(n):
            block = cot_rows[n].reshape(block_rows, width)
            hidden_grad[n] = dot_last(block, down_rows[...])

    def group(n):
        place = gather.zs[n]
        block = ffn_rows[place].reshape(block_rows, width)
        value, slope = gelu_parts(jnp.dot(block, up_cols[...], preferred_element_type=F32))
        hidden[place] = value.astype(BF16)
        grad = (hidden_grad[place] * slope).astype(BF16)
        up_grad[place] = grad
        part = dot_last(grad, up_cols[...]).astype(BF16)
        normed_part[place] = part.reshape(PLANE, rows, width)

    def down_product():
        @pl.loop(0, LINES)
        def _(n):
            part = jnp.dot(hidden[n], down_rows[...], preferred_element_type=F32)
            down_part[n] = part.astype(BF16).reshape(PLANE, rows, width)

    def up_gradient():
        grads = up_grad[...].reshape(LINES * block_rows, span)

        @pl.loop(0, LINES)
        def _(n):
            cols = pl.ds(pl.multiple_of(n * span, 128), span)
            block = ffn_rows[:, :, :, cols].reshape(LINES * block_rows, span)
            part = dot_first(block, grads).astype(BF16)
            up_grad_part[n] = part.reshape(PLANE, 2, shard, span)

    def down_gradient():
        rows_up = hidden[...].reshape(LINES * block_rows, span)

        @pl.loop(0, LINES)
        def _(n):
            cols = pl.ds(pl.multiple_of(n * span, 128), span)
            block = cot_rows[:, :, :, cols].reshape(LINES * block_rows, span)
            part = dot_first(rows_up, block)
            down_grad_part[:, :, cols] = part.reshape(2, span // 2, span)

    def unsettle():
        unsettle_kernel(
            normed_grad,
            middle,
            gain_ref,
            cot_ref,
            out_weight,
            attention,
            sums,
            ENTROPY_WEIGHT * patches / counts_ref[3:4, 0:1],
            middle_grad_out,
            low_out,
            gain_grad_out,
            weighted_grad_out,
            terms_out,
            attn_grad,
        )
        grad_table_out[z] = weighted_grad_out[...]
        packed[...] = pack_rows(terms_out[...])
        terms_table_out[z] = packed[...]

    def new_rows():
        new_latents_out[...] = (middle[...] + down_sum[...]).astype(BF16)

    settle()
    gather.first()
    gather.corner_x(0)
    gather.corner_y(0)
    gather.column(0)
    gather.column(1)
    hidden_back()
    gather.last(0)
    group(0)
    back.corner(0)
    gather.corner_x(1)
    gather.corner_y(1)
    gather.column(2)
    gather.corner_x(2)
    gather.corner_y(2)
    gather.last(1)
    group(1)
    back.corner(1)
    gather.corner_x(3)
    back.side_y(0)
    gather.corner_y(3)
    back.side_x(0)
    gather.last(2)
    group(2)
    back.corner(2)
    gather.last(3)
    group(3)
    back.corner(3)
    back.side_x(1)
    back.side_y(1)
    back.line(0)
    down_gradient()
    up_gradient()
    give.first()
    back.side_x(2)
    back.side_y(2)
    back.side_y(3)
    down_product()
    down.start()
    back.side_x(3)
    down.corner()
    give.columns()
    back.line(2)
    back.line(3)
    give.rows()
    back.line(1)
    down.side_x()
    down.side_y()
    back.relay()
    back.finish()
    unsettle()
    grad_line.first()
    grad_line.take(0)
    terms_line.first()
    down.line()
    terms_line.take(0)
    terms_line.take(1)
    grad_line.take(1)
    grad_line.take(2)
    terms_line.take(2)
    down.relay()
    give.finish()
    down.finish()
    new_rows()
    wires.drain()


def middle_part(
    patches,
    weighted,
    stats,
    own_weighted,
    own_stats,
    w_out,
    up_cols,
    down_rows,
    cot_rows,
    latents,
    tables,
    cot,
    counts,
):
    rows, width = latents.shape
    span = up_cols.shape[1]
    shard = width // 32
    plane = (LINES, PLANE, rows, width)
    block = (LINES, PLANE * rows, span)
    wires = spread_sems(False) + STEP_SEMS + fold_sems(False) + GIVE_SEMS + 2 * LINE_SEMS
    own = (rows, width)
    terms = own_stats.shape
    bf = [
        w_out.shape,
        up_cols.shape,
        down_rows.shape,
        plane,
        plane,
    ]
    scratch = [pltpu.VMEM(shape, BF16) for shape in bf] + [
        pltpu.VMEM(own, F32),
        pltpu.VMEM(terms, F32),
        pltpu.VMEM(own, F32),
        pltpu.VMEM(own, BF16),
        pltpu.VMEM(block, F32),
        pltpu.VMEM(block, BF16),
        pltpu.VMEM(block, BF16),
        pltpu.VMEM(plane, BF16),
        pltpu.VMEM(plane, BF16),
        pltpu.VMEM((LINES, PLANE, 2, shard, span), BF16),
        pltpu.VMEM((2, span // 2, width), F32),
        pltpu.VMEM((LINES, PLANE, shard, span), BF16),
        pltpu.VMEM((span // 2, width), F32),
        pltpu.VMEM((LINES, PLANE, shard, span), BF16),
        pltpu.VMEM(own, F32),
        pltpu.VMEM(own, F32),
        pltpu.VMEM(own, F32),
        pltpu.VMEM((rows // 4, 128), F32),
    ]
    scratch += fold_scratch(rows, width, False) * 2
    return pl.pallas_call(
        partial(middle_kernel, patches),
        out_shape=[
            jax.ShapeDtypeStruct(own, BF16),
            jax.ShapeDtypeStruct(own, BF16),
            jax.ShapeDtypeStruct(own, F32),
            jax.ShapeDtypeStruct((1, width), F32),
            jax.ShapeDtypeStruct(own, BF16),
            jax.ShapeDtypeStruct(terms, F32),
            jax.ShapeDtypeStruct((LINES,) + own, BF16),
            jax.ShapeDtypeStruct((LINES, rows // 4, 128), F32),
            jax.ShapeDtypeStruct(own, BF16),
            jax.ShapeDtypeStruct((shard, span * 16), F32),
            jax.ShapeDtypeStruct((span // 2, width), F32),
        ],
        in_specs=[VMEM] * 4 + [LEFT] * 4 + [VMEM] * 4,
        out_specs=[VMEM] * 11,
        scratch_shapes=[sems(wires), sems(wires), sems(4)] + scratch,
        compiler_params=params(1),
        name="middle",
    )(
        weighted,
        stats,
        own_weighted,
        own_stats,
        w_out,
        up_cols,
        down_rows,
        cot_rows.reshape(plane),
        latents,
        tables,
        cot,
        counts,
    )


def ending_kernel(shard, *refs):
    count = (len(refs) - 6) // 3
    sources, small = refs[:count], refs[count]
    outs = refs[count + 1 : 2 * count + 1]
    small_outs = refs[2 * count + 1 : 2 * count + 5]
    held, arrive = refs[2 * count + 5 : 3 * count + 5], refs[3 * count + 5]
    loads, stores = [], []
    for n in range(count):
        loads.append(pltpu.make_async_copy(sources[n], held[n], arrive.at[n]))
        stores.append(pltpu.make_async_copy(held[n], outs[n], arrive.at[n]))
        loads[n].start()
    z, g, _, _ = here()
    width = small.shape[1]
    turned = pltpu.roll(small[...], width - (8 * z + g) * shard, 1)
    small_outs[0][...] = turned[:8, :shard]
    for n in range(3):
        small_outs[n + 1][...] = turned[8 + n : 9 + n, :shard]
    for n in range(count):
        loads[n].wait()
        stores[n].start()
    for n in range(count):
        stores[n].wait()


def ending(results, small, shard):
    count = len(results)
    return pl.pallas_call(
        partial(ending_kernel, shard),
        out_shape=[jax.ShapeDtypeStruct(r.shape, r.dtype) for r in results]
        + [jax.ShapeDtypeStruct((8, shard), F32)]
        + [jax.ShapeDtypeStruct((1, shard), F32)] * 3,
        in_specs=[LEFT] * count + [VMEM],
        out_specs=[LEFT] * count + [VMEM] * 4,
        scratch_shapes=[pltpu.VMEM(r.shape, r.dtype) for r in results] + [sems(count)],
        name="ending",
    )(*results, small)


def per_device(
    media,
    latents,
    frame_counts,
    time_index,
    valid,
    time_table,
    media_gain,
    latent_gain,
    ffn_gain,
    w_query,
    w_key,
    w_value,
    w_out,
    w_up,
    w_down,
    cotangent,
):
    frames = time_index.shape[0]
    patches = valid.shape[0] // frames
    width = latents.shape[1]
    shard = media_gain.shape[0]
    scale = (width // H) ** (-0.5)
    valid_rows = valid.reshape(frames, 1, patches)
    (
        tables,
        counts,
        full_key,
        full_value,
        full_query,
        full_out,
        up_cols,
        down_rows,
        cot_rows,
        normed,
        keys,
        values,
        table,
        line_normed,
        got_weighted,
        got_stats,
        own_weighted,
        own_stats,
    ) = opening(
        scale,
        (
            time_table,
            media_gain.reshape(1, shard),
            latent_gain.reshape(1, shard),
            ffn_gain.reshape(1, shard),
        ),
        (w_key, w_value, w_query, w_out),
        latents,
        w_up,
        w_down,
        cotangent,
        media,
        valid_rows,
        frame_counts,
        time_index,
    )
    (
        attn_low,
        middle_low,
        middle_grad,
        grad_ffn_gain,
        weighted_grad,
        terms,
        grad_table,
        terms_table,
        new_latents,
        shard_up,
        shard_down,
    ) = middle_part(
        valid.shape[0] * lax.axis_size(AXES),
        got_weighted,
        got_stats,
        own_weighted,
        own_stats,
        full_out,
        up_cols.reshape(width, -1),
        down_rows.reshape(-1, width),
        cot_rows,
        latents,
        tables,
        cotangent,
        counts,
    )
    (
        media_grad,
        latents_grad,
        smalls_grad,
        shard_out,
        shard_value,
        shard_key,
        shard_query,
    ) = closing(
        scale,
        table,
        grad_table,
        terms_table,
        keys,
        values,
        normed,
        valid_rows,
        attn_low,
        middle_low,
        weighted_grad,
        terms,
        line_normed,
        full_query,
        full_key,
        full_value,
        media,
        tables,
        latents,
        middle_grad,
        grad_ffn_gain,
        frame_counts,
        time_index,
    )
    results = ending(
        (
            new_latents,
            media_grad,
            latents_grad,
            shard_query,
            shard_key,
            shard_value,
            shard_out,
            shard_up,
            shard_down,
        ),
        smalls_grad,
        shard,
    )
    time_grad, *gains = results[9:]
    return (
        *results[:3],
        time_grad,
        *(gain.reshape(shard) for gain in gains),
        *results[3:9],
    )


def solution(mesh):
    in_specs = (
        P(("gx", "gy"), None),
        P(("gx", "gy"), None),
        P(),
        P(("gx", "gy")),
        P(("gx", "gy")),
        P(None, ("gx", "gy")),
        P(("gx", "gy")),
        P(("gx", "gy")),
        P(("gx", "gy")),
        P(("gx", "gy"), None),
        P(("gx", "gy"), None),
        P(("gx", "gy"), None),
        P(("gx", "gy"), None),
        P(("gx", "gy"), None),
        P(("gx", "gy"), None),
        P(("gx", "gy"), None),
    )
    out_specs = (
        P(("gx", "gy"), None),
        P(("gx", "gy"), None),
        P(("gx", "gy"), None),
        P(None, ("gx", "gy")),
        P(("gx", "gy")),
        P(("gx", "gy")),
        P(("gx", "gy")),
        P(("gx", "gy"), None),
        P(("gx", "gy"), None),
        P(("gx", "gy"), None),
        P(("gx", "gy"), None),
        P(("gx", "gy"), None),
        P(("gx", "gy"), None),
    )
    return jax.shard_map(
        per_device if dict(mesh.shape) == {"gx": 4, "gy": 8} else plain_device,
        mesh=mesh, in_specs=in_specs, out_specs=out_specs, check_vma=False
    )
```

```python
from functools import partial

import jax
import jax.numpy as jnp
from jax import lax
from jax.experimental import pallas as pl
from jax.experimental.pallas import tpu as pltpu
from jax.sharding import PartitionSpec as P

H = 16


ENTROPY_WEIGHT = 4.0
NORM_STABILIZER = 1e-05
AXES = ("gx", "gy")
LINES = 4
PLANE = 4
HBM = pl.ANY
BF16 = jnp.bfloat16
F32 = jnp.float32


def here():
    z = lax.axis_index("gx")
    g = lax.axis_index("gy")
    return z, g, g // 2, g % 2


def sibling(g):
    return g + 1 - 2 * (g % 2)


def along_x(g):
    return g + 2 - 4 * ((g // 2) % 2)


def along_y(g):
    return (g + 4) % 8


def turn(z, k):
    return (z + k) % LINES


def greet(devices):
    barrier = pltpu.get_barrier_semaphore()
    for device in devices:
        pl.semaphore_signal(
            barrier, inc=1, device_id=device, device_id_type=pl.DeviceIdType.MESH
        )
    pl.semaphore_wait(barrier, len(devices))


def line_of(z, g):
    return [(turn(z, k), g) for k in (1, 2, 3)]


class Wires:
    def __init__(self, send_sems, recv_sems):
        self.send_sems, self.recv_sems, self.used, self.sent = send_sems, recv_sems, 0, []

    def reserve(self, count):
        first = self.used
        self.used += count
        return first

    def copy(self, source, target, device, send, recv):
        return pltpu.make_async_remote_copy(
            src_ref=source,
            dst_ref=target,
            send_sem=self.send_sems.at[send],
            recv_sem=self.recv_sems.at[recv],
            device_id=device,
            device_id_type=pl.DeviceIdType.MESH,
        )

    def send(self, source, target, device):
        n = self.reserve(1)
        copy = self.copy(source, target, device, n, n)
        copy.start()
        self.sent.append((None, copy))
        return copy

    def send_if(self, condition, source, target, device, send, recv):
        copy = self.copy(source, target, device, send, recv)
        self.sent.append((condition, copy))

        @pl.when(condition)
        def _():
            copy.start()

        return copy

    def drain(self):
        for condition, copy in self.sent:
            if condition is None:
                copy.wait_send()
            else:
                pl.when(condition)(copy.wait_send)


class Line:
    def __init__(self, wires, shard, slot):
        self.wires, self.shard, self.slot = wires, shard, slot
        self.z, self.g, _, _ = here()
        self.base = wires.reserve(4)
        low, high = (3 - self.z) // 3, self.z // 3
        self.order = (1 + 2 * low, 3 - low - high, 2 - low + high)

    def first(self):
        z, g = self.z, self.g
        own = self.slot(z)
        base = self.base
        self.wires.send_if(z < 3, self.shard, own, (turn(z, 1), g), base + 1, base + 1)
        self.wires.send_if(z > 0, self.shard, own, (turn(z, 3), g), base + 3, base + 3)
        self.across = self.wires.copy(self.shard, own, (turn(z, 2), g), base + 2, base + 2)
        self.across.start()
        self.wires.sent.append((None, self.across))

    def take(self, step):
        z, g = self.z, self.g
        k = self.order[step]
        origin = turn(z, LINES - k)
        held = self.slot(origin)
        self.wires.copy(held, held, (z, g), 0, self.base + k).wait_recv()
        if step == 2:
            self.relay(z == 2, 3, 3)
        if step == 2:
            self.relay(z == 1, 0, 1)
        return origin

    def relay(self, condition, there, k):
        held = self.slot(turn(self.z, 2))
        self.wires.send_if(
            condition, held, held, (there, self.g), self.base, self.base + k
        )


class LineSplit:
    def __init__(self, wires, shard, slot):
        self.wires, self.shard, self.slot = wires, shard, slot
        self.z, self.g, _, _ = here()
        self.base = wires.reserve(LINES)
        low, high = (3 - self.z) // 3, self.z // 3
        self.order = (1 + 2 * low, 3 - low - high, 2 - low + high)

    def first(self):
        for k in (2, 1, 3):
            there = turn(self.z, k)
            copy = self.wires.copy(
                piece_of(self.shard, there),
                self.slot(self.z),
                (there, self.g),
                self.base + k,
                self.base + k,
            )
            copy.start()
            self.wires.sent.append((None, copy))

    def take(self, step):
        k = self.order[step]
        origin = turn(self.z, LINES - k)
        held = self.slot(origin)
        self.wires.copy(held, held, (self.z, self.g), 0, self.base + k).wait_recv()
        return origin


def piece_of(shard, place):
    width = shard.shape[-1] // LINES
    return shard.at[:, pl.ds(pl.multiple_of(place * width, 128), width)]


class Spread:
    def __init__(self, wires, shard, slot, half, whole, split=False):
        self.wires, self.shard, self.slot, self.half, self.whole = wires, shard, slot, half, whole
        self.z, self.g, _, _ = here()
        self.line = (LineSplit if split else Line)(wires, shard, lambda z: slot(z, self.g))
        if split:
            self.shard = piece_of(shard, self.z)
        self.zs, self.x, self.y, self.dx, self.dy, self.sib = [self.z], [], [], {}, {}, []

    def side(self, gy):
        return (self.z, gy)

    def to_sibling(self, held):
        if self.whole:
            self.sib.append(self.wires.send(held, held, self.side(sibling(self.g))))

    def first(self):
        own = self.slot(self.z, self.g)
        self.line.first()
        self.x.append(self.wires.send(self.shard, own, self.side(along_x(self.g))))
        self.y.append(self.wires.send(self.shard, own, self.side(along_y(self.g))))
        if self.whole:
            self.sib.append(self.wires.send(self.shard, own, self.side(sibling(self.g))))

    def column(self, step):
        self.zs.append(self.line.take(step))
        held = self.slot(self.zs[-1], self.g)
        self.x.append(self.wires.send(held, held, self.side(along_x(self.g))))
        self.y.append(self.wires.send(held, held, self.side(along_y(self.g))))
        self.to_sibling(held)

    def corner(self, n):
        self.corner_x(n)
        self.corner_y(n)

    def corner_x(self, n):
        self.x[n].wait_recv()
        held = self.slot(self.zs[n], along_x(self.g))
        part = self.half(held, 0)
        self.dy[n] = self.wires.send(part, part, self.side(along_y(self.g)))
        self.to_sibling(held)

    def corner_y(self, n):
        self.y[n].wait_recv()
        held = self.slot(self.zs[n], along_y(self.g))
        part = self.half(held, 1)
        self.dx[n] = self.wires.send(part, part, self.side(along_x(self.g)))
        self.to_sibling(held)

    def last(self, n):
        self.dy[n].wait_recv()
        self.dx[n].wait_recv()
        self.to_sibling(self.slot(self.zs[n], along_y(along_x(self.g))))

    def finish(self):
        for copy in self.sib:
            copy.wait_recv()


def spread_all(flows):
    for flow in flows:
        flow.first()
    for flow in flows:
        flow.corner(0)
    for step in range(3):
        for flow in flows:
            flow.column(step)
        for flow in flows:
            flow.corner(step + 1)
    for n in range(4):
        for flow in flows:
            flow.last(n)
    for flow in flows:
        flow.finish()


LINE_SEMS = 4


def spread_sems(whole):
    return LINE_SEMS + 8 + 8 + (16 if whole else 0)


def columns_half(ref, which):
    width = ref.shape[-1] // 2
    return ref.at[..., pl.ds(which * width, width)]


def rows_half(ref, which):
    rows = ref.shape[0] // 2
    return ref.at[pl.ds(which * rows, rows)]


def rows_parts(ref, which):
    return ref.at[pl.ds(32, 16)] if which else ref.at[pl.ds(0, 32)]


def sides_of(z, g, whole):
    near = [(z, along_x(g)), (z, along_y(g))]
    return near + [(z, sibling(g))] if whole else near


def params(ident):
    return pltpu.CompilerParams(
        collective_id=ident, has_side_effects=True, vmem_limit_bytes=60 * 2**20
    )


def sems(count):
    return pltpu.SemaphoreType.DMA((count,))


VMEM = pl.BlockSpec(memory_space=pltpu.VMEM)
LEFT = pl.BlockSpec(memory_space=HBM)


class SumLine:
    def __init__(self, wires, source, out, relayed=None):
        self.wires, self.source, self.out, self.relayed = wires, source, out, relayed
        self.z, self.g, _, _ = here()
        self.base = wires.reserve(LINES)
        low, high = (3 - self.z) // 3, self.z // 3
        self.back = (0, 1 + 2 * low, 3 - low - high, 2 - low + high)
        self.places = [turn(self.z, LINES - k) if n else self.z for n, k in enumerate(self.back)]
        self.end = low + high > 0
        self.inner = low + high < 1
        self.beside = 1 + high

    def step(self, n):
        place = self.places[n]
        if n < 3 or self.relayed is None:
            k = LINES - self.back[n]
            copy = self.wires.copy(
                self.source.at[place],
                self.out.at[self.z],
                (place, self.g),
                self.base + k,
                self.base + k,
            )
            copy.start()
            self.wires.sent.append((None, copy))
        else:
            self.wires.send_if(
                self.end,
                self.source.at[place],
                self.relayed,
                (self.beside, self.g),
                self.base,
                self.base,
            )

    def first(self):
        for n in (2, 1, 3):
            self.step(n)
        self.clear()
        self.out[self.z] = self.source[self.z]

    def clear(self):
        if self.relayed is None:
            return

        @pl.when(self.end)
        def _():
            self.out[3 - self.z] = jnp.zeros(self.out.shape[1:], self.out.dtype)

    def relay(self):
        place = self.places[3]
        held = self.source.at[place]
        across = self.wires.copy(
            held, self.out.at[self.z], (place, self.g), self.base + 2, self.base + 2
        )
        came = self.wires.copy(
            self.relayed, self.relayed, (self.z, self.g), self.base, self.base
        )
        self.wires.sent.append((self.inner, across))

        @pl.when(self.inner)
        def _():
            came.wait_recv()
            held[...] = held[...] + self.relayed[...]
            across.start()

    def finish(self):
        for k, condition in ((1, self.z > 0), (3, self.z < 3), (2, None)):
            if self.relayed is None:
                condition = None
            held = self.out.at[turn(self.z, LINES - k)]
            copy = self.wires.copy(held, held, (self.z, self.g), 0, self.base + k)
            if condition is None:
                copy.wait_recv()
            else:
                pl.when(condition)(copy.wait_recv)


class Exchange:
    def __init__(self, wires, arrays):
        self.lines = [SumLine(wires, *array) for array in arrays]

    def first(self):
        for line in self.lines:
            line.first()

    def relay(self):
        for line in self.lines:
            line.relay()

    def finish(self):
        for line in self.lines:
            line.finish()


def add_slots(target, source, count):
    @pl.loop(0, count)
    def _(n):
        target[n] = (target[n].astype(F32) + source[n].astype(F32)).astype(target.dtype)


def sum_slots(ref):
    found = ref[0].astype(F32)
    for n in range(1, LINES):
        found = found + ref[n].astype(F32)
    return found


class Fold:
    summed = True

    def __init__(self, wires, parts, whole, scratch, out):
        self.wires, self.parts, self.whole, self.out = wires, parts, whole, out
        self.from_sib, self.cx, self.cy, self.fx, self.fy, self.fz, self.relayed = scratch
        self.z, self.g, self.chip, self.core = here()
        self.cut = self.cy.shape[-1]
        self.lines = SumLine(wires, self.fx, self.fz, self.relayed) if self.summed else None

    def send(self, source, target, gy):
        return self.wires.send(source, target, (self.z, gy))

    def column(self, q):
        return self.parts.at[:, q, self.core] if self.whole else self.parts.at[:, q]

    def half(self, ref, which):
        if which:
            return ref.at[:, :, pl.ds(self.cut, ref.shape[-1] - self.cut)]
        return ref.at[:, :, pl.ds(0, self.cut)]

    def merge(self, q):
        if self.whole:
            core = self.core

            @pl.loop(0, LINES)
            def _(n):
                self.parts[n, q, core] = self.parts[n, q, core] + self.from_sib[n, q]

    def start(self):
        if self.whole:
            theirs = self.parts.at[:, :, 1 - self.core]
            self.sib = self.send(theirs, self.from_sib, sibling(self.g))

    def corner(self):
        if self.whole:
            self.sib.wait_recv()
        q = along_y(along_x(self.g)) // 2
        self.merge(q)
        far = self.column(q)
        self.to_y = self.send(self.half(far, 0), self.cy, along_y(self.g))
        self.to_x = self.send(self.half(far, 1), self.cx, along_x(self.g))

    def side(self, gy, came, corner, which, target):
        q = gy // 2
        self.merge(q)
        came.wait_recv()
        column = self.column(q)
        cols = slice(self.cut, None) if which else slice(0, self.cut)

        @pl.loop(0, LINES)
        def _(n):
            column[n, :, cols] = column[n, :, cols] + corner[n]

        return self.send(column, target, gy)

    def side_x(self):
        self.by_x = self.side(along_x(self.g), self.to_y, self.cy, 0, self.fx)

    def side_y(self):
        self.by_y = self.side(along_y(self.g), self.to_x, self.cx, 1, self.fy)

    def line(self):
        self.merge(self.chip)
        self.by_x.wait_recv()
        self.by_y.wait_recv()
        column = self.column(self.chip)
        for n in (3, 2, 1):
            there = self.lines.places[n]
            self.fx[there] = (
                column[there].astype(F32)
                + self.fx[there].astype(F32)
                + self.fy[there].astype(F32)
            ).astype(BF16)
            self.lines.step(n)
        z = self.z
        self.lines.clear()
        self.fz[z] = jnp.zeros(self.fz.shape[1:], BF16)
        self.out[...] = column[z].astype(F32) + self.fx[z].astype(F32) + self.fy[z].astype(F32)

    def relay(self):
        self.lines.relay()

    def finish(self):
        self.lines.finish()
        self.out[...] += sum_slots(self.fz)


class FoldSplit(Fold):
    summed = False

    def line(self):
        self.merge(self.chip)
        self.by_x.wait_recv()
        self.by_y.wait_recv()
        column = self.column(self.chip)
        self.zs = []
        for k in (2, 1, 3, 0):
            there = turn(self.z, k) if k else self.z
            found = (
                column[there].astype(F32)
                + self.fx[there].astype(F32)
                + self.fy[there].astype(F32)
            ).astype(BF16)
            if k:
                self.fx[there] = found
                self.zs.append(
                    self.wires.send(self.fx.at[there], self.fz.at[self.z], (there, self.g))
                )
            else:
                self.fz[self.z] = found

    def finish(self):
        for copy in self.zs:
            copy.wait_recv()
        width = self.fz.shape[-1]
        for place in range(LINES):
            self.out[:, place * width : (place + 1) * width] = self.fz[place].astype(F32)


def fold_scratch(rows, cols, whole, split=False):
    cut = 256 if split else cols // 2
    return [
        pltpu.VMEM((LINES, PLANE, rows, cols) if whole else (1, 1, 16, 128), BF16),
        pltpu.VMEM((LINES, rows, cols - cut), BF16),
        pltpu.VMEM((LINES, rows, cut), BF16),
        pltpu.VMEM((LINES, rows, cols), BF16),
        pltpu.VMEM((LINES, rows, cols), BF16),
        pltpu.VMEM((LINES, rows, cols), BF16),
        pltpu.VMEM((rows, cols), BF16),
    ]


FOLD = 7


def fold_sems(whole):
    return (1 if whole else 0) + 4 + LINES


class FoldSteps:
    def __init__(self, wires, parts, scratch, out):
        self.wires, self.parts, self.out = wires, parts, out
        _, self.cx, self.cy, self.fx, self.fy, self.fz, relayed = scratch
        self.z, self.g, self.chip, _ = here()
        self.width = parts.shape[-1] // 2
        self.lines = SumLine(wires, self.fx, self.fz, relayed)
        self.zs = self.lines.places
        self.to_x, self.to_y, self.by_x, self.by_y = {}, {}, {}, {}

    def half(self, n, q, which):
        return self.parts.at[self.zs[n], q, :, pl.ds(which * self.width, self.width)]

    def corner(self, n):
        far = along_y(along_x(self.g)) // 2
        place = self.zs[n]
        self.to_y[n] = self.wires.send(
            self.half(n, far, 0), self.cy.at[place], (self.z, along_y(self.g))
        )
        self.to_x[n] = self.wires.send(
            self.half(n, far, 1), self.cx.at[place], (self.z, along_x(self.g))
        )

    def side(self, n, gy, came, corner, which, target):
        came.wait_recv()
        q, place = gy // 2, self.zs[n]
        cols = slice(which * self.width, (which + 1) * self.width)
        self.parts[place, q, :, cols] = self.parts[place, q, :, cols] + corner[place]
        return self.wires.send(self.parts.at[place, q], target.at[place], (self.z, gy))

    def side_x(self, n):
        self.by_x[n] = self.side(n, along_x(self.g), self.to_y[n], self.cy, 0, self.fx)

    def side_y(self, n):
        self.by_y[n] = self.side(n, along_y(self.g), self.to_x[n], self.cx, 1, self.fy)

    def line(self, n):
        self.by_x[n].wait_recv()
        self.by_y[n].wait_recv()
        place = self.zs[n]
        found = (
            self.parts[place, self.chip].astype(F32)
            + self.fx[place].astype(F32)
            + self.fy[place].astype(F32)
        )
        if n == 0:
            self.out[...] = found
            self.lines.clear()
            self.fz[self.z] = jnp.zeros(self.fz.shape[1:], BF16)
        else:
            self.fx[place] = found.astype(BF16)
            self.lines.step(n)

    def relay(self):
        self.lines.relay()

    def finish(self):
        self.lines.finish()
        self.out[...] += sum_slots(self.fz)


STEP_SEMS = 16 + LINES


def layer_norm(row_block, gain_row):
    row_mean = jnp.mean(row_block, axis=-1, keepdims=True)
    centred = row_block - row_mean
    variance = jnp.mean(centred * centred, axis=-1, keepdims=True)
    return centred * lax.rsqrt(variance + NORM_STABILIZER) * gain_row


def product(left_side, right_side):
    return jnp.dot(left_side, right_side, preferred_element_type=jnp.float32)


def inner_first(left_side, right_side):
    return lax.dot_general(
        left_side, right_side, (((0,), (0,)), ((), ())), preferred_element_type=jnp.float32
    )


def inner_last(left_side, right_side):
    return lax.dot_general(
        left_side, right_side, (((1,), (1,)), ((), ())), preferred_element_type=jnp.float32
    )


def collect(onehot_rows, value_rows):
    return lax.dot_general(
        onehot_rows,
        value_rows,
        (((0,), (0,)), ((), ())),
        precision=lax.Precision.HIGHEST,
        preferred_element_type=jnp.float32,
    )


def plain_device(
    media,
    latents,
    frame_counts,
    time_index,
    valid,
    time_table,
    media_gain,
    latent_gain,
    ffn_gain,
    w_query,
    w_key,
    w_value,
    w_out,
    w_up,
    w_down,
    cotangent,
):
    frames = time_index.shape[0]
    patches = valid.shape[0] // frames
    latent_rows = latents.shape[0]
    model_width = latents.shape[1]
    head_size = model_width // H
    score_scale = head_size ** (-0.5)
    across = lax.axis_size("gx")
    column = lax.axis_index("gx")
    row_index = lax.axis_index("gy")
    frame_ends = jnp.cumsum(frame_counts[row_index])
    position = column * frames + jnp.arange(frames, dtype=jnp.int32)
    item_index = jnp.sum((frame_ends[None, :] <= position[:, None]).astype(jnp.int32), axis=1)
    item_onehot = (item_index[:, None] == jnp.arange(across, dtype=jnp.int32)[None, :]).astype(
        jnp.float32
    )
    (
        full_query,
        full_key,
        full_value,
        full_out,
        full_up,
        full_down,
        full_media_gain,
        full_latent_gain,
        full_ffn_gain,
        full_time,
    ) = (
        lax.all_gather(w_query, ("gx", "gy"), axis=0, tiled=True),
        lax.all_gather(w_key, ("gx", "gy"), axis=0, tiled=True),
        lax.all_gather(w_value, ("gx", "gy"), axis=0, tiled=True),
        lax.all_gather(w_out, ("gx", "gy"), axis=0, tiled=True),
        lax.all_gather(w_up, ("gx", "gy"), axis=0, tiled=True),
        lax.all_gather(w_down, ("gx", "gy"), axis=0, tiled=True),
        lax.all_gather(media_gain, ("gx", "gy"), axis=0, tiled=True),
        lax.all_gather(latent_gain, ("gx", "gy"), axis=0, tiled=True),
        lax.all_gather(ffn_gain, ("gx", "gy"), axis=0, tiled=True),
        lax.all_gather(time_table, ("gx", "gy"), axis=1, tiled=True),
    )
    time_onehot = (
        time_index[:, None] == jnp.arange(full_time.shape[0], dtype=jnp.int32)[None, :]
    ).astype(jnp.float32)
    time_rows = product(time_onehot.astype(jnp.bfloat16), full_time)
    media_in = (
        media.astype(jnp.float32).reshape(frames, patches, model_width) + time_rows[:, None, :]
    ).reshape(-1, model_width)
    media_normed = layer_norm(media_in, full_media_gain.astype(jnp.float32)).astype(jnp.bfloat16)
    key_heads = (
        product(media_normed, full_key).astype(jnp.bfloat16).reshape(frames, patches, H, head_size)
    )
    value_heads = (
        product(media_normed, full_value)
        .astype(jnp.bfloat16)
        .reshape(frames, patches, H, head_size)
    )
    latent_in = latents.astype(jnp.float32)
    latent_normed = layer_norm(latent_in, full_latent_gain.astype(jnp.float32)).astype(jnp.bfloat16)
    own_query = product(latent_normed, full_query).astype(jnp.bfloat16)
    own_key = product(latent_normed, full_key).astype(jnp.bfloat16)
    own_value = product(latent_normed, full_value).astype(jnp.bfloat16)
    valid_total = lax.psum(jnp.sum(valid.astype(jnp.float32)), ("gx", "gy"))
    coefficient = ENTROPY_WEIGHT * (valid.shape[0] * lax.axis_size(("gx", "gy"))) / valid_total
    query_table = lax.all_gather(own_query, "gx", axis=0, tiled=True)
    picked = query_table.reshape(-1, latent_rows, H, head_size)[item_index]
    media_score = (
        jnp.einsum("flhd,fphd->flhp", picked, key_heads, preferred_element_type=jnp.float32)
        * score_scale
    )
    valid_mask = valid.reshape(frames, 1, 1, patches) > 0
    media_expo = jnp.where(valid_mask, jnp.exp(media_score), 0.0)
    expo_low = media_expo.astype(jnp.bfloat16)
    media_total = jnp.sum(media_expo, axis=-1)
    media_moment = jnp.sum(media_expo * media_score, axis=-1)
    media_weighted = jnp.einsum(
        "flhp,fphd->flhd", expo_low, value_heads, preferred_element_type=jnp.float32
    )
    dense_weighted = collect(item_onehot, media_weighted.reshape(frames, -1)).reshape(
        -1, model_width
    )
    dense_total = collect(item_onehot, media_total.reshape(frames, -1)).reshape(-1, H)
    dense_moment = collect(item_onehot, media_moment.reshape(frames, -1)).reshape(-1, H)
    got_weighted, got_total, got_moment = (
        lax.psum_scatter(dense_weighted, "gx", scatter_dimension=0, tiled=True),
        lax.psum_scatter(dense_total, "gx", scatter_dimension=0, tiled=True),
        lax.psum_scatter(dense_moment, "gx", scatter_dimension=0, tiled=True),
    )
    query_head_count = own_query.reshape(latent_rows, H, head_size)
    latent_key_rows = own_key.reshape(latent_rows, H, head_size)
    latent_value_rows = own_value.reshape(latent_rows, H, head_size)
    latent_score = (
        jnp.einsum(
            "uer,zer->uez", query_head_count, latent_key_rows, preferred_element_type=jnp.float32
        )
        * score_scale
    )
    latent_expo = jnp.exp(latent_score)
    latent_reduced_precision = latent_expo.astype(jnp.bfloat16)
    weighted = got_weighted.reshape(latent_rows, H, head_size) + jnp.einsum(
        "nwr,rwb->nwb",
        latent_reduced_precision,
        latent_value_rows,
        preferred_element_type=jnp.float32,
    )
    totals = got_total + jnp.sum(latent_expo, axis=-1)
    moment = got_moment + jnp.sum(latent_expo * latent_score, axis=-1)
    attention = weighted / totals[..., None]
    attn_low = attention.reshape(latent_rows, model_width).astype(jnp.bfloat16)
    middle = latent_in + product(attn_low, full_out)
    ffn_normed = layer_norm(middle, full_ffn_gain.astype(jnp.float32)).astype(jnp.bfloat16)
    up_rows = product(ffn_normed, full_up)
    hidden = jax.nn.gelu(up_rows, approximate=False).astype(jnp.bfloat16)
    new_latents = (middle + product(hidden, full_down)).astype(jnp.bfloat16)
    (
        back_query,
        back_key,
        back_value,
        back_out,
        back_up,
        back_down,
        back_media_gain,
        back_latent_gain,
        back_ffn_gain,
    ) = (
        lax.all_gather(w_query, ("gx", "gy"), axis=0, tiled=True),
        lax.all_gather(w_key, ("gx", "gy"), axis=0, tiled=True),
        lax.all_gather(w_value, ("gx", "gy"), axis=0, tiled=True),
        lax.all_gather(w_out, ("gx", "gy"), axis=0, tiled=True),
        lax.all_gather(w_up, ("gx", "gy"), axis=0, tiled=True),
        lax.all_gather(w_down, ("gx", "gy"), axis=0, tiled=True),
        lax.all_gather(media_gain, ("gx", "gy"), axis=0, tiled=True),
        lax.all_gather(latent_gain, ("gx", "gy"), axis=0, tiled=True),
        lax.all_gather(ffn_gain, ("gx", "gy"), axis=0, tiled=True),
    )
    owned_latent, owned_attn, owned_ffn, owned_hidden = (
        lax.all_to_all(latent_normed, ("gx", "gy"), split_axis=1, concat_axis=0, tiled=True),
        lax.all_to_all(attn_low, ("gx", "gy"), split_axis=1, concat_axis=0, tiled=True),
        lax.all_to_all(ffn_normed, ("gx", "gy"), split_axis=1, concat_axis=0, tiled=True),
        lax.all_to_all(hidden, ("gx", "gy"), split_axis=1, concat_axis=0, tiled=True),
    )
    hidden_grad = inner_last(cotangent, back_down)
    gelu_pull = jax.vjp(partial(jax.nn.gelu, approximate=False), up_rows)[1]
    up_grad = gelu_pull(hidden_grad)[0].astype(jnp.bfloat16)
    ffn_normed_grad = inner_last(up_grad, back_up)
    ffn_pull = jax.vjp(layer_norm, middle, back_ffn_gain.astype(jnp.float32))[1]
    middle_part, grad_ffn_gain = ffn_pull(ffn_normed_grad)
    middle_grad = cotangent.astype(jnp.float32) + middle_part
    middle_low = middle_grad.astype(jnp.bfloat16)
    attn_grad = inner_last(middle_low, back_out).reshape(latent_rows, H, head_size)
    weighted_sum_gradient = (attn_grad / totals[..., None]).astype(jnp.bfloat16)
    slope_term = -coefficient / totals
    shift_term = (
        -jnp.sum(attn_grad * attention, axis=-1) / totals
        + coefficient * (1.0 / totals + moment / (totals * totals))
        + slope_term
    )
    latent_mix = jnp.einsum(
        "uer,zer->uez", weighted_sum_gradient, latent_value_rows, preferred_element_type=jnp.float32
    )
    latent_sgrad = latent_expo * (
        latent_mix + shift_term[..., None] + slope_term[..., None] * latent_score
    )
    latent_residual_gradient = (latent_sgrad * score_scale).astype(jnp.bfloat16)
    query_part = jnp.einsum(
        "nwr,rwb->nwb",
        latent_residual_gradient,
        latent_key_rows,
        preferred_element_type=jnp.float32,
    )
    own_key_grad = (
        jnp.einsum(
            "zry,zrj->yrj",
            latent_residual_gradient,
            query_head_count,
            preferred_element_type=jnp.float32,
        )
        .astype(jnp.bfloat16)
        .reshape(latent_rows, model_width)
    )
    own_value_grad = (
        jnp.einsum(
            "zry,zrj->yrj",
            latent_reduced_precision,
            weighted_sum_gradient,
            preferred_element_type=jnp.float32,
        )
        .astype(jnp.bfloat16)
        .reshape(latent_rows, model_width)
    )
    grad_table = lax.all_gather(
        weighted_sum_gradient.reshape(latent_rows, model_width), "gx", axis=0, tiled=True
    )
    shift_table, slope_table = (
        lax.all_gather(shift_term, "gx", axis=0, tiled=True),
        lax.all_gather(slope_term, "gx", axis=0, tiled=True),
    )
    picked_grad = grad_table.reshape(-1, latent_rows, H, head_size)[item_index]
    picked_shift = shift_table.reshape(-1, latent_rows, H)[item_index]
    picked_slope = slope_table.reshape(-1, latent_rows, H)[item_index]
    media_mix = jnp.einsum(
        "flhd,fphd->flhp", picked_grad, value_heads, preferred_element_type=jnp.float32
    )
    media_sgrad = media_expo * (
        media_mix + picked_shift[..., None] + picked_slope[..., None] * media_score
    )
    media_rgrad = (media_sgrad * score_scale).astype(jnp.bfloat16)
    query_terms = jnp.einsum(
        "flhp,fphd->flhd", media_rgrad, key_heads, preferred_element_type=jnp.float32
    )
    dense_query = collect(item_onehot, query_terms.reshape(frames, -1)).reshape(-1, model_width)
    got_query = lax.psum_scatter(
        dense_query.astype(jnp.bfloat16), "gx", scatter_dimension=0, tiled=True
    ).astype(jnp.float32)
    media_key_grad = (
        jnp.einsum("flhp,flhd->fphd", media_rgrad, picked, preferred_element_type=jnp.float32)
        .astype(jnp.bfloat16)
        .reshape(-1, model_width)
    )
    media_value_grad = (
        jnp.einsum("flhp,flhd->fphd", expo_low, picked_grad, preferred_element_type=jnp.float32)
        .astype(jnp.bfloat16)
        .reshape(-1, model_width)
    )
    grad_key = inner_first(media_normed, media_key_grad) + inner_first(latent_normed, own_key_grad)
    grad_value = inner_first(media_normed, media_value_grad) + inner_first(
        latent_normed, own_value_grad
    )
    media_normed_grad = inner_last(media_key_grad, back_key) + inner_last(
        media_value_grad, back_value
    )
    media_pull = jax.vjp(layer_norm, media_in, back_media_gain.astype(jnp.float32))[1]
    media_grad, grad_media_gain = media_pull(media_normed_grad)
    frame_sums = jnp.sum(media_grad.reshape(frames, patches, model_width), axis=1)
    grad_time = collect(time_onehot, frame_sums)
    query_grad = (
        (got_query.reshape(latent_rows, H, head_size) + query_part)
        .astype(jnp.bfloat16)
        .reshape(latent_rows, model_width)
    )
    latent_normed_grad = (
        inner_last(query_grad, back_query)
        + inner_last(own_key_grad, back_key)
        + inner_last(own_value_grad, back_value)
    )
    latent_pull = jax.vjp(layer_norm, latent_in, back_latent_gain.astype(jnp.float32))[1]
    latent_part, grad_latent_gain = latent_pull(latent_normed_grad)
    latents_grad = middle_grad + latent_part
    piece_query = lax.all_gather(query_grad, ("gx", "gy"), axis=0, tiled=True)
    piece_middle = lax.all_gather(middle_low, ("gx", "gy"), axis=0, tiled=True)
    piece_up = lax.all_gather(up_grad, ("gx", "gy"), axis=0, tiled=True)
    piece_cot = lax.all_gather(cotangent, ("gx", "gy"), axis=0, tiled=True)
    shard_query = inner_first(owned_latent, piece_query)
    shard_out = inner_first(owned_attn, piece_middle)
    shard_up = inner_first(owned_ffn, piece_up)
    shard_down = inner_first(owned_hidden, piece_cot)
    shard_grads = (
        lax.psum_scatter(grad_key, ("gx", "gy"), scatter_dimension=0, tiled=True),
        lax.psum_scatter(grad_value, ("gx", "gy"), scatter_dimension=0, tiled=True),
        lax.psum_scatter(grad_media_gain, ("gx", "gy"), scatter_dimension=0, tiled=True),
        lax.psum_scatter(grad_latent_gain, ("gx", "gy"), scatter_dimension=0, tiled=True),
        lax.psum_scatter(grad_ffn_gain, ("gx", "gy"), scatter_dimension=0, tiled=True),
        lax.psum_scatter(grad_time, ("gx", "gy"), scatter_dimension=1, tiled=True),
    )
    return (
        new_latents,
        media_grad,
        latents_grad,
        shard_grads[5],
        shard_grads[2],
        shard_grads[3],
        shard_grads[4],
        shard_query,
        shard_grads[0],
        shard_grads[1],
        shard_out,
        shard_up,
        shard_down,
    )


GROUP = 4


def mates_of(z, chip, core):
    mates = []
    for j in range(1, 16):
        there = (4 * z + chip + j) % 16
        mates.append((there // 4, 2 * (there % 4) + core))
    return mates


class GiveBack:
    def __init__(self, wires, up_part, down_part, scratch, up_out, down_out):
        self.wires, self.up_part, self.down_part = wires, up_part, down_part
        self.up_out, self.down_out = up_out, down_out
        self.up_near, self.down_near, self.up_got = scratch
        self.z, self.g, self.chip, self.core = here()
        self.places = up_places(self.z, self.chip)

    def first(self):
        near = (self.z, sibling(self.g))
        theirs = 1 - self.core
        self.up = self.wires.send(self.up_part.at[:, :, theirs], self.up_near, near)
        self.down = self.wires.send(self.down_part.at[theirs], self.down_near, near)

    def columns(self):
        self.up.wait_recv()
        core = self.core

        @pl.loop(0, LINES)
        def _(n):
            for q in range(PLANE):
                self.up_part[n, q, core] = self.up_part[n, q, core] + self.up_near[n, q]

        self.moved = []
        for there, _ in self.places:
            self.moved.append(
                self.wires.send(
                    self.up_part.at[there[0], there[1], core],
                    self.up_got.at[self.z, self.chip],
                    (there[0], 2 * there[1] + core),
                )
            )
        self.up_got[self.z, self.chip] = self.up_part[self.z, self.chip, core]

    def rows(self):
        self.down.wait_recv()
        rows = self.down_out.shape[0] // 8
        core = self.core

        @pl.loop(0, 8)
        def _(n):
            block = pl.ds(pl.multiple_of(n * rows, 8), rows)
            self.down_out[block] = self.down_part[core, block] + self.down_near[block]

    def finish(self):
        for copy in self.moved:
            copy.wait_recv()
        width = self.up_got.shape[-1]
        for n in range(LINES):
            for q in range(PLANE):
                first = (n * PLANE + q) * width
                self.up_out[:, first : first + width] = self.up_got[n, q].astype(F32)


GIVE_SEMS = 17


class Total:
    def __init__(self, wires, mine, out, sums, got):
        self.wires, self.out, self.sums, self.got = wires, out, sums, got
        self.z, self.g, _, _ = here()
        self.source = mine
        self.step = 0

    def push(self):
        sides = [sibling(self.g), along_x(self.g), along_y(self.g)]
        if self.step < 3:
            self.copies = [
                self.wires.send(self.source, self.got.at[self.step], (self.z, sides[self.step]))
            ]
        else:
            self.copies = [
                self.wires.send(self.source, self.got.at[3 + k], device)
                for k, device in enumerate(line_of(self.z, self.g))
            ]

    def pull(self):
        for copy in self.copies:
            copy.wait_recv()
        if self.step < 3:
            self.sums[self.step] = self.source[...] + self.got[self.step]
            self.source = self.sums.at[self.step]
            self.step += 1
        else:
            self.out[...] = self.source[...] + self.got[3] + self.got[4] + self.got[5]


def head_masks(rows, width, head_size):
    lane = lax.broadcasted_iota(jnp.int32, (rows, width), 1)
    return [(lane >= h * head_size) & (lane < (h + 1) * head_size) for h in range(GROUP)]


def stacked(block, masks):
    zero = jnp.zeros_like(block)
    return jnp.concatenate([jnp.where(mask, block, zero) for mask in masks], axis=0)


def unstacked(block, masks):
    rows = block.shape[0] // GROUP
    total = jnp.where(masks[0], block[:rows], 0.0)
    for h in range(1, GROUP):
        total = jnp.where(masks[h], block[h * rows : (h + 1) * rows], total)
    return total


def dot_last(a, b):
    return lax.dot_general(a, b, (((1,), (1,)), ((), ())), preferred_element_type=F32)


def dot_first(a, b):
    return lax.dot_general(a, b, (((0,), (0,)), ((), ())), preferred_element_type=F32)


def spread_heads(columns, first, masks):
    out = jnp.where(masks[0], columns[:, first : first + 1], 0.0)
    for h in range(1, GROUP):
        out = jnp.where(masks[h], columns[:, first + h : first + h + 1], out)
    return out


def attend(queries, keys, values, valid, scale, masks):
    rows = queries.shape[0]
    score = dot_last(stacked(queries, masks), keys) * scale
    expo = jnp.exp(score)
    if valid is not None:
        expo = jnp.where(valid > 0, expo, 0.0)
    totals = jnp.sum(expo, axis=1, keepdims=True)
    moments = jnp.sum(expo * score, axis=1, keepdims=True)
    weighted = jnp.dot(expo.astype(BF16), values, preferred_element_type=F32)
    heads = [(totals[h * rows : (h + 1) * rows], moments[h * rows : (h + 1) * rows]) for h in range(GROUP)]
    return unstacked(weighted, masks), heads


def pack_rows(terms):
    part = terms.shape[0] // 4
    out = terms[:part]
    for k in range(1, 4):
        out = out + pltpu.roll(terms[k * part : (k + 1) * part], 32 * k, 1)
    return out


def unpack_rows(packed):
    turned = [pltpu.roll(packed, 128 - 32 * k, 1) for k in range(1, 4)]
    return jnp.concatenate([packed] + turned, axis=0)


def put_heads(heads, group, lane):
    out = jnp.zeros(lane.shape, F32)
    for h, (total, moment) in enumerate(heads):
        out = jnp.where(lane == group * GROUP + h, total, out)
        out = jnp.where(lane == H + group * GROUP + h, moment, out)
    return out


def assemble(smalls, out):
    count, rows, lanes = smalls.shape
    shard = out.shape[1] // count
    block = 8
    row = lax.broadcasted_iota(jnp.int32, (block * lanes, block * shard), 0)
    col = lax.broadcasted_iota(jnp.int32, (block * lanes, block * shard), 1)
    lane = row % lanes
    chosen = ((row // lanes) * shard + lane == col) & (lane < shard)
    place = jnp.where(chosen, 1.0, 0.0).astype(BF16)
    for n in range(count // block):
        pieces = jnp.concatenate([smalls[n * block + d] for d in range(block)], axis=1)
        out[:, n * block * shard : (n + 1) * block * shard] = jnp.dot(
            pieces.astype(BF16), place, preferred_element_type=F32
        )


def up_places(z, chip):
    places = []
    for dz in range(LINES):
        for dx, dy in ((0, 0), (1, 0), (0, 1), (1, 1)):
            if dz or dx or dy:
                x, y = chip % 2, chip // 2
                there = (y + dy) % 2 * 2 + (x + dx) % 2
                places.append(((turn(z, dz), there), (turn(z, LINES - dz) if dz else z, there)))
    return places


def shares(counts_ref, z, g, frame, frames, items):
    position = z * frames + frame
    end, slot = 0, 0
    for item in range(items):
        end = end + counts_ref[g, item]
        slot = slot + jnp.where(end <= position, 1, 0)
    return [jnp.where(slot == item, 1.0, 0.0) for item in range(items)]


def put_times(out, tables, times_ref, frames):
    for frame in range(frames):
        row = jnp.zeros((1, out.shape[1]), F32)
        for t in range(8):
            row = row + jnp.where(times_ref[frame] == t, 1.0, 0.0) * tables[t : t + 1]
        out[frame : frame + 1] = row


def opening_kernel(scale, *refs):
    (
        time_table_ref,
        media_gain_ref,
        latent_gain_ref,
        ffn_gain_ref,
        key_shard,
        value_shard,
        query_shard,
        out_shard,
        latents_ref,
        up_ref,
        down_ref,
        cot_ref,
        media_ref,
        valid_ref,
        counts_ref,
        times_ref,
        tables_out,
        counts_out,
        key_weight_out,
        value_weight_out,
        query_weight_out,
        out_weight_out,
        up_out,
        down_out,
        cot_out,
        normed_out,
        keys_out,
        values_out,
        table_out,
        line_normed_out,
        got_weighted,
        got_stats,
        own_weighted,
        own_stats,
        send_sems,
        recv_sems,
        local_sems,
        up_own,
        small_ref,
        smalls,
        key_weight,
        value_weight,
        query_weight,
        line_latents,
        line_normed,
        normed,
        keys,
        values,
        own_table,
        table,
        time_rows,
        sums,
        weighted,
        stats,
        packed,
    ) = refs
    z, g, chip, core = here()
    here_chip = 4 * z + chip
    me = 2 * here_chip + core
    items, rows, width = line_latents.shape
    frames, _, patches = valid_ref.shape
    shard = key_shard.shape[0]
    span = width // (H // GROUP)
    up_width = up_out.shape[-1]
    near = (z, sibling(g))
    places = up_places(z, chip)
    greet([(there[0], 2 * there[1] + core) for there, _ in places] + [near])
    wires = Wires(send_sems, recv_sems)
    masks = head_masks(rows, span, span // GROUP)
    lane = lax.broadcasted_iota(jnp.int32, (rows, 128), 1)
    local = []
    small_ref[...] = jnp.zeros_like(small_ref)
    for place, source in (
        (slice(0, 8), time_table_ref),
        (slice(8, 9), media_gain_ref),
        (slice(9, 10), latent_gain_ref),
        (slice(10, 11), ffn_gain_ref),
    ):
        small_ref[place, :shard] = source[...].astype(F32)
    found = valid_ref[0].astype(F32)
    for n in range(1, frames):
        found = found + valid_ref[n].astype(F32)
    small_ref[11:12] = jnp.sum(found, axis=1, keepdims=True) + jnp.zeros((1, 128), F32)

    def keep(source, target):
        copy = pltpu.make_async_copy(source, target, local_sems.at[len(local)])
        copy.start()
        local.append(copy)
        return copy

    def rows_of(ref):
        return lambda zz, gg: ref.at[pl.ds(pl.multiple_of((zz * 8 + gg) * shard, 16), shard)]

    def piece(place):
        return up_ref.at[:, pl.ds(pl.multiple_of((4 * place[0] + place[1]) * up_width, 128), up_width)]

    def whole(source, slot):
        return Spread(wires, source, slot, columns_half, True), keep(source, slot(z, g))

    def small_slot(zz, gg):
        return smalls.at[zz * 8 + gg]

    small = Spread(wires, small_ref, small_slot, rows_half, True)
    small_kept = keep(small_ref, small_slot(z, g))
    key, key_kept = whole(key_shard, rows_of(key_weight))
    value, value_kept = whole(value_shard, rows_of(value_weight))
    query = Spread(wires, query_shard, rows_of(query_weight), rows_parts, True, True)
    query_kept = keep(piece_of(query_shard, z), rows_of(query_weight)(z, g))
    query_line = Line(wires, own_table, lambda zz: table.at[zz])
    out, out_kept = whole(out_shard, rows_of(out_weight_out))
    cot = Spread(wires, cot_ref, lambda zz, gg: cot_out.at[zz * 4 + gg // 2], columns_half, False)
    line = Line(wires, latents_ref, lambda zz: line_latents.at[zz])
    exchange = Exchange(
        wires,
        [(weighted, got_weighted), (packed, got_stats)],
    )
    line_kept = keep(latents_ref, line_latents.at[z])
    up_load = keep(piece((z, chip)), up_own)
    late = [
        out_kept,
        keep(cot_ref, cot_out.at[here_chip]),
        keep(down_ref, down_out.at[core]),
    ]
    prompt = len(local)
    moved, given, down = [], [], []
    chunk = 32

    def normalise(first, last):
        @pl.loop(first, last)
        def _(n):
            block = pl.ds(pl.multiple_of(n * chunk, chunk), chunk)
            frame = n // (patches // chunk)
            row = media_ref[block].astype(F32) + time_rows[pl.ds(frame, 1)]
            normed[block] = layer_norm(row, tables_out[8:9]).astype(BF16)

    def normalise_latents():
        gain = tables_out[9:10]
        line_kept.wait()
        for item in range(items):

            @pl.loop(0, rows // chunk)
            def _(n):
                block = pl.ds(pl.multiple_of(n * chunk, chunk), chunk)
                row = line_latents[item, block].astype(F32)
                line_normed[item, block] = layer_norm(row, gain).astype(BF16)

        normed[frames * patches :] = line_normed[z]

    def tabulate():
        small_kept.wait()
        assemble(smalls, tables_out)
        counts = smalls[0, 8:]
        for n in range(1, smalls.shape[0]):
            counts = counts + smalls[n, 8:]
        counts_out[...] = counts
        put_times(time_rows, tables_out, times_ref, frames)

    def project(left, weight, out, first):
        @pl.loop(first, first + 2)
        def _(n):
            cols = pl.ds(pl.multiple_of(n * span, 128), span)
            out[:, cols] = jnp.dot(
                left[...], weight[:, cols], preferred_element_type=F32
            ).astype(BF16)

    def project_keys(first):
        if first == 0:
            key_kept.wait()
            keep(key_weight, key_weight_out)
            keep(normed, normed_out)
        project(normed, key_weight, keys, first)
        if first > 0:
            keep(keys, keys_out)

    def project_values(first):
        if first == 0:
            value_kept.wait()
            keep(value_weight, value_weight_out)
        project(normed, value_weight, values, first)
        if first > 0:
            keep(values, values_out)

    def project_queries():
        query_kept.wait()
        keep(query_weight, query_weight_out)
        for item in range(items):
            own_table[item] = jnp.dot(
                line_normed[item], query_weight[...], preferred_element_type=F32
            ).astype(BF16)
        table[z] = own_table[...]
        query_line.first()

    def attend_own():
        keep(table, table_out)
        keep(line_normed, line_normed_out)
        sums[...] = jnp.zeros_like(sums)
        stats[...] = jnp.zeros_like(stats)
        last = slice(frames * patches, frames * patches + rows)
        own = jnp.zeros((rows, 128), F32)
        for group in range(H // GROUP):
            cols = slice(group * span, (group + 1) * span)
            part, heads = attend(
                table[group, z], keys[last, cols], values[last, cols], None, scale, masks
            )
            own_weighted[:, cols] = part
            own = own + put_heads(heads, group, lane)
        own_stats[...] = own

    def attend_frames(first, last):
        @pl.loop(first, last)
        def _(frame):
            share = shares(counts_ref, z, g, frame, frames, items)
            block = pl.ds(pl.multiple_of(frame * patches, patches), patches)
            valid = valid_ref[frame]
            found = jnp.zeros((rows, 128), F32)
            for group in range(H // GROUP):
                cols = slice(group * span, (group + 1) * span)
                chosen = share[0] * table[group, 0].astype(F32)
                for item in range(1, items):
                    chosen = chosen + share[item] * table[group, item].astype(F32)
                part, heads = attend(
                    chosen.astype(BF16), keys[block, cols], values[block, cols], valid, scale, masks
                )
                found = found + put_heads(heads, group, lane)
                for item in range(items):
                    sums[item, :, cols] += share[item] * part
            for item in range(items):
                stats[item] += share[item] * found

    def down_first():
        down.append(wires.send(down_ref, down_out.at[core], near))

    def up_first():
        up_load.wait()
        keep(up_own, up_out.at[me])
        given.append(wires.send(up_own, up_out.at[me], near))
        for there, _ in places:
            moved.append(
                wires.send(piece(there), up_out.at[me], (there[0], 2 * there[1] + core))
            )

    def up_last():
        for n, (_, origin) in enumerate(places):
            moved[n].wait_recv()
            held = up_out.at[2 * (4 * origin[0] + origin[1]) + core]
            given.append(wires.send(held, held, near))
        for copy in given:
            copy.wait_recv()

    def sums_first():
        weighted[...] = sums[...].astype(BF16)
        for item in range(items):
            packed[item] = pack_rows(stats[item])
        exchange.first()

    small.first()
    query.first()
    value.first()
    key.first()
    query.column(0)
    small.column(0)
    small.column(1)
    small.column(2)
    query.column(1)
    down_first()
    value.column(0)
    small.corner_x(0)
    small.corner_y(2)
    small.corner_y(3)
    query.corner_y(2)
    value.column(1)
    small.corner_x(1)
    key.column(0)
    small.corner_y(0)
    small.corner_y(1)
    value.corner_x(1)
    small.corner_x(3)
    small.corner_x(2)
    value.corner_y(2)
    value.corner_y(1)
    key.column(1)
    line.first()
    query.corner_x(0)
    query.corner_x(2)
    value.corner_y(0)
    query.corner_y(0)
    small.last(1)
    query.column(2)
    value.column(2)
    small.last(3)
    query.corner_x(1)
    small.last(0)
    small.last(2)
    query.corner_y(1)
    key.corner_x(2)
    small.finish()
    value.corner_x(0)
    query.corner_x(3)
    query.corner_y(3)
    key.corner_x(1)
    line.take(0)
    cot.first()
    tabulate()
    line.take(1)
    key.corner_y(1)
    value.corner_x(3)
    value.corner_x(2)
    query.last(2)
    normalise(0, 8)
    key.corner_y(2)
    value.last(0)
    query.last(0)
    query.last(1)
    value.corner_y(3)
    key.column(2)
    value.last(1)
    key.corner_y(0)
    normalise(8, 16)
    query.last(3)
    line.take(2)
    key.corner_x(0)
    cot.corner_y(0)
    normalise_latents()
    cot.column(0)
    key.last(1)
    value.last(3)
    cot.corner_x(0)
    value.last(2)
    query.finish()
    project_queries()
    value.finish()
    key.corner_x(3)
    cot.column(1)
    project_values(0)
    key.last(2)
    key.corner_y(3)
    out.first()
    cot.corner_y(1)
    up_first()
    project_values(2)
    cot.column(2)
    query_line.take(0)
    key.last(0)
    key.last(3)
    cot.corner_x(1)
    key.finish()
    project_keys(0)
    out.column(0)
    query_line.take(1)
    out.column(1)
    out.corner_x(0)
    cot.last(0)
    out.corner_y(0)
    project_keys(2)
    query_line.take(2)
    attend_own()
    attend_frames(0, 2)
    attend_frames(2, 4)
    out.column(2)
    cot.corner_x(2)
    out.corner_x(1)
    out.corner_y(1)
    cot.corner_y(3)
    sums_first()
    cot.corner_x(3)
    out.corner_y(3)
    out.corner_x(2)
    down[0].wait_recv()
    out.last(0)
    out.corner_x(3)
    out.corner_y(2)
    cot.last(3)
    up_last()
    cot.last(1)
    cot.corner_y(2)
    out.last(1)
    out.last(2)
    out.last(3)
    cot.last(2)
    out.finish()
    exchange.finish()
    for copy in late + local[prompt:]:
        copy.wait()
    wires.drain()


def opening(scale, small, weights, latents, w_up, w_down, cotangent, media, valid, counts, times):
    rows, width = latents.shape
    shard = weights[0].shape[0]
    up_rows, up_width = w_up.shape
    all_rows = media.shape[0] + rows
    wires = 5 * spread_sems(True) + spread_sems(False) + 2 * LINE_SEMS + 31 + 1 + 2 * LINES
    span = width // LINES
    square = jax.ShapeDtypeStruct((width, width), BF16)
    table = jax.ShapeDtypeStruct((LINES, rows, width), BF16)
    keys = jax.ShapeDtypeStruct((all_rows, width), BF16)
    smem = pl.BlockSpec(memory_space=pltpu.SMEM)
    return pl.pallas_call(
        partial(opening_kernel, scale),
        out_shape=[
            jax.ShapeDtypeStruct((16, width), F32),
            jax.ShapeDtypeStruct((8, 128), F32),
            square,
            square,
            jax.ShapeDtypeStruct((width, span), BF16),
            square,
            jax.ShapeDtypeStruct((32, up_rows, up_width // 16), BF16),
            jax.ShapeDtypeStruct((2,) + w_down.shape, BF16),
            jax.ShapeDtypeStruct((16,) + cotangent.shape, BF16),
            keys,
            keys,
            keys,
            jax.ShapeDtypeStruct((LINES, LINES, rows, span), BF16),
            table,
            table,
            jax.ShapeDtypeStruct((LINES, rows // 4, 128), F32),
            jax.ShapeDtypeStruct((rows, width), F32),
            jax.ShapeDtypeStruct((rows, 128), F32),
        ],
        in_specs=[VMEM] * 8 + [LEFT] * 2 + [VMEM] * 4 + [smem] * 2,
        out_specs=[VMEM] * 2 + [LEFT] * 12 + [VMEM] * 4,
        scratch_shapes=[
            sems(wires),
            sems(wires),
            sems(24),
            pltpu.VMEM((up_rows, up_width // 16), BF16),
            pltpu.VMEM((16, 128), F32),
            pltpu.VMEM((32, 16, 128), F32),
            pltpu.VMEM((width, width), BF16),
            pltpu.VMEM((width, width), BF16),
            pltpu.VMEM((width, span), BF16),
            pltpu.VMEM((LINES, rows, width), BF16),
            pltpu.VMEM((LINES, rows, width), BF16),
            pltpu.VMEM((all_rows, width), BF16),
            pltpu.VMEM((all_rows, width), BF16),
            pltpu.VMEM((all_rows, width), BF16),
            pltpu.VMEM((LINES, rows, span), BF16),
            pltpu.VMEM((LINES, LINES, rows, span), BF16),
            pltpu.VMEM((8, width), F32),
            pltpu.VMEM((LINES, rows, width), F32),
            pltpu.VMEM((LINES, rows, width), BF16),
            pltpu.VMEM((LINES, rows, 128), F32),
            pltpu.VMEM((LINES, rows // 4, 128), F32),
        ],
        compiler_params=params(0),
        name="opening",
    )(*small, *weights, latents, w_up, w_down, cotangent, media, valid, counts, times)


def repel(queries, grads, keys, values, valid, shift, slope, scale, masks):
    query_stack = stacked(queries, masks)
    grad_stack = stacked(grads, masks)
    score = dot_last(query_stack, keys) * scale
    expo = jnp.exp(score)
    if valid is not None:
        expo = jnp.where(valid > 0, expo, 0.0)
    mix = dot_last(grad_stack, values)
    raw = (expo * (mix + shift + slope * score) * scale).astype(BF16)
    query_grad = unstacked(jnp.dot(raw, keys, preferred_element_type=F32), masks)
    key_grad = dot_first(raw, query_stack).astype(BF16)
    value_grad = dot_first(expo.astype(BF16), grad_stack).astype(BF16)
    return query_grad, key_grad, value_grad


def stacked_columns(terms, first):
    return jnp.concatenate([terms[:, first + h : first + h + 1] for h in range(GROUP)], axis=0)


def closing_kernel(scale, *refs):
    (
        table_ref,
        grad_ref,
        terms_ref,
        keys_ref,
        values_ref,
        normed_ref,
        valid_ref,
        attn_ref,
        low_ref,
        own_grad_ref,
        own_terms_ref,
        line_normed_ref,
        query_weight_ref,
        key_weight_ref,
        value_weight_ref,
        media_ref,
        tables_ref,
        latents_ref,
        middle_grad_ref,
        ffn_gain_ref,
        counts_ref,
        times_ref,
        media_grad_out,
        latents_grad_out,
        small_out,
        out_out,
        value_out,
        key_out,
        query_out,
        send_sems,
        recv_sems,
        local_sems,
        table,
        grads,
        keys,
        values,
        normed,
        key_grad,
        value_grad,
        weight_a,
        weight_b,
        sums,
        terms_query,
        got_query,
        query_grad,
        got_line,
        media_grad,
        latent_grad,
        small,
        small_sums,
        small_got,
        time_rows_ref,
        part_a,
        part_b,
        part_c,
        part_d,
        query_relay,
        line_relay,
        *fold,
    ) = refs
    z, g, _, core = here()
    items, rows, width = grads.shape
    frames, _, patches = valid_ref.shape
    media_rows = frames * patches
    shard = width // 32
    groups = H // GROUP
    span = width // groups
    masks = head_masks(rows, span, span // GROUP)
    greet(line_of(z, g) + sides_of(z, g, True))
    wires = Wires(send_sems, recv_sems)
    out = Fold(wires, part_a, True, fold[:FOLD], out_out)
    value = Fold(wires, part_b, True, fold[FOLD : 2 * FOLD], value_out)
    key = Fold(wires, part_c, True, fold[2 * FOLD : 3 * FOLD], key_out)
    query = FoldSplit(wires, part_d, True, fold[3 * FOLD :], query_out)
    total = Total(wires, small, small_out, small_sums, small_got)
    exchange = SumLine(wires, terms_query, got_query, query_relay)
    line_exchange = SumLine(wires, grads, got_line, line_relay)
    local = []

    def load(source, target):
        copy = pltpu.make_async_copy(source, target, local_sems.at[len(local)])
        copy.start()
        local.append(copy)
        return copy

    loads = [
        load(table_ref, table),
        load(grad_ref, grads),
        load(keys_ref, keys),
        load(values_ref, values),
    ]
    normed_load = load(normed_ref, normed)
    key_load = load(key_weight_ref, weight_a)
    value_load = load(value_weight_ref, weight_b)
    stored = []

    def weight_part(part, left, right, first, last):
        @pl.loop(first, last)
        def _(n):
            cols = pl.ds(pl.multiple_of(n * span, 128), span)
            block = dot_first(left[:, cols], right[...]).astype(BF16)
            part[n] = block.reshape(PLANE, 2, shard, width)

    def out_part():
        weight_part(part_a, attn_ref, low_ref, 0, LINES)
        out.start()

    def value_part(first):
        weight_part(part_b, normed, value_grad, first, first + 2)
        if first > 0:
            value.start()

    def key_part(first):
        weight_part(part_c, normed, key_grad, first, first + 2)
        if first > 0:
            key.start()

    def repel_own():
        for copy in loads:
            copy.wait()
        normed_load.wait()
        sums[...] = jnp.zeros_like(sums)
        own_terms = own_terms_ref[...]
        for group in range(groups):
            cols = slice(group * span, (group + 1) * span)
            (
                sums[group, z],
                key_grad[media_rows:, cols],
                value_grad[media_rows:, cols],
            ) = repel(
                table[group, z],
                own_grad_ref[:, cols],
                keys[media_rows:, cols],
                values[media_rows:, cols],
                None,
                stacked_columns(own_terms, group * GROUP),
                stacked_columns(own_terms, H + group * GROUP),
                scale,
                masks,
            )

    def repel_frames(first, last):
        @pl.loop(first, last)
        def _(frame):
            block = pl.ds(pl.multiple_of(frame * patches, patches), patches)
            valid = valid_ref[frame]
            share = shares(counts_ref, z, g, frame, frames, items)

            def pick(ref, cols):
                chosen = share[0] * ref[0, :, cols].astype(F32)
                for item in range(1, items):
                    chosen = chosen + share[item] * ref[item, :, cols].astype(F32)
                return chosen

            everything = slice(None)
            terms = unpack_rows(pick(terms_ref, everything))
            for group in range(groups):
                cols = slice(group * span, (group + 1) * span)
                query_part, key_grad[block, cols], value_grad[block, cols] = repel(
                    pick(table.at[group], everything).astype(BF16),
                    pick(grads, cols).astype(BF16),
                    keys[block, cols],
                    values[block, cols],
                    valid,
                    stacked_columns(terms, group * GROUP),
                    stacked_columns(terms, H + group * GROUP),
                    scale,
                    masks,
                )
                for item in range(items):
                    sums[group, item] += share[item] * query_part

    def queries_first():
        terms_query[...] = sums[...].astype(BF16)
        exchange.first()

    def media_product(n):
        if n == 0:
            key_load.wait()
            value_load.wait()
            small[...] = jnp.zeros_like(small)
            small[10:11] = ffn_gain_ref[...]
            put_times(time_rows_ref, tables_ref, times_ref, frames)
        if n == 2:
            stored[-1].wait()
        count = media_rows // 2
        block = slice(n // 2 * count, (n // 2 + 1) * count)

        @pl.loop(n % 2 * 2, n % 2 * 2 + 2)
        def _(t):
            cols = pl.ds(pl.multiple_of(t * span, 128), span)
            media_grad[:, cols] = dot_last(key_grad[block], weight_a[cols]) + dot_last(
                value_grad[block], weight_b[cols]
            )

    def media_pull(frame):
        count = media_rows // 2
        gain = tables_ref[8:9]
        chunk = 32
        f = frame % (frames // 2)
        moving = time_rows_ref[frame : frame + 1]

        def step(t, carry):
            gain_sum, row_sum = carry
            here_rows = pl.ds(pl.multiple_of(f * patches + t * chunk, chunk), chunk)
            there_rows = pl.ds(pl.multiple_of(frame * patches + t * chunk, chunk), chunk)
            row = media_ref[there_rows].astype(F32) + moving
            pulled, summand = norm_pull(row, gain, media_grad[here_rows])
            media_grad[here_rows] = pulled
            return (
                gain_sum + jnp.sum(summand, axis=0, keepdims=True),
                row_sum + jnp.sum(pulled, axis=0, keepdims=True),
            )

        zero = jnp.zeros((1, width), F32)
        gain_sum, row_sum = lax.fori_loop(0, patches // chunk, step, (zero, zero))
        small[8:9] += gain_sum
        for t in range(8):
            small[t : t + 1] += jnp.where(times_ref[frame] == t, 1.0, 0.0) * row_sum
        if f == frames // 2 - 1:
            first = frame // (frames // 2) * count
            stored.append(load(media_grad, media_grad_out.at[pl.ds(first, count)]))

    def latents_side():
        @pl.loop(0, groups)
        def _(t):
            cols = pl.ds(pl.multiple_of(t * span, 128), span)
            latent_grad[:, cols] = dot_last(key_grad[media_rows:], weight_a[cols]) + dot_last(
                value_grad[media_rows:], weight_b[cols]
            )

    def query_part():
        for item in range(items):
            found = got_query[0, item].astype(F32)
            for place in range(1, LINES):
                found = found + got_query[place, item].astype(F32)
            query_grad[item] = found.astype(BF16)
        grads_all = query_grad[...].reshape(items * rows, span)

        @pl.loop(0, LINES)
        def _(n):
            cols = pl.ds(pl.multiple_of(n * span, 128), span)
            left = line_normed_ref[:, :, cols].reshape(items * rows, span)
            block = dot_first(left, grads_all).astype(BF16)
            part_d[n] = block.reshape(PLANE, 2, shard, span)

        query.start()

    def line_first():
        for item in range(items):
            grads[item] = dot_last(query_grad[item], query_weight_ref[...]).astype(BF16)
        line_exchange.first()

    def latents_end():
        for place in range(LINES):
            latent_grad[...] += got_line[place].astype(F32)
        pulled, summand = norm_pull(
            latents_ref[...].astype(F32), tables_ref[9:10], latent_grad[...]
        )
        latents_grad_out[...] = middle_grad_ref[...] + pulled
        small[9:10] = jnp.sum(summand, axis=0, keepdims=True)
        total.push()

    def total_next():
        total.pull()
        total.push()

    out_part()
    repel_own()
    repel_frames(0, 2)
    repel_frames(2, 4)
    out.corner()
    queries_first()
    media_product(0)
    key_part(0)
    key_part(2)
    out.side_x()
    out.side_y()
    media_product(1)
    media_pull(0)
    exchange.relay()
    key.corner()
    value_part(0)
    value_part(2)
    media_pull(1)
    exchange.finish()
    query_part()
    line_first()
    value.corner()
    media_product(2)
    media_product(3)
    key.side_x()
    key.side_y()
    media_pull(2)
    value.side_x()
    out.line()
    line_exchange.relay()
    value.side_y()
    media_pull(3)
    key.line()
    out.relay()
    line_exchange.finish()
    key.relay()
    query.corner()
    latents_side()
    latents_end()
    value.line()
    total_next()
    out.finish()
    query.side_x()
    query.side_y()
    key.finish()
    value.relay()
    total_next()
    query.line()
    total_next()
    query.finish()
    value.finish()
    total.pull()
    stored[1].wait()
    wires.drain()


def closing(scale, *args):
    (table, grads, terms, keys, values, normed) = args[:6]
    media, latents = args[15], args[17]
    span = table.shape[-1]
    rows, width = latents.shape
    shard = width // 32
    wires = 4 * fold_sems(True) + 6 + 2 * LINES
    bf = [
        table.shape,
        grads.shape,
        keys.shape,
        keys.shape,
        keys.shape,
        keys.shape,
        keys.shape,
        (width, width),
        (width, width),
    ]
    part = pltpu.VMEM((LINES, PLANE, 2, shard, width), BF16)
    small = (16, width)
    scratch = [pltpu.VMEM(shape, BF16) for shape in bf] + [
        pltpu.VMEM(table.shape, F32),
        pltpu.VMEM(table.shape, BF16),
        pltpu.VMEM(table.shape, BF16),
        pltpu.VMEM(table.shape[1:], BF16),
        pltpu.VMEM(grads.shape, BF16),
        pltpu.VMEM((media.shape[0] // 2, width), F32),
        pltpu.VMEM((rows, width), F32),
        pltpu.VMEM(small, F32),
        pltpu.VMEM((3,) + small, F32),
        pltpu.VMEM((6,) + small, F32),
        pltpu.VMEM((8, width), F32),
        part,
        part,
        part,
        pltpu.VMEM((LINES, PLANE, 2, shard, span), BF16),
        pltpu.VMEM(table.shape[1:], BF16),
        pltpu.VMEM((rows, width), BF16),
    ]
    scratch += fold_scratch(shard, width, True) * 3 + fold_scratch(shard, span, True, True)
    smem = pl.BlockSpec(memory_space=pltpu.SMEM)
    return pl.pallas_call(
        partial(closing_kernel, scale),
        out_shape=[
            jax.ShapeDtypeStruct(media.shape, F32),
            jax.ShapeDtypeStruct(latents.shape, F32),
            jax.ShapeDtypeStruct(small, F32),
        ]
        + [jax.ShapeDtypeStruct((shard, width), F32)] * 4,
        in_specs=[LEFT, LEFT, VMEM, LEFT, LEFT, LEFT]
        + [VMEM] * 7
        + [LEFT] * 2
        + [VMEM] * 5
        + [smem] * 2,
        out_specs=[LEFT] + [VMEM] * 6,
        scratch_shapes=[sems(wires), sems(wires), sems(12)] + scratch,
        compiler_params=pltpu.CompilerParams(
            collective_id=3, has_side_effects=True, vmem_limit_bytes=67043328
        ),
        name="closing",
    )(*args)


def settle_kernel(
    weighted_ref,
    stats_ref,
    own_weighted_ref,
    own_stats_ref,
    out_ref,
    latents_ref,
    gain_ref,
    attention_ref,
    attn_ref,
    sums_ref,
    middle_ref,
    normed_ref,
    ready,
):
    rows, width = latents_ref.shape
    span = width // (H // GROUP)
    masks = head_masks(rows, span, span // GROUP)
    found = stats_ref[0]
    for n in range(1, stats_ref.shape[0]):
        found = found + stats_ref[n]
    stats = own_stats_ref[...] + unpack_rows(found)
    sums_ref[...] = stats
    for group in range(H // GROUP):
        cols = pl.ds(group * span, span)
        weighted = own_weighted_ref[:, cols]
        for n in range(weighted_ref.shape[0]):
            weighted = weighted + weighted_ref[n, :, cols].astype(F32)
        attention = weighted / spread_heads(stats, group * GROUP, masks)
        attention_ref[:, cols] = attention
        attn_ref[:, cols] = attention.astype(BF16)
    ready()
    middle = latents_ref[...].astype(F32) + jnp.dot(
        attn_ref[...], out_ref[...], preferred_element_type=F32
    )
    middle_ref[...] = middle
    normed_ref[...] = layer_norm(middle, gain_ref[...]).astype(BF16)


def norm_pull(rows, gain, grad):
    mean = jnp.mean(rows, axis=-1, keepdims=True)
    centred = rows - mean
    inverse = lax.rsqrt(jnp.mean(centred * centred, axis=-1, keepdims=True) + NORM_STABILIZER)
    xhat = centred * inverse
    t = grad * gain
    pulled = (
        t
        - jnp.mean(t, axis=-1, keepdims=True)
        - xhat * jnp.mean(t * xhat, axis=-1, keepdims=True)
    ) * inverse
    return pulled, grad * xhat


def unsettle_kernel(
    normed_grad_ref,
    middle_ref,
    gain_ref,
    cot_ref,
    out_ref,
    attention_ref,
    stats_ref,
    coef,
    middle_grad_ref,
    low_ref,
    gain_grad_ref,
    weighted_grad_ref,
    terms_ref,
    attn_grad,
):
    rows, width = middle_ref.shape
    span = width // (H // GROUP)
    masks = head_masks(rows, span, span // GROUP)
    pulled, summand = norm_pull(middle_ref[...], gain_ref[...], normed_grad_ref[...])
    gain_grad_ref[...] = jnp.sum(summand, axis=0, keepdims=True)
    middle_grad = cot_ref[...].astype(F32) + pulled
    middle_grad_ref[...] = middle_grad
    low_ref[...] = middle_grad.astype(BF16)
    attn_grad[...] = dot_last(low_ref[...], out_ref[...])
    stats = stats_ref[...]
    lane = lax.broadcasted_iota(jnp.int32, (rows, 128), 1)
    terms = jnp.zeros((rows, 128), F32)
    for group in range(H // GROUP):
        cols = pl.ds(group * span, span)
        grad = attn_grad[:, cols]
        first = group * GROUP
        weighted_grad_ref[:, cols] = (grad / spread_heads(stats, first, masks)).astype(BF16)
        along = grad * attention_ref[:, cols]
        for h in range(GROUP):
            inner = jnp.sum(jnp.where(masks[h], along, 0.0), axis=1, keepdims=True)
            total = stats[:, first + h : first + h + 1]
            moment = stats[:, H + first + h : H + first + h + 1]
            slope = -coef / total
            shift = -inner / total + coef * (1.0 / total + moment / (total * total)) + slope
            terms = jnp.where(lane == first + h, shift, terms)
            terms = jnp.where(lane == H + first + h, slope, terms)
    terms_ref[...] = terms


def gelu_parts(rows):
    below = 0.5 * (1.0 + lax.erf(rows * (0.5**0.5)))
    density = jnp.exp(-0.5 * rows * rows) * ((0.5 / jnp.pi) ** 0.5)
    return rows * below, below + rows * density


def middle_kernel(patches, *refs):
    (
        weighted_ref,
        stats_ref,
        own_weighted_ref,
        own_stats_ref,
        out_weight_ref,
        up_ref,
        down_ref,
        cot_rows_ref,
        latents_ref,
        tables_ref,
        cot_ref,
        counts_ref,
        attn_out,
        low_out,
        middle_grad_out,
        gain_grad_out,
        weighted_grad_out,
        terms_out,
        grad_table_out,
        terms_table_out,
        new_latents_out,
        up_grad_out,
        down_grad_out,
        send_sems,
        recv_sems,
        local_sems,
        out_weight,
        up_cols,
        down_rows,
        cot_rows,
        ffn_rows,
        attention,
        sums,
        middle,
        normed,
        hidden_grad,
        up_grad,
        hidden,
        normed_part,
        down_part,
        up_grad_part,
        down_grad_part,
        up_near,
        down_near,
        up_got,
        normed_grad,
        down_sum,
        attn_grad,
        packed,
        *fold,
    ) = refs
    z, g, chip, core = here()
    rows, width = latents_ref.shape
    span = up_cols.shape[1]
    shard = width // 32
    block_rows = PLANE * rows
    near = (z, sibling(g))
    gain_ref = tables_ref.at[10:11]
    greet([(there[0], 2 * there[1] + core) for there, _ in up_places(z, chip)] + [near])
    wires = Wires(send_sems, recv_sems)
    gather = Spread(
        wires, normed, lambda zz, gg: ffn_rows.at[zz, gg // 2], columns_half, False
    )
    back = FoldSteps(wires, normed_part, fold[:FOLD], normed_grad)
    down = Fold(wires, down_part, False, fold[FOLD:], down_sum)
    give = GiveBack(
        wires,
        up_grad_part,
        down_grad_part,
        (up_near, down_near, up_got),
        up_grad_out,
        down_grad_out,
    )
    grad_line = Line(wires, weighted_grad_out, lambda zz: grad_table_out.at[zz])
    terms_line = Line(wires, packed, lambda zz: terms_table_out.at[zz])
    loads = [
        pltpu.make_async_copy(source, target, local_sems.at[n])
        for n, (source, target) in enumerate(
            (
                (out_weight_ref, out_weight),
                (down_ref, down_rows),
                (cot_rows_ref, cot_rows),
                (up_ref, up_cols),
            )
        )
    ]
    for load in loads:
        load.start()

    def settle():
        settle_kernel(
            weighted_ref,
            stats_ref,
            own_weighted_ref,
            own_stats_ref,
            out_weight,
            latents_ref,
            gain_ref,
            attention,
            attn_out,
            sums,
            middle,
            normed,
            loads[0].wait,
        )
        ffn_rows[z, chip] = normed[...]

    def hidden_back():
        loads[1].wait()
        loads[2].wait()
        loads[3].wait()

        @pl.loop(0, LINES)
        def _(n):
            block = cot_rows[n].reshape(block_rows, width)
            hidden_grad[n] = dot_last(block, down_rows[...])

    def group(n):
        place = gather.zs[n]
        block = ffn_rows[place].reshape(block_rows, width)
        value, slope = gelu_parts(jnp.dot(block, up_cols[...], preferred_element_type=F32))
        hidden[place] = value.astype(BF16)
        grad = (hidden_grad[place] * slope).astype(BF16)
        up_grad[place] = grad
        part = dot_last(grad, up_cols[...]).astype(BF16)
        normed_part[place] = part.reshape(PLANE, rows, width)

    def down_product():
        @pl.loop(0, LINES)
        def _(n):
            part = jnp.dot(hidden[n], down_rows[...], preferred_element_type=F32)
            down_part[n] = part.astype(BF16).reshape(PLANE, rows, width)

    def up_gradient():
        grads = up_grad[...].reshape(LINES * block_rows, span)

        @pl.loop(0, LINES)
        def _(n):
            cols = pl.ds(pl.multiple_of(n * span, 128), span)
            block = ffn_rows[:, :, :, cols].reshape(LINES * block_rows, span)
            part = dot_first(block, grads).astype(BF16)
            up_grad_part[n] = part.reshape(PLANE, 2, shard, span)

    def down_gradient():
        rows_up = hidden[...].reshape(LINES * block_rows, span)

        @pl.loop(0, LINES)
        def _(n):
            cols = pl.ds(pl.multiple_of(n * span, 128), span)
            block = cot_rows[:, :, :, cols].reshape(LINES * block_rows, span)
            part = dot_first(rows_up, block)
            down_grad_part[:, :, cols] = part.reshape(2, span // 2, span)

    def unsettle():
        unsettle_kernel(
            normed_grad,
            middle,
            gain_ref,
            cot_ref,
            out_weight,
            attention,
            sums,
            ENTROPY_WEIGHT * patches / counts_ref[3:4, 0:1],
            middle_grad_out,
            low_out,
            gain_grad_out,
            weighted_grad_out,
            terms_out,
            attn_grad,
        )
        grad_table_out[z] = weighted_grad_out[...]
        packed[...] = pack_rows(terms_out[...])
        terms_table_out[z] = packed[...]

    def new_rows():
        new_latents_out[...] = (middle[...] + down_sum[...]).astype(BF16)

    settle()
    gather.first()
    gather.corner_x(0)
    gather.corner_y(0)
    gather.column(0)
    gather.column(1)
    hidden_back()
    gather.last(0)
    group(0)
    back.corner(0)
    gather.corner_x(1)
    gather.corner_y(1)
    gather.column(2)
    gather.corner_x(2)
    gather.corner_y(2)
    gather.last(1)
    group(1)
    back.corner(1)
    gather.corner_x(3)
    back.side_y(0)
    gather.corner_y(3)
    back.side_x(0)
    gather.last(2)
    group(2)
    back.corner(2)
    gather.last(3)
    group(3)
    back.corner(3)
    back.side_x(1)
    back.side_y(1)
    back.line(0)
    down_gradient()
    up_gradient()
    give.first()
    back.side_x(2)
    back.side_y(2)
    back.side_y(3)
    down_product()
    down.start()
    back.side_x(3)
    down.corner()
    give.columns()
    back.line(2)
    back.line(3)
    give.rows()
    back.line(1)
    down.side_x()
    down.side_y()
    back.relay()
    back.finish()
    unsettle()
    grad_line.first()
    grad_line.take(0)
    terms_line.first()
    down.line()
    terms_line.take(0)
    terms_line.take(1)
    grad_line.take(1)
    grad_line.take(2)
    terms_line.take(2)
    down.relay()
    give.finish()
    down.finish()
    new_rows()
    wires.drain()


def middle_part(
    patches,
    weighted,
    stats,
    own_weighted,
    own_stats,
    w_out,
    up_cols,
    down_rows,
    cot_rows,
    latents,
    tables,
    cot,
    counts,
):
    rows, width = latents.shape
    span = up_cols.shape[1]
    shard = width // 32
    plane = (LINES, PLANE, rows, width)
    block = (LINES, PLANE * rows, span)
    wires = spread_sems(False) + STEP_SEMS + fold_sems(False) + GIVE_SEMS + 2 * LINE_SEMS
    own = (rows, width)
    terms = own_stats.shape
    bf = [
        w_out.shape,
        up_cols.shape,
        down_rows.shape,
        plane,
        plane,
    ]
    scratch = [pltpu.VMEM(shape, BF16) for shape in bf] + [
        pltpu.VMEM(own, F32),
        pltpu.VMEM(terms, F32),
        pltpu.VMEM(own, F32),
        pltpu.VMEM(own, BF16),
        pltpu.VMEM(block, F32),
        pltpu.VMEM(block, BF16),
        pltpu.VMEM(block, BF16),
        pltpu.VMEM(plane, BF16),
        pltpu.VMEM(plane, BF16),
        pltpu.VMEM((LINES, PLANE, 2, shard, span), BF16),
        pltpu.VMEM((2, span // 2, width), F32),
        pltpu.VMEM((LINES, PLANE, shard, span), BF16),
        pltpu.VMEM((span // 2, width), F32),
        pltpu.VMEM((LINES, PLANE, shard, span), BF16),
        pltpu.VMEM(own, F32),
        pltpu.VMEM(own, F32),
        pltpu.VMEM(own, F32),
        pltpu.VMEM((rows // 4, 128), F32),
    ]
    scratch += fold_scratch(rows, width, False) * 2
    return pl.pallas_call(
        partial(middle_kernel, patches),
        out_shape=[
            jax.ShapeDtypeStruct(own, BF16),
            jax.ShapeDtypeStruct(own, BF16),
            jax.ShapeDtypeStruct(own, F32),
            jax.ShapeDtypeStruct((1, width), F32),
            jax.ShapeDtypeStruct(own, BF16),
            jax.ShapeDtypeStruct(terms, F32),
            jax.ShapeDtypeStruct((LINES,) + own, BF16),
            jax.ShapeDtypeStruct((LINES, rows // 4, 128), F32),
            jax.ShapeDtypeStruct(own, BF16),
            jax.ShapeDtypeStruct((shard, span * 16), F32),
            jax.ShapeDtypeStruct((span // 2, width), F32),
        ],
        in_specs=[VMEM] * 4 + [LEFT] * 4 + [VMEM] * 4,
        out_specs=[VMEM] * 11,
        scratch_shapes=[sems(wires), sems(wires), sems(4)] + scratch,
        compiler_params=params(1),
        name="middle",
    )(
        weighted,
        stats,
        own_weighted,
        own_stats,
        w_out,
        up_cols,
        down_rows,
        cot_rows.reshape(plane),
        latents,
        tables,
        cot,
        counts,
    )


def ending_kernel(shard, *refs):
    count = (len(refs) - 6) // 3
    sources, small = refs[:count], refs[count]
    outs = refs[count + 1 : 2 * count + 1]
    small_outs = refs[2 * count + 1 : 2 * count + 5]
    held, arrive = refs[2 * count + 5 : 3 * count + 5], refs[3 * count + 5]
    loads, stores = [], []
    for n in range(count):
        loads.append(pltpu.make_async_copy(sources[n], held[n], arrive.at[n]))
        stores.append(pltpu.make_async_copy(held[n], outs[n], arrive.at[n]))
    largest = sorted(range(count), key=lambda n: -sources[n].shape[0] * sources[n].shape[1])
    for n in largest:
        loads[n].start()
    z, g, _, _ = here()
    width = small.shape[1]
    turned = pltpu.roll(small[...], width - (8 * z + g) * shard, 1)
    small_outs[0][...] = turned[:8, :shard]
    for n in range(3):
        small_outs[n + 1][...] = turned[8 + n : 9 + n, :shard]
    for n in largest:
        loads[n].wait()
        stores[n].start()
    for n in range(count):
        stores[n].wait()


def ending(results, small, shard):
    count = len(results)
    return pl.pallas_call(
        partial(ending_kernel, shard),
        out_shape=[jax.ShapeDtypeStruct(r.shape, r.dtype) for r in results]
        + [jax.ShapeDtypeStruct((8, shard), F32)]
        + [jax.ShapeDtypeStruct((1, shard), F32)] * 3,
        in_specs=[LEFT] * count + [VMEM],
        out_specs=[LEFT] * count + [VMEM] * 4,
        scratch_shapes=[pltpu.VMEM(r.shape, r.dtype) for r in results] + [sems(count)],
        name="ending",
    )(*results, small)


def per_device(
    media,
    latents,
    frame_counts,
    time_index,
    valid,
    time_table,
    media_gain,
    latent_gain,
    ffn_gain,
    w_query,
    w_key,
    w_value,
    w_out,
    w_up,
    w_down,
    cotangent,
):
    frames = time_index.shape[0]
    patches = valid.shape[0] // frames
    width = latents.shape[1]
    shard = media_gain.shape[0]
    scale = (width // H) ** (-0.5)
    valid_rows = valid.reshape(frames, 1, patches)
    (
        tables,
        counts,
        full_key,
        full_value,
        full_query,
        full_out,
        up_cols,
        down_rows,
        cot_rows,
        normed,
        keys,
        values,
        table,
        line_normed,
        got_weighted,
        got_stats,
        own_weighted,
        own_stats,
    ) = opening(
        scale,
        (
            time_table,
            media_gain.reshape(1, shard),
            latent_gain.reshape(1, shard),
            ffn_gain.reshape(1, shard),
        ),
        (w_key, w_value, w_query, w_out),
        latents,
        w_up,
        w_down,
        cotangent,
        media,
        valid_rows,
        frame_counts,
        time_index,
    )
    (
        attn_low,
        middle_low,
        middle_grad,
        grad_ffn_gain,
        weighted_grad,
        terms,
        grad_table,
        terms_table,
        new_latents,
        shard_up,
        shard_down,
    ) = middle_part(
        valid.shape[0] * lax.axis_size(AXES),
        got_weighted,
        got_stats,
        own_weighted,
        own_stats,
        full_out,
        up_cols.reshape(width, -1),
        down_rows.reshape(-1, width),
        cot_rows,
        latents,
        tables,
        cotangent,
        counts,
    )
    (
        media_grad,
        latents_grad,
        smalls_grad,
        shard_out,
        shard_value,
        shard_key,
        shard_query,
    ) = closing(
        scale,
        table,
        grad_table,
        terms_table,
        keys,
        values,
        normed,
        valid_rows,
        attn_low,
        middle_low,
        weighted_grad,
        terms,
        line_normed,
        full_query,
        full_key,
        full_value,
        media,
        tables,
        latents,
        middle_grad,
        grad_ffn_gain,
        frame_counts,
        time_index,
    )
    results = ending(
        (
            new_latents,
            media_grad,
            latents_grad,
            shard_query,
            shard_key,
            shard_value,
            shard_out,
            shard_up,
            shard_down,
        ),
        smalls_grad,
        shard,
    )
    time_grad, *gains = results[9:]
    return (
        *results[:3],
        time_grad,
        *(gain.reshape(shard) for gain in gains),
        *results[3:9],
    )


def solution(mesh):
    in_specs = (
        P(("gx", "gy"), None),
        P(("gx", "gy"), None),
        P(),
        P(("gx", "gy")),
        P(("gx", "gy")),
        P(None, ("gx", "gy")),
        P(("gx", "gy")),
        P(("gx", "gy")),
        P(("gx", "gy")),
        P(("gx", "gy"), None),
        P(("gx", "gy"), None),
        P(("gx", "gy"), None),
        P(("gx", "gy"), None),
        P(("gx", "gy"), None),
        P(("gx", "gy"), None),
        P(("gx", "gy"), None),
    )
    out_specs = (
        P(("gx", "gy"), None),
        P(("gx", "gy"), None),
        P(("gx", "gy"), None),
        P(None, ("gx", "gy")),
        P(("gx", "gy")),
        P(("gx", "gy")),
        P(("gx", "gy")),
        P(("gx", "gy"), None),
        P(("gx", "gy"), None),
        P(("gx", "gy"), None),
        P(("gx", "gy"), None),
        P(("gx", "gy"), None),
        P(("gx", "gy"), None),
    )
    return jax.shard_map(
        per_device if dict(mesh.shape) == {"gx": 4, "gy": 8} else plain_device,
        mesh=mesh, in_specs=in_specs, out_specs=out_specs, check_vma=False
    )
```
